32 devices in a mesh: rows: 8 (over z, y), blk: 4 (over x, core).
Axes of the slice: x: 2, y: 2, z: 4, core: 2. Of those that a mesh axis runs over, the one named last changes fastest.
Arguments:
- byte_vals: int32 [32, 1024], P('rows', 'blk'), may hold values from 0 to 255
- segment_ids: int32 [32, 1024], P('rows', 'blk'), may hold values from 0 to 7, never falling along the last dimension, each value on 1 to 512 neighbouring positions
- buckets: int32 [2048], replicated, may hold values from 0 to 31
- emb_table: bfloat16 [256, 512], replicated, may hold values from -6 to 6
- conv_taps: bfloat16 [9, 512], replicated, may hold values from -3 to 3
- w_proj: bfloat16 [512, 512], replicated, may hold values from -0.25 to 0.25
- gain_one: float32 [512], replicated, may hold values from 0.1 to 1.9
- w_qkv: bfloat16 [512, 1536], replicated, may hold values from -0.25 to 0.25
- rel_bias: float32 [32, 8], replicated, may hold values from -4 to 4
- w_out: bfloat16 [512, 512], replicated, may hold values from -1.5 to 1.5
- gain_two: float32 [512], replicated, may hold values from 0.1 to 1.9
- w_in: bfloat16 [512, 4096], replicated, may hold values from -0.25 to 0.25
- w_down: bfloat16 [2048, 512], replicated, may hold values from -0.125 to 0.125
- out_grad: bfloat16 [32, 1024, 512], P('rows', 'blk'), may hold values from -6 to 6
Outputs:
- output: bfloat16 [32, 1024, 512], P('rows', 'blk')
- input_grad: float32 [32, 1024, 512], P('rows', 'blk')
- d_emb_table: float32 [256, 512], replicated
- d_conv_taps: float32 [9, 512], replicated
- d_w_proj: float32 [512, 512], replicated
- d_gain_one: float32 [512], replicated
- d_w_qkv: float32 [512, 1536], replicated
- d_rel_bias: float32 [32, 8], replicated
- d_w_out: float32 [512, 512], replicated
- d_gain_two: float32 [512], replicated
- d_w_in: float32 [512, 4096], replicated
- d_w_down: float32 [2048, 512], replicated
The draws below stay inside these ranges and needn't reach their ends.
Inputs may be any that keep to these rules, and one draw needn't show every extreme that they name: `segment_ids`: segment numbers never fall along a row; every segment of a row lasts 1 to 512 bytes.
All inputs are finite; a program needn't handle non-finite values.
Results may differ from the reference program's by a relative error of at most 0.014.
Values may be sent and summed in bfloat16 or wider, within the bound.
No kernel may reach another device: no remote copies, remote signals or barrier semaphores. Data moves between devices by JAX's collectives and lax.ppermute only.
A program may use at most 192 MiB of HBM per device.

```python
import functools
import math
import jax
import jax.numpy as jnp
import numpy as np
from jax import lax

WIDTH = 512
HEADS = 8
HIDDEN_SIZE = 2048
VOCAB = 256
BUCKETS = 32
ROW_LEN = 1024
DOCS = 8
ROWS = 32


def with_ends(array, rng, least, largest):
    dims = array.shape
    place = [jax.random.randint(jax.random.fold_in(rng, axis), (), 0, dims[axis]) for axis in range(len(dims))]
    array = array.at[tuple(place)].set(least)
    longest = dims.index(max(dims))
    place[longest] = (place[longest] + 1) % dims[longest]
    return array.at[tuple(place)].set(largest)


def steps_of(own_key, shape, shards, least, largest):
    def one(axis_at, parts):
        heights = jax.random.uniform(jax.random.fold_in(jax.random.fold_in(own_key, 6), axis_at), (parts,), jnp.float32, least / len(shards), largest / len(shards))
        return jnp.repeat(jnp.exp(heights), shape[axis_at] // parts).reshape((-1,) + (1,) * (len(shape) - axis_at - 1))

    factor_of = one(*shards[0])
    for cut in shards[1:]:
        factor_of = factor_of * one(*cut)
    return factor_of


def split_up(number_of, total, reach, lean):
    weights = [(1 << 20) // math.isqrt(standing ** lean) + 1 for standing in range(2, number_of + 1)]
    surplus, holding = total - reach - (number_of - 1), [1] * (number_of - 1)
    while surplus > 0:
        movable = [i for i in range(number_of - 1) if holding[i] < reach]
        pool, budget = sum([weights[i] for i in movable]), surplus
        for i in movable:
            addition = min(reach - holding[i], max(1, budget * weights[i] // pool), surplus)
            holding[i] = holding[i] + addition
            surplus = surplus - addition
    return np.array([reach] + holding)


def uneven_parts(rng, count, total, bound, skew):
    if count == 2:
        one = jax.random.randint(rng, (), max(1, total - bound), min(bound, total - 1) + 1)
        return jnp.stack([one, total - one])
    sizes = jnp.asarray(split_up(count, total, bound, skew), jnp.int32)
    couples = (count - 1) // 2
    donor, sink = sizes[1:1 + 2 * couples:2], sizes[2:2 + 2 * couples:2]
    margin = jnp.minimum(donor - 1, bound - sink)
    passed = jax.random.randint(jax.random.fold_in(rng, 1), (couples,), 0, 1 << 20) % (margin + 1)
    sizes = sizes.at[1:1 + 2 * couples:2].set(donor - passed).at[2:2 + 2 * couples:2].set(sink + passed)
    return sizes[jax.random.permutation(jax.random.fold_in(rng, 2), count)]


def normal_values(key, dims, scale, limit, pieces=(), kind=jnp.bfloat16):
    values = jax.random.normal(key, dims, jnp.float32) * scale
    if len(pieces) > 0:
        values = steps_of(key, dims, pieces, -0.22, 0.18) * values
    return jnp.clip(values, min=-limit, max=limit).astype(kind)


def setup_inputs(seed: int = 0) -> dict:
    splits = jax.random.split(jax.random.key(seed), 15)
    byte_vals = with_ends(jax.random.randint(splits[0], (ROWS, ROW_LEN), 0, VOCAB), jax.random.fold_in(splits[0], 1), 0, VOCAB - 1).astype(jnp.int32)
    segment_ids = jax.vmap(lambda own: jnp.searchsorted(jnp.cumsum(uneven_parts(own, DOCS, ROW_LEN, ROW_LEN // 2, 2)), jnp.arange(ROW_LEN), side="right"))(jax.random.split(splits[1], ROWS)).reshape((ROWS, ROW_LEN)).astype(jnp.int32)
    buckets = with_ends(jax.random.randint(splits[2], (2 * ROW_LEN,), 0, BUCKETS), jax.random.fold_in(splits[2], 1), 0, BUCKETS - 1).astype(jnp.int32)
    emb_table = normal_values(splits[3], (VOCAB, WIDTH), 1.0, 6.0)
    conv_taps = normal_values(splits[4], (9, WIDTH), 0.5, 3.0)
    w_proj = normal_values(splits[5], (WIDTH, WIDTH), WIDTH ** -0.5, 0.25)
    gain_one = jnp.clip(1.0 + 0.18 * jax.random.normal(splits[6], (WIDTH,), jnp.float32), 0.1, 1.9)
    w_qkv = normal_values(splits[7], (WIDTH, 3 * WIDTH), WIDTH ** -0.5, 0.25)
    rel_bias = normal_values(splits[8], (BUCKETS, HEADS), 1.0, 4.0, (), jnp.float32)
    w_out = normal_values(splits[9], (WIDTH, WIDTH), (WIDTH // 32) ** -0.5, 1.5)
    gain_two = jnp.clip(1.0 + 0.18 * jax.random.normal(splits[10], (WIDTH,), jnp.float32), 0.1, 1.9)
    w_in = normal_values(splits[11], (WIDTH, 2 * HIDDEN_SIZE), WIDTH ** -0.5, 0.25)
    w_down = normal_values(splits[12], (HIDDEN_SIZE, WIDTH), HIDDEN_SIZE ** -0.5, 0.125)
    out_grad = normal_values(splits[13], (ROWS, ROW_LEN, WIDTH), 1.0, 6.0, ((0, 8), (1, 4)))
    return dict(byte_vals=byte_vals, segment_ids=segment_ids, buckets=buckets, emb_table=emb_table, conv_taps=conv_taps, w_proj=w_proj, gain_one=gain_one, w_qkv=w_qkv, rel_bias=rel_bias, w_out=w_out, gain_two=gain_two, w_in=w_in, w_down=w_down, out_grad=out_grad)


EPSILON = 1e-06
SCORE_SCALE = 0.125
NEGATIVE = -1000000000.0
WINDOWS = ((0, 2), (2, 3), (5, 4))
HIGHEST_PRECISION = lax.Precision.HIGHEST

@jax.custom_vjp
def low(v):
    return lax.optimization_barrier(v.astype(jnp.bfloat16)).astype(jnp.float32)

@jax.custom_vjp
def low_back(v):
    return v

def low_keep(v):
    return (low(v), None)

def low_pass(kept, grad):
    return (grad,)

def back_keep(v):
    return (v, None)

def back_low(kept, grad):
    return (low(grad),)
low.defvjp(low_keep, low_pass)
low_back.defvjp(back_keep, back_low)

def rms_scale(values, gain):
    return values * lax.rsqrt(lax.optimization_barrier(jnp.mean(values * values, axis=-1, keepdims=True)) + EPSILON) * gain

def matmul(left, right):
    return jnp.dot(left, right, precision=HIGHEST_PRECISION)

def conv_mix(embedded, taps, segments):
    length = embedded.shape[1]
    total = jnp.zeros_like(embedded)
    for first, span in WINDOWS:
        summed = jnp.zeros_like(embedded)
        for lag in range(span):
            moved = jnp.pad(embedded, ((0, 0), (lag, 0), (0, 0)))[:, :length]
            moved_seg = jnp.pad(segments, ((0, 0), (lag, 0)), constant_values=-1)[:, :length]
            keep = (moved_seg == segments)[..., None]
            summed = summed + jnp.where(keep, moved, 0.0) * taps[first + lag]
        total = total + jax.nn.gelu(summed, approximate=True)
    return total

def attend_row(rel_bias, buckets, item):
    row_qkv, row_seg = item
    length = row_qkv.shape[0]
    width = row_qkv.shape[1] // 3
    heads = rel_bias.shape[1]
    head_dim = width // heads
    queries = row_qkv[:, :width].reshape(length, heads, head_dim)
    keys = row_qkv[:, width:2 * width].reshape(length, heads, head_dim)
    values = row_qkv[:, 2 * width:].reshape(length, heads, head_dim)
    scores = jnp.einsum('qhd,khd->hqk', queries, keys, precision=HIGHEST_PRECISION) * SCORE_SCALE
    places = jnp.arange(length, dtype=jnp.int32)
    picked = buckets[places[:, None] - places[None, :] + length]
    bias = jnp.transpose(rel_bias[picked], (2, 0, 1))
    scores = low_back(scores + bias)
    same = (row_seg[:, None] == row_seg[None, :])[None]
    scores = jnp.where(same, scores, NEGATIVE)
    probs = low(jax.nn.softmax(scores, axis=-1))
    mixed = jnp.einsum('hqk,khd->qhd', probs, values, precision=HIGHEST_PRECISION)
    return mixed.reshape(length, width)

def forward(embedded, segments, buckets, params):
    taps, w_proj, gain_one, w_qkv, rel_bias, w_out, gain_two, w_in, w_down = params
    hidden = w_down.shape[0]
    conv_sum = low(conv_mix(embedded, taps, segments))
    resid = low_back(matmul(conv_sum, w_proj))
    normed_one = low(rms_scale(resid, gain_one))
    qkv = low_back(low(matmul(normed_one, w_qkv)))
    attn = lax.map(jax.checkpoint(functools.partial(attend_row, rel_bias, buckets)), (qkv, segments))
    attn = low_back(low(attn))
    mid = resid + low_back(matmul(attn, w_out))
    normed_two = low(rms_scale(mid, gain_two))
    gate_up = matmul(normed_two, w_in)
    gate = low_back(gate_up[..., :hidden])
    upper = low_back(gate_up[..., hidden:])
    inner = low(jax.nn.gelu(gate, approximate=True) * upper)
    return mid + matmul(inner, w_down)

def reference(byte_vals, segment_ids, buckets, emb_table, conv_taps, w_proj, gain_one, w_qkv, rel_bias, w_out, gain_two, w_in, w_down, out_grad):
    params = tuple((weight.astype(jnp.float32) for weight in (conv_taps, w_proj, gain_one, w_qkv, rel_bias, w_out, gain_two, w_in, w_down)))
    table = emb_table.astype(jnp.float32)
    group = math.gcd(ROWS, max(1, 4096 // ROW_LEN))
    count = ROWS // group
    items = (byte_vals.reshape(count, group, ROW_LEN), segment_ids.reshape(count, group, ROW_LEN), out_grad.reshape(count, group, ROW_LEN, WIDTH))

    def group_step(totals, item):
        row_bytes, row_segs, row_grads = item
        embedded, table_back = jax.vjp(lambda whole: whole[row_bytes], table)
        result, pull_back = jax.vjp(lambda inputs, weights: forward(inputs, row_segs, buckets, weights), embedded, params)
        d_embedded, d_params = pull_back(row_grads.astype(jnp.float32))
        d_table, = table_back(d_embedded)
        totals = jax.tree.map(jnp.add, totals, (d_table,) + tuple(d_params))
        return (totals, (result.astype(jnp.bfloat16), d_embedded))
    zeros = (jnp.zeros_like(table),) + tuple((jnp.zeros_like(weight) for weight in params))
    totals, (outputs, input_grads) = lax.scan(group_step, zeros, items)
    return (outputs.reshape(ROWS, ROW_LEN, WIDTH), input_grads.reshape(ROWS, ROW_LEN, WIDTH), totals[0], totals[1], totals[2], totals[3], totals[4], totals[5], totals[6], totals[7], totals[8], totals[9])
```

```python
import functools

import jax
import jax.numpy as jnp
from jax import lax
from jax.experimental import pallas as pl
from jax.experimental.pallas import tpu as pltpu
from jax.sharding import PartitionSpec as P

EPSILON = 1e-06
SCORE_SCALE = 0.125
WINDOWS = ((0, 2), (2, 3), (5, 4))
HIGHEST_PRECISION = lax.Precision.HIGHEST
LANES = 128
QUERY_TILE = 256
KEY_TILE = 128
MASKED = -(2.0**30)
REACH = 512
BAND = 12 * LANES
BAND_FIRST = 3 * LANES
VMEM_LIMIT = 60 * 2**20


def vmem():
    return pl.BlockSpec(memory_space=pltpu.VMEM)


def smem():
    return pl.BlockSpec(memory_space=pltpu.SMEM)


def params():
    return pltpu.CompilerParams(vmem_limit_bytes=VMEM_LIMIT)


def dot_nt(left, right):
    return lax.dot_general(
        left, right, (((1,), (1,)), ((), ())), preferred_element_type=jnp.float32
    )


def dot_nn(left, right):
    return jnp.dot(left, right, preferred_element_type=jnp.float32)


def bias_tables_kernel(base_ref, out_ref):
    heads = base_ref.shape[0]
    for head in range(heads):
        line = jnp.broadcast_to(base_ref[head : head + 1, :], (KEY_TILE, BAND))
        out_ref[head] = pltpu.roll(line, 0, 1, stride=1, stride_axis=0)


def bias_tables(base):
    heads = base.shape[0]
    return pl.pallas_call(
        bias_tables_kernel,
        out_shape=jax.ShapeDtypeStruct((heads, KEY_TILE, BAND), jnp.float32),
        in_specs=[vmem()],
        out_specs=vmem(),
        compiler_params=params(),
        name="bias_tables",
    )(base)


def table_lanes(query_block, key_block):
    place = (query_block * (QUERY_TILE // LANES) - key_block + 5) * LANES
    return pl.ds(pl.multiple_of(place, LANES), QUERY_TILE)


def attend_kernel(
    heads, bounds_ref, qkv_ref, same_q_ref, same_k_ref, table_ref,
    attn_ref, lse_ref,
    value_t_ref, query_ref, top_ref, total_ref, mixed_ref,
):
    length = qkv_ref.shape[0]
    width = qkv_ref.shape[1] // 3
    head_dim = width // heads
    lane = lax.broadcasted_iota(jnp.int32, (1, LANES), 1)
    low_half = (lane < head_dim).astype(jnp.bfloat16)
    high_half = (lane >= head_dim).astype(jnp.bfloat16)
    value_t_ref[...] = qkv_ref[:, 2 * width :].T

    def block(i, carry):
        rows = pl.ds(pl.multiple_of(i * QUERY_TILE, QUERY_TILE), QUERY_TILE)
        for pair in range(heads // 2):
            query = qkv_ref[rows, pair * LANES : (pair + 1) * LANES] * jnp.bfloat16(SCORE_SCALE)
            query_ref[2 * pair, :, :LANES] = query * low_half
            query_ref[2 * pair + 1, :, :LANES] = query * high_half
            query_ref[2 * pair, :, LANES:] = same_q_ref[rows, :]
            query_ref[2 * pair + 1, :, LANES:] = same_q_ref[rows, :]
        top_ref[...] = jnp.full_like(top_ref, -3.0e38)
        total_ref[...] = jnp.zeros_like(total_ref)
        mixed_ref[...] = jnp.zeros_like(mixed_ref)

        def step(j, inner):
            keys = pl.ds(pl.multiple_of(j * KEY_TILE, KEY_TILE), KEY_TILE)
            lanes = table_lanes(i, j)
            for head in range(heads):
                pair = head // 2
                key = jnp.concatenate(
                    [
                        qkv_ref[keys, width + pair * LANES : width + (pair + 1) * LANES],
                        same_k_ref[keys, :],
                    ],
                    axis=1,
                )
                scores = dot_nt(key, query_ref[head]) + table_ref[head, :, lanes]
                old = top_ref[head : head + 1, :]
                top = jnp.maximum(old, jnp.max(scores, axis=0, keepdims=True))
                fade = jnp.exp(old - top)
                expo = jnp.exp(scores - top)
                top_ref[head : head + 1, :] = top
                total_ref[head : head + 1, :] = total_ref[head : head + 1, :] * fade + jnp.sum(
                    expo, axis=0, keepdims=True
                )
                own = slice(head * head_dim, (head + 1) * head_dim)
                mixed_ref[own, :] = mixed_ref[own, :] * fade + dot_nn(
                    value_t_ref[own, keys], expo.astype(jnp.bfloat16)
                )
            return inner

        lax.fori_loop(bounds_ref[0, i], bounds_ref[1, i], step, 0)
        for head in range(heads):
            own = slice(head * head_dim, (head + 1) * head_dim)
            mixed_ref[own, :] = mixed_ref[own, :] / total_ref[head : head + 1, :]
        attn_ref[rows, :] = mixed_ref[...].T.astype(jnp.bfloat16)
        lse_ref[:, rows] = top_ref[...] + jnp.log(total_ref[...])
        return carry

    lax.fori_loop(0, length // QUERY_TILE, block, 0)


def attend(bounds, qkv, same_q, same_k, table):
    length = qkv.shape[0]
    width = qkv.shape[1] // 3
    heads = table.shape[0]
    return pl.pallas_call(
        functools.partial(attend_kernel, heads),
        out_shape=(
            jax.ShapeDtypeStruct((length, width), jnp.bfloat16),
            jax.ShapeDtypeStruct((heads, length), jnp.float32),
        ),
        in_specs=[smem(), vmem(), vmem(), vmem(), vmem()],
        out_specs=(vmem(), vmem()),
        scratch_shapes=[
            pltpu.VMEM((width, length), jnp.bfloat16),
            pltpu.VMEM((heads, QUERY_TILE, 2 * LANES), jnp.bfloat16),
            pltpu.VMEM((heads, QUERY_TILE), jnp.float32),
            pltpu.VMEM((heads, QUERY_TILE), jnp.float32),
            pltpu.VMEM((width, QUERY_TILE), jnp.float32),
        ],
        compiler_params=params(),
        cost_estimate=pl.CostEstimate(
            flops=4 * length * length * width,
            bytes_accessed=12 * 2**20,
            transcendentals=length * length * heads,
        ),
        name="attend",
    )(bounds, qkv, same_q, same_k, table)


def attend_back_kernel(
    heads, bounds_ref, qkv_ref, same_q_ref, same_k_ref, table_ref, lse_ref, attn_ref, grad_ref,
    back_ref, band_ref,
    key_t_ref, query_ref, grads_ref, inner_ref, query_back_ref, key_back_ref, value_back_ref,
    skewed_ref,
):
    length = qkv_ref.shape[0]
    width = qkv_ref.shape[1] // 3
    head_dim = width // heads
    lane = lax.broadcasted_iota(jnp.int32, (1, LANES), 1)
    halves = (
        (lane < head_dim).astype(jnp.bfloat16),
        (lane >= head_dim).astype(jnp.bfloat16),
    )
    owner = lax.broadcasted_iota(jnp.int32, (heads, width), 1) // head_dim
    own_head = (owner == lax.broadcasted_iota(jnp.int32, (heads, width), 0)).astype(jnp.bfloat16)
    key_t_ref[...] = qkv_ref[:, width : 2 * width].T
    key_back_ref[...] = jnp.zeros_like(key_back_ref)
    value_back_ref[...] = jnp.zeros_like(value_back_ref)
    skewed_ref[...] = jnp.zeros_like(skewed_ref)

    def block(i, carry):
        rows = pl.ds(pl.multiple_of(i * QUERY_TILE, QUERY_TILE), QUERY_TILE)
        for pair in range(heads // 2):
            own = slice(pair * LANES, (pair + 1) * LANES)
            query = qkv_ref[rows, own] * jnp.bfloat16(SCORE_SCALE)
            grad = grad_ref[rows, own]
            for side in range(2):
                part = slice(side * QUERY_TILE, (side + 1) * QUERY_TILE)
                query_ref[pair, part, :LANES] = query * halves[side]
                query_ref[pair, part, LANES:] = same_q_ref[rows, :]
                grads_ref[pair, part, :] = grad * halves[side]
        product = grad_ref[rows, :].astype(jnp.float32) * attn_ref[rows, :].astype(jnp.float32)
        rough = product.astype(jnp.bfloat16)
        rest = (product - rough.astype(jnp.float32)).astype(jnp.bfloat16)
        inner_ref[...] = dot_nt(own_head, rough) + dot_nt(own_head, rest)
        query_back_ref[...] = jnp.zeros_like(query_back_ref)

        def step(j, inner):
            keys = pl.ds(pl.multiple_of(j * KEY_TILE, KEY_TILE), KEY_TILE)
            lanes = table_lanes(i, j)
            for pair in range(heads // 2):
                own = slice(pair * LANES, (pair + 1) * LANES)
                key = jnp.concatenate(
                    [
                        qkv_ref[keys, width + pair * LANES : width + (pair + 1) * LANES],
                        same_k_ref[keys, :],
                    ],
                    axis=1,
                )
                value = qkv_ref[keys, 2 * width + pair * LANES : 2 * width + (pair + 1) * LANES]
                probs = []
                d_scores = []
                for side in range(2):
                    head = 2 * pair + side
                    part = slice(side * QUERY_TILE, (side + 1) * QUERY_TILE)
                    scores = dot_nt(key, query_ref[pair, part, :]) + table_ref[head, :, lanes]
                    exact = jnp.exp(scores - lse_ref[head : head + 1, rows])
                    d_probs = dot_nt(value, grads_ref[pair, part, :])
                    d_score = exact * (d_probs - inner_ref[head : head + 1, :])
                    skewed_ref[head, :, lanes] = skewed_ref[head, :, lanes] + d_score
                    probs.append(exact.astype(jnp.bfloat16))
                    d_scores.append(d_score.astype(jnp.bfloat16))
                    mine = slice(head * head_dim, (head + 1) * head_dim)
                    query_back_ref[mine, :] += dot_nn(key_t_ref[mine, keys], d_scores[side])
                value_back_ref[keys, own] += dot_nn(
                    jnp.concatenate(probs, axis=1), grads_ref[pair]
                )
                key_back_ref[keys, own] += dot_nn(
                    jnp.concatenate(d_scores, axis=1), query_ref[pair, :, :LANES]
                )
            return inner

        lax.fori_loop(bounds_ref[0, i], bounds_ref[1, i], step, 0)
        back_ref[rows, :width] = (query_back_ref[...].T * SCORE_SCALE).astype(jnp.bfloat16)
        return carry

    lax.fori_loop(0, length // QUERY_TILE, block, 0)
    back_ref[:, width : 2 * width] = key_back_ref[...].astype(jnp.bfloat16)
    back_ref[:, 2 * width :] = value_back_ref[...].astype(jnp.bfloat16)
    for head in range(heads):
        height = KEY_TILE
        while height > 8:
            height //= 2
            skewed_ref[head, :height, :] = skewed_ref[head, :height, :] + pltpu.roll(
                skewed_ref[head, height : 2 * height, :], BAND - height, 1
            )
        total = skewed_ref[head, 0:1, :]
        for row in range(1, 8):
            total = total + pltpu.roll(skewed_ref[head, row : row + 1, :], BAND - row, 1)
        band_ref[head : head + 1, :] = total


def attend_back(bounds, qkv, same_q, same_k, table, lse, attn, grad):
    length = qkv.shape[0]
    width = qkv.shape[1] // 3
    heads = table.shape[0]
    return pl.pallas_call(
        functools.partial(attend_back_kernel, heads),
        out_shape=(
            jax.ShapeDtypeStruct((length, 3 * width), jnp.bfloat16),
            jax.ShapeDtypeStruct((heads, BAND), jnp.float32),
        ),
        in_specs=[smem()] + [vmem()] * 7,
        out_specs=(vmem(), vmem()),
        scratch_shapes=[
            pltpu.VMEM((width, length), jnp.bfloat16),
            pltpu.VMEM((heads // 2, 2 * QUERY_TILE, 2 * LANES), jnp.bfloat16),
            pltpu.VMEM((heads // 2, 2 * QUERY_TILE, LANES), jnp.bfloat16),
            pltpu.VMEM((heads, QUERY_TILE), jnp.float32),
            pltpu.VMEM((width, QUERY_TILE), jnp.float32),
            pltpu.VMEM((length, width), jnp.float32),
            pltpu.VMEM((length, width), jnp.float32),
            pltpu.VMEM((heads, KEY_TILE, BAND), jnp.float32),
        ],
        compiler_params=params(),
        cost_estimate=pl.CostEstimate(
            flops=10 * length * length * width,
            bytes_accessed=16 * 2**20,
            transcendentals=length * length * heads,
        ),
        name="attend_back",
    )(bounds, qkv, same_q, same_k, table, lse, attn, grad)


def document_bounds(segments):
    length = segments.shape[0]
    starts = segments[::QUERY_TILE]
    ends = segments[QUERY_TILE - 1 :: QUERY_TILE]
    before = jnp.sum((segments[None, :] < starts[:, None]).astype(jnp.int32), axis=1)
    upto = jnp.sum((segments[None, :] <= ends[:, None]).astype(jnp.int32), axis=1)
    return jnp.stack([before // KEY_TILE, (upto + KEY_TILE - 1) // KEY_TILE])


def document_marks(segments):
    own = segments[:, None] == jnp.arange(LANES, dtype=jnp.int32)[None, :]
    return own.astype(jnp.bfloat16), jnp.where(own, 0.0, MASKED).astype(jnp.bfloat16)


def rms_scale(values, gain):
    return values * lax.rsqrt(jnp.mean(values * values, axis=-1, keepdims=True) + EPSILON) * gain


def gelu_tanh(values):
    return jax.nn.gelu(values, approximate=True)


def gated(gate, upper):
    return gelu_tanh(gate) * upper


def dot_tn(left, right):
    return lax.dot_general(
        left, right, (((0,), (0,)), ((), ())), preferred_element_type=jnp.float32
    )


def to_rows(block, share):
    rows, stretch = block.shape[:2]
    pieces = jnp.repeat(block, share, axis=0) if share > 1 else block
    pieces = lax.all_to_all(pieces, "blk", 0, 0, tiled=True)
    return pieces.reshape((rows * share * stretch,) + block.shape[2:])


def to_blocks(row, share):
    blocks = lax.axis_size("blk")
    pieces = row.reshape((blocks, row.shape[0] // blocks) + row.shape[1:])
    return lax.all_to_all(pieces, "blk", 0, 0, tiled=True)[::share]


def later(values, lag):
    if lag == 0:
        return values
    return jnp.pad(values, ((lag, 0), (0, 0)))[: values.shape[0]]


def earlier(values, lag):
    if lag == 0:
        return values
    return jnp.pad(values, ((0, lag), (0, 0)))[lag:]


def on_device(
    byte_vals,
    segment_ids,
    buckets,
    emb_table,
    conv_taps,
    w_proj,
    gain_one,
    w_qkv,
    rel_bias,
    w_out,
    gain_two,
    w_in,
    w_down,
    out_grad,
):
    rows, stretch = byte_vals.shape
    vocab, width = emb_table.shape
    bucket_count, heads = rel_bias.shape
    hidden = w_down.shape[0]
    blocks = lax.axis_size("blk")
    share = blocks // rows
    length = stretch * blocks

    packed = to_rows(byte_vals + vocab * segment_ids, share)
    letters_own = packed % vocab
    segments = packed // vocab
    grad_low = to_rows(out_grad, share)

    own_hot = (letters_own[:, None] == jnp.arange(vocab, dtype=jnp.int32)[None, :]).astype(
        jnp.bfloat16
    )
    embedded = dot_nn(own_hot, emb_table)
    taps = conv_taps.astype(jnp.float32)
    seg_col = segments[:, None] + 1
    keeps = [later(seg_col, lag) == seg_col for lag in range(4)]
    shifted = [jnp.where(keeps[lag], later(embedded, lag), 0.0) for lag in range(4)]
    conv_sum = jnp.zeros((length, width), jnp.float32)
    gelu_backs = []
    for first, span in WINDOWS:
        summed = jnp.zeros((length, width), jnp.float32)
        for lag in range(span):
            summed = summed + shifted[lag] * taps[first + lag]
        activated, gelu_back = jax.vjp(gelu_tanh, summed)
        gelu_backs.append(gelu_back)
        conv_sum = conv_sum + activated
    conv_low = conv_sum.astype(jnp.bfloat16)
    resid = dot_nn(conv_low, w_proj)
    normed_f, norm_one_back = jax.vjp(rms_scale, resid, gain_one)
    normed_one = normed_f.astype(jnp.bfloat16)
    qkv = dot_nn(normed_one, w_qkv).astype(jnp.bfloat16)

    band_buckets = lax.slice_in_dim(buckets, BAND_FIRST, BAND_FIRST + BAND - LANES)
    band_buckets = jnp.concatenate(
        [band_buckets, lax.slice_in_dim(buckets, BAND_FIRST - LANES, BAND_FIRST)]
    )
    bucket_hot = (
        band_buckets[:, None] == jnp.arange(bucket_count, dtype=jnp.int32)[None, :]
    ).astype(jnp.float32)
    base = lax.dot_general(
        rel_bias, bucket_hot, (((0,), (1,)), ((), ())), precision=HIGHEST_PRECISION
    )
    table = bias_tables(base)
    bounds = document_bounds(segments)
    same_q, same_k = document_marks(segments)
    attn, lse = attend(bounds, qkv, same_q, same_k, table)

    mid = resid + dot_nn(attn, w_out)
    normed_g, norm_two_back = jax.vjp(rms_scale, mid, gain_two)
    normed_two = normed_g.astype(jnp.bfloat16)
    gate_up = dot_nn(normed_two, w_in)
    inner, gated_back = jax.vjp(gated, gate_up[:, :hidden], gate_up[:, hidden:])
    inner_low = inner.astype(jnp.bfloat16)
    output = to_blocks((mid + dot_nn(inner_low, w_down)).astype(jnp.bfloat16), share)
    d_w_down = dot_tn(inner_low, grad_low)
    d_inner = dot_nt(grad_low, w_down)
    d_gate, d_upper = gated_back(d_inner)
    d_gate_up = jnp.concatenate([d_gate, d_upper], axis=1).astype(jnp.bfloat16)
    d_w_in = dot_tn(normed_two, d_gate_up)
    d_normed_two = dot_nt(d_gate_up, w_in)
    d_mid_norm, d_gain_two = norm_two_back(d_normed_two)
    d_mid = grad_low.astype(jnp.float32) + d_mid_norm
    d_branch = d_mid.astype(jnp.bfloat16)
    d_w_out = dot_tn(attn, d_branch)
    d_attn = dot_nt(d_branch, w_out).astype(jnp.bfloat16)

    early = lax.psum(
        tuple(grad.astype(jnp.bfloat16) for grad in (d_w_in, d_w_down, d_w_out)), ("rows", "blk")
    )

    d_qkv, band = attend_back(bounds, qkv, same_q, same_k, table, lse, attn, d_attn)
    d_rel_bias = lax.dot_general(
        bucket_hot, band, (((0,), (1,)), ((), ())), precision=HIGHEST_PRECISION
    )
    d_w_qkv = dot_tn(normed_one, d_qkv)
    d_normed_one = dot_nt(d_qkv, w_qkv)
    d_resid_norm, d_gain_one = norm_one_back(d_normed_one)
    d_resid = (d_mid + d_resid_norm).astype(jnp.bfloat16)
    d_w_proj = dot_tn(conv_low, d_resid)
    d_conv = dot_nt(d_resid, w_proj)
    d_shifted = [jnp.zeros((length, width), jnp.float32) for lag in range(4)]
    tap_rows = [None] * 9
    for index, (first, span) in enumerate(WINDOWS):
        (d_pre,) = gelu_backs[index](d_conv)
        for lag in range(span):
            tap_rows[first + lag] = jnp.sum(d_pre * shifted[lag], axis=0)
            d_shifted[lag] = d_shifted[lag] + d_pre * taps[first + lag]
    d_conv_taps = jnp.stack(tap_rows, axis=0)
    input_row = jnp.zeros((length, width), jnp.float32)
    for lag in range(4):
        input_row = input_row + earlier(jnp.where(keeps[lag], d_shifted[lag], 0.0), lag)
    input_low = input_row.astype(jnp.bfloat16)
    input_grad = to_blocks(input_low, share).astype(jnp.float32)
    d_emb_table = dot_tn(own_hot, input_low)

    late = lax.psum(
        tuple(grad.astype(jnp.bfloat16) for grad in (d_emb_table, d_w_proj, d_w_qkv)),
        ("rows", "blk"),
    )
    small = lax.psum((d_conv_taps, d_gain_one, d_rel_bias, d_gain_two), ("rows", "blk"))
    scale = 1.0 / share
    d_w_in, d_w_down, d_w_out = (grad.astype(jnp.float32) * scale for grad in early)
    d_emb_table, d_w_proj, d_w_qkv = (grad.astype(jnp.float32) * scale for grad in late)
    d_conv_taps, d_gain_one, d_rel_bias, d_gain_two = (grad * scale for grad in small)
    return (
        output,
        input_grad,
        d_emb_table,
        d_conv_taps,
        d_w_proj,
        d_gain_one,
        d_w_qkv,
        d_rel_bias,
        d_w_out,
        d_gain_two,
        d_w_in,
        d_w_down,
    )


def solution(mesh):
    split = P("rows", "blk")
    split_wide = P("rows", "blk", None)
    return jax.shard_map(
        on_device,
        mesh=mesh,
        in_specs=(split, split) + (P(),) * 11 + (split_wide,),
        out_specs=(split_wide, split_wide) + (P(),) * 10,
        check_vma=False,
    )
```

```python
import functools

import jax
import jax.numpy as jnp
from jax import lax
from jax.experimental import pallas as pl
from jax.experimental.pallas import tpu as pltpu
from jax.sharding import PartitionSpec as P

EPSILON = 1e-06
SCORE_SCALE = 0.125
WINDOWS = ((0, 2), (2, 3), (5, 4))
HIGHEST_PRECISION = lax.Precision.HIGHEST
LANES = 128
QUERY_TILE = 256
KEY_TILE = 128
MASKED = -(2.0**30)
PARTS = 2
BAND = 12 * LANES
BAND_FIRST = 3 * LANES
VMEM_LIMIT = 60 * 2**20


def vmem():
    return pl.BlockSpec(memory_space=pltpu.VMEM)


def smem():
    return pl.BlockSpec(memory_space=pltpu.SMEM)


def params():
    return pltpu.CompilerParams(vmem_limit_bytes=VMEM_LIMIT)


def dot_nt(left, right):
    return lax.dot_general(
        left, right, (((1,), (1,)), ((), ())), preferred_element_type=jnp.float32
    )


def dot_nn(left, right):
    return jnp.dot(left, right, preferred_element_type=jnp.float32)


def bias_tables_kernel(base_ref, out_ref):
    heads = base_ref.shape[0]
    for head in range(heads):
        line = jnp.broadcast_to(base_ref[head : head + 1, :], (KEY_TILE, BAND))
        out_ref[head] = pltpu.roll(line, 0, 1, stride=1, stride_axis=0)


def bias_tables(base):
    heads = base.shape[0]
    return pl.pallas_call(
        bias_tables_kernel,
        out_shape=jax.ShapeDtypeStruct((heads, KEY_TILE, BAND), jnp.float32),
        in_specs=[vmem()],
        out_specs=vmem(),
        compiler_params=params(),
        name="bias_tables",
    )(base)


def table_lanes(query_block, key_block):
    place = (query_block * (QUERY_TILE // LANES) - key_block + 5) * LANES
    return pl.ds(pl.multiple_of(place, LANES), QUERY_TILE)


def attend_kernel(
    heads, bounds_ref, qkv_ref, same_q_ref, same_k_ref, table_ref,
    attn_ref, lse_ref,
    value_t_ref, query_ref, top_ref, total_ref, mixed_ref, score_ref, expo_ref, fade_ref,
):
    length = qkv_ref.shape[0]
    width = qkv_ref.shape[1] // 3
    head_dim = width // heads
    lane = lax.broadcasted_iota(jnp.int32, (1, LANES), 1)
    halves = (
        (lane < head_dim).astype(jnp.bfloat16),
        (lane >= head_dim).astype(jnp.bfloat16),
    )
    value_t_ref[...] = qkv_ref[:, 2 * width :].T

    def block(i, carry):
        rows = pl.ds(pl.multiple_of(i * QUERY_TILE, QUERY_TILE), QUERY_TILE)
        for pair in range(heads // 2):
            query = qkv_ref[rows, pair * LANES : (pair + 1) * LANES] * jnp.bfloat16(SCORE_SCALE)
            for side in range(2):
                query_ref[2 * pair + side, :LANES, :] = (query * halves[side]).T
                query_ref[2 * pair + side, LANES:, :] = same_q_ref[:, rows]
        top_ref[...] = jnp.full_like(top_ref, -3.0e38)
        total_ref[...] = jnp.zeros_like(total_ref)
        mixed_ref[...] = jnp.zeros_like(mixed_ref)

        def step(j, inner):
            keys = pl.ds(pl.multiple_of(j * KEY_TILE, KEY_TILE), KEY_TILE)
            lanes = table_lanes(i, j)
            for head in range(heads):
                pair = head // 2
                key = jnp.concatenate(
                    [
                        qkv_ref[keys, width + pair * LANES : width + (pair + 1) * LANES],
                        same_k_ref[keys, :],
                    ],
                    axis=1,
                )
                score_ref[head] = dot_nn(key, query_ref[head]) + table_ref[head, :, lanes]
            for head in range(heads):
                scores = score_ref[head]
                old = top_ref[head : head + 1, :]
                top = jnp.maximum(old, jnp.max(scores, axis=0, keepdims=True))
                fade = jnp.exp(old - top)
                expo = jnp.exp(scores - top)
                top_ref[head : head + 1, :] = top
                total_ref[head : head + 1, :] = total_ref[head : head + 1, :] * fade + jnp.sum(
                    expo, axis=0, keepdims=True
                )
                fade_ref[head : head + 1, :] = fade
                expo_ref[head] = expo.astype(jnp.bfloat16)
            for head in range(heads):
                own = slice(head * head_dim, (head + 1) * head_dim)
                mixed_ref[own, :] = mixed_ref[own, :] * fade_ref[head : head + 1, :] + dot_nn(
                    value_t_ref[own, keys], expo_ref[head]
                )
            return inner

        lax.fori_loop(bounds_ref[0, i], bounds_ref[1, i], step, 0)
        for head in range(heads):
            own = slice(head * head_dim, (head + 1) * head_dim)
            mixed_ref[own, :] = mixed_ref[own, :] / total_ref[head : head + 1, :]
        attn_ref[rows, :] = mixed_ref[...].T.astype(jnp.bfloat16)
        lse_ref[:, rows] = top_ref[...] + jnp.log(total_ref[...])
        return carry

    lax.fori_loop(0, length // QUERY_TILE, block, 0)


def attend(bounds, qkv, same_q, same_k, table):
    length = qkv.shape[0]
    width = qkv.shape[1] // 3
    heads = table.shape[0]
    return pl.pallas_call(
        functools.partial(attend_kernel, heads),
        out_shape=(
            jax.ShapeDtypeStruct((length, width), jnp.bfloat16),
            jax.ShapeDtypeStruct((heads, length), jnp.float32),
        ),
        in_specs=[smem(), vmem(), vmem(), vmem(), vmem()],
        out_specs=(vmem(), vmem()),
        scratch_shapes=[
            pltpu.VMEM((width, length), jnp.bfloat16),
            pltpu.VMEM((heads, 2 * LANES, QUERY_TILE), jnp.bfloat16),
            pltpu.VMEM((heads, QUERY_TILE), jnp.float32),
            pltpu.VMEM((heads, QUERY_TILE), jnp.float32),
            pltpu.VMEM((width, QUERY_TILE), jnp.float32),
            pltpu.VMEM((heads, KEY_TILE, QUERY_TILE), jnp.float32),
            pltpu.VMEM((heads, KEY_TILE, QUERY_TILE), jnp.bfloat16),
            pltpu.VMEM((heads, QUERY_TILE), jnp.float32),
        ],
        compiler_params=params(),
        cost_estimate=pl.CostEstimate(
            flops=4 * length * length * width,
            bytes_accessed=12 * 2**20,
            transcendentals=length * length * heads,
        ),
        name="attend",
    )(bounds, qkv, same_q, same_k, table)


def attend_back_kernel(
    first, bounds_ref, q_ref, k_ref, v_ref, same_q_ref, same_k_ref, table_ref, lse_ref,
    attn_ref, grad_ref, *refs,
):
    (
        query_out_ref, key_out_ref, value_out_ref, band_ref,
        key_t_ref, query_ref, grads_ref, query_t_ref, grads_t_ref, inner_ref,
        query_back_ref, key_back_ref, value_back_ref, skewed_ref,
        exact_ref, probs_ref, d_scores_ref,
    ) = refs[-17:]
    length, width = q_ref.shape
    heads = table_ref.shape[0]
    head_dim = width // heads
    lane = lax.broadcasted_iota(jnp.int32, (1, LANES), 1)
    halves = (
        (lane < head_dim).astype(jnp.bfloat16),
        (lane >= head_dim).astype(jnp.bfloat16),
    )
    owner = lax.broadcasted_iota(jnp.int32, (heads, width), 1) // head_dim
    own_head = (owner == lax.broadcasted_iota(jnp.int32, (heads, width), 0)).astype(jnp.bfloat16)
    key_t_ref[...] = k_ref[...].T
    key_back_ref[...] = jnp.zeros_like(key_back_ref)
    value_back_ref[...] = jnp.zeros_like(value_back_ref)
    skewed_ref[...] = jnp.zeros_like(skewed_ref)

    def block(i, carry):
        rows = pl.ds(pl.multiple_of(i * QUERY_TILE, QUERY_TILE), QUERY_TILE)
        for pair in range(heads // 2):
            own = slice(pair * LANES, (pair + 1) * LANES)
            query = q_ref[rows, own] * jnp.bfloat16(SCORE_SCALE)
            grad = grad_ref[rows, own]
            for side in range(2):
                part = slice(side * QUERY_TILE, (side + 1) * QUERY_TILE)
                query_ref[pair, part, :] = query * halves[side]
                grads_ref[pair, part, :] = grad * halves[side]
                query_t_ref[2 * pair + side, :LANES, :] = (query * halves[side]).T
                query_t_ref[2 * pair + side, LANES:, :] = same_q_ref[:, rows]
                grads_t_ref[2 * pair + side] = (grad * halves[side]).T
        product = grad_ref[rows, :].astype(jnp.float32) * attn_ref[rows, :].astype(jnp.float32)
        rough = product.astype(jnp.bfloat16)
        rest = (product - rough.astype(jnp.float32)).astype(jnp.bfloat16)
        inner_ref[...] = dot_nt(own_head, rough) + dot_nt(own_head, rest)
        query_back_ref[...] = jnp.zeros_like(query_back_ref)

        def step(j, inner):
            keys = pl.ds(pl.multiple_of(j * KEY_TILE, KEY_TILE), KEY_TILE)
            lanes = table_lanes(i, j)
            for head in range(heads):
                pair = head // 2
                key = jnp.concatenate(
                    [k_ref[keys, pair * LANES : (pair + 1) * LANES], same_k_ref[keys, :]], axis=1
                )
                scores = dot_nn(key, query_t_ref[head]) + table_ref[head, :, lanes]
                exact_ref[head] = jnp.exp(scores - lse_ref[first + head : first + head + 1, rows])
            for head in range(heads):
                pair = head // 2
                part = slice((head % 2) * QUERY_TILE, (head % 2 + 1) * QUERY_TILE)
                d_probs = dot_nn(v_ref[keys, pair * LANES : (pair + 1) * LANES], grads_t_ref[head])
                exact = exact_ref[head]
                d_score = exact * (d_probs - inner_ref[head : head + 1, :])
                skewed_ref[head, :, lanes] = skewed_ref[head, :, lanes] + d_score
                probs_ref[pair, :, part] = exact.astype(jnp.bfloat16)
                d_scores_ref[pair, :, part] = d_score.astype(jnp.bfloat16)
            for pair in range(heads // 2):
                own = slice(pair * LANES, (pair + 1) * LANES)
                value_back_ref[keys, own] += dot_nn(probs_ref[pair], grads_ref[pair])
                key_back_ref[keys, own] += dot_nn(d_scores_ref[pair], query_ref[pair])
            for head in range(heads):
                part = slice((head % 2) * QUERY_TILE, (head % 2 + 1) * QUERY_TILE)
                mine = slice(head * head_dim, (head + 1) * head_dim)
                query_back_ref[mine, :] += dot_nn(
                    key_t_ref[mine, keys], d_scores_ref[head // 2, :, part]
                )
            return inner

        lax.fori_loop(bounds_ref[0, i], bounds_ref[1, i], step, 0)
        query_out_ref[rows, :] = (query_back_ref[...].T * SCORE_SCALE).astype(jnp.bfloat16)
        return carry

    lax.fori_loop(0, length // QUERY_TILE, block, 0)
    key_out_ref[...] = key_back_ref[...].astype(jnp.bfloat16)
    value_out_ref[...] = value_back_ref[...].astype(jnp.bfloat16)
    for head in range(heads):
        height = KEY_TILE
        while height > 8:
            height //= 2
            skewed_ref[head, :height, :] = skewed_ref[head, :height, :] + pltpu.roll(
                skewed_ref[head, height : 2 * height, :], BAND - height, 1
            )
        total = skewed_ref[head, 0:1, :]
        for row in range(1, 8):
            total = total + pltpu.roll(skewed_ref[head, row : row + 1, :], BAND - row, 1)
        band_ref[head : head + 1, :] = total


def attend_back(part, parts, bounds, qkv, same_q, same_k, table, lse, attn, grad, earlier_parts=()):
    length = qkv.shape[0]
    width = qkv.shape[1] // 3
    heads = table.shape[0] // parts
    span = width // parts

    def columns(group):
        return pl.BlockSpec(
            (length, span),
            lambda _: (0, group * parts + part),
            pipeline_mode=pl.Buffered(1),
        )

    whole = [smem(), columns(0), columns(1), columns(2), vmem(), vmem()]
    whole += [
        pl.BlockSpec(
            (heads, KEY_TILE, BAND), lambda _: (part, 0, 0), pipeline_mode=pl.Buffered(1)
        ),
        vmem(),
    ]
    whole += [columns(0), columns(0)] + [pl.BlockSpec(memory_space=pl.ANY)] * len(earlier_parts)
    return pl.pallas_call(
        functools.partial(attend_back_kernel, part * heads),
        out_shape=[jax.ShapeDtypeStruct((length, width), jnp.bfloat16)] * 3
        + [jax.ShapeDtypeStruct((heads, BAND), jnp.float32)],
        grid=(1,),
        in_specs=whole,
        out_specs=[columns(0)] * 3 + [vmem()],
        input_output_aliases={10 + at: at for at in range(len(earlier_parts))},
        scratch_shapes=[
            pltpu.VMEM((span, length), jnp.bfloat16),
            pltpu.VMEM((heads // 2, 2 * QUERY_TILE, LANES), jnp.bfloat16),
            pltpu.VMEM((heads // 2, 2 * QUERY_TILE, LANES), jnp.bfloat16),
            pltpu.VMEM((heads, 2 * LANES, QUERY_TILE), jnp.bfloat16),
            pltpu.VMEM((heads, LANES, QUERY_TILE), jnp.bfloat16),
            pltpu.VMEM((heads, QUERY_TILE), jnp.float32),
            pltpu.VMEM((span, QUERY_TILE), jnp.float32),
            pltpu.VMEM((length, span), jnp.float32),
            pltpu.VMEM((length, span), jnp.float32),
            pltpu.VMEM((heads, KEY_TILE, BAND), jnp.float32),
            pltpu.VMEM((heads, KEY_TILE, QUERY_TILE), jnp.float32),
            pltpu.VMEM((heads // 2, KEY_TILE, 2 * QUERY_TILE), jnp.bfloat16),
            pltpu.VMEM((heads // 2, KEY_TILE, 2 * QUERY_TILE), jnp.bfloat16),
        ],
        compiler_params=params(),
        cost_estimate=pl.CostEstimate(
            flops=40 * length * length * span,
            bytes_accessed=8 * 2**20,
            transcendentals=length * length * heads,
        ),
        name="attend_back",
    )(bounds, qkv, qkv, qkv, same_q, same_k, table, lse, attn, grad, *earlier_parts)


def document_bounds(segments):
    length = segments.shape[0]
    starts = segments[::QUERY_TILE]
    ends = segments[QUERY_TILE - 1 :: QUERY_TILE]
    before = jnp.sum((segments[None, :] < starts[:, None]).astype(jnp.int32), axis=1)
    upto = jnp.sum((segments[None, :] <= ends[:, None]).astype(jnp.int32), axis=1)
    return jnp.stack([before // KEY_TILE, (upto + KEY_TILE - 1) // KEY_TILE])


def document_marks(segments):
    own = segments[:, None] == jnp.arange(LANES, dtype=jnp.int32)[None, :]
    own_t = segments[None, :] == jnp.arange(LANES, dtype=jnp.int32)[:, None]
    return own_t.astype(jnp.bfloat16), jnp.where(own, 0.0, MASKED).astype(jnp.bfloat16)
HIDDEN_TILE = 256
GELU_SLOPE = 0.7978845608028654
GELU_CUBIC = 0.044715


def gelu_parts(values):
    square = values * values
    bend = jnp.tanh(values * (GELU_SLOPE + GELU_SLOPE * GELU_CUBIC * square))
    half = 0.5 + 0.5 * bend
    slope = half + values * (1.0 - bend * bend) * (
        0.5 * GELU_SLOPE + 1.5 * GELU_SLOPE * GELU_CUBIC * square
    )
    return values * half, slope


def feed_forward_kernel(
    attn_ref, resid_ref, grad_ref, w_out_ref, gain_ref, w_gate_ref, w_upper_ref, w_down_ref,
    output_ref, weight_back_ref, d_mid_ref, d_attn_ref, d_w_out_ref, d_gain_ref,
    mid_ref, rinv_ref, normed_ref, normed_t_ref, grad_t_ref, sum_ref, back_ref,
    gate_ref, upper_ref, d_inner_ref, inner_ref, d_gate_ref, d_upper_ref,
):
    step = pl.program_id(0)
    width = attn_ref.shape[1]

    @pl.when(step == 0)
    def _():
        mid = resid_ref[...] + dot_nn(attn_ref[...], w_out_ref[...])
        rinv = lax.rsqrt(jnp.mean(mid * mid, axis=-1, keepdims=True) + EPSILON)
        normed = (mid * rinv * gain_ref[...]).astype(jnp.bfloat16)
        mid_ref[...] = mid
        rinv_ref[...] = jnp.broadcast_to(rinv, rinv_ref.shape)
        normed_ref[...] = normed
        normed_t_ref[...] = normed.T
        grad_t_ref[...] = grad_ref[...].T
        sum_ref[...] = mid
        back_ref[...] = jnp.zeros_like(back_ref)

    gate_ref[...] = dot_nn(normed_ref[...], w_gate_ref[...])
    upper_ref[...] = dot_nn(normed_ref[...], w_upper_ref[...])
    d_inner_ref[...] = dot_nt(grad_ref[...], w_down_ref[...])
    upper = upper_ref[...]
    d_inner = d_inner_ref[...]
    bent, slope = gelu_parts(gate_ref[...])
    inner_ref[...] = (bent * upper).astype(jnp.bfloat16)
    d_gate_ref[...] = (d_inner * upper * slope).astype(jnp.bfloat16)
    d_upper_ref[...] = (d_inner * bent).astype(jnp.bfloat16)
    weight_back_ref[0] = dot_nn(normed_t_ref[...], d_gate_ref[...]).astype(jnp.bfloat16)
    weight_back_ref[1] = dot_nn(normed_t_ref[...], d_upper_ref[...]).astype(jnp.bfloat16)
    weight_back_ref[2] = dot_nn(grad_t_ref[...], inner_ref[...]).astype(jnp.bfloat16)
    sum_ref[...] += dot_nn(inner_ref[...], w_down_ref[...])
    back_ref[...] += dot_nt(d_gate_ref[...], w_gate_ref[...]) + dot_nt(
        d_upper_ref[...], w_upper_ref[...]
    )

    @pl.when(step == pl.num_programs(0) - 1)
    def _():
        output_ref[...] = sum_ref[...].astype(jnp.bfloat16)
        rinv = rinv_ref[:, :1]
        mid = mid_ref[...]
        d_normed = back_ref[...]
        d_gain_ref[...] = jnp.sum(d_normed * mid * rinv, axis=0, keepdims=True)
        scaled = d_normed * gain_ref[...]
        lean = jnp.mean(scaled * mid, axis=-1, keepdims=True) * (rinv * rinv * rinv)
        d_mid = grad_ref[...].astype(jnp.float32) + rinv * scaled - mid * lean
        d_mid_ref[...] = d_mid
        d_branch = d_mid.astype(jnp.bfloat16)
        d_attn_ref[...] = dot_nt(d_branch, w_out_ref[...]).astype(jnp.bfloat16)
        d_w_out_ref[...] = dot_nn(attn_ref[...].T, d_branch).astype(jnp.bfloat16)


def feed_forward(attn, resid, grad, w_out, gain, w_in, w_down):
    length, width = attn.shape
    hidden = w_down.shape[0]
    steps = hidden // HIDDEN_TILE

    def fixed(*shape):
        return pl.BlockSpec(shape, lambda c: (0,) * len(shape), pipeline_mode=pl.Buffered(1))

    low = jnp.bfloat16
    return pl.pallas_call(
        feed_forward_kernel,
        grid=(steps,),
        out_shape=(
            jax.ShapeDtypeStruct((length, width), low),
            jax.ShapeDtypeStruct((3, width, hidden), low),
            jax.ShapeDtypeStruct((length, width), jnp.float32),
            jax.ShapeDtypeStruct((length, width), low),
            jax.ShapeDtypeStruct((width, width), low),
            jax.ShapeDtypeStruct((1, width), jnp.float32),
        ),
        in_specs=[
            fixed(length, width),
            fixed(length, width),
            fixed(length, width),
            fixed(width, width),
            fixed(1, width),
            pl.BlockSpec((width, HIDDEN_TILE), lambda c: (0, c)),
            pl.BlockSpec((width, HIDDEN_TILE), lambda c: (0, steps + c)),
            pl.BlockSpec((HIDDEN_TILE, width), lambda c: (c, 0)),
        ],
        out_specs=(
            fixed(length, width),
            pl.BlockSpec((3, width, HIDDEN_TILE), lambda c: (0, 0, c)),
            fixed(length, width),
            fixed(length, width),
            fixed(width, width),
            fixed(1, width),
        ),
        scratch_shapes=[
            pltpu.VMEM((length, width), jnp.float32),
            pltpu.VMEM((length, LANES), jnp.float32),
            pltpu.VMEM((length, width), low),
            pltpu.VMEM((width, length), low),
            pltpu.VMEM((width, length), low),
            pltpu.VMEM((length, width), jnp.float32),
            pltpu.VMEM((length, width), jnp.float32),
            pltpu.VMEM((length, HIDDEN_TILE), jnp.float32),
            pltpu.VMEM((length, HIDDEN_TILE), jnp.float32),
            pltpu.VMEM((length, HIDDEN_TILE), jnp.float32),
            pltpu.VMEM((length, HIDDEN_TILE), low),
            pltpu.VMEM((length, HIDDEN_TILE), low),
            pltpu.VMEM((length, HIDDEN_TILE), low),
        ],
        compiler_params=params(),
        cost_estimate=pl.CostEstimate(
            flops=18 * length * width * hidden + 6 * length * width * width,
            bytes_accessed=24 * 2**20,
            transcendentals=length * hidden,
        ),
        name="feed_forward",
    )(attn, resid, grad, w_out, gain.reshape(1, width), w_in, w_in, w_down)


def rms_scale(values, gain):
    return values * lax.rsqrt(jnp.mean(values * values, axis=-1, keepdims=True) + EPSILON) * gain


def gelu_tanh(values):
    return jax.nn.gelu(values, approximate=True)


def dot_tn(left, right):
    return lax.dot_general(
        left, right, (((0,), (0,)), ((), ())), preferred_element_type=jnp.float32
    )


def to_rows(block, share):
    rows, stretch = block.shape[:2]
    pieces = jnp.repeat(block, share, axis=0) if share > 1 else block
    pieces = lax.all_to_all(pieces, "blk", 0, 0, tiled=True)
    return pieces.reshape((rows * share * stretch,) + block.shape[2:])


def to_blocks(row, share):
    blocks = lax.axis_size("blk")
    pieces = row.reshape((blocks, row.shape[0] // blocks) + row.shape[1:])
    return lax.all_to_all(pieces, "blk", 0, 0, tiled=True)[::share]


def later(values, lag):
    if lag == 0:
        return values
    return jnp.pad(values, ((lag, 0), (0, 0)))[: values.shape[0]]


def earlier(values, lag):
    if lag == 0:
        return values
    return jnp.pad(values, ((0, lag), (0, 0)))[lag:]


def own_bit(axis, bit):
    return (lax.axis_index(axis) >> bit) & 1


def swapped(block, axis, bit):
    devices = range(lax.axis_size(axis))
    return lax.ppermute(block, axis, [(i, i ^ (1 << bit)) for i in devices])


def bits_of(axis):
    return lax.axis_size(axis).bit_length() - 1


def reduced_half(block, axis, bit):
    half = block.shape[-2] // 2
    mine = own_bit(axis, bit)
    at = block.ndim - 2
    sent = lax.dynamic_slice_in_dim(block, (1 - mine) * half, half, axis=at)
    kept = lax.dynamic_slice_in_dim(block, mine * half, half, axis=at)
    return kept + swapped(sent, axis, bit)


def gathered_pair(block, axis, bit):
    other = swapped(block, axis, bit)
    first = own_bit(axis, bit) == 0
    return jnp.concatenate(
        [jnp.where(first, block, other), jnp.where(first, other, block)], axis=block.ndim - 2
    )


def sum_steps(cut):
    row_bits = [("rows", bit) for bit in range(bits_of("rows"))]
    chip_bits = [("blk", bit) for bit in range(1, bits_of("blk"))]
    orders = (chip_bits + row_bits, row_bits + chip_bits)
    count = len(row_bits) + len(chip_bits)

    def first(state):
        block = reduced_half(state[0], "blk", 0)
        return (block[..., :cut], block[..., cut:])

    def reduce_step(at):
        return lambda state: tuple(
            reduced_half(lane, *order[at]) for lane, order in zip(state, orders)
        )

    def gather_step(at):
        return lambda state: tuple(
            gathered_pair(lane, *order[at]) for lane, order in zip(state, orders)
        )

    def last(state):
        return tuple(gathered_pair(lane, "blk", 0) for lane in state)

    steps = [first] + [reduce_step(at) for at in range(count)]
    return steps + [gather_step(at) for at in reversed(range(count))] + [last]


class Travel:
    def __init__(self, block, cut):
        self.state = (block,)
        self.steps = sum_steps(cut)

    def go(self, count=1):
        for step in self.steps[:count]:
            self.state = step(self.state)
        self.steps = self.steps[count:]

    def beside(self, values, count=1):
        self.go(count)
        self.state, values = lax.optimization_barrier((self.state, values))
        return values

    def result(self):
        self.go(len(self.steps))
        return jnp.concatenate(self.state, axis=-1)


def on_device(
    byte_vals,
    segment_ids,
    buckets,
    emb_table,
    conv_taps,
    w_proj,
    gain_one,
    w_qkv,
    rel_bias,
    w_out,
    gain_two,
    w_in,
    w_down,
    out_grad,
):
    rows, stretch = byte_vals.shape
    vocab, width = emb_table.shape
    bucket_count, heads = rel_bias.shape
    hidden = w_down.shape[0]
    blocks = lax.axis_size("blk")
    share = blocks // rows
    length = stretch * blocks
    low = jnp.bfloat16

    packed = to_rows(byte_vals + vocab * segment_ids, share)
    letters_own = packed % vocab
    segments = packed // vocab
    grad_low = to_rows(out_grad, share)

    own_hot = (letters_own[:, None] == jnp.arange(vocab, dtype=jnp.int32)[None, :]).astype(low)
    embedded = dot_nn(own_hot, emb_table)
    taps = conv_taps.astype(jnp.float32)
    seg_col = segments[:, None] + 1
    keeps = [later(seg_col, lag) == seg_col for lag in range(4)]
    shifted = [jnp.where(keeps[lag], later(embedded, lag), 0.0) for lag in range(4)]
    conv_sum = jnp.zeros((length, width), jnp.float32)
    gelu_backs = []
    for first, span in WINDOWS:
        summed = jnp.zeros((length, width), jnp.float32)
        for lag in range(span):
            summed = summed + shifted[lag] * taps[first + lag]
        activated, gelu_back = jax.vjp(gelu_tanh, summed)
        gelu_backs.append(gelu_back)
        conv_sum = conv_sum + activated
    conv_low = conv_sum.astype(low)
    resid = dot_nn(conv_low, w_proj)
    normed_f, norm_one_back = jax.vjp(rms_scale, resid, gain_one)
    normed_one = normed_f.astype(low)
    qkv = dot_nn(normed_one, w_qkv).astype(low)

    band_buckets = lax.slice_in_dim(buckets, BAND_FIRST, BAND_FIRST + BAND - LANES)
    band_buckets = jnp.concatenate(
        [band_buckets, lax.slice_in_dim(buckets, BAND_FIRST - LANES, BAND_FIRST)]
    )
    bucket_hot = (
        band_buckets[:, None] == jnp.arange(bucket_count, dtype=jnp.int32)[None, :]
    ).astype(jnp.float32)
    base = lax.dot_general(
        rel_bias, bucket_hot, (((0,), (1,)), ((), ())), precision=HIGHEST_PRECISION
    )
    table = bias_tables(base)
    bounds = document_bounds(segments)
    same_q, same_k = document_marks(segments)
    attn, lse = attend(bounds, qkv, same_q, same_k, table)

    output_row, early, d_mid, d_attn, d_w_out, d_gain_two = feed_forward(
        attn, resid, grad_low, w_out, gain_two, w_in, w_down
    )

    early = Travel(early, hidden // 2)
    d_attn = early.beside(d_attn)
    parts = ()
    bands = []
    for part in range(PARTS):
        *parts, band = attend_back(
            part, PARTS, bounds, qkv, same_q, same_k, table, lse, attn, d_attn, parts
        )
        bands.append(band)
        parts = early.beside(parts)
    d_rel_bias = lax.dot_general(
        bucket_hot, jnp.concatenate(bands), (((0,), (1,)), ((), ())), precision=HIGHEST_PRECISION
    )
    d_normed_one = sum(
        dot_nt(part, w_qkv[:, at * width : (at + 1) * width]) for at, part in enumerate(parts)
    )
    d_resid_norm, d_gain_one = norm_one_back(d_normed_one)
    d_resid = (d_mid + d_resid_norm).astype(low)
    d_w_proj = dot_tn(conv_low, d_resid).astype(low)
    d_resid, parts, d_w_proj = early.beside((d_resid, parts, d_w_proj))
    d_conv = dot_nt(d_resid, w_proj)
    d_w_qkv = [dot_tn(normed_one, part).astype(low) for part in parts]
    d_conv, d_w_qkv = early.beside((d_conv, d_w_qkv))
    d_shifted = [jnp.zeros((length, width), jnp.float32) for lag in range(4)]
    tap_rows = [None] * 9
    for index, (first, span) in enumerate(WINDOWS):
        (d_pre,) = gelu_backs[index](d_conv)
        for lag in range(span):
            tap_rows[first + lag] = jnp.sum(d_pre * shifted[lag], axis=0)
            d_shifted[lag] = d_shifted[lag] + d_pre * taps[first + lag]
    d_conv_taps = jnp.stack(tap_rows, axis=0)
    input_row = jnp.zeros((length, width), jnp.float32)
    for lag in range(4):
        input_row = input_row + earlier(jnp.where(keeps[lag], d_shifted[lag], 0.0), lag)
    input_low = early.beside(input_row.astype(low))
    d_emb_table = dot_tn(own_hot, input_low)

    flat = jnp.concatenate(
        [d_conv_taps.reshape(-1), d_gain_one, d_gain_two[0], d_rel_bias.reshape(-1)]
    ).reshape(-1, LANES)
    small_rows = flat.shape[0]
    late = jnp.concatenate(
        d_w_qkv
        + [
            d_w_proj,
            d_w_out,
            jnp.concatenate(
                [d_emb_table[:, : width // 2], d_emb_table[:, width // 2 :]], axis=0
            ).astype(low),
            jnp.pad(flat, ((0, width - small_rows), (0, 0))).astype(low),
        ],
        axis=1,
    )
    late = early.beside(late)
    late = Travel(late, late.shape[1] // (2 * LANES) * LANES)
    while late.steps:
        early.state = late.beside(early.state)
        early.go()
    input_grad = to_blocks(input_low, share).astype(jnp.float32)
    output = to_blocks(output_row, share)

    scale = 1.0 / share
    early = early.result()
    late = late.result().astype(jnp.float32) * scale
    d_w_in = jnp.concatenate([early[0], early[1]], axis=1).astype(jnp.float32) * scale
    d_w_down = early[2].T.astype(jnp.float32) * scale
    d_w_qkv = late[:, : 3 * width]
    d_w_proj = late[:, 3 * width : 4 * width]
    d_w_out = late[:, 4 * width : 5 * width]
    table_grad = late[:, 5 * width : 5 * width + width // 2]
    d_emb_table = jnp.concatenate([table_grad[:vocab], table_grad[vocab:]], axis=1)
    flat = late[:small_rows, 5 * width + width // 2 :].reshape(-1)
    d_conv_taps = flat[: 9 * width].reshape(9, width)
    d_gain_one = flat[9 * width : 10 * width]
    d_gain_two = flat[10 * width : 11 * width]
    d_rel_bias = flat[11 * width :].reshape(bucket_count, heads)
    return (
        output,
        input_grad,
        d_emb_table,
        d_conv_taps,
        d_w_proj,
        d_gain_one,
        d_w_qkv,
        d_rel_bias,
        d_w_out,
        d_gain_two,
        d_w_in,
        d_w_down,
    )


def solution(mesh):
    split = P("rows", "blk")
    split_wide = P("rows", "blk", None)
    return jax.shard_map(
        on_device,
        mesh=mesh,
        in_specs=(split, split) + (P(),) * 11 + (split_wide,),
        out_specs=(split_wide, split_wide) + (P(),) * 10,
        check_vma=False,
    )
```

```python
import functools

import jax
import jax.numpy as jnp
from jax import lax
from jax.experimental import pallas as pl
from jax.experimental.pallas import tpu as pltpu
from jax.sharding import PartitionSpec as P

EPSILON = 1e-06
SCORE_SCALE = 0.125
WINDOWS = ((0, 2), (2, 3), (5, 4))
HIGHEST_PRECISION = lax.Precision.HIGHEST
LANES = 128
QUERY_TILE = 256
KEY_TILE = 128
MASKED = -(2.0**30)
PARTS = 2
BAND = 12 * LANES
BAND_FIRST = 3 * LANES
MIB = 2**20


def vmem():
    return pl.BlockSpec(memory_space=pltpu.VMEM)


def smem():
    return pl.BlockSpec(memory_space=pltpu.SMEM)


def params(mib):
    return pltpu.CompilerParams(vmem_limit_bytes=mib * MIB)


def dot_nt(left, right):
    return lax.dot_general(
        left, right, (((1,), (1,)), ((), ())), preferred_element_type=jnp.float32
    )


def dot_nn(left, right):
    return jnp.dot(left, right, preferred_element_type=jnp.float32)


def bias_tables_kernel(base_ref, out_ref):
    heads = base_ref.shape[0]
    for head in range(heads):
        line = jnp.broadcast_to(base_ref[head : head + 1, :], (KEY_TILE, BAND))
        out_ref[head] = pltpu.roll(line, 0, 1, stride=1, stride_axis=0)


def bias_tables(base):
    heads = base.shape[0]
    return pl.pallas_call(
        bias_tables_kernel,
        out_shape=jax.ShapeDtypeStruct((heads, KEY_TILE, BAND), jnp.float32),
        in_specs=[vmem()],
        out_specs=vmem(),
        compiler_params=params(10),
        name="bias_tables",
    )(base)


def table_lanes(query_block, key_block):
    place = (query_block * (QUERY_TILE // LANES) - key_block + 5) * LANES
    return pl.ds(pl.multiple_of(place, LANES), QUERY_TILE)


def attend_kernel(
    heads, bounds_ref, qkv_ref, same_q_ref, same_k_ref, table_ref,
    attn_ref, lse_ref,
    value_t_ref, query_ref, top_ref, total_ref, mixed_ref, score_ref, expo_ref, fade_ref,
):
    length = qkv_ref.shape[0]
    width = qkv_ref.shape[1] // 3
    head_dim = width // heads
    lane = lax.broadcasted_iota(jnp.int32, (1, LANES), 1)
    halves = (
        (lane < head_dim).astype(jnp.bfloat16),
        (lane >= head_dim).astype(jnp.bfloat16),
    )
    value_t_ref[...] = qkv_ref[:, 2 * width :].T

    def block(i, carry):
        rows = pl.ds(pl.multiple_of(i * QUERY_TILE, QUERY_TILE), QUERY_TILE)
        for pair in range(heads // 2):
            query = qkv_ref[rows, pair * LANES : (pair + 1) * LANES] * jnp.bfloat16(SCORE_SCALE)
            for side in range(2):
                query_ref[2 * pair + side, :LANES, :] = (query * halves[side]).T
                query_ref[2 * pair + side, LANES:, :] = same_q_ref[:, rows]
        top_ref[...] = jnp.full_like(top_ref, -3.0e38)
        total_ref[...] = jnp.zeros_like(total_ref)
        mixed_ref[...] = jnp.zeros_like(mixed_ref)

        def step(j, inner):
            keys = pl.ds(pl.multiple_of(j * KEY_TILE, KEY_TILE), KEY_TILE)
            lanes = table_lanes(i, j)
            for head in range(heads):
                pair = head // 2
                key = jnp.concatenate(
                    [
                        qkv_ref[keys, width + pair * LANES : width + (pair + 1) * LANES],
                        same_k_ref[keys, :],
                    ],
                    axis=1,
                )
                score_ref[head] = dot_nn(key, query_ref[head]) + table_ref[head, :, lanes]
            for head in range(heads):
                scores = score_ref[head]
                old = top_ref[head : head + 1, :]
                top = jnp.maximum(old, jnp.max(scores, axis=0, keepdims=True))
                fade = jnp.exp(old - top)
                expo = jnp.exp(scores - top)
                top_ref[head : head + 1, :] = top
                total_ref[head : head + 1, :] = total_ref[head : head + 1, :] * fade + jnp.sum(
                    expo, axis=0, keepdims=True
                )
                fade_ref[head : head + 1, :] = fade
                expo_ref[head] = expo.astype(jnp.bfloat16)
            for head in range(heads):
                own = slice(head * head_dim, (head + 1) * head_dim)
                mixed_ref[own, :] = mixed_ref[own, :] * fade_ref[head : head + 1, :] + dot_nn(
                    value_t_ref[own, keys], expo_ref[head]
                )
            return inner

        lax.fori_loop(bounds_ref[0, i], bounds_ref[1, i], step, 0)
        for head in range(heads):
            own = slice(head * head_dim, (head + 1) * head_dim)
            mixed_ref[own, :] = mixed_ref[own, :] / total_ref[head : head + 1, :]
        attn_ref[rows, :] = mixed_ref[...].T.astype(jnp.bfloat16)
        lse_ref[:, rows] = top_ref[...] + jnp.log(total_ref[...])
        return carry

    lax.fori_loop(0, length // QUERY_TILE, block, 0)


def attend(bounds, qkv, same_q, same_k, table):
    length = qkv.shape[0]
    width = qkv.shape[1] // 3
    heads = table.shape[0]
    return pl.pallas_call(
        functools.partial(attend_kernel, heads),
        out_shape=(
            jax.ShapeDtypeStruct((length, width), jnp.bfloat16),
            jax.ShapeDtypeStruct((heads, length), jnp.float32),
        ),
        in_specs=[smem(), vmem(), vmem(), vmem(), vmem()],
        out_specs=(vmem(), vmem()),
        scratch_shapes=[
            pltpu.VMEM((width, length), jnp.bfloat16),
            pltpu.VMEM((heads, 2 * LANES, QUERY_TILE), jnp.bfloat16),
            pltpu.VMEM((heads, QUERY_TILE), jnp.float32),
            pltpu.VMEM((heads, QUERY_TILE), jnp.float32),
            pltpu.VMEM((width, QUERY_TILE), jnp.float32),
            pltpu.VMEM((heads, KEY_TILE, QUERY_TILE), jnp.float32),
            pltpu.VMEM((heads, KEY_TILE, QUERY_TILE), jnp.bfloat16),
            pltpu.VMEM((heads, QUERY_TILE), jnp.float32),
        ],
        compiler_params=params(16),
        cost_estimate=pl.CostEstimate(
            flops=4 * length * length * width,
            bytes_accessed=12 * 2**20,
            transcendentals=length * length * heads,
        ),
        name="attend",
    )(bounds, qkv, same_q, same_k, table)


def attend_back_kernel(
    first, bounds_ref, q_ref, k_ref, v_ref, same_q_ref, same_k_ref, table_ref, lse_ref,
    attn_ref, grad_ref, *refs,
):
    (
        query_out_ref, key_out_ref, value_out_ref, band_ref,
        key_t_ref, query_ref, grads_ref, query_t_ref, grads_t_ref, inner_ref,
        query_back_ref, key_back_ref, value_back_ref, skewed_ref,
        exact_ref, probs_ref, d_scores_ref,
    ) = refs[-17:]
    length, width = q_ref.shape
    heads = table_ref.shape[0]
    head_dim = width // heads
    lane = lax.broadcasted_iota(jnp.int32, (1, LANES), 1)
    halves = (
        (lane < head_dim).astype(jnp.bfloat16),
        (lane >= head_dim).astype(jnp.bfloat16),
    )
    owner = lax.broadcasted_iota(jnp.int32, (heads, width), 1) // head_dim
    own_head = (owner == lax.broadcasted_iota(jnp.int32, (heads, width), 0)).astype(jnp.bfloat16)
    key_t_ref[...] = k_ref[...].T
    key_back_ref[...] = jnp.zeros_like(key_back_ref)
    value_back_ref[...] = jnp.zeros_like(value_back_ref)
    skewed_ref[...] = jnp.zeros_like(skewed_ref)

    def block(i, carry):
        rows = pl.ds(pl.multiple_of(i * QUERY_TILE, QUERY_TILE), QUERY_TILE)
        for pair in range(heads // 2):
            own = slice(pair * LANES, (pair + 1) * LANES)
            query = q_ref[rows, own] * jnp.bfloat16(SCORE_SCALE)
            grad = grad_ref[rows, own]
            for side in range(2):
                part = slice(side * QUERY_TILE, (side + 1) * QUERY_TILE)
                query_ref[pair, part, :] = query * halves[side]
                grads_ref[pair, part, :] = grad * halves[side]
                query_t_ref[2 * pair + side, :LANES, :] = (query * halves[side]).T
                query_t_ref[2 * pair + side, LANES:, :] = same_q_ref[:, rows]
                grads_t_ref[2 * pair + side] = (grad * halves[side]).T
        product = grad_ref[rows, :].astype(jnp.float32) * attn_ref[rows, :].astype(jnp.float32)
        rough = product.astype(jnp.bfloat16)
        rest = (product - rough.astype(jnp.float32)).astype(jnp.bfloat16)
        inner_ref[...] = dot_nt(own_head, rough) + dot_nt(own_head, rest)
        query_back_ref[...] = jnp.zeros_like(query_back_ref)

        def step(j, inner):
            keys = pl.ds(pl.multiple_of(j * KEY_TILE, KEY_TILE), KEY_TILE)
            lanes = table_lanes(i, j)
            for head in range(heads):
                pair = head // 2
                key = jnp.concatenate(
                    [k_ref[keys, pair * LANES : (pair + 1) * LANES], same_k_ref[keys, :]], axis=1
                )
                scores = dot_nn(key, query_t_ref[head]) + table_ref[head, :, lanes]
                exact_ref[head] = jnp.exp(scores - lse_ref[first + head : first + head + 1, rows])
            for head in range(heads):
                pair = head // 2
                part = slice((head % 2) * QUERY_TILE, (head % 2 + 1) * QUERY_TILE)
                d_probs = dot_nn(v_ref[keys, pair * LANES : (pair + 1) * LANES], grads_t_ref[head])
                exact = exact_ref[head]
                d_score = exact * (d_probs - inner_ref[head : head + 1, :])
                skewed_ref[head, :, lanes] = skewed_ref[head, :, lanes] + d_score
                probs_ref[pair, :, part] = exact.astype(jnp.bfloat16)
                d_scores_ref[pair, :, part] = d_score.astype(jnp.bfloat16)
            for pair in range(heads // 2):
                own = slice(pair * LANES, (pair + 1) * LANES)
                value_back_ref[keys, own] += dot_nn(probs_ref[pair], grads_ref[pair])
                key_back_ref[keys, own] += dot_nn(d_scores_ref[pair], query_ref[pair])
            for head in range(heads):
                part = slice((head % 2) * QUERY_TILE, (head % 2 + 1) * QUERY_TILE)
                mine = slice(head * head_dim, (head + 1) * head_dim)
                query_back_ref[mine, :] += dot_nn(
                    key_t_ref[mine, keys], d_scores_ref[head // 2, :, part]
                )
            return inner

        lax.fori_loop(bounds_ref[0, i], bounds_ref[1, i], step, 0)
        query_out_ref[rows, :] = (query_back_ref[...].T * SCORE_SCALE).astype(jnp.bfloat16)
        return carry

    lax.fori_loop(0, length // QUERY_TILE, block, 0)
    key_out_ref[...] = key_back_ref[...].astype(jnp.bfloat16)
    value_out_ref[...] = value_back_ref[...].astype(jnp.bfloat16)
    for head in range(heads):
        height = KEY_TILE
        while height > 8:
            height //= 2
            skewed_ref[head, :height, :] = skewed_ref[head, :height, :] + pltpu.roll(
                skewed_ref[head, height : 2 * height, :], BAND - height, 1
            )
        total = skewed_ref[head, 0:1, :]
        for row in range(1, 8):
            total = total + pltpu.roll(skewed_ref[head, row : row + 1, :], BAND - row, 1)
        band_ref[head : head + 1, :] = total


def attend_back(part, parts, bounds, qkv, same_q, same_k, table, lse, attn, grad, earlier_parts=()):
    length = qkv.shape[0]
    width = qkv.shape[1] // 3
    heads = table.shape[0] // parts
    span = width // parts

    def columns(group):
        return pl.BlockSpec(
            (length, span),
            lambda _: (0, group * parts + part),
            pipeline_mode=pl.Buffered(1),
        )

    whole = [smem(), columns(0), columns(1), columns(2), vmem(), vmem()]
    whole += [
        pl.BlockSpec(
            (heads, KEY_TILE, BAND), lambda _: (part, 0, 0), pipeline_mode=pl.Buffered(1)
        ),
        vmem(),
    ]
    whole += [columns(0), columns(0)] + [pl.BlockSpec(memory_space=pl.ANY)] * len(earlier_parts)
    return pl.pallas_call(
        functools.partial(attend_back_kernel, part * heads),
        out_shape=[jax.ShapeDtypeStruct((length, width), jnp.bfloat16)] * 3
        + [jax.ShapeDtypeStruct((heads, BAND), jnp.float32)],
        grid=(1,),
        in_specs=whole,
        out_specs=[columns(0)] * 3 + [vmem()],
        input_output_aliases={10 + at: at for at in range(len(earlier_parts))},
        scratch_shapes=[
            pltpu.VMEM((span, length), jnp.bfloat16),
            pltpu.VMEM((heads // 2, 2 * QUERY_TILE, LANES), jnp.bfloat16),
            pltpu.VMEM((heads // 2, 2 * QUERY_TILE, LANES), jnp.bfloat16),
            pltpu.VMEM((heads, 2 * LANES, QUERY_TILE), jnp.bfloat16),
            pltpu.VMEM((heads, LANES, QUERY_TILE), jnp.bfloat16),
            pltpu.VMEM((heads, QUERY_TILE), jnp.float32),
            pltpu.VMEM((span, QUERY_TILE), jnp.float32),
            pltpu.VMEM((length, span), jnp.float32),
            pltpu.VMEM((length, span), jnp.float32),
            pltpu.VMEM((heads, KEY_TILE, BAND), jnp.float32),
            pltpu.VMEM((heads, KEY_TILE, QUERY_TILE), jnp.float32),
            pltpu.VMEM((heads // 2, KEY_TILE, 2 * QUERY_TILE), jnp.bfloat16),
            pltpu.VMEM((heads // 2, KEY_TILE, 2 * QUERY_TILE), jnp.bfloat16),
        ],
        compiler_params=params(34),
        cost_estimate=pl.CostEstimate(
            flops=40 * length * length * span,
            bytes_accessed=8 * 2**20,
            transcendentals=length * length * heads,
        ),
        name="attend_back",
    )(bounds, qkv, qkv, qkv, same_q, same_k, table, lse, attn, grad, *earlier_parts)


def document_bounds(segments):
    length = segments.shape[0]
    starts = segments[::QUERY_TILE]
    ends = segments[QUERY_TILE - 1 :: QUERY_TILE]
    before = jnp.sum((segments[None, :] < starts[:, None]).astype(jnp.int32), axis=1)
    upto = jnp.sum((segments[None, :] <= ends[:, None]).astype(jnp.int32), axis=1)
    return jnp.stack([before // KEY_TILE, (upto + KEY_TILE - 1) // KEY_TILE])


def document_marks(segments):
    own = segments[:, None] == jnp.arange(LANES, dtype=jnp.int32)[None, :]
    own_t = segments[None, :] == jnp.arange(LANES, dtype=jnp.int32)[:, None]
    return own_t.astype(jnp.bfloat16), jnp.where(own, 0.0, MASKED).astype(jnp.bfloat16)
HIDDEN_TILE = 512
GELU_SLOPE = 0.7978845608028654
GELU_CUBIC = 0.044715


def gelu_parts(values):
    square = values * values
    bend = jnp.tanh(values * (GELU_SLOPE + GELU_SLOPE * GELU_CUBIC * square))
    half = 0.5 + 0.5 * bend
    slope = half + values * (1.0 - bend * bend) * (
        0.5 * GELU_SLOPE + 1.5 * GELU_SLOPE * GELU_CUBIC * square
    )
    return values * half, slope


def feed_forward_kernel(
    mine_ref, attn_ref, resid_ref, grad_ref, w_out_ref, gain_ref, w_gate_ref, w_upper_ref, w_down_ref,
    output_ref, kept_ref, sent_ref, d_mid_ref, d_attn_ref, d_w_out_ref, d_gain_ref,
    mid_ref, rinv_ref, normed_ref, normed_t_ref, grad_t_ref, sum_ref, back_ref,
    gate_ref, upper_ref, d_inner_ref, inner_ref, d_gate_ref, d_upper_ref,
):
    step = pl.program_id(0)
    width = attn_ref.shape[1]

    @pl.when(step == 0)
    def _():
        mid = resid_ref[...] + dot_nn(attn_ref[...], w_out_ref[...])
        rinv = lax.rsqrt(jnp.mean(mid * mid, axis=-1, keepdims=True) + EPSILON)
        normed = (mid * rinv * gain_ref[...]).astype(jnp.bfloat16)
        mid_ref[...] = mid
        rinv_ref[...] = jnp.broadcast_to(rinv, rinv_ref.shape)
        normed_ref[...] = normed
        normed_t_ref[...] = normed.T
        grad_t_ref[...] = grad_ref[...].T
        sum_ref[...] = mid
        back_ref[...] = jnp.zeros_like(back_ref)

    gate_ref[...] = dot_nn(normed_ref[...], w_gate_ref[...])
    upper_ref[...] = dot_nn(normed_ref[...], w_upper_ref[...])
    d_inner_ref[...] = dot_nt(grad_ref[...], w_down_ref[...])
    upper = upper_ref[...]
    d_inner = d_inner_ref[...]
    bent, slope = gelu_parts(gate_ref[...])
    inner_ref[...] = (bent * upper).astype(jnp.bfloat16)
    d_gate_ref[...] = (d_inner * upper * slope).astype(jnp.bfloat16)
    d_upper_ref[...] = (d_inner * bent).astype(jnp.bfloat16)
    half = width // 2
    for back_half_ref, side in ((sent_ref, 1 - mine_ref[0]), (kept_ref, mine_ref[0])):
        part = pl.ds(pl.multiple_of(side * half, half), half)
        normed_t = normed_t_ref[part, :]
        back_half_ref[0] = dot_nn(normed_t, d_gate_ref[...]).astype(jnp.bfloat16)
        back_half_ref[1] = dot_nn(normed_t, d_upper_ref[...]).astype(jnp.bfloat16)
        back_half_ref[2] = dot_nn(grad_t_ref[part, :], inner_ref[...]).astype(jnp.bfloat16)
    sum_ref[...] += dot_nn(inner_ref[...], w_down_ref[...])
    back_ref[...] += dot_nt(d_gate_ref[...], w_gate_ref[...]) + dot_nt(
        d_upper_ref[...], w_upper_ref[...]
    )

    @pl.when(step == pl.num_programs(0) - 1)
    def _():
        output_ref[...] = sum_ref[...].astype(jnp.bfloat16)
        rinv = rinv_ref[:, :1]
        mid = mid_ref[...]
        d_normed = back_ref[...]
        d_gain_ref[...] = jnp.sum(d_normed * mid * rinv, axis=0, keepdims=True)
        scaled = d_normed * gain_ref[...]
        lean = jnp.mean(scaled * mid, axis=-1, keepdims=True) * (rinv * rinv * rinv)
        d_mid = grad_ref[...].astype(jnp.float32) + rinv * scaled - mid * lean
        d_mid_ref[...] = d_mid
        d_branch = d_mid.astype(jnp.bfloat16)
        d_attn_ref[...] = dot_nt(d_branch, w_out_ref[...]).astype(jnp.bfloat16)
        d_w_out_ref[...] = dot_nn(attn_ref[...].T, d_branch).astype(jnp.bfloat16)


def feed_forward(mine, attn, resid, grad, w_out, gain, w_in, w_down):
    length, width = attn.shape
    hidden = w_down.shape[0]
    steps = hidden // HIDDEN_TILE

    low = jnp.bfloat16
    return pl.pallas_call(
        feed_forward_kernel,
        grid=(steps,),
        out_shape=(
            jax.ShapeDtypeStruct((length, width), low),
            jax.ShapeDtypeStruct((3, width // 2, hidden), low),
            jax.ShapeDtypeStruct((3, width // 2, hidden), low),
            jax.ShapeDtypeStruct((length, width), jnp.float32),
            jax.ShapeDtypeStruct((length, width), low),
            jax.ShapeDtypeStruct((width, width), low),
            jax.ShapeDtypeStruct((1, width), jnp.float32),
        ),
        in_specs=[
            smem(),
            vmem(),
            vmem(),
            vmem(),
            vmem(),
            vmem(),
            pl.BlockSpec((width, HIDDEN_TILE), lambda c: (0, c)),
            pl.BlockSpec((width, HIDDEN_TILE), lambda c: (0, steps + c)),
            pl.BlockSpec((HIDDEN_TILE, width), lambda c: (c, 0)),
        ],
        out_specs=(
            vmem(),
            pl.BlockSpec((3, width // 2, HIDDEN_TILE), lambda c: (0, 0, c)),
            pl.BlockSpec((3, width // 2, HIDDEN_TILE), lambda c: (0, 0, c)),
            vmem(),
            vmem(),
            vmem(),
            vmem(),
        ),
        scratch_shapes=[
            pltpu.VMEM((length, width), jnp.float32),
            pltpu.VMEM((length, LANES), jnp.float32),
            pltpu.VMEM((length, width), low),
            pltpu.VMEM((width, length), low),
            pltpu.VMEM((width, length), low),
            pltpu.VMEM((length, width), jnp.float32),
            pltpu.VMEM((length, width), jnp.float32),
            pltpu.VMEM((length, HIDDEN_TILE), jnp.float32),
            pltpu.VMEM((length, HIDDEN_TILE), jnp.float32),
            pltpu.VMEM((length, HIDDEN_TILE), jnp.float32),
            pltpu.VMEM((length, HIDDEN_TILE), low),
            pltpu.VMEM((length, HIDDEN_TILE), low),
            pltpu.VMEM((length, HIDDEN_TILE), low),
        ],
        compiler_params=params(40),
        cost_estimate=pl.CostEstimate(
            flops=18 * length * width * hidden + 6 * length * width * width,
            bytes_accessed=24 * 2**20,
            transcendentals=length * hidden,
        ),
        name="feed_forward",
    )(mine, attn, resid, grad, w_out, gain.reshape(1, width), w_in, w_in, w_down)


FINISH_TILE = 512


def finish_early_kernel(
    steps, scale, mine_ref, own_a_ref, other_a_ref, own_b_ref, other_b_ref, d_w_in_ref, d_w_down_ref
):
    plane, tile = pl.program_id(0), pl.program_id(1)
    half = own_a_ref.shape[0]
    mine = mine_ref[0]

    def fill(own_ref, other_ref):
        for piece_ref, side in ((own_ref, mine), (other_ref, 1 - mine)):
            part = pl.ds(pl.multiple_of(side * half, half), half)
            piece = piece_ref[...].astype(jnp.float32) * scale

            @pl.when(plane < 2)
            def _():
                d_w_in_ref[part, :] = piece

            @pl.when(plane == 2)
            def _():
                d_w_down_ref[:, part] = piece.T

    @pl.when(tile < steps)
    def _():
        fill(own_a_ref, other_a_ref)

    @pl.when(tile >= steps)
    def _():
        fill(own_b_ref, other_b_ref)


def finish_early(mine, own_a, other_a, own_b, other_b, scale):
    half, columns = own_a.shape[1:]
    steps = columns // FINISH_TILE
    width, hidden = 2 * half, 2 * columns
    block = (None, half, FINISH_TILE)
    low_block = pl.BlockSpec(block, lambda p, c: (p, 0, jnp.minimum(c, steps - 1)))
    high_block = pl.BlockSpec(block, lambda p, c: (p, 0, jnp.maximum(c - steps, 0)))
    return pl.pallas_call(
        functools.partial(finish_early_kernel, steps, scale),
        grid=(3, 2 * steps),
        out_shape=(
            jax.ShapeDtypeStruct((width, 2 * hidden), jnp.float32),
            jax.ShapeDtypeStruct((hidden, width), jnp.float32),
        ),
        in_specs=[smem(), low_block, low_block, high_block, high_block],
        out_specs=(
            pl.BlockSpec(
                (width, FINISH_TILE),
                lambda p, c: (0, jnp.where(p < 2, p * 2 * steps + c, 4 * steps - 1)),
            ),
            pl.BlockSpec((FINISH_TILE, width), lambda p, c: (jnp.where(p < 2, 0, c), 0)),
        ),
        compiler_params=params(16),
        cost_estimate=pl.CostEstimate(
            flops=6 * width * hidden, bytes_accessed=18 * width * hidden, transcendentals=0
        ),
        name="finish_early",
    )(mine, own_a, other_a, own_b, other_b)


def rms_scale(values, gain):
    return values * lax.rsqrt(jnp.mean(values * values, axis=-1, keepdims=True) + EPSILON) * gain


def gelu_tanh(values):
    return jax.nn.gelu(values, approximate=True)


def dot_tn(left, right):
    return lax.dot_general(
        left, right, (((0,), (0,)), ((), ())), preferred_element_type=jnp.float32
    )


def to_rows(block, share):
    rows, stretch = block.shape[:2]
    pieces = jnp.repeat(block, share, axis=0) if share > 1 else block
    pieces = lax.all_to_all(pieces, "blk", 0, 0, tiled=True)
    return pieces.reshape((rows * share * stretch,) + block.shape[2:])


def to_blocks(row, share):
    blocks = lax.axis_size("blk")
    pieces = row.reshape((blocks, row.shape[0] // blocks) + row.shape[1:])
    return lax.all_to_all(pieces, "blk", 0, 0, tiled=True)[::share]


def later(values, lag):
    if lag == 0:
        return values
    return jnp.pad(values, ((lag, 0), (0, 0)))[: values.shape[0]]


def earlier(values, lag):
    if lag == 0:
        return values
    return jnp.pad(values, ((0, lag), (0, 0)))[lag:]


def own_bit(axis, bit):
    return (lax.axis_index(axis) >> bit) & 1


def swapped(block, axis, bit):
    devices = range(lax.axis_size(axis))
    return lax.ppermute(block, axis, [(i, i ^ (1 << bit)) for i in devices])


def bits_of(axis):
    return lax.axis_size(axis).bit_length() - 1


def halves(terms, axis, bit):
    at = terms[0].ndim - 2
    half = terms[0].shape[at] // 2
    mine = own_bit(axis, bit)

    def pick(side):
        return sum(lax.dynamic_slice_in_dim(term, side * half, half, axis=at) for term in terms)

    return pick(1 - mine), pick(mine)


def joined(own, other, axis, bit):
    first = own_bit(axis, bit) == 0
    return jnp.concatenate(
        [jnp.where(first, own, other), jnp.where(first, other, own)], axis=own.ndim - 2
    )


class Travel:
    def __init__(self, kept, sent, cut):
        row_bits = [("rows", bit) for bit in range(bits_of("rows"))]
        chip_bits = [("blk", bit) for bit in range(1, bits_of("blk"))]
        self.orders = (chip_bits + row_bits, row_bits + chip_bits)
        self.count = len(row_bits) + len(chip_bits)
        terms = (kept, swapped(sent, "blk", 0))
        self.lanes = [[term[..., :cut] for term in terms], [term[..., cut:] for term in terms]]
        self.at = 0

    @classmethod
    def whole(cls, block, cut):
        sent, kept = halves([block], "blk", 0)
        return cls(kept, sent, cut)

    def add(self, other):
        assert self.at == other.at == self.count
        self.lanes = [
            [jnp.concatenate([sum(mine), sum(its)], axis=-1)]
            for mine, its in zip(self.lanes, other.lanes)
        ]

    def go(self):
        if self.at < self.count:
            for lane, order in zip(self.lanes, self.orders):
                sent, kept = halves(lane, *order[self.at])
                lane[:] = [kept, swapped(sent, *order[self.at])]
        elif self.at < 2 * self.count:
            for lane, order in zip(self.lanes, self.orders):
                hop = order[2 * self.count - 1 - self.at]
                own = sum(lane)
                lane[:] = [joined(own, swapped(own, *hop), *hop)]
        elif self.at == 2 * self.count:
            for lane in self.lanes:
                lane[:] = [lane[0], swapped(lane[0], "blk", 0)]
        self.at += 1

    def done(self):
        return self.at > 2 * self.count


def beside(values, *travels):
    for travel in travels:
        travel.go()
    lanes, values = lax.optimization_barrier(([travel.lanes for travel in travels], values))
    for travel, state in zip(travels, lanes):
        travel.lanes = state
    return values


def on_device(
    byte_vals,
    segment_ids,
    buckets,
    emb_table,
    conv_taps,
    w_proj,
    gain_one,
    w_qkv,
    rel_bias,
    w_out,
    gain_two,
    w_in,
    w_down,
    out_grad,
):
    rows, stretch = byte_vals.shape
    vocab, width = emb_table.shape
    bucket_count, heads = rel_bias.shape
    hidden = w_down.shape[0]
    blocks = lax.axis_size("blk")
    share = blocks // rows
    length = stretch * blocks
    low = jnp.bfloat16

    packed = to_rows(byte_vals + vocab * segment_ids, share)
    letters_own = packed % vocab
    segments = packed // vocab
    grad_low = to_rows(out_grad, share)

    own_hot = (letters_own[:, None] == jnp.arange(vocab, dtype=jnp.int32)[None, :]).astype(low)
    embedded = dot_nn(own_hot, emb_table)
    taps = conv_taps.astype(jnp.float32)
    seg_col = segments[:, None] + 1
    keeps = [later(seg_col, lag) == seg_col for lag in range(4)]
    shifted = [jnp.where(keeps[lag], later(embedded, lag), 0.0) for lag in range(4)]
    conv_sum = jnp.zeros((length, width), jnp.float32)
    gelu_backs = []
    for first, span in WINDOWS:
        summed = jnp.zeros((length, width), jnp.float32)
        for lag in range(span):
            summed = summed + shifted[lag] * taps[first + lag]
        activated, gelu_back = jax.vjp(gelu_tanh, summed)
        gelu_backs.append(gelu_back)
        conv_sum = conv_sum + activated
    conv_low = conv_sum.astype(low)
    resid = dot_nn(conv_low, w_proj)
    normed_f, norm_one_back = jax.vjp(rms_scale, resid, gain_one)
    normed_one = normed_f.astype(low)
    qkv = dot_nn(normed_one, w_qkv).astype(low)

    band_buckets = lax.slice_in_dim(buckets, BAND_FIRST, BAND_FIRST + BAND - LANES)
    band_buckets = jnp.concatenate(
        [band_buckets, lax.slice_in_dim(buckets, BAND_FIRST - LANES, BAND_FIRST)]
    )
    bucket_hot = (
        band_buckets[:, None] == jnp.arange(bucket_count, dtype=jnp.int32)[None, :]
    ).astype(jnp.float32)
    base = lax.dot_general(
        rel_bias, bucket_hot, (((0,), (1,)), ((), ())), precision=HIGHEST_PRECISION
    )
    table = bias_tables(base)
    bounds = document_bounds(segments)
    same_q, same_k = document_marks(segments)
    attn, lse = attend(bounds, qkv, same_q, same_k, table)

    mine = own_bit("blk", 0).astype(jnp.int32).reshape(1)
    output_row, kept, sent, d_mid, d_attn, d_w_out, d_gain_two = feed_forward(
        mine, attn, resid, grad_low, w_out, gain_two, w_in, w_down
    )
    early = Travel(kept, sent, hidden // 2)
    output = to_blocks(output_row, share)
    early.lanes, d_attn = lax.optimization_barrier((early.lanes, d_attn))

    parts = ()
    bands = []
    for part in range(PARTS):
        *parts, band = attend_back(
            part, PARTS, bounds, qkv, same_q, same_k, table, lse, attn, d_attn, parts
        )
        bands.append(band)
        parts = beside(parts, early)
    parts, output = lax.optimization_barrier((parts, output))
    d_rel_bias = lax.dot_general(
        bucket_hot, jnp.concatenate(bands), (((0,), (1,)), ((), ())), precision=HIGHEST_PRECISION
    )
    d_normed_one = sum(
        dot_nt(part, w_qkv[:, at * width : (at + 1) * width]) for at, part in enumerate(parts)
    )
    d_resid_norm, d_gain_one = norm_one_back(d_normed_one)
    d_resid = (d_mid + d_resid_norm).astype(low)
    d_resid, parts = beside((d_resid, parts), early)
    d_w_proj = dot_tn(conv_low, d_resid).astype(low)
    middle = jnp.concatenate(
        [dot_tn(normed_one, part).astype(low) for part in parts] + [d_w_proj, d_w_out], axis=1
    )
    d_conv, middle = beside((dot_nt(d_resid, w_proj), middle), early)
    middle = Travel.whole(middle, middle.shape[1] // (2 * LANES) * LANES)

    d_shifted = [jnp.zeros((length, width), jnp.float32) for lag in range(4)]
    tap_rows = [None] * 9
    for index, (first, span) in enumerate(WINDOWS):
        (d_pre,) = gelu_backs[index](d_conv)
        for lag in range(span):
            tap_rows[first + lag] = jnp.sum(d_pre * shifted[lag], axis=0)
            d_shifted[lag] = d_shifted[lag] + d_pre * taps[first + lag]
    d_conv_taps = jnp.stack(tap_rows, axis=0)
    input_row = jnp.zeros((length, width), jnp.float32)
    for lag in range(4):
        input_row = input_row + earlier(jnp.where(keeps[lag], d_shifted[lag], 0.0), lag)
    input_low = beside(input_row.astype(low), early)
    d_emb_table = dot_tn(own_hot, input_low)

    flat = jnp.concatenate(
        [d_conv_taps.reshape(-1), d_gain_one, d_gain_two[0], d_rel_bias.reshape(-1)]
    ).reshape(-1, LANES)
    small_rows = flat.shape[0]
    late = jnp.concatenate(
        [
            jnp.concatenate([d_emb_table[:, : width // 2], d_emb_table[:, width // 2 :]], axis=0),
            jnp.pad(flat, ((0, width - small_rows), (0, 0))),
        ],
        axis=1,
    ).astype(low)
    late = beside(late, early, middle)
    late = Travel.whole(late, width // 2)
    input_grad = to_blocks(input_low, share)
    while late.at < late.count:
        late.lanes = beside(late.lanes, early, *([middle] if middle.at < middle.count else []))
        late.go()
    while middle.at < middle.count:
        middle.go()
    middle_columns = middle.lanes[0][0].shape[-1], middle.lanes[1][0].shape[-1]
    middle.add(late)
    while not early.done():
        middle.lanes = beside(middle.lanes, early)
        middle.go()
    scale = 1.0 / share
    d_w_in, d_w_down = finish_early(mine, *early.lanes[0], *early.lanes[1], scale)
    while not middle.done():
        middle.go()
    wide = [joined(*lane, "blk", 0).astype(jnp.float32) * scale for lane in middle.lanes]
    middle = jnp.concatenate(
        [lane[:, :columns] for lane, columns in zip(wide, middle_columns)], axis=1
    )
    table_grad, flat = [lane[:, columns:] for lane, columns in zip(wide, middle_columns)]
    input_grad = input_grad.astype(jnp.float32)
    d_w_qkv = middle[:, : 3 * width]
    d_w_proj = middle[:, 3 * width : 4 * width]
    d_w_out = middle[:, 4 * width :]
    d_emb_table = jnp.concatenate([table_grad[:vocab], table_grad[vocab:]], axis=1)
    flat = flat[:small_rows].reshape(-1)
    d_conv_taps = flat[: 9 * width].reshape(9, width)
    d_gain_one = flat[9 * width : 10 * width]
    d_gain_two = flat[10 * width : 11 * width]
    d_rel_bias = flat[11 * width :].reshape(bucket_count, heads)
    return (
        output,
        input_grad,
        d_emb_table,
        d_conv_taps,
        d_w_proj,
        d_gain_one,
        d_w_qkv,
        d_rel_bias,
        d_w_out,
        d_gain_two,
        d_w_in,
        d_w_down,
    )


def solution(mesh):
    split = P("rows", "blk")
    split_wide = P("rows", "blk", None)
    return jax.shard_map(
        on_device,
        mesh=mesh,
        in_specs=(split, split) + (P(),) * 11 + (split_wide,),
        out_specs=(split_wide, split_wide) + (P(),) * 10,
        check_vma=False,
    )
```

```python
import functools

import jax
import jax.numpy as jnp
from jax import lax
from jax.experimental import pallas as pl
from jax.experimental.pallas import tpu as pltpu
from jax.sharding import PartitionSpec as P

EPSILON = 1e-06
SCORE_SCALE = 0.125
WINDOWS = ((0, 2), (2, 3), (5, 4))
HIGHEST_PRECISION = lax.Precision.HIGHEST
LANES = 128
QUERY_TILE = 256
KEY_TILE = 128
MASKED = -(2.0**30)
BAND = 12 * LANES
BAND_FIRST = 3 * LANES
MIB = 2**20


def vmem():
    return pl.BlockSpec(memory_space=pltpu.VMEM)


def smem():
    return pl.BlockSpec(memory_space=pltpu.SMEM)


def params(mib):
    return pltpu.CompilerParams(vmem_limit_bytes=mib * MIB)


def dot_nt(left, right):
    return lax.dot_general(
        left, right, (((1,), (1,)), ((), ())), preferred_element_type=jnp.float32
    )


def dot_nn(left, right):
    return jnp.dot(left, right, preferred_element_type=jnp.float32)


def bias_tables_kernel(base_ref, out_ref):
    heads = base_ref.shape[0]
    for head in range(heads):
        line = jnp.broadcast_to(base_ref[head : head + 1, :], (KEY_TILE, BAND))
        out_ref[head] = pltpu.roll(line, 0, 1, stride=1, stride_axis=0)


def bias_tables(base):
    heads = base.shape[0]
    return pl.pallas_call(
        bias_tables_kernel,
        out_shape=jax.ShapeDtypeStruct((heads, KEY_TILE, BAND), jnp.float32),
        in_specs=[vmem()],
        out_specs=vmem(),
        compiler_params=params(10),
        name="bias_tables",
    )(base)


def table_lanes(query_block, key_block):
    place = (query_block * (QUERY_TILE // LANES) - key_block + 5) * LANES
    return pl.ds(pl.multiple_of(place, LANES), QUERY_TILE)


def attend_kernel(
    heads, bounds_ref, qkv_ref, same_q_ref, same_k_ref, table_ref,
    attn_ref, lse_ref,
    value_t_ref, query_ref, top_ref, total_ref, mixed_ref, score_ref, expo_ref, fade_ref,
):
    length = qkv_ref.shape[0]
    width = qkv_ref.shape[1] // 3
    head_dim = width // heads
    lane = lax.broadcasted_iota(jnp.int32, (1, LANES), 1)
    halves = (
        (lane < head_dim).astype(jnp.bfloat16),
        (lane >= head_dim).astype(jnp.bfloat16),
    )
    value_t_ref[...] = qkv_ref[:, 2 * width :].T

    def block(i, carry):
        rows = pl.ds(pl.multiple_of(i * QUERY_TILE, QUERY_TILE), QUERY_TILE)
        for pair in range(heads // 2):
            query = qkv_ref[rows, pair * LANES : (pair + 1) * LANES] * jnp.bfloat16(SCORE_SCALE)
            for side in range(2):
                query_ref[2 * pair + side, :LANES, :] = (query * halves[side]).T
                query_ref[2 * pair + side, LANES:, :] = same_q_ref[:, rows]
        top_ref[...] = jnp.full_like(top_ref, -3.0e38)
        total_ref[...] = jnp.zeros_like(total_ref)
        mixed_ref[...] = jnp.zeros_like(mixed_ref)

        def step(j, inner):
            keys = pl.ds(pl.multiple_of(j * KEY_TILE, KEY_TILE), KEY_TILE)
            lanes = table_lanes(i, j)
            for head in range(heads):
                pair = head // 2
                key = jnp.concatenate(
                    [
                        qkv_ref[keys, width + pair * LANES : width + (pair + 1) * LANES],
                        same_k_ref[keys, :],
                    ],
                    axis=1,
                )
                score_ref[head] = dot_nn(key, query_ref[head]) + table_ref[head, :, lanes]
            for head in range(heads):
                scores = score_ref[head]
                old = top_ref[head : head + 1, :]
                top = jnp.maximum(old, jnp.max(scores, axis=0, keepdims=True))
                fade = jnp.exp(old - top)
                expo = jnp.exp(scores - top)
                top_ref[head : head + 1, :] = top
                total_ref[head : head + 1, :] = total_ref[head : head + 1, :] * fade + jnp.sum(
                    expo, axis=0, keepdims=True
                )
                fade_ref[head : head + 1, :] = fade
                expo_ref[head] = expo.astype(jnp.bfloat16)
            for head in range(heads):
                own = slice(head * head_dim, (head + 1) * head_dim)
                mixed_ref[own, :] = mixed_ref[own, :] * fade_ref[head : head + 1, :] + dot_nn(
                    value_t_ref[own, keys], expo_ref[head]
                )
            return inner

        lax.fori_loop(bounds_ref[0, i], bounds_ref[1, i], step, 0)
        for head in range(heads):
            own = slice(head * head_dim, (head + 1) * head_dim)
            mixed_ref[own, :] = mixed_ref[own, :] / total_ref[head : head + 1, :]
        attn_ref[rows, :] = mixed_ref[...].T.astype(jnp.bfloat16)
        lse_ref[:, rows] = top_ref[...] + jnp.log(total_ref[...])
        return carry

    lax.fori_loop(0, length // QUERY_TILE, block, 0)


def attend(bounds, qkv, same_q, same_k, table):
    length = qkv.shape[0]
    width = qkv.shape[1] // 3
    heads = table.shape[0]
    return pl.pallas_call(
        functools.partial(attend_kernel, heads),
        out_shape=(
            jax.ShapeDtypeStruct((length, width), jnp.bfloat16),
            jax.ShapeDtypeStruct((heads, length), jnp.float32),
        ),
        in_specs=[smem(), vmem(), vmem(), vmem(), vmem()],
        out_specs=(vmem(), vmem()),
        scratch_shapes=[
            pltpu.VMEM((width, length), jnp.bfloat16),
            pltpu.VMEM((heads, 2 * LANES, QUERY_TILE), jnp.bfloat16),
            pltpu.VMEM((heads, QUERY_TILE), jnp.float32),
            pltpu.VMEM((heads, QUERY_TILE), jnp.float32),
            pltpu.VMEM((width, QUERY_TILE), jnp.float32),
            pltpu.VMEM((heads, KEY_TILE, QUERY_TILE), jnp.float32),
            pltpu.VMEM((heads, KEY_TILE, QUERY_TILE), jnp.bfloat16),
            pltpu.VMEM((heads, QUERY_TILE), jnp.float32),
        ],
        compiler_params=params(16),
        cost_estimate=pl.CostEstimate(
            flops=4 * length * length * width,
            bytes_accessed=12 * 2**20,
            transcendentals=length * length * heads,
        ),
        name="attend",
    )(bounds, qkv, same_q, same_k, table)


def attend_back_kernel(
    first, bounds_ref, q_ref, k_ref, v_ref, same_q_ref, same_k_ref, table_ref, lse_ref,
    attn_ref, grad_ref, *refs,
):
    (
        query_out_ref, key_out_ref, value_out_ref, band_ref,
        key_t_ref, query_ref, grads_ref, query_t_ref, grads_t_ref, inner_ref,
        query_back_ref, key_back_ref, value_back_ref, skewed_ref,
        exact_ref, probs_ref, d_scores_ref,
    ) = refs[-17:]
    length, width = q_ref.shape
    heads = table_ref.shape[0]
    head_dim = width // heads
    lane = lax.broadcasted_iota(jnp.int32, (1, LANES), 1)
    halves = (
        (lane < head_dim).astype(jnp.bfloat16),
        (lane >= head_dim).astype(jnp.bfloat16),
    )
    owner = lax.broadcasted_iota(jnp.int32, (heads, width), 1) // head_dim
    own_head = (owner == lax.broadcasted_iota(jnp.int32, (heads, width), 0)).astype(jnp.bfloat16)
    key_t_ref[...] = k_ref[...].T
    key_back_ref[...] = jnp.zeros_like(key_back_ref)
    value_back_ref[...] = jnp.zeros_like(value_back_ref)
    skewed_ref[...] = jnp.zeros_like(skewed_ref)

    def block(i, carry):
        rows = pl.ds(pl.multiple_of(i * QUERY_TILE, QUERY_TILE), QUERY_TILE)
        for pair in range(heads // 2):
            own = slice(pair * LANES, (pair + 1) * LANES)
            query = q_ref[rows, own] * jnp.bfloat16(SCORE_SCALE)
            grad = grad_ref[rows, own]
            for side in range(2):
                part = slice(side * QUERY_TILE, (side + 1) * QUERY_TILE)
                query_ref[pair, part, :] = query * halves[side]
                grads_ref[pair, part, :] = grad * halves[side]
                query_t_ref[2 * pair + side, :LANES, :] = (query * halves[side]).T
                query_t_ref[2 * pair + side, LANES:, :] = same_q_ref[:, rows]
                grads_t_ref[2 * pair + side] = (grad * halves[side]).T
        product = grad_ref[rows, :].astype(jnp.float32) * attn_ref[rows, :].astype(jnp.float32)
        rough = product.astype(jnp.bfloat16)
        rest = (product - rough.astype(jnp.float32)).astype(jnp.bfloat16)
        inner_ref[...] = dot_nt(own_head, rough) + dot_nt(own_head, rest)
        query_back_ref[...] = jnp.zeros_like(query_back_ref)

        def step(j, inner):
            keys = pl.ds(pl.multiple_of(j * KEY_TILE, KEY_TILE), KEY_TILE)
            lanes = table_lanes(i, j)
            for head in range(heads):
                pair = head // 2
                key = jnp.concatenate(
                    [k_ref[keys, pair * LANES : (pair + 1) * LANES], same_k_ref[keys, :]], axis=1
                )
                scores = dot_nn(key, query_t_ref[head]) + table_ref[head, :, lanes]
                exact_ref[head] = jnp.exp(scores - lse_ref[first + head : first + head + 1, rows])
            for head in range(heads):
                pair = head // 2
                part = slice((head % 2) * QUERY_TILE, (head % 2 + 1) * QUERY_TILE)
                d_probs = dot_nn(v_ref[keys, pair * LANES : (pair + 1) * LANES], grads_t_ref[head])
                exact = exact_ref[head]
                d_score = exact * (d_probs - inner_ref[head : head + 1, :])
                skewed_ref[head, :, lanes] = skewed_ref[head, :, lanes] + d_score
                probs_ref[pair, :, part] = exact.astype(jnp.bfloat16)
                d_scores_ref[pair, :, part] = d_score.astype(jnp.bfloat16)
            for pair in range(heads // 2):
                own = slice(pair * LANES, (pair + 1) * LANES)
                value_back_ref[keys, own] += dot_nn(probs_ref[pair], grads_ref[pair])
                key_back_ref[keys, own] += dot_nn(d_scores_ref[pair], query_ref[pair])
            for head in range(heads):
                part = slice((head % 2) * QUERY_TILE, (head % 2 + 1) * QUERY_TILE)
                mine = slice(head * head_dim, (head + 1) * head_dim)
                query_back_ref[mine, :] += dot_nn(
                    key_t_ref[mine, keys], d_scores_ref[head // 2, :, part]
                )
            return inner

        lax.fori_loop(bounds_ref[0, i], bounds_ref[1, i], step, 0)
        query_out_ref[rows, :] = (query_back_ref[...].T * SCORE_SCALE).astype(jnp.bfloat16)
        return carry

    lax.fori_loop(0, length // QUERY_TILE, block, 0)
    key_out_ref[...] = key_back_ref[...].astype(jnp.bfloat16)
    value_out_ref[...] = value_back_ref[...].astype(jnp.bfloat16)
    for head in range(heads):
        height = KEY_TILE
        while height > 8:
            height //= 2
            skewed_ref[head, :height, :] = skewed_ref[head, :height, :] + pltpu.roll(
                skewed_ref[head, height : 2 * height, :], BAND - height, 1
            )
        total = skewed_ref[head, 0:1, :]
        for row in range(1, 8):
            total = total + pltpu.roll(skewed_ref[head, row : row + 1, :], BAND - row, 1)
        band_ref[head : head + 1, :] = total


def attend_back(part, parts, bounds, qkv, same_q, same_k, table, lse, attn, grad, earlier_parts=()):
    length = qkv.shape[0]
    width = qkv.shape[1] // 3
    heads = table.shape[0] // parts
    span = width // parts

    def columns(group):
        return pl.BlockSpec(
            (length, span),
            lambda _: (0, group * parts + part),
            pipeline_mode=pl.Buffered(1),
        )

    whole = [smem(), columns(0), columns(1), columns(2), vmem(), vmem()]
    whole += [
        pl.BlockSpec(
            (heads, KEY_TILE, BAND), lambda _: (part, 0, 0), pipeline_mode=pl.Buffered(1)
        ),
        vmem(),
    ]
    whole += [columns(0), columns(0)] + [pl.BlockSpec(memory_space=pl.ANY)] * len(earlier_parts)
    return pl.pallas_call(
        functools.partial(attend_back_kernel, part * heads),
        out_shape=[jax.ShapeDtypeStruct((length, width), jnp.bfloat16)] * 3
        + [jax.ShapeDtypeStruct((heads, BAND), jnp.float32)],
        grid=(1,),
        in_specs=whole,
        out_specs=[columns(0)] * 3 + [vmem()],
        input_output_aliases={10 + at: at for at in range(len(earlier_parts))},
        scratch_shapes=[
            pltpu.VMEM((span, length), jnp.bfloat16),
            pltpu.VMEM((heads // 2, 2 * QUERY_TILE, LANES), jnp.bfloat16),
            pltpu.VMEM((heads // 2, 2 * QUERY_TILE, LANES), jnp.bfloat16),
            pltpu.VMEM((heads, 2 * LANES, QUERY_TILE), jnp.bfloat16),
            pltpu.VMEM((heads, LANES, QUERY_TILE), jnp.bfloat16),
            pltpu.VMEM((heads, QUERY_TILE), jnp.float32),
            pltpu.VMEM((span, QUERY_TILE), jnp.float32),
            pltpu.VMEM((length, span), jnp.float32),
            pltpu.VMEM((length, span), jnp.float32),
            pltpu.VMEM((heads, KEY_TILE, BAND), jnp.float32),
            pltpu.VMEM((heads, KEY_TILE, QUERY_TILE), jnp.float32),
            pltpu.VMEM((heads // 2, KEY_TILE, 2 * QUERY_TILE), jnp.bfloat16),
            pltpu.VMEM((heads // 2, KEY_TILE, 2 * QUERY_TILE), jnp.bfloat16),
        ],
        compiler_params=params(34),
        cost_estimate=pl.CostEstimate(
            flops=40 * length * length * span,
            bytes_accessed=8 * 2**20,
            transcendentals=length * length * heads,
        ),
        name="attend_back",
    )(bounds, qkv, qkv, qkv, same_q, same_k, table, lse, attn, grad, *earlier_parts)


def document_bounds(segments):
    length = segments.shape[0]
    starts = segments[::QUERY_TILE]
    ends = segments[QUERY_TILE - 1 :: QUERY_TILE]
    before = jnp.sum((segments[None, :] < starts[:, None]).astype(jnp.int32), axis=1)
    upto = jnp.sum((segments[None, :] <= ends[:, None]).astype(jnp.int32), axis=1)
    return jnp.stack([before // KEY_TILE, (upto + KEY_TILE - 1) // KEY_TILE])


def document_marks(segments):
    own = segments[:, None] == jnp.arange(LANES, dtype=jnp.int32)[None, :]
    own_t = segments[None, :] == jnp.arange(LANES, dtype=jnp.int32)[:, None]
    return own_t.astype(jnp.bfloat16), jnp.where(own, 0.0, MASKED).astype(jnp.bfloat16)
HIDDEN_TILE = 512
GELU_SLOPE = 0.7978845608028654
GELU_CUBIC = 0.044715


def gelu_parts(values):
    square = values * values
    bend = jnp.tanh(values * (GELU_SLOPE + GELU_SLOPE * GELU_CUBIC * square))
    half = 0.5 + 0.5 * bend
    slope = half + values * (1.0 - bend * bend) * (
        0.5 * GELU_SLOPE + 1.5 * GELU_SLOPE * GELU_CUBIC * square
    )
    return values * half, slope


def feed_forward_kernel(
    mine_ref, attn_ref, resid_ref, grad_ref, w_out_ref, gain_ref, w_gate_ref, w_upper_ref, w_down_ref,
    output_ref, kept_ref, sent_ref, d_mid_ref, d_attn_ref, d_w_out_ref, d_gain_ref,
    mid_ref, rinv_ref, normed_ref, normed_t_ref, grad_t_ref, sum_ref, back_ref,
    gate_ref, upper_ref, d_inner_ref, inner_ref, d_gate_ref, d_upper_ref,
):
    step = pl.program_id(0)
    width = attn_ref.shape[1]

    @pl.when(step == 0)
    def _():
        mid = resid_ref[...] + dot_nn(attn_ref[...], w_out_ref[...])
        rinv = lax.rsqrt(jnp.mean(mid * mid, axis=-1, keepdims=True) + EPSILON)
        normed = (mid * rinv * gain_ref[...]).astype(jnp.bfloat16)
        mid_ref[...] = mid
        rinv_ref[...] = jnp.broadcast_to(rinv, rinv_ref.shape)
        normed_ref[...] = normed
        normed_t_ref[...] = normed.T
        grad_t_ref[...] = grad_ref[...].T
        sum_ref[...] = mid
        back_ref[...] = jnp.zeros_like(back_ref)

    gate_ref[...] = dot_nn(normed_ref[...], w_gate_ref[...])
    upper_ref[...] = dot_nn(normed_ref[...], w_upper_ref[...])
    d_inner_ref[...] = dot_nt(grad_ref[...], w_down_ref[...])
    upper = upper_ref[...]
    d_inner = d_inner_ref[...]
    bent, slope = gelu_parts(gate_ref[...])
    inner_ref[...] = (bent * upper).astype(jnp.bfloat16)
    d_gate_ref[...] = (d_inner * upper * slope).astype(jnp.bfloat16)
    d_upper_ref[...] = (d_inner * bent).astype(jnp.bfloat16)
    half = width // 2
    for back_half_ref, side in ((sent_ref, 1 - mine_ref[0]), (kept_ref, mine_ref[0])):
        part = pl.ds(pl.multiple_of(side * half, half), half)
        normed_t = normed_t_ref[part, :]
        for plane, (left, right_ref) in enumerate(
            ((normed_t, d_gate_ref), (normed_t, d_upper_ref), (grad_t_ref[part, :], inner_ref))
        ):
            columns = slice(plane * HIDDEN_TILE, (plane + 1) * HIDDEN_TILE)
            back_half_ref[:, columns] = dot_nn(left, right_ref[...]).astype(jnp.bfloat16)
    sum_ref[...] += dot_nn(inner_ref[...], w_down_ref[...])
    back_ref[...] += dot_nt(d_gate_ref[...], w_gate_ref[...]) + dot_nt(
        d_upper_ref[...], w_upper_ref[...]
    )

    @pl.when(step == pl.num_programs(0) - 1)
    def _():
        output_ref[...] = sum_ref[...].astype(jnp.bfloat16)
        rinv = rinv_ref[:, :1]
        mid = mid_ref[...]
        d_normed = back_ref[...]
        d_gain_ref[...] = jnp.sum(d_normed * mid * rinv, axis=0, keepdims=True)
        scaled = d_normed * gain_ref[...]
        lean = jnp.mean(scaled * mid, axis=-1, keepdims=True) * (rinv * rinv * rinv)
        d_mid = grad_ref[...].astype(jnp.float32) + rinv * scaled - mid * lean
        d_mid_ref[...] = d_mid
        d_branch = d_mid.astype(jnp.bfloat16)
        d_attn_ref[...] = dot_nt(d_branch, w_out_ref[...]).astype(jnp.bfloat16)
        d_w_out_ref[...] = dot_nn(attn_ref[...].T, d_branch).astype(jnp.bfloat16)


def feed_forward(mine, attn, resid, grad, w_out, gain, w_in, w_down):
    length, width = attn.shape
    hidden = w_down.shape[0]
    steps = hidden // HIDDEN_TILE

    low = jnp.bfloat16
    return pl.pallas_call(
        feed_forward_kernel,
        grid=(steps,),
        out_shape=(
            jax.ShapeDtypeStruct((length, width), low),
            jax.ShapeDtypeStruct((width // 2, 3 * hidden), low),
            jax.ShapeDtypeStruct((width // 2, 3 * hidden), low),
            jax.ShapeDtypeStruct((length, width), jnp.float32),
            jax.ShapeDtypeStruct((length, width), low),
            jax.ShapeDtypeStruct((width, width), low),
            jax.ShapeDtypeStruct((1, width), jnp.float32),
        ),
        in_specs=[
            smem(),
            vmem(),
            vmem(),
            vmem(),
            vmem(),
            vmem(),
            pl.BlockSpec((width, HIDDEN_TILE), lambda c: (0, c)),
            pl.BlockSpec((width, HIDDEN_TILE), lambda c: (0, steps + c)),
            pl.BlockSpec((HIDDEN_TILE, width), lambda c: (c, 0)),
        ],
        out_specs=(
            vmem(),
            pl.BlockSpec((width // 2, 3 * HIDDEN_TILE), lambda c: (0, c)),
            pl.BlockSpec((width // 2, 3 * HIDDEN_TILE), lambda c: (0, c)),
            vmem(),
            vmem(),
            vmem(),
            vmem(),
        ),
        scratch_shapes=[
            pltpu.VMEM((length, width), jnp.float32),
            pltpu.VMEM((length, LANES), jnp.float32),
            pltpu.VMEM((length, width), low),
            pltpu.VMEM((width, length), low),
            pltpu.VMEM((width, length), low),
            pltpu.VMEM((length, width), jnp.float32),
            pltpu.VMEM((length, width), jnp.float32),
            pltpu.VMEM((length, HIDDEN_TILE), jnp.float32),
            pltpu.VMEM((length, HIDDEN_TILE), jnp.float32),
            pltpu.VMEM((length, HIDDEN_TILE), jnp.float32),
            pltpu.VMEM((length, HIDDEN_TILE), low),
            pltpu.VMEM((length, HIDDEN_TILE), low),
            pltpu.VMEM((length, HIDDEN_TILE), low),
        ],
        compiler_params=params(40),
        cost_estimate=pl.CostEstimate(
            flops=18 * length * width * hidden + 6 * length * width * width,
            bytes_accessed=24 * 2**20,
            transcendentals=length * hidden,
        ),
        name="feed_forward",
    )(mine, attn, resid, grad, w_out, gain.reshape(1, width), w_in, w_in, w_down)


def finish_wide_kernel(lanes, scale, mine_ref, *refs):
    *piece_refs, d_w_in_ref, d_w_down_ref = refs
    plane, tile = pl.program_id(0), pl.program_id(1)
    half = piece_refs[0].shape[0]
    mine = mine_ref[0]
    for lane, (first, last) in enumerate(lanes):

        @pl.when((tile >= first) & (tile < last))
        def _():
            for piece_ref, side in (
                (piece_refs[2 * lane], mine),
                (piece_refs[2 * lane + 1], 1 - mine),
            ):
                part = pl.ds(pl.multiple_of(side * half, half), half)
                piece = piece_ref[...].astype(jnp.float32) * scale

                @pl.when(plane < 2)
                def _():
                    d_w_in_ref[part, :] = piece

                @pl.when(plane == 2)
                def _():
                    d_w_down_ref[:, part] = piece.T


def finish_wide(mine, lanes, scale):
    half = lanes[0][0].shape[0]
    width = 2 * half
    spans = []
    specs = []
    first = 0
    for own, other in lanes:
        count = own.shape[1] // (3 * HIDDEN_TILE)

        def place(p, c, first=first, count=count):
            return (0, jnp.clip(c - first, 0, count - 1) * 3 + p)

        specs += [pl.BlockSpec((half, HIDDEN_TILE), place)] * 2
        spans.append((first, first + count))
        first += count
    hidden = first * HIDDEN_TILE
    return pl.pallas_call(
        functools.partial(finish_wide_kernel, tuple(spans), scale),
        grid=(3, first),
        out_shape=(
            jax.ShapeDtypeStruct((width, 2 * hidden), jnp.float32),
            jax.ShapeDtypeStruct((hidden, width), jnp.float32),
        ),
        in_specs=[smem()] + specs,
        out_specs=(
            pl.BlockSpec(
                (width, HIDDEN_TILE), lambda p, c: (0, jnp.where(p < 2, p * first + c, 2 * first - 1))
            ),
            pl.BlockSpec((HIDDEN_TILE, width), lambda p, c: (jnp.where(p < 2, 0, c), 0)),
        ),
        compiler_params=params(16),
        cost_estimate=pl.CostEstimate(
            flops=6 * width * hidden, bytes_accessed=18 * width * hidden, transcendentals=0
        ),
        name="finish_wide",
    )(mine, *[piece for lane in lanes for piece in lane])


def finish_rest_kernel(scale, mine_ref, own_ref, other_ref, *refs):
    qkv_ref, proj_ref, out_ref, emb_ref, taps_ref, one_ref, two_ref, bias_ref, joined_ref = refs
    half = own_ref.shape[0]
    mine = mine_ref[0]
    for piece_ref, side in ((own_ref, mine), (other_ref, 1 - mine)):
        part = pl.ds(pl.multiple_of(side * half, half), half)
        joined_ref[part, :] = piece_ref[...].astype(jnp.float32) * scale
    at = 0
    for ref in (qkv_ref, proj_ref, out_ref):
        span = ref.shape[1]
        ref[...] = joined_ref[:, at : at + span]
        at += span
    row = 0
    for ref in (emb_ref, taps_ref, one_ref, two_ref, bias_ref):
        rows, span = ref.shape
        ref[...] = joined_ref[row : row + rows, at : at + span]
        row += rows


def finish_rest(mine, own, other, scale, shapes):
    half, columns = own.shape
    return pl.pallas_call(
        functools.partial(finish_rest_kernel, scale),
        out_shape=[jax.ShapeDtypeStruct(shape, jnp.float32) for shape in shapes],
        in_specs=[smem(), vmem(), vmem()],
        out_specs=[vmem()] * len(shapes),
        scratch_shapes=[pltpu.VMEM((2 * half, columns), jnp.float32)],
        compiler_params=params(16),
        cost_estimate=pl.CostEstimate(
            flops=4 * half * columns, bytes_accessed=12 * half * columns, transcendentals=0
        ),
        name="finish_rest",
    )(mine, own, other)


def rms_scale(values, gain):
    return values * lax.rsqrt(jnp.mean(values * values, axis=-1, keepdims=True) + EPSILON) * gain


def gelu_tanh(values):
    return jax.nn.gelu(values, approximate=True)


def dot_tn(left, right):
    return lax.dot_general(
        left, right, (((0,), (0,)), ((), ())), preferred_element_type=jnp.float32
    )


def to_rows(block, share):
    rows, stretch = block.shape[:2]
    pieces = jnp.repeat(block, share, axis=0) if share > 1 else block
    pieces = lax.all_to_all(pieces, "blk", 0, 0, tiled=True)
    return pieces.reshape((rows * share * stretch,) + block.shape[2:])


def to_blocks(row, share):
    blocks = lax.axis_size("blk")
    place = lax.axis_index("blk")
    stretch = row.shape[0] // blocks

    def piece(owner):
        return lax.dynamic_slice_in_dim(row, owner * stretch, stretch, axis=0)

    pieces = [piece(place)]
    for gap in range(1, blocks):
        devices = range(blocks)
        pieces.append(lax.ppermute(piece(place ^ gap), "blk", [(i, i ^ gap) for i in devices]))
    return pieces


def placed(pieces, share):
    place = lax.axis_index("blk")
    gap = 1
    while gap < len(pieces):
        stays = (place & gap) == 0
        pieces = [jnp.where(stays, pieces[at], pieces[at ^ gap]) for at in range(len(pieces))]
        gap *= 2
    return jnp.stack(pieces[::share])


def later(values, lag):
    if lag == 0:
        return values
    return jnp.pad(values, ((lag, 0), (0, 0)))[: values.shape[0]]


def earlier(values, lag):
    if lag == 0:
        return values
    return jnp.pad(values, ((0, lag), (0, 0)))[lag:]


def own_bit(axis, bit):
    return (lax.axis_index(axis) >> bit) & 1


def swapped(block, axis, bit):
    devices = range(lax.axis_size(axis))
    return lax.ppermute(block, axis, [(i, i ^ (1 << bit)) for i in devices])


def bits_of(axis):
    return lax.axis_size(axis).bit_length() - 1


def group_of(free):
    blk = lax.axis_size("blk")
    devices = range(lax.axis_size("rows") * blk)
    weights = [(blk if axis == "rows" else 1) << bit for axis, bit in free]
    place = sum(own_bit(axis, bit) << at for at, (axis, bit) in enumerate(free))
    groups = []
    for device in devices:
        if all(not device & weight for weight in weights):
            members = [device]
            for weight in weights:
                members += [member + weight for member in members]
            groups.append(members)

    def send(block, gap):
        shift = sum(weight for at, weight in enumerate(weights) if gap >> at & 1)
        return lax.ppermute(block, ("rows", "blk"), [(i, i ^ shift) for i in devices])

    def exchange(pieces):
        return lax.all_to_all(
            pieces, ("rows", "blk"), 0, 0, axis_index_groups=groups, tiled=True
        )

    return 1 << len(free), place, send, exchange


class Travel:
    def __init__(self, kept, sent, at_once=False):
        self.at_once = at_once
        near = [("blk", bit) for bit in range(1, bits_of("blk"))] + [("rows", 0)]
        far = [("rows", bit) for bit in range(1, bits_of("rows"))]
        stages = (group_of(near), group_of(far))
        terms = [kept, swapped(sent, "blk", 0)]
        self.state = [terms]
        self.orders = [stages]
        self.at = 0

    @classmethod
    def whole(cls, block):
        half = block.shape[0] // 2
        mine = own_bit("blk", 0)
        sent = lax.dynamic_slice_in_dim(block, (1 - mine) * half, half, axis=0)
        kept = lax.dynamic_slice_in_dim(block, mine * half, half, axis=0)
        return cls(kept, sent)

    def add(self, other):
        assert self.at == other.at == 2 and len(self.state) == len(other.state) == 1
        self.state = [[jnp.concatenate([total(self.state[0]), total(other.state[0])], axis=1)]]

    def go(self):
        self.state = [self.lane_step(*lane) for lane in zip(self.state, self.orders)]
        self.at += 1

    def lane_step(self, terms, order):
        block = total(terms)
        if self.at == 4:
            return [block, swapped(block, "blk", 0)]
        count, place, send, exchange = order[self.at if self.at < 2 else 3 - self.at]
        if self.at < 2:
            rows = block.shape[0] // count
            if self.at_once:
                pieces = exchange(block)
                return [pieces[at * rows : (at + 1) * rows] for at in range(count)]

            def piece(owner):
                return lax.dynamic_slice_in_dim(block, owner * rows, rows, axis=0)

            return [piece(place)] + [send(piece(place ^ gap), gap) for gap in range(1, count)]
        if self.at_once:
            return [exchange(jnp.concatenate([block] * count, axis=0))]
        pieces = [block] + [send(block, gap) for gap in range(1, count)]
        gap = 1
        while gap < count:
            stays = (place & gap) == 0
            pieces = [jnp.where(stays, pieces[at], pieces[at ^ gap]) for at in range(count)]
            gap *= 2
        return [jnp.concatenate(pieces, axis=0)]


def total(terms):
    first, *others = terms
    if not others:
        return first
    wide = first.astype(jnp.float32)
    for other in others:
        wide = wide + other.astype(jnp.float32)
    return wide.astype(first.dtype)


def beside(values, *travels):
    for travel in travels:
        travel.go()
    return settled(values, *travels)


def settled(values, *travels):
    states, values = lax.optimization_barrier(([travel.state for travel in travels], values))
    for travel, state in zip(travels, states):
        travel.state = state
    return values


def on_device(
    byte_vals,
    segment_ids,
    buckets,
    emb_table,
    conv_taps,
    w_proj,
    gain_one,
    w_qkv,
    rel_bias,
    w_out,
    gain_two,
    w_in,
    w_down,
    out_grad,
):
    rows, stretch = byte_vals.shape
    vocab, width = emb_table.shape
    bucket_count, heads = rel_bias.shape
    hidden = w_down.shape[0]
    blocks = lax.axis_size("blk")
    share = blocks // rows
    length = stretch * blocks
    low = jnp.bfloat16

    packed = to_rows(byte_vals + vocab * segment_ids, share)
    letters_own = packed % vocab
    segments = packed // vocab
    grad_low = to_rows(out_grad, share)

    own_hot = (letters_own[:, None] == jnp.arange(vocab, dtype=jnp.int32)[None, :]).astype(low)
    embedded = dot_nn(own_hot, emb_table)
    taps = conv_taps.astype(jnp.float32)
    seg_col = segments[:, None] + 1
    keeps = [later(seg_col, lag) == seg_col for lag in range(4)]
    shifted = [jnp.where(keeps[lag], later(embedded, lag), 0.0) for lag in range(4)]
    conv_sum = jnp.zeros((length, width), jnp.float32)
    gelu_backs = []
    for first, span in WINDOWS:
        summed = jnp.zeros((length, width), jnp.float32)
        for lag in range(span):
            summed = summed + shifted[lag] * taps[first + lag]
        activated, gelu_back = jax.vjp(gelu_tanh, summed)
        gelu_backs.append(gelu_back)
        conv_sum = conv_sum + activated
    conv_low = conv_sum.astype(low)
    resid = dot_nn(conv_low, w_proj)
    normed_f, norm_one_back = jax.vjp(rms_scale, resid, gain_one)
    normed_one = normed_f.astype(low)
    qkv = dot_nn(normed_one, w_qkv).astype(low)

    band_buckets = lax.slice_in_dim(buckets, BAND_FIRST, BAND_FIRST + BAND - LANES)
    band_buckets = jnp.concatenate(
        [band_buckets, lax.slice_in_dim(buckets, BAND_FIRST - LANES, BAND_FIRST)]
    )
    bucket_hot = (
        band_buckets[:, None] == jnp.arange(bucket_count, dtype=jnp.int32)[None, :]
    ).astype(jnp.float32)
    base = lax.dot_general(
        rel_bias, bucket_hot, (((0,), (1,)), ((), ())), precision=HIGHEST_PRECISION
    )
    table = bias_tables(base)
    bounds = document_bounds(segments)
    same_q, same_k = document_marks(segments)
    attn, lse = attend(bounds, qkv, same_q, same_k, table)

    mine = own_bit("blk", 0).astype(jnp.int32).reshape(1)
    output_row, kept, sent, d_mid, d_attn, d_w_out, d_gain_two = feed_forward(
        mine, attn, resid, grad_low, w_out, gain_two, w_in, w_down
    )
    early = Travel(kept, sent, at_once=True)
    d_attn, output_row = settled((d_attn, output_row), early)
    output = to_blocks(output_row, share)

    *parts, band = attend_back(0, 1, bounds, qkv, same_q, same_k, table, lse, attn, d_attn)
    parts, output = beside((parts, output), early)
    output = placed(output, share)
    d_rel_bias = lax.dot_general(
        bucket_hot, band, (((0,), (1,)), ((), ())), precision=HIGHEST_PRECISION
    )
    d_normed_one = sum(
        dot_nt(part, w_qkv[:, at * width : (at + 1) * width]) for at, part in enumerate(parts)
    )
    d_resid_norm, d_gain_one = norm_one_back(d_normed_one)
    d_resid = (d_mid + d_resid_norm).astype(low)
    d_w_proj = dot_tn(conv_low, d_resid).astype(low)
    middle = jnp.concatenate(
        [dot_tn(normed_one, part).astype(low) for part in parts] + [d_w_proj, d_w_out], axis=1
    )
    d_resid, middle = beside((d_resid, middle), early)
    middle = Travel.whole(middle)
    d_conv = settled(beside(dot_nt(d_resid, w_proj), early), middle)

    d_shifted = [jnp.zeros((length, width), jnp.float32) for lag in range(4)]
    tap_rows = [None] * 9
    for index, (first, span) in enumerate(WINDOWS):
        (d_pre,) = gelu_backs[index](d_conv)
        for lag in range(span):
            tap_rows[first + lag] = jnp.sum(d_pre * shifted[lag], axis=0)
            d_shifted[lag] = d_shifted[lag] + d_pre * taps[first + lag]
    d_conv_taps = jnp.stack(tap_rows, axis=0)
    input_row = jnp.zeros((length, width), jnp.float32)
    for lag in range(4):
        input_row = input_row + earlier(jnp.where(keeps[lag], d_shifted[lag], 0.0), lag)
    early.go()
    input_low = beside(input_row.astype(low), middle)
    input_grad = to_blocks(input_low, share)
    d_emb_table = dot_tn(own_hot, input_low)

    late = jnp.concatenate(
        [
            d_emb_table,
            d_conv_taps,
            d_gain_one[None],
            d_gain_two,
            jnp.pad(d_rel_bias.reshape(1, -1), ((0, 0), (0, width - d_rel_bias.size))),
            jnp.zeros((width - vocab - 12, width), jnp.float32),
        ],
        axis=0,
    ).astype(low)
    late = Travel.whole(late)
    input_grad = settled(beside(input_grad, middle, late), early)
    early.go()
    late.go()
    scale = 1.0 / share
    middle.add(late)
    middle.state = settled(middle.state, early)
    middle.go()
    middle.go()
    d_w_in, d_w_down = finish_wide(mine, early.state, scale)
    middle.go()
    (
        d_w_qkv,
        d_w_proj,
        d_w_out,
        d_emb_table,
        d_conv_taps,
        d_gain_one,
        d_gain_two,
        d_rel_bias,
    ) = finish_rest(
        mine,
        *middle.state[0],
        scale,
        (
            (width, 3 * width),
            (width, width),
            (width, width),
            (vocab, width),
            (9, width),
            (1, width),
            (1, width),
            (1, bucket_count * heads),
        ),
    )
    d_gain_one = d_gain_one.reshape(width)
    d_gain_two = d_gain_two.reshape(width)
    d_rel_bias = d_rel_bias.reshape(bucket_count, heads)
    input_grad = placed(input_grad, share).astype(jnp.float32)
    return (
        output,
        input_grad,
        d_emb_table,
        d_conv_taps,
        d_w_proj,
        d_gain_one,
        d_w_qkv,
        d_rel_bias,
        d_w_out,
        d_gain_two,
        d_w_in,
        d_w_down,
    )


def solution(mesh):
    split = P("rows", "blk")
    split_wide = P("rows", "blk", None)
    return jax.shard_map(
        on_device,
        mesh=mesh,
        in_specs=(split, split) + (P(),) * 11 + (split_wide,),
        out_specs=(split_wide, split_wide) + (P(),) * 10,
        check_vma=False,
    )
```

```python
import functools

import jax
import jax.numpy as jnp
from jax import lax
from jax.experimental import pallas as pl
from jax.experimental.pallas import tpu as pltpu
from jax.sharding import PartitionSpec as P

EPSILON = 1e-06
SCORE_SCALE = 0.125
WINDOWS = ((0, 2), (2, 3), (5, 4))
HIGHEST_PRECISION = lax.Precision.HIGHEST
LANES = 128
QUERY_TILE = 256
KEY_TILE = 128
MASKED = -(2.0**30)
BAND = 12 * LANES
BAND_FIRST = 3 * LANES
MIB = 2**20


def vmem():
    return pl.BlockSpec(memory_space=pltpu.VMEM)


def smem():
    return pl.BlockSpec(memory_space=pltpu.SMEM)


def params(mib):
    return pltpu.CompilerParams(vmem_limit_bytes=mib * MIB)


def dot_nt(left, right):
    return lax.dot_general(
        left, right, (((1,), (1,)), ((), ())), preferred_element_type=jnp.float32
    )


def dot_nn(left, right):
    return jnp.dot(left, right, preferred_element_type=jnp.float32)


def bias_tables_kernel(base_ref, out_ref):
    heads = base_ref.shape[0]
    for head in range(heads):
        line = jnp.broadcast_to(base_ref[head : head + 1, :], (KEY_TILE, BAND))
        out_ref[head] = pltpu.roll(line, 0, 1, stride=1, stride_axis=0)


def bias_tables(base):
    heads = base.shape[0]
    return pl.pallas_call(
        bias_tables_kernel,
        out_shape=jax.ShapeDtypeStruct((heads, KEY_TILE, BAND), jnp.float32),
        in_specs=[vmem()],
        out_specs=vmem(),
        compiler_params=params(10),
        name="bias_tables",
    )(base)


def table_lanes(query_block, key_block):
    place = (query_block * (QUERY_TILE // LANES) - key_block + 5) * LANES
    return pl.ds(pl.multiple_of(place, LANES), QUERY_TILE)


def attend_kernel(
    heads, bounds_ref, qkv_ref, same_q_ref, same_k_ref, table_ref,
    attn_ref, lse_ref,
    value_t_ref, query_ref, top_ref, total_ref, mixed_ref, score_ref, expo_ref, fade_ref,
):
    length = qkv_ref.shape[0]
    width = qkv_ref.shape[1] // 3
    head_dim = width // heads
    lane = lax.broadcasted_iota(jnp.int32, (1, LANES), 1)
    halves = (
        (lane < head_dim).astype(jnp.bfloat16),
        (lane >= head_dim).astype(jnp.bfloat16),
    )
    value_t_ref[...] = qkv_ref[:, 2 * width :].T

    def block(i, carry):
        rows = pl.ds(pl.multiple_of(i * QUERY_TILE, QUERY_TILE), QUERY_TILE)
        for pair in range(heads // 2):
            query = qkv_ref[rows, pair * LANES : (pair + 1) * LANES] * jnp.bfloat16(SCORE_SCALE)
            for side in range(2):
                query_ref[2 * pair + side, :LANES, :] = (query * halves[side]).T
                query_ref[2 * pair + side, LANES:, :] = same_q_ref[:, rows]
        top_ref[...] = jnp.full_like(top_ref, -3.0e38)
        total_ref[...] = jnp.zeros_like(total_ref)
        mixed_ref[...] = jnp.zeros_like(mixed_ref)

        def step(j, inner):
            keys = pl.ds(pl.multiple_of(j * KEY_TILE, KEY_TILE), KEY_TILE)
            lanes = table_lanes(i, j)
            for head in range(heads):
                pair = head // 2
                key = jnp.concatenate(
                    [
                        qkv_ref[keys, width + pair * LANES : width + (pair + 1) * LANES],
                        same_k_ref[keys, :],
                    ],
                    axis=1,
                )
                score_ref[head] = dot_nn(key, query_ref[head]) + table_ref[head, :, lanes]
            for head in range(heads):
                scores = score_ref[head]
                old = top_ref[head : head + 1, :]
                top = jnp.maximum(old, jnp.max(scores, axis=0, keepdims=True))
                fade = jnp.exp(old - top)
                expo = jnp.exp(scores - top)
                top_ref[head : head + 1, :] = top
                total_ref[head : head + 1, :] = total_ref[head : head + 1, :] * fade + jnp.sum(
                    expo, axis=0, keepdims=True
                )
                fade_ref[head : head + 1, :] = fade
                expo_ref[head] = expo.astype(jnp.bfloat16)
            for head in range(heads):
                own = slice(head * head_dim, (head + 1) * head_dim)
                mixed_ref[own, :] = mixed_ref[own, :] * fade_ref[head : head + 1, :] + dot_nn(
                    value_t_ref[own, keys], expo_ref[head]
                )
            return inner

        lax.fori_loop(bounds_ref[0, i], bounds_ref[1, i], step, 0)
        for head in range(heads):
            own = slice(head * head_dim, (head + 1) * head_dim)
            mixed_ref[own, :] = mixed_ref[own, :] / total_ref[head : head + 1, :]
        attn_ref[rows, :] = mixed_ref[...].T.astype(jnp.bfloat16)
        lse_ref[:, rows] = top_ref[...] + jnp.log(total_ref[...])
        return carry

    lax.fori_loop(0, length // QUERY_TILE, block, 0)


def attend(bounds, qkv, same_q, same_k, table):
    length = qkv.shape[0]
    width = qkv.shape[1] // 3
    heads = table.shape[0]
    return pl.pallas_call(
        functools.partial(attend_kernel, heads),
        out_shape=(
            jax.ShapeDtypeStruct((length, width), jnp.bfloat16),
            jax.ShapeDtypeStruct((heads, length), jnp.float32),
        ),
        in_specs=[smem(), vmem(), vmem(), vmem(), vmem()],
        out_specs=(vmem(), vmem()),
        scratch_shapes=[
            pltpu.VMEM((width, length), jnp.bfloat16),
            pltpu.VMEM((heads, 2 * LANES, QUERY_TILE), jnp.bfloat16),
            pltpu.VMEM((heads, QUERY_TILE), jnp.float32),
            pltpu.VMEM((heads, QUERY_TILE), jnp.float32),
            pltpu.VMEM((width, QUERY_TILE), jnp.float32),
            pltpu.VMEM((heads, KEY_TILE, QUERY_TILE), jnp.float32),
            pltpu.VMEM((heads, KEY_TILE, QUERY_TILE), jnp.bfloat16),
            pltpu.VMEM((heads, QUERY_TILE), jnp.float32),
        ],
        compiler_params=params(16),
        cost_estimate=pl.CostEstimate(
            flops=4 * length * length * width,
            bytes_accessed=12 * 2**20,
            transcendentals=length * length * heads,
        ),
        name="attend",
    )(bounds, qkv, same_q, same_k, table)


def attend_back_kernel(
    first, bounds_ref, q_ref, k_ref, v_ref, same_q_ref, same_k_ref, table_ref, lse_ref,
    attn_ref, grad_ref, *refs,
):
    (
        query_out_ref, key_out_ref, value_out_ref, band_ref,
        key_t_ref, query_ref, grads_ref, query_t_ref, grads_t_ref, inner_ref,
        query_back_ref, key_back_ref, value_back_ref, skewed_ref,
        exact_ref, probs_ref, d_scores_ref,
    ) = refs[-17:]
    length, width = q_ref.shape
    heads = table_ref.shape[0]
    head_dim = width // heads
    lane = lax.broadcasted_iota(jnp.int32, (1, LANES), 1)
    halves = (
        (lane < head_dim).astype(jnp.bfloat16),
        (lane >= head_dim).astype(jnp.bfloat16),
    )
    owner = lax.broadcasted_iota(jnp.int32, (heads, width), 1) // head_dim
    own_head = (owner == lax.broadcasted_iota(jnp.int32, (heads, width), 0)).astype(jnp.bfloat16)
    key_t_ref[...] = k_ref[...].T
    key_back_ref[...] = jnp.zeros_like(key_back_ref)
    value_back_ref[...] = jnp.zeros_like(value_back_ref)
    skewed_ref[...] = jnp.zeros_like(skewed_ref)

    def block(i, carry):
        rows = pl.ds(pl.multiple_of(i * QUERY_TILE, QUERY_TILE), QUERY_TILE)
        for pair in range(heads // 2):
            own = slice(pair * LANES, (pair + 1) * LANES)
            query = q_ref[rows, own] * jnp.bfloat16(SCORE_SCALE)
            grad = grad_ref[rows, own]
            for side in range(2):
                part = slice(side * QUERY_TILE, (side + 1) * QUERY_TILE)
                query_ref[pair, part, :] = query * halves[side]
                grads_ref[pair, part, :] = grad * halves[side]
                query_t_ref[2 * pair + side, :LANES, :] = (query * halves[side]).T
                query_t_ref[2 * pair + side, LANES:, :] = same_q_ref[:, rows]
                grads_t_ref[2 * pair + side] = (grad * halves[side]).T
        product = grad_ref[rows, :].astype(jnp.float32) * attn_ref[rows, :].astype(jnp.float32)
        rough = product.astype(jnp.bfloat16)
        rest = (product - rough.astype(jnp.float32)).astype(jnp.bfloat16)
        inner_ref[...] = dot_nt(own_head, rough) + dot_nt(own_head, rest)
        query_back_ref[...] = jnp.zeros_like(query_back_ref)

        def step(j, inner):
            keys = pl.ds(pl.multiple_of(j * KEY_TILE, KEY_TILE), KEY_TILE)
            lanes = table_lanes(i, j)
            for head in range(heads):
                pair = head // 2
                key = jnp.concatenate(
                    [k_ref[keys, pair * LANES : (pair + 1) * LANES], same_k_ref[keys, :]], axis=1
                )
                scores = dot_nn(key, query_t_ref[head]) + table_ref[head, :, lanes]
                exact_ref[head] = jnp.exp(scores - lse_ref[first + head : first + head + 1, rows])
            for head in range(heads):
                pair = head // 2
                part = slice((head % 2) * QUERY_TILE, (head % 2 + 1) * QUERY_TILE)
                d_probs = dot_nn(v_ref[keys, pair * LANES : (pair + 1) * LANES], grads_t_ref[head])
                exact = exact_ref[head]
                d_score = exact * (d_probs - inner_ref[head : head + 1, :])
                skewed_ref[head, :, lanes] = skewed_ref[head, :, lanes] + d_score
                probs_ref[pair, :, part] = exact.astype(jnp.bfloat16)
                d_scores_ref[pair, :, part] = d_score.astype(jnp.bfloat16)
            for pair in range(heads // 2):
                own = slice(pair * LANES, (pair + 1) * LANES)
                value_back_ref[keys, own] += dot_nn(probs_ref[pair], grads_ref[pair])
                key_back_ref[keys, own] += dot_nn(d_scores_ref[pair], query_ref[pair])
            for head in range(heads):
                part = slice((head % 2) * QUERY_TILE, (head % 2 + 1) * QUERY_TILE)
                mine = slice(head * head_dim, (head + 1) * head_dim)
                query_back_ref[mine, :] += dot_nn(
                    key_t_ref[mine, keys], d_scores_ref[head // 2, :, part]
                )
            return inner

        lax.fori_loop(bounds_ref[0, i], bounds_ref[1, i], step, 0)
        query_out_ref[rows, :] = (query_back_ref[...].T * SCORE_SCALE).astype(jnp.bfloat16)
        return carry

    lax.fori_loop(0, length // QUERY_TILE, block, 0)
    key_out_ref[...] = key_back_ref[...].astype(jnp.bfloat16)
    value_out_ref[...] = value_back_ref[...].astype(jnp.bfloat16)
    for head in range(heads):
        height = KEY_TILE
        while height > 8:
            height //= 2
            skewed_ref[head, :height, :] = skewed_ref[head, :height, :] + pltpu.roll(
                skewed_ref[head, height : 2 * height, :], BAND - height, 1
            )
        total = skewed_ref[head, 0:1, :]
        for row in range(1, 8):
            total = total + pltpu.roll(skewed_ref[head, row : row + 1, :], BAND - row, 1)
        band_ref[head : head + 1, :] = total


def attend_back(part, parts, bounds, qkv, same_q, same_k, table, lse, attn, grad, earlier_parts=()):
    length = qkv.shape[0]
    width = qkv.shape[1] // 3
    heads = table.shape[0] // parts
    span = width // parts

    def columns(group):
        return pl.BlockSpec(
            (length, span),
            lambda _: (0, group * parts + part),
            pipeline_mode=pl.Buffered(1),
        )

    whole = [smem(), columns(0), columns(1), columns(2), vmem(), vmem()]
    whole += [
        pl.BlockSpec(
            (heads, KEY_TILE, BAND), lambda _: (part, 0, 0), pipeline_mode=pl.Buffered(1)
        ),
        vmem(),
    ]
    whole += [columns(0), columns(0)] + [pl.BlockSpec(memory_space=pl.ANY)] * len(earlier_parts)
    return pl.pallas_call(
        functools.partial(attend_back_kernel, part * heads),
        out_shape=[jax.ShapeDtypeStruct((length, width), jnp.bfloat16)] * 3
        + [jax.ShapeDtypeStruct((heads, BAND), jnp.float32)],
        grid=(1,),
        in_specs=whole,
        out_specs=[columns(0)] * 3 + [vmem()],
        input_output_aliases={10 + at: at for at in range(len(earlier_parts))},
        scratch_shapes=[
            pltpu.VMEM((span, length), jnp.bfloat16),
            pltpu.VMEM((heads // 2, 2 * QUERY_TILE, LANES), jnp.bfloat16),
            pltpu.VMEM((heads // 2, 2 * QUERY_TILE, LANES), jnp.bfloat16),
            pltpu.VMEM((heads, 2 * LANES, QUERY_TILE), jnp.bfloat16),
            pltpu.VMEM((heads, LANES, QUERY_TILE), jnp.bfloat16),
            pltpu.VMEM((heads, QUERY_TILE), jnp.float32),
            pltpu.VMEM((span, QUERY_TILE), jnp.float32),
            pltpu.VMEM((length, span), jnp.float32),
            pltpu.VMEM((length, span), jnp.float32),
            pltpu.VMEM((heads, KEY_TILE, BAND), jnp.float32),
            pltpu.VMEM((heads, KEY_TILE, QUERY_TILE), jnp.float32),
            pltpu.VMEM((heads // 2, KEY_TILE, 2 * QUERY_TILE), jnp.bfloat16),
            pltpu.VMEM((heads // 2, KEY_TILE, 2 * QUERY_TILE), jnp.bfloat16),
        ],
        compiler_params=params(34),
        cost_estimate=pl.CostEstimate(
            flops=40 * length * length * span,
            bytes_accessed=8 * 2**20,
            transcendentals=length * length * heads,
        ),
        name="attend_back",
    )(bounds, qkv, qkv, qkv, same_q, same_k, table, lse, attn, grad, *earlier_parts)


def document_bounds(segments):
    length = segments.shape[0]
    starts = segments[::QUERY_TILE]
    ends = segments[QUERY_TILE - 1 :: QUERY_TILE]
    before = jnp.sum((segments[None, :] < starts[:, None]).astype(jnp.int32), axis=1)
    upto = jnp.sum((segments[None, :] <= ends[:, None]).astype(jnp.int32), axis=1)
    return jnp.stack([before // KEY_TILE, (upto + KEY_TILE - 1) // KEY_TILE])


def document_marks(segments):
    own = segments[:, None] == jnp.arange(LANES, dtype=jnp.int32)[None, :]
    own_t = segments[None, :] == jnp.arange(LANES, dtype=jnp.int32)[:, None]
    return own_t.astype(jnp.bfloat16), jnp.where(own, 0.0, MASKED).astype(jnp.bfloat16)
HIDDEN_TILE = 512
GELU_SLOPE = 0.7978845608028654
GELU_CUBIC = 0.044715


def gelu_parts(values):
    square = values * values
    bend = jnp.tanh(values * (GELU_SLOPE + GELU_SLOPE * GELU_CUBIC * square))
    half = 0.5 + 0.5 * bend
    slope = half + values * (1.0 - bend * bend) * (
        0.5 * GELU_SLOPE + 1.5 * GELU_SLOPE * GELU_CUBIC * square
    )
    return values * half, slope


def feed_forward_kernel(
    attn_ref, resid_ref, grad_ref, w_out_ref, gain_ref, w_gate_ref, w_upper_ref, w_down_ref,
    output_ref, weight_back_ref, d_mid_ref, d_attn_ref, d_w_out_ref, d_gain_ref,
    mid_ref, rinv_ref, normed_ref, normed_t_ref, grad_t_ref, sum_ref, back_ref,
    gate_ref, upper_ref, d_inner_ref, inner_ref, d_gate_ref, d_upper_ref,
):
    step = pl.program_id(0)
    width = attn_ref.shape[1]

    @pl.when(step == 0)
    def _():
        mid = resid_ref[...] + dot_nn(attn_ref[...], w_out_ref[...])
        rinv = lax.rsqrt(jnp.mean(mid * mid, axis=-1, keepdims=True) + EPSILON)
        normed = (mid * rinv * gain_ref[...]).astype(jnp.bfloat16)
        mid_ref[...] = mid
        rinv_ref[...] = jnp.broadcast_to(rinv, rinv_ref.shape)
        normed_ref[...] = normed
        normed_t_ref[...] = normed.T
        grad_t_ref[...] = grad_ref[...].T
        sum_ref[...] = mid
        back_ref[...] = jnp.zeros_like(back_ref)

    gate_ref[...] = dot_nn(normed_ref[...], w_gate_ref[...])
    upper_ref[...] = dot_nn(normed_ref[...], w_upper_ref[...])
    d_inner_ref[...] = dot_nt(grad_ref[...], w_down_ref[...])
    upper = upper_ref[...]
    d_inner = d_inner_ref[...]
    bent, slope = gelu_parts(gate_ref[...])
    inner_ref[...] = (bent * upper).astype(jnp.bfloat16)
    d_gate_ref[...] = (d_inner * upper * slope).astype(jnp.bfloat16)
    d_upper_ref[...] = (d_inner * bent).astype(jnp.bfloat16)
    for plane, (left_ref, right_ref) in enumerate(
        ((normed_t_ref, d_gate_ref), (normed_t_ref, d_upper_ref), (grad_t_ref, inner_ref))
    ):
        columns = slice(plane * HIDDEN_TILE, (plane + 1) * HIDDEN_TILE)
        weight_back_ref[:, columns] = dot_nn(left_ref[...], right_ref[...]).astype(jnp.bfloat16)
    sum_ref[...] += dot_nn(inner_ref[...], w_down_ref[...])
    back_ref[...] += dot_nt(d_gate_ref[...], w_gate_ref[...]) + dot_nt(
        d_upper_ref[...], w_upper_ref[...]
    )

    @pl.when(step == pl.num_programs(0) - 1)
    def _():
        output_ref[...] = sum_ref[...].astype(jnp.bfloat16)
        rinv = rinv_ref[:, :1]
        mid = mid_ref[...]
        d_normed = back_ref[...]
        d_gain_ref[...] = jnp.sum(d_normed * mid * rinv, axis=0, keepdims=True)
        scaled = d_normed * gain_ref[...]
        lean = jnp.mean(scaled * mid, axis=-1, keepdims=True) * (rinv * rinv * rinv)
        d_mid = grad_ref[...].astype(jnp.float32) + rinv * scaled - mid * lean
        d_mid_ref[...] = d_mid
        d_branch = d_mid.astype(jnp.bfloat16)
        d_attn_ref[...] = dot_nt(d_branch, w_out_ref[...]).astype(jnp.bfloat16)
        d_w_out_ref[...] = dot_nn(attn_ref[...].T, d_branch).astype(jnp.bfloat16)


def feed_forward(attn, resid, grad, w_out, gain, w_in, w_down):
    length, width = attn.shape
    hidden = w_down.shape[0]
    steps = hidden // HIDDEN_TILE

    low = jnp.bfloat16
    return pl.pallas_call(
        feed_forward_kernel,
        grid=(steps,),
        out_shape=(
            jax.ShapeDtypeStruct((length, width), low),
            jax.ShapeDtypeStruct((width, 3 * hidden), low),
            jax.ShapeDtypeStruct((length, width), jnp.float32),
            jax.ShapeDtypeStruct((length, width), low),
            jax.ShapeDtypeStruct((width, width), low),
            jax.ShapeDtypeStruct((1, width), jnp.float32),
        ),
        in_specs=[
            vmem(),
            vmem(),
            vmem(),
            vmem(),
            vmem(),
            pl.BlockSpec((width, HIDDEN_TILE), lambda c: (0, c)),
            pl.BlockSpec((width, HIDDEN_TILE), lambda c: (0, steps + c)),
            pl.BlockSpec((HIDDEN_TILE, width), lambda c: (c, 0)),
        ],
        out_specs=(
            vmem(),
            pl.BlockSpec((width, 3 * HIDDEN_TILE), lambda c: (0, c)),
            vmem(),
            vmem(),
            vmem(),
            vmem(),
        ),
        scratch_shapes=[
            pltpu.VMEM((length, width), jnp.float32),
            pltpu.VMEM((length, LANES), jnp.float32),
            pltpu.VMEM((length, width), low),
            pltpu.VMEM((width, length), low),
            pltpu.VMEM((width, length), low),
            pltpu.VMEM((length, width), jnp.float32),
            pltpu.VMEM((length, width), jnp.float32),
            pltpu.VMEM((length, HIDDEN_TILE), jnp.float32),
            pltpu.VMEM((length, HIDDEN_TILE), jnp.float32),
            pltpu.VMEM((length, HIDDEN_TILE), jnp.float32),
            pltpu.VMEM((length, HIDDEN_TILE), low),
            pltpu.VMEM((length, HIDDEN_TILE), low),
            pltpu.VMEM((length, HIDDEN_TILE), low),
        ],
        compiler_params=params(40),
        cost_estimate=pl.CostEstimate(
            flops=18 * length * width * hidden + 6 * length * width * width,
            bytes_accessed=24 * 2**20,
            transcendentals=length * hidden,
        ),
        name="feed_forward",
    )(attn, resid, grad, w_out, gain.reshape(1, width), w_in, w_in, w_down)


def finish_wide_kernel(scale, piece_ref, d_w_in_ref, d_w_down_ref):
    piece = piece_ref[...].astype(jnp.float32) * scale

    @pl.when(pl.program_id(0) < 2)
    def _():
        d_w_in_ref[...] = piece

    @pl.when(pl.program_id(0) == 2)
    def _():
        d_w_down_ref[...] = piece.T


def finish_wide(total, scale):
    width = total.shape[0]
    hidden = total.shape[1] // 3
    tiles = hidden // HIDDEN_TILE
    return pl.pallas_call(
        functools.partial(finish_wide_kernel, scale),
        grid=(3, tiles),
        out_shape=(
            jax.ShapeDtypeStruct((width, 2 * hidden), jnp.float32),
            jax.ShapeDtypeStruct((hidden, width), jnp.float32),
        ),
        in_specs=[pl.BlockSpec((width, HIDDEN_TILE), lambda p, c: (0, c * 3 + p))],
        out_specs=(
            pl.BlockSpec(
                (width, HIDDEN_TILE), lambda p, c: (0, jnp.where(p < 2, p * tiles + c, 2 * tiles - 1))
            ),
            pl.BlockSpec((HIDDEN_TILE, width), lambda p, c: (jnp.where(p < 2, 0, c), 0)),
        ),
        compiler_params=params(16),
        cost_estimate=pl.CostEstimate(
            flops=6 * width * hidden, bytes_accessed=18 * width * hidden, transcendentals=0
        ),
        name="finish_wide",
    )(total)


def finish_rest_kernel(scale, mine_ref, own_ref, other_ref, *refs):
    qkv_ref, proj_ref, out_ref, emb_ref, taps_ref, one_ref, two_ref, bias_ref, joined_ref = refs
    half = own_ref.shape[0]
    mine = mine_ref[0]
    for piece_ref, side in ((own_ref, mine), (other_ref, 1 - mine)):
        part = pl.ds(pl.multiple_of(side * half, half), half)
        joined_ref[part, :] = piece_ref[...].astype(jnp.float32) * scale
    at = 0
    for ref in (qkv_ref, proj_ref, out_ref):
        span = ref.shape[1]
        ref[...] = joined_ref[:, at : at + span]
        at += span
    row = 0
    for ref in (emb_ref, taps_ref, one_ref, two_ref, bias_ref):
        rows, span = ref.shape
        ref[...] = joined_ref[row : row + rows, at : at + span]
        row += rows


def finish_rest(mine, own, other, scale, shapes):
    half, columns = own.shape
    return pl.pallas_call(
        functools.partial(finish_rest_kernel, scale),
        out_shape=[jax.ShapeDtypeStruct(shape, jnp.float32) for shape in shapes],
        in_specs=[smem(), vmem(), vmem()],
        out_specs=[vmem()] * len(shapes),
        scratch_shapes=[pltpu.VMEM((2 * half, columns), jnp.float32)],
        compiler_params=params(16),
        cost_estimate=pl.CostEstimate(
            flops=4 * half * columns, bytes_accessed=12 * half * columns, transcendentals=0
        ),
        name="finish_rest",
    )(mine, own, other)


def dot_tn(left, right):
    return lax.dot_general(
        left, right, (((0,), (0,)), ((), ())), preferred_element_type=jnp.float32
    )


def to_rows(block, share):
    rows, stretch = block.shape[:2]
    pieces = jnp.repeat(block, share, axis=0) if share > 1 else block
    pieces = lax.all_to_all(pieces, "blk", 0, 0, tiled=True)
    return pieces.reshape((rows * share * stretch,) + block.shape[2:])


def to_blocks(row, share):
    blocks = lax.axis_size("blk")
    place = lax.axis_index("blk")
    stretch = row.shape[0] // blocks

    def piece(owner):
        return lax.dynamic_slice_in_dim(row, owner * stretch, stretch, axis=0)

    pieces = [piece(place)]
    for gap in range(1, blocks):
        devices = range(blocks)
        pieces.append(lax.ppermute(piece(place ^ gap), "blk", [(i, i ^ gap) for i in devices]))
    return pieces


def placed(pieces, share):
    place = lax.axis_index("blk")
    gap = 1
    while gap < len(pieces):
        stays = (place & gap) == 0
        pieces = [jnp.where(stays, pieces[at], pieces[at ^ gap]) for at in range(len(pieces))]
        gap *= 2
    return jnp.stack(pieces[::share])


def later(values, lag):
    if lag == 0:
        return values
    return jnp.pad(values, ((lag, 0), (0, 0)))[: values.shape[0]]


def earlier(values, lag):
    if lag == 0:
        return values
    return jnp.pad(values, ((0, lag), (0, 0)))[lag:]


def own_bit(axis, bit):
    return (lax.axis_index(axis) >> bit) & 1


def swapped(block, axis, bit):
    devices = range(lax.axis_size(axis))
    return lax.ppermute(block, axis, [(i, i ^ (1 << bit)) for i in devices])


def bits_of(axis):
    return lax.axis_size(axis).bit_length() - 1


def group_of(free):
    blk = lax.axis_size("blk")
    devices = range(lax.axis_size("rows") * blk)
    weights = [(blk if axis == "rows" else 1) << bit for axis, bit in free]
    place = sum(own_bit(axis, bit) << at for at, (axis, bit) in enumerate(free))

    def send(block, gap):
        shift = sum(weight for at, weight in enumerate(weights) if gap >> at & 1)
        return lax.ppermute(block, ("rows", "blk"), [(i, i ^ shift) for i in devices])

    return 1 << len(free), place, send


class Travel:
    def __init__(self, kept, sent):
        near = [("blk", bit) for bit in range(1, bits_of("blk"))] + [("rows", 0)]
        far = [("rows", bit) for bit in range(1, bits_of("rows"))]
        stages = (group_of(near), group_of(far))
        terms = [kept, swapped(sent, "blk", 0)]
        self.state = [terms]
        self.orders = [stages]
        self.at = 0

    @classmethod
    def whole(cls, block):
        half = block.shape[0] // 2
        mine = own_bit("blk", 0)
        sent = lax.dynamic_slice_in_dim(block, (1 - mine) * half, half, axis=0)
        kept = lax.dynamic_slice_in_dim(block, mine * half, half, axis=0)
        return cls(kept, sent)

    def add(self, other):
        assert self.at == other.at == 2 and len(self.state) == len(other.state) == 1
        self.state = [[jnp.concatenate([total(self.state[0]), total(other.state[0])], axis=1)]]

    def go(self):
        self.state = [self.lane_step(*lane) for lane in zip(self.state, self.orders)]
        self.at += 1

    def lane_step(self, terms, order):
        block = total(terms)
        if self.at == 4:
            return [block, swapped(block, "blk", 0)]
        count, place, send = order[self.at if self.at < 2 else 3 - self.at]
        if self.at < 2:
            rows = block.shape[0] // count
            def piece(owner):
                return lax.dynamic_slice_in_dim(block, owner * rows, rows, axis=0)

            return [piece(place)] + [send(piece(place ^ gap), gap) for gap in range(1, count)]
        pieces = [block] + [send(block, gap) for gap in range(1, count)]
        gap = 1
        while gap < count:
            stays = (place & gap) == 0
            pieces = [jnp.where(stays, pieces[at], pieces[at ^ gap]) for at in range(count)]
            gap *= 2
        return [jnp.concatenate(pieces, axis=0)]


def total(terms):
    first, *others = terms
    if not others:
        return first
    wide = first.astype(jnp.float32)
    for other in others:
        wide = wide + other.astype(jnp.float32)
    return wide.astype(first.dtype)


def beside(values, *travels):
    for travel in travels:
        travel.go()
    return settled(values, *travels)


def settled(values, *travels):
    states, values = lax.optimization_barrier(([travel.state for travel in travels], values))
    for travel, state in zip(travels, states):
        travel.state = state
    return values


def on_device(
    byte_vals,
    segment_ids,
    buckets,
    emb_table,
    conv_taps,
    w_proj,
    gain_one,
    w_qkv,
    rel_bias,
    w_out,
    gain_two,
    w_in,
    w_down,
    out_grad,
):
    rows, stretch = byte_vals.shape
    vocab, width = emb_table.shape
    bucket_count, heads = rel_bias.shape
    hidden = w_down.shape[0]
    blocks = lax.axis_size("blk")
    share = blocks // rows
    length = stretch * blocks
    low = jnp.bfloat16

    packed = to_rows(byte_vals + vocab * segment_ids, share)
    letters_own = packed % vocab
    segments = packed // vocab
    grad_low = to_rows(out_grad, share)

    own_hot = (letters_own[:, None] == jnp.arange(vocab, dtype=jnp.int32)[None, :]).astype(low)
    embedded = dot_nn(own_hot, emb_table)
    taps = conv_taps.astype(jnp.float32)
    seg_col = segments[:, None] + 1

    def lagged():
        keeps = [later(seg_col, lag) == seg_col for lag in range(4)]
        shifted = [jnp.where(keeps[lag], later(embedded, lag), 0.0) for lag in range(4)]
        sums = [
            sum(shifted[lag] * taps[first + lag] for lag in range(span)) for first, span in WINDOWS
        ]
        return keeps, shifted, sums

    conv_low = sum(gelu_parts(summed)[0] for summed in lagged()[2]).astype(low)
    resid = dot_nn(conv_low, w_proj)
    rinv_one = lax.rsqrt(jnp.mean(resid * resid, axis=-1, keepdims=True) + EPSILON)
    normed_one = (resid * rinv_one * gain_one).astype(low)
    qkv = dot_nn(normed_one, w_qkv).astype(low)

    band_buckets = lax.slice_in_dim(buckets, BAND_FIRST, BAND_FIRST + BAND - LANES)
    band_buckets = jnp.concatenate(
        [band_buckets, lax.slice_in_dim(buckets, BAND_FIRST - LANES, BAND_FIRST)]
    )
    bucket_hot = (
        band_buckets[:, None] == jnp.arange(bucket_count, dtype=jnp.int32)[None, :]
    ).astype(jnp.float32)
    base = lax.dot_general(
        rel_bias, bucket_hot, (((0,), (1,)), ((), ())), precision=HIGHEST_PRECISION
    )
    table = bias_tables(base)
    bounds = document_bounds(segments)
    same_q, same_k = document_marks(segments)
    attn, lse = attend(bounds, qkv, same_q, same_k, table)

    mine = own_bit("blk", 0).astype(jnp.int32).reshape(1)
    scale = 1.0 / share
    output_row, d_wide, d_mid, d_attn, d_w_out, d_gain_two = feed_forward(
        attn, resid, grad_low, w_out, gain_two, w_in, w_down
    )

    def remainder():
        output = to_blocks(output_row, share)

        *parts, band = attend_back(0, 1, bounds, qkv, same_q, same_k, table, lse, attn, d_attn)
        parts, output = lax.optimization_barrier((parts, output))
        output = placed(output, share)
        d_rel_bias = lax.dot_general(
            bucket_hot, band, (((0,), (1,)), ((), ())), precision=HIGHEST_PRECISION
        )
        d_normed_one = sum(
            dot_nt(part, w_qkv[:, at * width : (at + 1) * width]) for at, part in enumerate(parts)
        )
        d_gain_one = jnp.sum(d_normed_one * resid * rinv_one, axis=0)
        scaled = d_normed_one * gain_one
        lean = jnp.mean(scaled * resid, axis=-1, keepdims=True) * (rinv_one * rinv_one * rinv_one)
        d_resid = (d_mid + rinv_one * scaled - resid * lean).astype(low)
        d_w_proj = dot_tn(conv_low, d_resid).astype(low)
        middle = jnp.concatenate(
            [dot_tn(normed_one, part).astype(low) for part in parts] + [d_w_proj, d_w_out], axis=1
        )
        d_resid, middle = lax.optimization_barrier((d_resid, middle))
        middle = Travel.whole(middle)
        d_conv = settled(dot_nt(d_resid, w_proj), middle)

        keeps, shifted, sums = lagged()
        d_shifted = [jnp.zeros((length, width), jnp.float32) for lag in range(4)]
        tap_rows = [None] * 9
        for index, (first, span) in enumerate(WINDOWS):
            d_pre = d_conv * gelu_parts(sums[index])[1]
            for lag in range(span):
                tap_rows[first + lag] = jnp.sum(d_pre * shifted[lag], axis=0)
                d_shifted[lag] = d_shifted[lag] + d_pre * taps[first + lag]
        d_conv_taps = jnp.stack(tap_rows, axis=0)
        input_row = jnp.zeros((length, width), jnp.float32)
        for lag in range(4):
            input_row = input_row + earlier(jnp.where(keeps[lag], d_shifted[lag], 0.0), lag)
        input_low = beside(input_row.astype(low), middle)
        input_grad = to_blocks(input_low, share)
        d_emb_table = dot_tn(own_hot, input_low)

        late = jnp.concatenate(
            [
                d_emb_table,
                d_conv_taps,
                d_gain_one[None],
                d_gain_two,
                jnp.pad(d_rel_bias.reshape(1, -1), ((0, 0), (0, width - d_rel_bias.size))),
                jnp.zeros((width - vocab - 12, width), jnp.float32),
            ],
            axis=0,
        ).astype(low)
        late = Travel.whole(late)
        input_grad = beside(input_grad, middle, late)
        late.go()
        middle.add(late)
        middle.go()
        middle.go()
        middle.go()
        finished = finish_rest(
            mine,
            *middle.state[0],
            scale,
            (
                (width, 3 * width),
                (width, width),
                (width, width),
                (vocab, width),
                (9, width),
                (1, width),
                (1, width),
                (1, bucket_count * heads),
            ),
        )
        input_grad = placed(input_grad, share).astype(jnp.float32)
        return output, input_grad, finished

    def nothing():
        return jax.tree.map(lambda leaf: jnp.zeros(leaf.shape, leaf.dtype), shapes)

    shapes = jax.eval_shape(remainder)
    d_wide = lax.psum(d_wide, ("rows", "blk"))
    output, input_grad, finished = lax.cond(segments[0] >= 0, remainder, nothing)
    (
        d_w_qkv,
        d_w_proj,
        d_w_out,
        d_emb_table,
        d_conv_taps,
        d_gain_one,
        d_gain_two,
        d_rel_bias,
    ) = finished
    d_w_in, d_w_down = finish_wide(d_wide, scale)
    d_gain_one = d_gain_one.reshape(width)
    d_gain_two = d_gain_two.reshape(width)
    d_rel_bias = d_rel_bias.reshape(bucket_count, heads)
    return (
        output,
        input_grad,
        d_emb_table,
        d_conv_taps,
        d_w_proj,
        d_gain_one,
        d_w_qkv,
        d_rel_bias,
        d_w_out,
        d_gain_two,
        d_w_in,
        d_w_down,
    )


def solution(mesh):
    split = P("rows", "blk")
    split_wide = P("rows", "blk", None)
    return jax.shard_map(
        on_device,
        mesh=mesh,
        in_specs=(split, split) + (P(),) * 11 + (split_wide,),
        out_specs=(split_wide, split_wide) + (P(),) * 10,
        check_vma=False,
    )
```

```python
import functools

import jax
import jax.numpy as jnp
from jax import lax
from jax.experimental import pallas as pl
from jax.experimental.pallas import tpu as pltpu
from jax.sharding import PartitionSpec as P

EPSILON = 1e-06
SCORE_SCALE = 0.125
WINDOWS = ((0, 2), (2, 3), (5, 4))
HIGHEST_PRECISION = lax.Precision.HIGHEST
LANES = 128
QUERY_TILE = 256
KEY_TILE = 128
MASKED = -(2.0**30)
BAND = 12 * LANES
BAND_FIRST = 3 * LANES
MIB = 2**20


def vmem():
    return pl.BlockSpec(memory_space=pltpu.VMEM)


def smem():
    return pl.BlockSpec(memory_space=pltpu.SMEM)


def params(mib):
    return pltpu.CompilerParams(vmem_limit_bytes=mib * MIB)


def dot_nt(left, right):
    return lax.dot_general(
        left, right, (((1,), (1,)), ((), ())), preferred_element_type=jnp.float32
    )


def dot_nn(left, right):
    return jnp.dot(left, right, preferred_element_type=jnp.float32)


def bias_tables_kernel(base_ref, out_ref):
    heads = base_ref.shape[0]
    for head in range(heads):
        line = jnp.broadcast_to(base_ref[head : head + 1, :], (KEY_TILE, BAND))
        out_ref[head] = pltpu.roll(line, 0, 1, stride=1, stride_axis=0)


def bias_tables(base):
    heads = base.shape[0]
    return pl.pallas_call(
        bias_tables_kernel,
        out_shape=jax.ShapeDtypeStruct((heads, KEY_TILE, BAND), jnp.float32),
        in_specs=[vmem()],
        out_specs=vmem(),
        compiler_params=params(10),
        name="bias_tables",
    )(base)


def table_lanes(query_block, key_block):
    place = (query_block * (QUERY_TILE // LANES) - key_block + 5) * LANES
    return pl.ds(pl.multiple_of(place, LANES), QUERY_TILE)


def attend_kernel(
    heads, bounds_ref, qkv_ref, same_q_ref, same_k_ref, table_ref,
    attn_ref, lse_ref,
    value_t_ref, query_ref, top_ref, total_ref, mixed_ref, score_ref, expo_ref, fade_ref,
):
    length = qkv_ref.shape[0]
    width = qkv_ref.shape[1] // 3
    head_dim = width // heads
    lane = lax.broadcasted_iota(jnp.int32, (1, LANES), 1)
    halves = (
        (lane < head_dim).astype(jnp.bfloat16),
        (lane >= head_dim).astype(jnp.bfloat16),
    )
    value_t_ref[...] = qkv_ref[:, 2 * width :].T

    def block(i, carry):
        rows = pl.ds(pl.multiple_of(i * QUERY_TILE, QUERY_TILE), QUERY_TILE)
        for pair in range(heads // 2):
            query = qkv_ref[rows, pair * LANES : (pair + 1) * LANES] * jnp.bfloat16(SCORE_SCALE)
            for side in range(2):
                query_ref[2 * pair + side, :LANES, :] = (query * halves[side]).T
                query_ref[2 * pair + side, LANES:, :] = same_q_ref[:, rows]
        top_ref[...] = jnp.full_like(top_ref, -3.0e38)
        total_ref[...] = jnp.zeros_like(total_ref)
        mixed_ref[...] = jnp.zeros_like(mixed_ref)

        def step(j, inner):
            keys = pl.ds(pl.multiple_of(j * KEY_TILE, KEY_TILE), KEY_TILE)
            lanes = table_lanes(i, j)
            for head in range(heads):
                pair = head // 2
                key = jnp.concatenate(
                    [
                        qkv_ref[keys, width + pair * LANES : width + (pair + 1) * LANES],
                        same_k_ref[keys, :],
                    ],
                    axis=1,
                )
                score_ref[head] = dot_nn(key, query_ref[head]) + table_ref[head, :, lanes]
            for head in range(heads):
                scores = score_ref[head]
                old = top_ref[head : head + 1, :]
                top = jnp.maximum(old, jnp.max(scores, axis=0, keepdims=True))
                fade = jnp.exp(old - top)
                expo = jnp.exp(scores - top)
                top_ref[head : head + 1, :] = top
                total_ref[head : head + 1, :] = total_ref[head : head + 1, :] * fade + jnp.sum(
                    expo, axis=0, keepdims=True
                )
                fade_ref[head : head + 1, :] = fade
                expo_ref[head] = expo.astype(jnp.bfloat16)
            for head in range(heads):
                own = slice(head * head_dim, (head + 1) * head_dim)
                mixed_ref[own, :] = mixed_ref[own, :] * fade_ref[head : head + 1, :] + dot_nn(
                    value_t_ref[own, keys], expo_ref[head]
                )
            return inner

        lax.fori_loop(bounds_ref[0, i], bounds_ref[1, i], step, 0)
        for head in range(heads):
            own = slice(head * head_dim, (head + 1) * head_dim)
            mixed_ref[own, :] = mixed_ref[own, :] / total_ref[head : head + 1, :]
        attn_ref[rows, :] = mixed_ref[...].T.astype(jnp.bfloat16)
        lse_ref[:, rows] = top_ref[...] + jnp.log(total_ref[...])
        return carry

    lax.fori_loop(0, length // QUERY_TILE, block, 0)


def attend(bounds, qkv, same_q, same_k, table):
    length = qkv.shape[0]
    width = qkv.shape[1] // 3
    heads = table.shape[0]
    return pl.pallas_call(
        functools.partial(attend_kernel, heads),
        out_shape=(
            jax.ShapeDtypeStruct((length, width), jnp.bfloat16),
            jax.ShapeDtypeStruct((heads, length), jnp.float32),
        ),
        in_specs=[smem(), vmem(), vmem(), vmem(), vmem()],
        out_specs=(vmem(), vmem()),
        scratch_shapes=[
            pltpu.VMEM((width, length), jnp.bfloat16),
            pltpu.VMEM((heads, 2 * LANES, QUERY_TILE), jnp.bfloat16),
            pltpu.VMEM((heads, QUERY_TILE), jnp.float32),
            pltpu.VMEM((heads, QUERY_TILE), jnp.float32),
            pltpu.VMEM((width, QUERY_TILE), jnp.float32),
            pltpu.VMEM((heads, KEY_TILE, QUERY_TILE), jnp.float32),
            pltpu.VMEM((heads, KEY_TILE, QUERY_TILE), jnp.bfloat16),
            pltpu.VMEM((heads, QUERY_TILE), jnp.float32),
        ],
        compiler_params=params(16),
        cost_estimate=pl.CostEstimate(
            flops=4 * length * length * width,
            bytes_accessed=12 * 2**20,
            transcendentals=length * length * heads,
        ),
        name="attend",
    )(bounds, qkv, same_q, same_k, table)


def attend_back_kernel(
    first, bounds_ref, q_ref, k_ref, v_ref, same_q_ref, same_k_ref, table_ref, lse_ref,
    attn_ref, grad_ref, *refs,
):
    (
        query_out_ref, key_out_ref, value_out_ref, band_ref,
        key_t_ref, query_ref, grads_ref, query_t_ref, grads_t_ref, inner_ref,
        query_back_ref, key_back_ref, value_back_ref, skewed_ref,
        exact_ref, probs_ref, d_scores_ref,
    ) = refs[-17:]
    length, width = q_ref.shape
    heads = table_ref.shape[0]
    head_dim = width // heads
    lane = lax.broadcasted_iota(jnp.int32, (1, LANES), 1)
    halves = (
        (lane < head_dim).astype(jnp.bfloat16),
        (lane >= head_dim).astype(jnp.bfloat16),
    )
    owner = lax.broadcasted_iota(jnp.int32, (heads, width), 1) // head_dim
    own_head = (owner == lax.broadcasted_iota(jnp.int32, (heads, width), 0)).astype(jnp.bfloat16)
    key_t_ref[...] = k_ref[...].T
    key_back_ref[...] = jnp.zeros_like(key_back_ref)
    value_back_ref[...] = jnp.zeros_like(value_back_ref)
    skewed_ref[...] = jnp.zeros_like(skewed_ref)

    def block(i, carry):
        rows = pl.ds(pl.multiple_of(i * QUERY_TILE, QUERY_TILE), QUERY_TILE)
        for pair in range(heads // 2):
            own = slice(pair * LANES, (pair + 1) * LANES)
            query = q_ref[rows, own] * jnp.bfloat16(SCORE_SCALE)
            grad = grad_ref[rows, own]
            for side in range(2):
                part = slice(side * QUERY_TILE, (side + 1) * QUERY_TILE)
                query_ref[pair, part, :] = query * halves[side]
                grads_ref[pair, part, :] = grad * halves[side]
                query_t_ref[2 * pair + side, :LANES, :] = (query * halves[side]).T
                query_t_ref[2 * pair + side, LANES:, :] = same_q_ref[:, rows]
                grads_t_ref[2 * pair + side] = (grad * halves[side]).T
        product = grad_ref[rows, :].astype(jnp.float32) * attn_ref[rows, :].astype(jnp.float32)
        rough = product.astype(jnp.bfloat16)
        rest = (product - rough.astype(jnp.float32)).astype(jnp.bfloat16)
        inner_ref[...] = dot_nt(own_head, rough) + dot_nt(own_head, rest)
        query_back_ref[...] = jnp.zeros_like(query_back_ref)

        def step(j, inner):
            keys = pl.ds(pl.multiple_of(j * KEY_TILE, KEY_TILE), KEY_TILE)
            lanes = table_lanes(i, j)
            for head in range(heads):
                pair = head // 2
                key = jnp.concatenate(
                    [k_ref[keys, pair * LANES : (pair + 1) * LANES], same_k_ref[keys, :]], axis=1
                )
                scores = dot_nn(key, query_t_ref[head]) + table_ref[head, :, lanes]
                exact_ref[head] = jnp.exp(scores - lse_ref[first + head : first + head + 1, rows])
            for head in range(heads):
                pair = head // 2
                part = slice((head % 2) * QUERY_TILE, (head % 2 + 1) * QUERY_TILE)
                d_probs = dot_nn(v_ref[keys, pair * LANES : (pair + 1) * LANES], grads_t_ref[head])
                exact = exact_ref[head]
                d_score = exact * (d_probs - inner_ref[head : head + 1, :])
                skewed_ref[head, :, lanes] = skewed_ref[head, :, lanes] + d_score
                probs_ref[pair, :, part] = exact.astype(jnp.bfloat16)
                d_scores_ref[pair, :, part] = d_score.astype(jnp.bfloat16)
            for pair in range(heads // 2):
                own = slice(pair * LANES, (pair + 1) * LANES)
                value_back_ref[keys, own] += dot_nn(probs_ref[pair], grads_ref[pair])
                key_back_ref[keys, own] += dot_nn(d_scores_ref[pair], query_ref[pair])
            for head in range(heads):
                part = slice((head % 2) * QUERY_TILE, (head % 2 + 1) * QUERY_TILE)
                mine = slice(head * head_dim, (head + 1) * head_dim)
                query_back_ref[mine, :] += dot_nn(
                    key_t_ref[mine, keys], d_scores_ref[head // 2, :, part]
                )
            return inner

        lax.fori_loop(bounds_ref[0, i], bounds_ref[1, i], step, 0)
        query_out_ref[rows, :] = (query_back_ref[...].T * SCORE_SCALE).astype(jnp.bfloat16)
        return carry

    lax.fori_loop(0, length // QUERY_TILE, block, 0)
    key_out_ref[...] = key_back_ref[...].astype(jnp.bfloat16)
    value_out_ref[...] = value_back_ref[...].astype(jnp.bfloat16)
    for head in range(heads):
        height = KEY_TILE
        while height > 8:
            height //= 2
            skewed_ref[head, :height, :] = skewed_ref[head, :height, :] + pltpu.roll(
                skewed_ref[head, height : 2 * height, :], BAND - height, 1
            )
        total = skewed_ref[head, 0:1, :]
        for row in range(1, 8):
            total = total + pltpu.roll(skewed_ref[head, row : row + 1, :], BAND - row, 1)
        band_ref[head : head + 1, :] = total


def attend_back(part, parts, bounds, qkv, same_q, same_k, table, lse, attn, grad, earlier_parts=()):
    length = qkv.shape[0]
    width = qkv.shape[1] // 3
    heads = table.shape[0] // parts
    span = width // parts

    def columns(group):
        return pl.BlockSpec(
            (length, span),
            lambda _: (0, group * parts + part),
            pipeline_mode=pl.Buffered(1),
        )

    whole = [smem(), columns(0), columns(1), columns(2), vmem(), vmem()]
    whole += [
        pl.BlockSpec(
            (heads, KEY_TILE, BAND), lambda _: (part, 0, 0), pipeline_mode=pl.Buffered(1)
        ),
        vmem(),
    ]
    whole += [columns(0), columns(0)] + [pl.BlockSpec(memory_space=pl.ANY)] * len(earlier_parts)
    return pl.pallas_call(
        functools.partial(attend_back_kernel, part * heads),
        out_shape=[jax.ShapeDtypeStruct((length, width), jnp.bfloat16)] * 3
        + [jax.ShapeDtypeStruct((heads, BAND), jnp.float32)],
        grid=(1,),
        in_specs=whole,
        out_specs=[columns(0)] * 3 + [vmem()],
        input_output_aliases={10 + at: at for at in range(len(earlier_parts))},
        scratch_shapes=[
            pltpu.VMEM((span, length), jnp.bfloat16),
            pltpu.VMEM((heads // 2, 2 * QUERY_TILE, LANES), jnp.bfloat16),
            pltpu.VMEM((heads // 2, 2 * QUERY_TILE, LANES), jnp.bfloat16),
            pltpu.VMEM((heads, 2 * LANES, QUERY_TILE), jnp.bfloat16),
            pltpu.VMEM((heads, LANES, QUERY_TILE), jnp.bfloat16),
            pltpu.VMEM((heads, QUERY_TILE), jnp.float32),
            pltpu.VMEM((span, QUERY_TILE), jnp.float32),
            pltpu.VMEM((length, span), jnp.float32),
            pltpu.VMEM((length, span), jnp.float32),
            pltpu.VMEM((heads, KEY_TILE, BAND), jnp.float32),
            pltpu.VMEM((heads, KEY_TILE, QUERY_TILE), jnp.float32),
            pltpu.VMEM((heads // 2, KEY_TILE, 2 * QUERY_TILE), jnp.bfloat16),
            pltpu.VMEM((heads // 2, KEY_TILE, 2 * QUERY_TILE), jnp.bfloat16),
        ],
        compiler_params=params(34),
        cost_estimate=pl.CostEstimate(
            flops=40 * length * length * span,
            bytes_accessed=8 * 2**20,
            transcendentals=length * length * heads,
        ),
        name="attend_back",
    )(bounds, qkv, qkv, qkv, same_q, same_k, table, lse, attn, grad, *earlier_parts)


def document_bounds(segments):
    length = segments.shape[0]
    starts = segments[::QUERY_TILE]
    ends = segments[QUERY_TILE - 1 :: QUERY_TILE]
    before = jnp.sum((segments[None, :] < starts[:, None]).astype(jnp.int32), axis=1)
    upto = jnp.sum((segments[None, :] <= ends[:, None]).astype(jnp.int32), axis=1)
    return jnp.stack([before // KEY_TILE, (upto + KEY_TILE - 1) // KEY_TILE])


def document_marks(segments):
    own = segments[:, None] == jnp.arange(LANES, dtype=jnp.int32)[None, :]
    own_t = segments[None, :] == jnp.arange(LANES, dtype=jnp.int32)[:, None]
    return own_t.astype(jnp.bfloat16), jnp.where(own, 0.0, MASKED).astype(jnp.bfloat16)
HIDDEN_TILE = 512
GELU_SLOPE = 0.7978845608028654
GELU_CUBIC = 0.044715


def gelu_parts(values):
    square = values * values
    bend = jnp.tanh(values * (GELU_SLOPE + GELU_SLOPE * GELU_CUBIC * square))
    half = 0.5 + 0.5 * bend
    slope = half + values * (1.0 - bend * bend) * (
        0.5 * GELU_SLOPE + 1.5 * GELU_SLOPE * GELU_CUBIC * square
    )
    return values * half, slope


def middle_and_norm(attn_ref, resid_ref, w_out_ref):
    mid = resid_ref[...] + dot_nn(attn_ref[...], w_out_ref[...])
    return mid, lax.rsqrt(jnp.mean(mid * mid, axis=-1, keepdims=True) + EPSILON)


def hidden_kernel(
    attn_ref, resid_ref, grad_ref, w_out_ref, gain_ref, w_gate_ref, w_upper_ref, w_down_ref,
    weight_back_ref, acts_ref,
    normed_ref, normed_t_ref, grad_t_ref, gate_ref, upper_ref, d_inner_ref,
):
    @pl.when(pl.program_id(0) == 0)
    def _():
        mid, rinv = middle_and_norm(attn_ref, resid_ref, w_out_ref)
        normed = (mid * rinv * gain_ref[...]).astype(jnp.bfloat16)
        normed_ref[...] = normed
        normed_t_ref[...] = normed.T
        grad_t_ref[...] = grad_ref[...].T

    gate_ref[...] = dot_nn(normed_ref[...], w_gate_ref[...])
    upper_ref[...] = dot_nn(normed_ref[...], w_upper_ref[...])
    d_inner_ref[...] = dot_nt(grad_ref[...], w_down_ref[...])
    upper = upper_ref[...]
    d_inner = d_inner_ref[...]
    bent, slope = gelu_parts(gate_ref[...])
    low = jnp.bfloat16
    inner_at, gate_at, upper_at = (
        slice(plane * HIDDEN_TILE, (plane + 1) * HIDDEN_TILE) for plane in (2, 0, 1)
    )
    acts_ref[:, inner_at] = (bent * upper).astype(low)
    acts_ref[:, gate_at] = (d_inner * upper * slope).astype(low)
    acts_ref[:, upper_at] = (d_inner * bent).astype(low)
    for left_ref, at in ((normed_t_ref, gate_at), (normed_t_ref, upper_at), (grad_t_ref, inner_at)):
        weight_back_ref[:, at] = dot_nn(left_ref[...], acts_ref[:, at]).astype(low)


def hidden_layer(attn, resid, grad, w_out, gain, w_in, w_down):
    length, width = attn.shape
    hidden = w_down.shape[0]
    steps = hidden // HIDDEN_TILE
    low = jnp.bfloat16
    return pl.pallas_call(
        hidden_kernel,
        grid=(steps,),
        out_shape=(
            jax.ShapeDtypeStruct((width, 3 * hidden), low),
            jax.ShapeDtypeStruct((length, 3 * hidden), low),
        ),
        in_specs=[vmem()] * 5
        + [
            pl.BlockSpec((width, HIDDEN_TILE), lambda c: (0, c)),
            pl.BlockSpec((width, HIDDEN_TILE), lambda c: (0, steps + c)),
            pl.BlockSpec((HIDDEN_TILE, width), lambda c: (c, 0)),
        ],
        out_specs=(
            pl.BlockSpec((width, 3 * HIDDEN_TILE), lambda c: (0, c)),
            pl.BlockSpec((length, 3 * HIDDEN_TILE), lambda c: (0, c)),
        ),
        scratch_shapes=[
            pltpu.VMEM((length, width), low),
            pltpu.VMEM((width, length), low),
            pltpu.VMEM((width, length), low),
            pltpu.VMEM((length, HIDDEN_TILE), jnp.float32),
            pltpu.VMEM((length, HIDDEN_TILE), jnp.float32),
            pltpu.VMEM((length, HIDDEN_TILE), jnp.float32),
        ],
        compiler_params=params(34),
        cost_estimate=pl.CostEstimate(
            flops=12 * length * width * hidden,
            bytes_accessed=32 * 2**20,
            transcendentals=length * hidden,
        ),
        name="hidden_layer",
    )(attn, resid, grad, w_out, gain.reshape(1, width), w_in, w_in, w_down)


def outer_kernel(
    attn_ref, resid_ref, grad_ref, w_out_ref, gain_ref, acts_ref, w_gate_ref, w_upper_ref,
    w_down_ref,
    output_ref, d_mid_ref, d_attn_ref, d_w_out_ref, d_gain_ref,
    mid_ref, rinv_ref, sum_ref, back_ref,
):
    step = pl.program_id(0)

    @pl.when(step == 0)
    def _():
        mid, rinv = middle_and_norm(attn_ref, resid_ref, w_out_ref)
        mid_ref[...] = mid
        rinv_ref[...] = jnp.broadcast_to(rinv, rinv_ref.shape)
        sum_ref[...] = mid
        back_ref[...] = jnp.zeros_like(back_ref)

    sum_ref[...] += dot_nn(acts_ref[:, 2 * HIDDEN_TILE :], w_down_ref[...])
    back_ref[...] += dot_nt(acts_ref[:, :HIDDEN_TILE], w_gate_ref[...]) + dot_nt(
        acts_ref[:, HIDDEN_TILE : 2 * HIDDEN_TILE], w_upper_ref[...]
    )

    @pl.when(step == pl.num_programs(0) - 1)
    def _():
        output_ref[...] = sum_ref[...].astype(jnp.bfloat16)
        rinv = rinv_ref[:, :1]
        mid = mid_ref[...]
        d_normed = back_ref[...]
        d_gain_ref[...] = jnp.sum(d_normed * mid * rinv, axis=0, keepdims=True)
        scaled = d_normed * gain_ref[...]
        lean = jnp.mean(scaled * mid, axis=-1, keepdims=True) * (rinv * rinv * rinv)
        d_mid = grad_ref[...].astype(jnp.float32) + rinv * scaled - mid * lean
        d_mid_ref[...] = d_mid
        d_branch = d_mid.astype(jnp.bfloat16)
        d_attn_ref[...] = dot_nt(d_branch, w_out_ref[...]).astype(jnp.bfloat16)
        d_w_out_ref[...] = dot_nn(attn_ref[...].T, d_branch).astype(jnp.bfloat16)


def outer_layer(attn, resid, grad, w_out, gain, acts, w_in, w_down):
    length, width = attn.shape
    hidden = w_down.shape[0]
    steps = hidden // HIDDEN_TILE
    low = jnp.bfloat16
    return pl.pallas_call(
        outer_kernel,
        grid=(steps,),
        out_shape=(
            jax.ShapeDtypeStruct((length, width), low),
            jax.ShapeDtypeStruct((length, width), jnp.float32),
            jax.ShapeDtypeStruct((length, width), low),
            jax.ShapeDtypeStruct((width, width), low),
            jax.ShapeDtypeStruct((1, width), jnp.float32),
        ),
        in_specs=[vmem()] * 5
        + [
            pl.BlockSpec((length, 3 * HIDDEN_TILE), lambda c: (0, c)),
            pl.BlockSpec((width, HIDDEN_TILE), lambda c: (0, c)),
            pl.BlockSpec((width, HIDDEN_TILE), lambda c: (0, steps + c)),
            pl.BlockSpec((HIDDEN_TILE, width), lambda c: (c, 0)),
        ],
        out_specs=(vmem(),) * 5,
        scratch_shapes=[
            pltpu.VMEM((length, width), jnp.float32),
            pltpu.VMEM((length, LANES), jnp.float32),
            pltpu.VMEM((length, width), jnp.float32),
            pltpu.VMEM((length, width), jnp.float32),
        ],
        compiler_params=params(30),
        cost_estimate=pl.CostEstimate(
            flops=6 * length * width * hidden + 6 * length * width * width,
            bytes_accessed=24 * 2**20,
            transcendentals=0,
        ),
        name="outer_layer",
    )(attn, resid, grad, w_out, gain.reshape(1, width), acts, w_in, w_in, w_down)


def finish_wide_kernel(scale, piece_ref, d_w_in_ref, d_w_down_ref):
    piece = piece_ref[...].astype(jnp.float32) * scale

    @pl.when(pl.program_id(0) < 2)
    def _():
        d_w_in_ref[...] = piece

    @pl.when(pl.program_id(0) == 2)
    def _():
        d_w_down_ref[...] = piece.T


def finish_wide(total, scale):
    width = total.shape[0]
    hidden = total.shape[1] // 3
    tiles = hidden // HIDDEN_TILE
    return pl.pallas_call(
        functools.partial(finish_wide_kernel, scale),
        grid=(3, tiles),
        out_shape=(
            jax.ShapeDtypeStruct((width, 2 * hidden), jnp.float32),
            jax.ShapeDtypeStruct((hidden, width), jnp.float32),
        ),
        in_specs=[pl.BlockSpec((width, HIDDEN_TILE), lambda p, c: (0, c * 3 + p))],
        out_specs=(
            pl.BlockSpec(
                (width, HIDDEN_TILE), lambda p, c: (0, jnp.where(p < 2, p * tiles + c, 2 * tiles - 1))
            ),
            pl.BlockSpec((HIDDEN_TILE, width), lambda p, c: (jnp.where(p < 2, 0, c), 0)),
        ),
        compiler_params=params(58),
        cost_estimate=pl.CostEstimate(
            flops=6 * width * hidden, bytes_accessed=18 * width * hidden, transcendentals=0
        ),
        name="finish_wide",
    )(total)


def finish_kernel(scale, spots, mine_ref, own_ref, other_ref, *refs):
    *out_refs, joined_ref = refs
    half = own_ref.shape[0]
    mine = mine_ref[0]
    for piece_ref, side in ((own_ref, mine), (other_ref, 1 - mine)):
        part = pl.ds(pl.multiple_of(side * half, half), half)
        joined_ref[part, :] = piece_ref[...].astype(jnp.float32) * scale
    for ref, (row, column) in zip(out_refs, spots):
        rows, columns = ref.shape
        ref[...] = joined_ref[row : row + rows, column : column + columns]


def finish(mine, own, other, scale, shapes, by_row):
    half, columns = own.shape
    spots = []
    at = 0
    for shape in shapes:
        spots.append((at, 0) if by_row else (0, at))
        at += shape[0 if by_row else 1]
    return pl.pallas_call(
        functools.partial(finish_kernel, scale, tuple(spots)),
        out_shape=[jax.ShapeDtypeStruct(shape, jnp.float32) for shape in shapes],
        in_specs=[smem(), vmem(), vmem()],
        out_specs=[vmem()] * len(shapes),
        scratch_shapes=[pltpu.VMEM((2 * half, columns), jnp.float32)],
        compiler_params=params(16),
        cost_estimate=pl.CostEstimate(
            flops=4 * half * columns, bytes_accessed=12 * half * columns, transcendentals=0
        ),
        name="finish",
    )(mine, own, other)


def dot_tn(left, right):
    return lax.dot_general(
        left, right, (((0,), (0,)), ((), ())), preferred_element_type=jnp.float32
    )


def to_rows(block, share):
    rows, stretch = block.shape[:2]
    pieces = jnp.repeat(block, share, axis=0) if share > 1 else block
    pieces = lax.all_to_all(pieces, "blk", 0, 0, tiled=True)
    return pieces.reshape((rows * share * stretch,) + block.shape[2:])


def to_blocks(row, share):
    blocks = lax.axis_size("blk")
    place = lax.axis_index("blk")
    stretch = row.shape[0] // blocks

    def piece(owner):
        return lax.dynamic_slice_in_dim(row, owner * stretch, stretch, axis=0)

    pieces = [piece(place)]
    for gap in range(1, blocks):
        devices = range(blocks)
        pieces.append(lax.ppermute(piece(place ^ gap), "blk", [(i, i ^ gap) for i in devices]))
    return pieces


def placed(pieces, share):
    place = lax.axis_index("blk")
    gap = 1
    while gap < len(pieces):
        stays = (place & gap) == 0
        pieces = [jnp.where(stays, pieces[at], pieces[at ^ gap]) for at in range(len(pieces))]
        gap *= 2
    return jnp.stack(pieces[::share])


def later(values, lag):
    if lag == 0:
        return values
    return jnp.pad(values, ((lag, 0), (0, 0)))[: values.shape[0]]


def earlier(values, lag):
    if lag == 0:
        return values
    return jnp.pad(values, ((0, lag), (0, 0)))[lag:]


def own_bit(axis, bit):
    return (lax.axis_index(axis) >> bit) & 1


def swapped(block, axis, bit):
    devices = range(lax.axis_size(axis))
    return lax.ppermute(block, axis, [(i, i ^ (1 << bit)) for i in devices])


def bits_of(axis):
    return lax.axis_size(axis).bit_length() - 1


def group_of(free):
    blk = lax.axis_size("blk")
    devices = range(lax.axis_size("rows") * blk)
    weights = [(blk if axis == "rows" else 1) << bit for axis, bit in free]
    place = sum(own_bit(axis, bit) << at for at, (axis, bit) in enumerate(free))

    def send(block, gap):
        shift = sum(weight for at, weight in enumerate(weights) if gap >> at & 1)
        return lax.ppermute(block, ("rows", "blk"), [(i, i ^ shift) for i in devices])

    return 1 << len(free), place, send


class Travel:
    def __init__(self, kept, sent):
        near = [("blk", bit) for bit in range(1, bits_of("blk"))] + [("rows", 0)]
        far = [("rows", bit) for bit in range(1, bits_of("rows"))]
        stages = (group_of(near), group_of(far))
        terms = [kept, swapped(sent, "blk", 0)]
        self.state = [terms]
        self.orders = [stages]
        self.at = 0

    @classmethod
    def whole(cls, block):
        half = block.shape[0] // 2
        mine = own_bit("blk", 0)
        sent = lax.dynamic_slice_in_dim(block, (1 - mine) * half, half, axis=0)
        kept = lax.dynamic_slice_in_dim(block, mine * half, half, axis=0)
        return cls(kept, sent)

    def go(self):
        self.state = [self.lane_step(*lane) for lane in zip(self.state, self.orders)]
        self.at += 1

    def lane_step(self, terms, order):
        block = total(terms)
        if self.at == 4:
            return [block, swapped(block, "blk", 0)]
        count, place, send = order[self.at if self.at < 2 else 3 - self.at]
        if self.at < 2:
            rows = block.shape[0] // count
            def piece(owner):
                return lax.dynamic_slice_in_dim(block, owner * rows, rows, axis=0)

            return [piece(place)] + [send(piece(place ^ gap), gap) for gap in range(1, count)]
        pieces = [block] + [send(block, gap) for gap in range(1, count)]
        gap = 1
        while gap < count:
            stays = (place & gap) == 0
            pieces = [jnp.where(stays, pieces[at], pieces[at ^ gap]) for at in range(count)]
            gap *= 2
        return [jnp.concatenate(pieces, axis=0)]


def total(terms):
    first, *others = terms
    if not others:
        return first
    wide = first.astype(jnp.float32)
    for other in others:
        wide = wide + other.astype(jnp.float32)
    return wide.astype(first.dtype)


def beside(values, *travels):
    for travel in travels:
        travel.go()
    return settled(values, *travels)


def settled(values, *travels):
    states, values = lax.optimization_barrier(([travel.state for travel in travels], values))
    for travel, state in zip(travels, states):
        travel.state = state
    return values


def on_device(
    byte_vals,
    segment_ids,
    buckets,
    emb_table,
    conv_taps,
    w_proj,
    gain_one,
    w_qkv,
    rel_bias,
    w_out,
    gain_two,
    w_in,
    w_down,
    out_grad,
):
    rows, stretch = byte_vals.shape
    vocab, width = emb_table.shape
    bucket_count, heads = rel_bias.shape
    hidden = w_down.shape[0]
    blocks = lax.axis_size("blk")
    share = blocks // rows
    length = stretch * blocks
    low = jnp.bfloat16

    packed = to_rows(byte_vals + vocab * segment_ids, share)
    letters_own = packed % vocab
    segments = packed // vocab
    grad_low = to_rows(out_grad, share)

    own_hot = (letters_own[:, None] == jnp.arange(vocab, dtype=jnp.int32)[None, :]).astype(low)
    embedded = dot_nn(own_hot, emb_table)
    taps = conv_taps.astype(jnp.float32)
    seg_col = segments[:, None] + 1

    def lagged():
        keeps = [later(seg_col, lag) == seg_col for lag in range(4)]
        shifted = [jnp.where(keeps[lag], later(embedded, lag), 0.0) for lag in range(4)]
        sums = [
            sum(shifted[lag] * taps[first + lag] for lag in range(span)) for first, span in WINDOWS
        ]
        return keeps, shifted, sums

    conv_low = sum(gelu_parts(summed)[0] for summed in lagged()[2]).astype(low)
    resid = dot_nn(conv_low, w_proj)
    rinv_one = lax.rsqrt(jnp.mean(resid * resid, axis=-1, keepdims=True) + EPSILON)
    normed_one = (resid * rinv_one * gain_one).astype(low)
    qkv = dot_nn(normed_one, w_qkv).astype(low)

    band_buckets = lax.slice_in_dim(buckets, BAND_FIRST, BAND_FIRST + BAND - LANES)
    band_buckets = jnp.concatenate(
        [band_buckets, lax.slice_in_dim(buckets, BAND_FIRST - LANES, BAND_FIRST)]
    )
    bucket_hot = (
        band_buckets[:, None] == jnp.arange(bucket_count, dtype=jnp.int32)[None, :]
    ).astype(jnp.float32)
    base = lax.dot_general(
        rel_bias, bucket_hot, (((0,), (1,)), ((), ())), precision=HIGHEST_PRECISION
    )
    table = bias_tables(base)
    bounds = document_bounds(segments)
    same_q, same_k = document_marks(segments)
    attn, lse = attend(bounds, qkv, same_q, same_k, table)

    mine = own_bit("blk", 0).astype(jnp.int32).reshape(1)
    scale = 1.0 / share
    d_wide, acts = hidden_layer(attn, resid, grad_low, w_out, gain_two, w_in, w_down)

    def remainder():
        output_row, d_mid, d_attn, d_w_out, d_gain_two = outer_layer(
            attn, resid, grad_low, w_out, gain_two, acts, w_in, w_down
        )
        output = to_blocks(output_row, share)
        *parts, band = attend_back(0, 1, bounds, qkv, same_q, same_k, table, lse, attn, d_attn)
        parts, output = lax.optimization_barrier((parts, output))
        output = placed(output, share)
        d_rel_bias = lax.dot_general(
            bucket_hot, band, (((0,), (1,)), ((), ())), precision=HIGHEST_PRECISION
        )
        d_normed_one = sum(
            dot_nt(part, w_qkv[:, at * width : (at + 1) * width]) for at, part in enumerate(parts)
        )
        d_gain_one = jnp.sum(d_normed_one * resid * rinv_one, axis=0)
        scaled = d_normed_one * gain_one
        lean = jnp.mean(scaled * resid, axis=-1, keepdims=True) * (rinv_one * rinv_one * rinv_one)
        d_resid = (d_mid + rinv_one * scaled - resid * lean).astype(low)
        d_w_proj = dot_tn(conv_low, d_resid).astype(low)
        middle = jnp.concatenate(
            [dot_tn(normed_one, part).astype(low) for part in parts] + [d_w_proj, d_w_out], axis=1
        )
        d_resid, middle = lax.optimization_barrier((d_resid, middle))
        middle = Travel.whole(middle)
        d_conv = settled(dot_nt(d_resid, w_proj), middle)

        keeps, shifted, sums = lagged()
        d_shifted = [jnp.zeros((length, width), jnp.float32) for lag in range(4)]
        tap_rows = [None] * 9
        for index, (first, span) in enumerate(WINDOWS):
            d_pre = d_conv * gelu_parts(sums[index])[1]
            for lag in range(span):
                tap_rows[first + lag] = jnp.sum(d_pre * shifted[lag], axis=0)
                d_shifted[lag] = d_shifted[lag] + d_pre * taps[first + lag]
        d_conv_taps = jnp.stack(tap_rows, axis=0)
        input_row = jnp.zeros((length, width), jnp.float32)
        for lag in range(4):
            input_row = input_row + earlier(jnp.where(keeps[lag], d_shifted[lag], 0.0), lag)
        input_low = beside(input_row.astype(low), middle)
        input_grad = to_blocks(input_low, share)
        d_emb_table = dot_tn(own_hot, input_low)

        late = jnp.concatenate(
            [
                d_emb_table,
                d_conv_taps,
                d_gain_one[None],
                d_gain_two,
                jnp.pad(d_rel_bias.reshape(1, -1), ((0, 0), (0, width - d_rel_bias.size))),
                jnp.zeros((width - vocab - 12, width), jnp.float32),
            ],
            axis=0,
        ).astype(low)
        late = Travel.whole(late)
        input_grad = beside(input_grad, middle, late)
        for travel in (middle, late, middle, late, middle, late, late):
            travel.go()
        most = finish(
            mine,
            *middle.state[0],
            scale,
            ((width, 3 * width), (width, width), (width, width)),
            False,
        )
        rest = finish(
            mine,
            *late.state[0],
            scale,
            ((vocab, width), (9, width), (1, width), (1, width), (1, bucket_count * heads)),
            True,
        )
        input_grad = placed(input_grad, share).astype(jnp.float32)
        return output, input_grad, most + rest

    def nothing():
        return jax.tree.map(lambda leaf: jnp.zeros(leaf.shape, leaf.dtype), shapes)

    shapes = jax.eval_shape(remainder)
    d_wide = lax.psum(d_wide, ("rows", "blk"))
    output, input_grad, finished = lax.cond(segments[0] >= 0, remainder, nothing)
    (
        d_w_qkv,
        d_w_proj,
        d_w_out,
        d_emb_table,
        d_conv_taps,
        d_gain_one,
        d_gain_two,
        d_rel_bias,
    ) = finished
    d_w_in, d_w_down = finish_wide(d_wide, scale)
    d_gain_one = d_gain_one.reshape(width)
    d_gain_two = d_gain_two.reshape(width)
    d_rel_bias = d_rel_bias.reshape(bucket_count, heads)
    return (
        output,
        input_grad,
        d_emb_table,
        d_conv_taps,
        d_w_proj,
        d_gain_one,
        d_w_qkv,
        d_rel_bias,
        d_w_out,
        d_gain_two,
        d_w_in,
        d_w_down,
    )


def solution(mesh):
    split = P("rows", "blk")
    split_wide = P("rows", "blk", None)
    return jax.shard_map(
        on_device,
        mesh=mesh,
        in_specs=(split, split) + (P(),) * 11 + (split_wide,),
        out_specs=(split_wide, split_wide) + (P(),) * 10,
        check_vma=False,
    )
```

```python
import functools

import jax
import jax.numpy as jnp
from jax import lax
from jax.experimental import pallas as pl
from jax.experimental.pallas import tpu as pltpu
from jax.sharding import PartitionSpec as P

EPSILON = 1e-06
SCORE_SCALE = 0.125
WINDOWS = ((0, 2), (2, 3), (5, 4))
HIGHEST_PRECISION = lax.Precision.HIGHEST
LANES = 128
QUERY_TILE = 256
KEY_TILE = 128
MASKED = -(2.0**30)
BAND = 12 * LANES
BAND_FIRST = 3 * LANES
MIB = 2**20


def vmem():
    return pl.BlockSpec(memory_space=pltpu.VMEM)


def smem():
    return pl.BlockSpec(memory_space=pltpu.SMEM)


def params(mib):
    return pltpu.CompilerParams(vmem_limit_bytes=mib * MIB)


def dot_nt(left, right):
    return lax.dot_general(
        left, right, (((1,), (1,)), ((), ())), preferred_element_type=jnp.float32
    )


def dot_nn(left, right):
    return jnp.dot(left, right, preferred_element_type=jnp.float32)


def fill_tables(table_ref, base_ref):
    for head in range(base_ref.shape[0]):
        line = jnp.broadcast_to(base_ref[head : head + 1, :], (KEY_TILE, BAND))
        table_ref[head] = pltpu.roll(line, 0, 1, stride=1, stride_axis=0)


def table_lanes(query_block, key_block):
    place = (query_block * (QUERY_TILE // LANES) - key_block + 5) * LANES
    return pl.ds(pl.multiple_of(place, LANES), QUERY_TILE)


def attend_kernel(
    heads, bounds_ref, qkv_ref, same_q_ref, same_k_ref, buckets_ref, bias_ref,
    attn_ref, lse_ref, base_ref,
    table_ref,
    value_t_ref, query_ref, top_ref, total_ref, mixed_ref, score_ref, expo_ref, fade_ref,
):
    length = qkv_ref.shape[0]
    width = qkv_ref.shape[1] // 3
    head_dim = width // heads
    lane = lax.broadcasted_iota(jnp.int32, (1, LANES), 1)
    halves = (
        (lane < head_dim).astype(jnp.bfloat16),
        (lane >= head_dim).astype(jnp.bfloat16),
    )
    bias = bias_ref[...]
    base = jnp.zeros((heads, BAND), jnp.float32)
    for bucket in range(bias.shape[1]):
        base = jnp.where(buckets_ref[...] == bucket, bias[:, bucket : bucket + 1], base)
    base_ref[...] = base
    fill_tables(table_ref, base_ref)
    value_t_ref[...] = qkv_ref[:, 2 * width :].T

    def block(i, carry):
        rows = pl.ds(pl.multiple_of(i * QUERY_TILE, QUERY_TILE), QUERY_TILE)
        for pair in range(heads // 2):
            query = qkv_ref[rows, pair * LANES : (pair + 1) * LANES] * jnp.bfloat16(SCORE_SCALE)
            for side in range(2):
                query_ref[2 * pair + side, :LANES, :] = (query * halves[side]).T
                query_ref[2 * pair + side, LANES:, :] = same_q_ref[:, rows]
        top_ref[...] = jnp.full_like(top_ref, -3.0e38)
        total_ref[...] = jnp.zeros_like(total_ref)
        mixed_ref[...] = jnp.zeros_like(mixed_ref)

        def step(j, inner):
            keys = pl.ds(pl.multiple_of(j * KEY_TILE, KEY_TILE), KEY_TILE)
            lanes = table_lanes(i, j)
            for head in range(heads):
                pair = head // 2
                key = jnp.concatenate(
                    [
                        qkv_ref[keys, width + pair * LANES : width + (pair + 1) * LANES],
                        same_k_ref[keys, :],
                    ],
                    axis=1,
                )
                score_ref[head] = dot_nn(key, query_ref[head]) + table_ref[head, :, lanes]
            for head in range(heads):
                scores = score_ref[head]
                old = top_ref[head : head + 1, :]
                top = jnp.maximum(old, jnp.max(scores, axis=0, keepdims=True))
                fade = jnp.exp(old - top)
                expo = jnp.exp(scores - top)
                top_ref[head : head + 1, :] = top
                total_ref[head : head + 1, :] = total_ref[head : head + 1, :] * fade + jnp.sum(
                    expo, axis=0, keepdims=True
                )
                fade_ref[head : head + 1, :] = fade
                expo_ref[head] = expo.astype(jnp.bfloat16)
            for head in range(heads):
                own = slice(head * head_dim, (head + 1) * head_dim)
                mixed_ref[own, :] = mixed_ref[own, :] * fade_ref[head : head + 1, :] + dot_nn(
                    value_t_ref[own, keys], expo_ref[head]
                )
            return inner

        lax.fori_loop(bounds_ref[0, i], bounds_ref[1, i], step, 0)
        for head in range(heads):
            own = slice(head * head_dim, (head + 1) * head_dim)
            mixed_ref[own, :] = mixed_ref[own, :] / total_ref[head : head + 1, :]
        attn_ref[rows, :] = mixed_ref[...].T.astype(jnp.bfloat16)
        lse_ref[:, rows] = top_ref[...] + jnp.log(total_ref[...])
        return carry

    lax.fori_loop(0, length // QUERY_TILE, block, 0)


def attend(bounds, qkv, same_q, same_k, band_buckets, bias):
    length = qkv.shape[0]
    width = qkv.shape[1] // 3
    heads = bias.shape[0]
    return pl.pallas_call(
        functools.partial(attend_kernel, heads),
        out_shape=(
            jax.ShapeDtypeStruct((length, width), jnp.bfloat16),
            jax.ShapeDtypeStruct((heads, length), jnp.float32),
            jax.ShapeDtypeStruct((heads, BAND), jnp.float32),
        ),
        in_specs=[smem()] + [vmem()] * 5,
        out_specs=(vmem(), vmem(), vmem()),
        scratch_shapes=[
            pltpu.VMEM((heads, KEY_TILE, BAND), jnp.float32),
            pltpu.VMEM((width, length), jnp.bfloat16),
            pltpu.VMEM((heads, 2 * LANES, QUERY_TILE), jnp.bfloat16),
            pltpu.VMEM((heads, QUERY_TILE), jnp.float32),
            pltpu.VMEM((heads, QUERY_TILE), jnp.float32),
            pltpu.VMEM((width, QUERY_TILE), jnp.float32),
            pltpu.VMEM((heads, KEY_TILE, QUERY_TILE), jnp.float32),
            pltpu.VMEM((heads, KEY_TILE, QUERY_TILE), jnp.bfloat16),
            pltpu.VMEM((heads, QUERY_TILE), jnp.float32),
        ],
        compiler_params=params(22),
        cost_estimate=pl.CostEstimate(
            flops=4 * length * length * width,
            bytes_accessed=12 * 2**20,
            transcendentals=length * length * heads,
        ),
        name="attend",
    )(bounds, qkv, same_q, same_k, band_buckets, bias)


def attend_back_kernel(
    bounds_ref, q_ref, k_ref, v_ref, same_q_ref, same_k_ref, base_ref, lse_ref,
    attn_ref, grad_ref,
    query_out_ref, key_out_ref, value_out_ref, band_ref,
    table_ref, key_t_ref, query_ref, grads_ref, query_t_ref, grads_t_ref, inner_ref,
    query_back_ref, key_back_ref, value_back_ref, skewed_ref,
    exact_ref, probs_ref, d_scores_ref,
):
    length, width = q_ref.shape
    heads = base_ref.shape[0]
    head_dim = width // heads
    lane = lax.broadcasted_iota(jnp.int32, (1, LANES), 1)
    halves = (
        (lane < head_dim).astype(jnp.bfloat16),
        (lane >= head_dim).astype(jnp.bfloat16),
    )
    owner = lax.broadcasted_iota(jnp.int32, (heads, width), 1) // head_dim
    own_head = (owner == lax.broadcasted_iota(jnp.int32, (heads, width), 0)).astype(jnp.bfloat16)
    fill_tables(table_ref, base_ref)
    key_t_ref[...] = k_ref[...].T
    key_back_ref[...] = jnp.zeros_like(key_back_ref)
    value_back_ref[...] = jnp.zeros_like(value_back_ref)
    skewed_ref[...] = jnp.zeros_like(skewed_ref)

    def block(i, carry):
        rows = pl.ds(pl.multiple_of(i * QUERY_TILE, QUERY_TILE), QUERY_TILE)
        for pair in range(heads // 2):
            own = slice(pair * LANES, (pair + 1) * LANES)
            query = q_ref[rows, own] * jnp.bfloat16(SCORE_SCALE)
            grad = grad_ref[rows, own]
            for side in range(2):
                part = slice(side * QUERY_TILE, (side + 1) * QUERY_TILE)
                query_ref[pair, part, :] = query * halves[side]
                grads_ref[pair, part, :] = grad * halves[side]
                query_t_ref[2 * pair + side, :LANES, :] = (query * halves[side]).T
                query_t_ref[2 * pair + side, LANES:, :] = same_q_ref[:, rows]
                grads_t_ref[2 * pair + side] = (grad * halves[side]).T
        product = grad_ref[rows, :].astype(jnp.float32) * attn_ref[rows, :].astype(jnp.float32)
        rough = product.astype(jnp.bfloat16)
        rest = (product - rough.astype(jnp.float32)).astype(jnp.bfloat16)
        inner_ref[...] = dot_nt(own_head, rough) + dot_nt(own_head, rest)
        query_back_ref[...] = jnp.zeros_like(query_back_ref)

        def step(j, inner):
            keys = pl.ds(pl.multiple_of(j * KEY_TILE, KEY_TILE), KEY_TILE)
            lanes = table_lanes(i, j)
            for head in range(heads):
                pair = head // 2
                key = jnp.concatenate(
                    [k_ref[keys, pair * LANES : (pair + 1) * LANES], same_k_ref[keys, :]], axis=1
                )
                scores = dot_nn(key, query_t_ref[head]) + table_ref[head, :, lanes]
                exact_ref[head] = jnp.exp(scores - lse_ref[head : head + 1, rows])
            for head in range(heads):
                pair = head // 2
                part = slice((head % 2) * QUERY_TILE, (head % 2 + 1) * QUERY_TILE)
                d_probs = dot_nn(v_ref[keys, pair * LANES : (pair + 1) * LANES], grads_t_ref[head])
                exact = exact_ref[head]
                d_score = exact * (d_probs - inner_ref[head : head + 1, :])
                skewed_ref[head, :, lanes] = skewed_ref[head, :, lanes] + d_score
                probs_ref[pair, :, part] = exact.astype(jnp.bfloat16)
                d_scores_ref[pair, :, part] = d_score.astype(jnp.bfloat16)
            for pair in range(heads // 2):
                own = slice(pair * LANES, (pair + 1) * LANES)
                value_back_ref[keys, own] += dot_nn(probs_ref[pair], grads_ref[pair])
                key_back_ref[keys, own] += dot_nn(d_scores_ref[pair], query_ref[pair])
            for head in range(heads):
                part = slice((head % 2) * QUERY_TILE, (head % 2 + 1) * QUERY_TILE)
                mine = slice(head * head_dim, (head + 1) * head_dim)
                query_back_ref[mine, :] += dot_nn(
                    key_t_ref[mine, keys], d_scores_ref[head // 2, :, part]
                )
            return inner

        lax.fori_loop(bounds_ref[0, i], bounds_ref[1, i], step, 0)
        query_out_ref[rows, :] = (query_back_ref[...].T * SCORE_SCALE).astype(jnp.bfloat16)
        return carry

    lax.fori_loop(0, length // QUERY_TILE, block, 0)
    key_out_ref[...] = key_back_ref[...].astype(jnp.bfloat16)
    value_out_ref[...] = value_back_ref[...].astype(jnp.bfloat16)
    for head in range(heads):
        height = KEY_TILE
        while height > 8:
            height //= 2
            skewed_ref[head, :height, :] = skewed_ref[head, :height, :] + pltpu.roll(
                skewed_ref[head, height : 2 * height, :], BAND - height, 1
            )
        total = skewed_ref[head, 0:1, :]
        for row in range(1, 8):
            total = total + pltpu.roll(skewed_ref[head, row : row + 1, :], BAND - row, 1)
        band_ref[head : head + 1, :] = total


def attend_back(bounds, qkv, same_q, same_k, base, lse, attn, grad):
    length = qkv.shape[0]
    width = qkv.shape[1] // 3
    heads = base.shape[0]

    def columns(group):
        return pl.BlockSpec(
            (length, width), lambda _: (0, group), pipeline_mode=pl.Buffered(1)
        )

    return pl.pallas_call(
        attend_back_kernel,
        out_shape=[jax.ShapeDtypeStruct((length, width), jnp.bfloat16)] * 3
        + [jax.ShapeDtypeStruct((heads, BAND), jnp.float32)],
        grid=(1,),
        in_specs=[smem(), columns(0), columns(1), columns(2)] + [vmem()] * 6,
        out_specs=[vmem()] * 4,
        scratch_shapes=[
            pltpu.VMEM((heads, KEY_TILE, BAND), jnp.float32),
            pltpu.VMEM((width, length), jnp.bfloat16),
            pltpu.VMEM((heads // 2, 2 * QUERY_TILE, LANES), jnp.bfloat16),
            pltpu.VMEM((heads // 2, 2 * QUERY_TILE, LANES), jnp.bfloat16),
            pltpu.VMEM((heads, 2 * LANES, QUERY_TILE), jnp.bfloat16),
            pltpu.VMEM((heads, LANES, QUERY_TILE), jnp.bfloat16),
            pltpu.VMEM((heads, QUERY_TILE), jnp.float32),
            pltpu.VMEM((width, QUERY_TILE), jnp.float32),
            pltpu.VMEM((length, width), jnp.float32),
            pltpu.VMEM((length, width), jnp.float32),
            pltpu.VMEM((heads, KEY_TILE, BAND), jnp.float32),
            pltpu.VMEM((heads, KEY_TILE, QUERY_TILE), jnp.float32),
            pltpu.VMEM((heads // 2, KEY_TILE, 2 * QUERY_TILE), jnp.bfloat16),
            pltpu.VMEM((heads // 2, KEY_TILE, 2 * QUERY_TILE), jnp.bfloat16),
        ],
        compiler_params=params(34),
        cost_estimate=pl.CostEstimate(
            flops=40 * length * length * width,
            bytes_accessed=8 * 2**20,
            transcendentals=length * length * heads,
        ),
        name="attend_back",
    )(bounds, qkv, qkv, qkv, same_q, same_k, base, lse, attn, grad)


def document_bounds(segments):
    length = segments.shape[0]
    starts = segments[::QUERY_TILE]
    ends = segments[QUERY_TILE - 1 :: QUERY_TILE]
    before = jnp.sum((segments[None, :] < starts[:, None]).astype(jnp.int32), axis=1)
    upto = jnp.sum((segments[None, :] <= ends[:, None]).astype(jnp.int32), axis=1)
    return jnp.stack([before // KEY_TILE, (upto + KEY_TILE - 1) // KEY_TILE])


def document_marks(segments):
    own = segments[:, None] == jnp.arange(LANES, dtype=jnp.int32)[None, :]
    own_t = segments[None, :] == jnp.arange(LANES, dtype=jnp.int32)[:, None]
    return own_t.astype(jnp.bfloat16), jnp.where(own, 0.0, MASKED).astype(jnp.bfloat16)
HIDDEN_TILE = 512
GELU_SLOPE = 0.7978845608028654
GELU_CUBIC = 0.044715


def gelu_value(values):
    square = values * values
    bend = jnp.tanh(values * (GELU_SLOPE + GELU_SLOPE * GELU_CUBIC * square))
    return values * (0.5 + 0.5 * bend)


def gelu_parts(values):
    square = values * values
    bend = jnp.tanh(values * (GELU_SLOPE + GELU_SLOPE * GELU_CUBIC * square))
    half = 0.5 + 0.5 * bend
    slope = half + values * (1.0 - bend * bend) * (
        0.5 * GELU_SLOPE + 1.5 * GELU_SLOPE * GELU_CUBIC * square
    )
    return values * half, slope


FRONT_TILE = 128
HALO = 8


def front_kernel(
    letters_ref, segments_ref, emb_ref, taps_ref, w_proj_ref, gain_ref, w_qkv_ref,
    conv_ref, resid_ref, normed_ref, qkv_ref,
    embedded_ref,
):
    length, width = resid_ref.shape
    vocab = emb_ref.shape[0]
    letters = lax.broadcasted_iota(jnp.int32, (vocab, length), 0)
    hot = (letters == letters_ref[...]).astype(jnp.float32).astype(jnp.bfloat16)
    embedded_ref[:HALO, :] = jnp.zeros((HALO, width), jnp.float32)
    embedded_ref[HALO:, :] = lax.dot_general(
        hot, emb_ref[...], (((0,), (0,)), ((), ())), preferred_element_type=jnp.float32
    )
    segments = segments_ref[...]
    place = lax.broadcasted_iota(jnp.int32, (1, length), 1)
    rows = [jnp.ones((1, length), jnp.float32)]
    for lag in range(1, HALO):
        same = (pltpu.roll(segments, lag, 1) == segments) & (place >= lag)
        rows.append(same.astype(jnp.float32))
    keeps = jnp.concatenate(rows, axis=0).T
    for at in range(0, length, FRONT_TILE):
        part = slice(at, at + FRONT_TILE)
        shifted = []
        for lag in range(4):
            moved = embedded_ref[HALO + at - lag : HALO + at - lag + FRONT_TILE, :]
            shifted.append(moved if lag == 0 else moved * keeps[part, lag : lag + 1])
        total = 0.0
        for first, span in WINDOWS:
            summed = shifted[0] * taps_ref[first : first + 1, :]
            for lag in range(1, span):
                summed = summed + shifted[lag] * taps_ref[first + lag : first + lag + 1, :]
            total = total + gelu_value(summed)
        conv_ref[part, :] = total.astype(jnp.bfloat16)
    resid = dot_nn(conv_ref[...], w_proj_ref[...])
    resid_ref[...] = resid
    rinv = lax.rsqrt(jnp.mean(resid * resid, axis=-1, keepdims=True) + EPSILON)
    normed_ref[...] = (resid * rinv * gain_ref[...]).astype(jnp.bfloat16)
    qkv_ref[...] = dot_nn(normed_ref[...], w_qkv_ref[...]).astype(jnp.bfloat16)


def front(letters, segments, emb_table, taps, w_proj, gain, w_qkv):
    length = letters.shape[0]
    vocab, width = emb_table.shape
    low = jnp.bfloat16
    return pl.pallas_call(
        front_kernel,
        out_shape=(
            jax.ShapeDtypeStruct((length, width), low),
            jax.ShapeDtypeStruct((length, width), jnp.float32),
            jax.ShapeDtypeStruct((length, width), low),
            jax.ShapeDtypeStruct((length, 3 * width), low),
        ),
        in_specs=[vmem()] * 7,
        out_specs=(vmem(),) * 4,
        scratch_shapes=[pltpu.VMEM((length + HALO, width), jnp.float32)],
        compiler_params=params(24),
        cost_estimate=pl.CostEstimate(
            flops=2 * length * width * (4 * width + vocab) + 60 * length * width,
            bytes_accessed=12 * 2**20,
            transcendentals=3 * length * width,
        ),
        name="front",
    )(
        letters.reshape(1, length),
        segments.reshape(1, length),
        emb_table,
        taps,
        w_proj,
        gain.reshape(1, width),
        w_qkv,
    )


def middle_and_norm(attn_ref, resid_ref, w_out_ref):
    mid = resid_ref[...] + dot_nn(attn_ref[...], w_out_ref[...])
    return mid, lax.rsqrt(jnp.mean(mid * mid, axis=-1, keepdims=True) + EPSILON)


def hidden_kernel(
    attn_ref, resid_ref, grad_ref, w_out_ref, gain_ref, w_gate_ref, w_upper_ref, w_down_ref,
    weight_back_ref, acts_ref,
    normed_ref, normed_t_ref, grad_t_ref, gate_ref, upper_ref, d_inner_ref,
):
    @pl.when(pl.program_id(0) == 0)
    def _():
        mid, rinv = middle_and_norm(attn_ref, resid_ref, w_out_ref)
        normed = (mid * rinv * gain_ref[...]).astype(jnp.bfloat16)
        normed_ref[...] = normed
        normed_t_ref[...] = normed.T
        grad_t_ref[...] = grad_ref[...].T

    gate_ref[...] = dot_nn(normed_ref[...], w_gate_ref[...])
    upper_ref[...] = dot_nn(normed_ref[...], w_upper_ref[...])
    d_inner_ref[...] = dot_nt(grad_ref[...], w_down_ref[...])
    upper = upper_ref[...]
    d_inner = d_inner_ref[...]
    bent, slope = gelu_parts(gate_ref[...])
    low = jnp.bfloat16
    inner_at, gate_at, upper_at = (
        slice(plane * HIDDEN_TILE, (plane + 1) * HIDDEN_TILE) for plane in (2, 0, 1)
    )
    acts_ref[:, inner_at] = (bent * upper).astype(low)
    acts_ref[:, gate_at] = (d_inner * upper * slope).astype(low)
    acts_ref[:, upper_at] = (d_inner * bent).astype(low)
    for left_ref, at in ((normed_t_ref, gate_at), (normed_t_ref, upper_at), (grad_t_ref, inner_at)):
        weight_back_ref[:, at] = dot_nn(left_ref[...], acts_ref[:, at]).astype(low)


def hidden_layer(attn, resid, grad, w_out, gain, w_in, w_down):
    length, width = attn.shape
    hidden = w_down.shape[0]
    steps = hidden // HIDDEN_TILE
    low = jnp.bfloat16
    return pl.pallas_call(
        hidden_kernel,
        grid=(steps,),
        out_shape=(
            jax.ShapeDtypeStruct((width, 3 * hidden), low),
            jax.ShapeDtypeStruct((length, 3 * hidden), low),
        ),
        in_specs=[vmem()] * 5
        + [
            pl.BlockSpec((width, HIDDEN_TILE), lambda c: (0, c)),
            pl.BlockSpec((width, HIDDEN_TILE), lambda c: (0, steps + c)),
            pl.BlockSpec((HIDDEN_TILE, width), lambda c: (c, 0)),
        ],
        out_specs=(
            pl.BlockSpec((width, 3 * HIDDEN_TILE), lambda c: (0, c)),
            pl.BlockSpec((length, 3 * HIDDEN_TILE), lambda c: (0, c)),
        ),
        scratch_shapes=[
            pltpu.VMEM((length, width), low),
            pltpu.VMEM((width, length), low),
            pltpu.VMEM((width, length), low),
            pltpu.VMEM((length, HIDDEN_TILE), jnp.float32),
            pltpu.VMEM((length, HIDDEN_TILE), jnp.float32),
            pltpu.VMEM((length, HIDDEN_TILE), jnp.float32),
        ],
        compiler_params=params(52),
        cost_estimate=pl.CostEstimate(
            flops=12 * length * width * hidden,
            bytes_accessed=32 * 2**20,
            transcendentals=length * hidden,
        ),
        name="hidden_layer",
    )(attn, resid, grad, w_out, gain.reshape(1, width), w_in, w_in, w_down)


def outer_kernel(
    attn_ref, resid_ref, grad_ref, w_out_ref, gain_ref, acts_ref, w_gate_ref, w_upper_ref,
    w_down_ref,
    output_ref, d_mid_ref, d_attn_ref, d_w_out_ref, d_gain_ref,
    mid_ref, rinv_ref, sum_ref, back_ref,
):
    step = pl.program_id(0)

    @pl.when(step == 0)
    def _():
        mid, rinv = middle_and_norm(attn_ref, resid_ref, w_out_ref)
        mid_ref[...] = mid
        rinv_ref[...] = jnp.broadcast_to(rinv, rinv_ref.shape)
        sum_ref[...] = mid
        back_ref[...] = jnp.zeros_like(back_ref)

    sum_ref[...] += dot_nn(acts_ref[:, 2 * HIDDEN_TILE :], w_down_ref[...])
    back_ref[...] += dot_nt(acts_ref[:, :HIDDEN_TILE], w_gate_ref[...]) + dot_nt(
        acts_ref[:, HIDDEN_TILE : 2 * HIDDEN_TILE], w_upper_ref[...]
    )

    @pl.when(step == pl.num_programs(0) - 1)
    def _():
        output_ref[...] = sum_ref[...].astype(jnp.bfloat16)
        rinv = rinv_ref[:, :1]
        mid = mid_ref[...]
        d_normed = back_ref[...]
        d_gain_ref[...] = jnp.sum(d_normed * mid * rinv, axis=0, keepdims=True)
        scaled = d_normed * gain_ref[...]
        lean = jnp.mean(scaled * mid, axis=-1, keepdims=True) * (rinv * rinv * rinv)
        d_mid = grad_ref[...].astype(jnp.float32) + rinv * scaled - mid * lean
        d_mid_ref[...] = d_mid
        d_branch = d_mid.astype(jnp.bfloat16)
        d_attn_ref[...] = dot_nt(d_branch, w_out_ref[...]).astype(jnp.bfloat16)
        d_w_out_ref[...] = dot_nn(attn_ref[...].T, d_branch).astype(jnp.bfloat16)


def outer_layer(attn, resid, grad, w_out, gain, acts, w_in, w_down):
    length, width = attn.shape
    hidden = w_down.shape[0]
    steps = hidden // HIDDEN_TILE
    low = jnp.bfloat16
    return pl.pallas_call(
        outer_kernel,
        grid=(steps,),
        out_shape=(
            jax.ShapeDtypeStruct((length, width), low),
            jax.ShapeDtypeStruct((length, width), jnp.float32),
            jax.ShapeDtypeStruct((length, width), low),
            jax.ShapeDtypeStruct((width, width), low),
            jax.ShapeDtypeStruct((1, width), jnp.float32),
        ),
        in_specs=[vmem()] * 5
        + [
            pl.BlockSpec((length, 3 * HIDDEN_TILE), lambda c: (0, c)),
            pl.BlockSpec((width, HIDDEN_TILE), lambda c: (0, c)),
            pl.BlockSpec((width, HIDDEN_TILE), lambda c: (0, steps + c)),
            pl.BlockSpec((HIDDEN_TILE, width), lambda c: (c, 0)),
        ],
        out_specs=(vmem(),) * 5,
        scratch_shapes=[
            pltpu.VMEM((length, width), jnp.float32),
            pltpu.VMEM((length, LANES), jnp.float32),
            pltpu.VMEM((length, width), jnp.float32),
            pltpu.VMEM((length, width), jnp.float32),
        ],
        compiler_params=params(30),
        cost_estimate=pl.CostEstimate(
            flops=6 * length * width * hidden + 6 * length * width * width,
            bytes_accessed=24 * 2**20,
            transcendentals=0,
        ),
        name="outer_layer",
    )(attn, resid, grad, w_out, gain.reshape(1, width), acts, w_in, w_in, w_down)


def finish_wide_kernel(scale, piece_ref, d_w_in_ref, d_w_down_ref):
    piece = piece_ref[...].astype(jnp.float32) * scale

    @pl.when(pl.program_id(0) < 2)
    def _():
        d_w_in_ref[...] = piece

    @pl.when(pl.program_id(0) == 2)
    def _():
        d_w_down_ref[...] = piece.T


def finish_wide(total, scale):
    width = total.shape[0]
    hidden = total.shape[1] // 3
    tiles = hidden // HIDDEN_TILE
    return pl.pallas_call(
        functools.partial(finish_wide_kernel, scale),
        grid=(3, tiles),
        out_shape=(
            jax.ShapeDtypeStruct((width, 2 * hidden), jnp.float32),
            jax.ShapeDtypeStruct((hidden, width), jnp.float32),
        ),
        in_specs=[pl.BlockSpec((width, HIDDEN_TILE), lambda p, c: (0, c * 3 + p))],
        out_specs=(
            pl.BlockSpec(
                (width, HIDDEN_TILE), lambda p, c: (0, jnp.where(p < 2, p * tiles + c, 2 * tiles - 1))
            ),
            pl.BlockSpec((HIDDEN_TILE, width), lambda p, c: (jnp.where(p < 2, 0, c), 0)),
        ),
        compiler_params=params(58),
        cost_estimate=pl.CostEstimate(
            flops=6 * width * hidden, bytes_accessed=18 * width * hidden, transcendentals=0
        ),
        name="finish_wide",
    )(total)


def finish_kernel(scale, spots, mine_ref, own_ref, other_ref, *refs):
    *out_refs, joined_ref = refs
    half = own_ref.shape[0]
    mine = mine_ref[0]
    for piece_ref, side in ((own_ref, mine), (other_ref, 1 - mine)):
        part = pl.ds(pl.multiple_of(side * half, half), half)
        joined_ref[part, :] = piece_ref[...].astype(jnp.float32) * scale
    for ref, (row, column) in zip(out_refs, spots):
        rows, columns = ref.shape
        ref[...] = joined_ref[row : row + rows, column : column + columns]


def finish(mine, own, other, scale, shapes, by_row):
    half, columns = own.shape
    spots = []
    at = 0
    for shape in shapes:
        spots.append((at, 0) if by_row else (0, at))
        at += shape[0 if by_row else 1]
    return pl.pallas_call(
        functools.partial(finish_kernel, scale, tuple(spots)),
        out_shape=[jax.ShapeDtypeStruct(shape, jnp.float32) for shape in shapes],
        in_specs=[smem(), vmem(), vmem()],
        out_specs=[vmem()] * len(shapes),
        scratch_shapes=[pltpu.VMEM((2 * half, columns), jnp.float32)],
        compiler_params=params(16),
        cost_estimate=pl.CostEstimate(
            flops=4 * half * columns, bytes_accessed=12 * half * columns, transcendentals=0
        ),
        name="finish",
    )(mine, own, other)


def dot_tn(left, right):
    return lax.dot_general(
        left, right, (((0,), (0,)), ((), ())), preferred_element_type=jnp.float32
    )


def to_rows(block, share):
    rows, stretch = block.shape[:2]
    pieces = jnp.repeat(block, share, axis=0) if share > 1 else block
    pieces = lax.all_to_all(pieces, "blk", 0, 0, tiled=True)
    return pieces.reshape((rows * share * stretch,) + block.shape[2:])


def to_blocks(row, share):
    blocks = lax.axis_size("blk")
    pieces = row.reshape((blocks, row.shape[0] // blocks) + row.shape[1:])
    return lax.all_to_all(pieces, "blk", 0, 0, tiled=True)[::share]


def later(values, lag):
    if lag == 0:
        return values
    return jnp.pad(values, ((lag, 0), (0, 0)))[: values.shape[0]]


def earlier(values, lag):
    if lag == 0:
        return values
    return jnp.pad(values, ((0, lag), (0, 0)))[lag:]


def own_bit(axis, bit):
    return (lax.axis_index(axis) >> bit) & 1


def swapped(block, axis, bit):
    devices = range(lax.axis_size(axis))
    return lax.ppermute(block, axis, [(i, i ^ (1 << bit)) for i in devices])


def bits_of(axis):
    return lax.axis_size(axis).bit_length() - 1


def group_of(free):
    blk = lax.axis_size("blk")
    devices = range(lax.axis_size("rows") * blk)
    weights = [(blk if axis == "rows" else 1) << bit for axis, bit in free]
    place = sum(own_bit(axis, bit) << at for at, (axis, bit) in enumerate(free))

    def send(block, gap):
        shift = sum(weight for at, weight in enumerate(weights) if gap >> at & 1)
        return lax.ppermute(block, ("rows", "blk"), [(i, i ^ shift) for i in devices])

    return 1 << len(free), place, send


class Travel:
    def __init__(self, kept, sent):
        near = [("blk", bit) for bit in range(1, bits_of("blk"))] + [("rows", 0)]
        far = [("rows", bit) for bit in range(1, bits_of("rows"))]
        stages = (group_of(near), group_of(far))
        terms = [kept, swapped(sent, "blk", 0)]
        self.state = [terms]
        self.orders = [stages]
        self.at = 0

    @classmethod
    def whole(cls, block):
        half = block.shape[0] // 2
        mine = own_bit("blk", 0)
        sent = lax.dynamic_slice_in_dim(block, (1 - mine) * half, half, axis=0)
        kept = lax.dynamic_slice_in_dim(block, mine * half, half, axis=0)
        return cls(kept, sent)

    def go(self):
        self.state = [self.lane_step(*lane) for lane in zip(self.state, self.orders)]
        self.at += 1

    def lane_step(self, terms, order):
        block = total(terms)
        if self.at == 4:
            return [block, swapped(block, "blk", 0)]
        count, place, send = order[self.at if self.at < 2 else 3 - self.at]
        if self.at < 2:
            rows = block.shape[0] // count
            def piece(owner):
                return lax.dynamic_slice_in_dim(block, owner * rows, rows, axis=0)

            return [piece(place)] + [send(piece(place ^ gap), gap) for gap in range(1, count)]
        pieces = [block] + [send(block, gap) for gap in range(1, count)]
        gap = 1
        while gap < count:
            stays = (place & gap) == 0
            pieces = [jnp.where(stays, pieces[at], pieces[at ^ gap]) for at in range(count)]
            gap *= 2
        return [jnp.concatenate(pieces, axis=0)]


def total(terms):
    first, *others = terms
    if not others:
        return first
    wide = first.astype(jnp.float32)
    for other in others:
        wide = wide + other.astype(jnp.float32)
    return wide.astype(first.dtype)


def beside(values, *travels):
    for travel in travels:
        travel.go()
    return settled(values, *travels)


def settled(values, *travels):
    states, values = lax.optimization_barrier(([travel.state for travel in travels], values))
    for travel, state in zip(travels, states):
        travel.state = state
    return values


def on_device(
    byte_vals,
    segment_ids,
    buckets,
    emb_table,
    conv_taps,
    w_proj,
    gain_one,
    w_qkv,
    rel_bias,
    w_out,
    gain_two,
    w_in,
    w_down,
    out_grad,
):
    rows, stretch = byte_vals.shape
    vocab, width = emb_table.shape
    bucket_count, heads = rel_bias.shape
    hidden = w_down.shape[0]
    blocks = lax.axis_size("blk")
    share = blocks // rows
    length = stretch * blocks
    low = jnp.bfloat16

    packed = to_rows(byte_vals + vocab * segment_ids, share)
    letters_own = lax.rem(packed, vocab)
    segments = lax.div(packed, vocab)
    grad_low = to_rows(out_grad, share)

    taps = conv_taps.astype(jnp.float32)
    conv_low, resid, normed_one, qkv = front(
        letters_own, segments, emb_table, taps, w_proj, gain_one, w_qkv
    )
    band_buckets = jnp.concatenate(
        [buckets[BAND_FIRST : BAND_FIRST + BAND - LANES], buckets[BAND_FIRST - LANES : BAND_FIRST]]
    )
    bounds = document_bounds(segments)
    same_q, same_k = document_marks(segments)
    attn, lse, base = attend(
        bounds, qkv, same_q, same_k, band_buckets.reshape(1, BAND), rel_bias.T
    )

    mine = own_bit("blk", 0).astype(jnp.int32).reshape(1)
    scale = 1.0 / share
    d_wide, acts = hidden_layer(attn, resid, grad_low, w_out, gain_two, w_in, w_down)

    def remainder():
        own_hot = (letters_own[:, None] == jnp.arange(vocab, dtype=jnp.int32)[None, :]).astype(low)
        embedded = dot_nn(own_hot, emb_table)
        seg_col = segments[:, None] + 1
        keeps = [later(seg_col, lag) == seg_col for lag in range(4)]
        shifted = [jnp.where(keeps[lag], later(embedded, lag), 0.0) for lag in range(4)]
        sums = [
            sum(shifted[lag] * taps[first + lag] for lag in range(span)) for first, span in WINDOWS
        ]
        bucket_hot = (
            band_buckets[:, None] == jnp.arange(bucket_count, dtype=jnp.int32)[None, :]
        ).astype(jnp.float32)
        rinv_one = lax.rsqrt(jnp.mean(resid * resid, axis=-1, keepdims=True) + EPSILON)
        output_row, d_mid, d_attn, d_w_out, d_gain_two = outer_layer(
            attn, resid, grad_low, w_out, gain_two, acts, w_in, w_down
        )
        output = to_blocks(output_row, share)
        *parts, band = attend_back(bounds, qkv, same_q, same_k, base, lse, attn, d_attn)
        parts, output = lax.optimization_barrier((parts, output))
        d_rel_bias = lax.dot_general(
            bucket_hot, band, (((0,), (1,)), ((), ())), precision=HIGHEST_PRECISION
        )
        d_normed_one = sum(
            dot_nt(part, w_qkv[:, at * width : (at + 1) * width]) for at, part in enumerate(parts)
        )
        d_gain_one = jnp.sum(d_normed_one * resid * rinv_one, axis=0)
        scaled = d_normed_one * gain_one
        lean = jnp.mean(scaled * resid, axis=-1, keepdims=True) * (rinv_one * rinv_one * rinv_one)
        d_resid = (d_mid + rinv_one * scaled - resid * lean).astype(low)
        d_w_proj = dot_tn(conv_low, d_resid).astype(low)
        middle = jnp.concatenate(
            [dot_tn(normed_one, part).astype(low) for part in parts] + [d_w_proj, d_w_out], axis=1
        )
        d_resid, middle = lax.optimization_barrier((d_resid, middle))
        middle = Travel.whole(middle)
        d_conv = settled(dot_nt(d_resid, w_proj), middle)

        d_shifted = [jnp.zeros((length, width), jnp.float32) for lag in range(4)]
        tap_rows = [None] * 9
        for index, (first, span) in enumerate(WINDOWS):
            d_pre = d_conv * gelu_parts(sums[index])[1]
            for lag in range(span):
                tap_rows[first + lag] = jnp.sum(d_pre * shifted[lag], axis=0)
                d_shifted[lag] = d_shifted[lag] + d_pre * taps[first + lag]
        d_conv_taps = jnp.stack(tap_rows, axis=0)
        input_row = jnp.zeros((length, width), jnp.float32)
        for lag in range(4):
            input_row = input_row + earlier(jnp.where(keeps[lag], d_shifted[lag], 0.0), lag)
        input_low = beside(input_row.astype(low), middle)
        input_grad = to_blocks(input_low, share)
        d_emb_table = dot_tn(own_hot, input_low)

        late = jnp.concatenate(
            [
                d_emb_table,
                d_conv_taps,
                d_gain_one[None],
                d_gain_two,
                jnp.pad(d_rel_bias.reshape(1, -1), ((0, 0), (0, width - d_rel_bias.size))),
                jnp.zeros((width - vocab - 12, width), jnp.float32),
            ],
            axis=0,
        ).astype(low)
        late = Travel.whole(late)
        input_grad = beside(input_grad, middle, late)
        for travel in (middle, late, middle, late, middle, late, late):
            travel.go()
        most = finish(
            mine,
            *middle.state[0],
            scale,
            ((width, 3 * width), (width, width), (width, width)),
            False,
        )
        rest = finish(
            mine,
            *late.state[0],
            scale,
            ((vocab, width), (9, width), (1, width), (1, width), (1, bucket_count * heads)),
            True,
        )
        input_grad = input_grad.astype(jnp.float32)
        return output, input_grad, most + rest

    def nothing():
        return jax.tree.map(lambda leaf: jnp.zeros(leaf.shape, leaf.dtype), shapes)

    shapes = jax.eval_shape(remainder)
    d_wide = lax.psum(d_wide, ("rows", "blk"))
    output, input_grad, finished = lax.cond(segments[0] >= 0, remainder, nothing)
    (
        d_w_qkv,
        d_w_proj,
        d_w_out,
        d_emb_table,
        d_conv_taps,
        d_gain_one,
        d_gain_two,
        d_rel_bias,
    ) = finished
    d_w_in, d_w_down = finish_wide(d_wide, scale)
    d_gain_one = d_gain_one.reshape(width)
    d_gain_two = d_gain_two.reshape(width)
    d_rel_bias = d_rel_bias.reshape(bucket_count, heads)
    return (
        output,
        input_grad,
        d_emb_table,
        d_conv_taps,
        d_w_proj,
        d_gain_one,
        d_w_qkv,
        d_rel_bias,
        d_w_out,
        d_gain_two,
        d_w_in,
        d_w_down,
    )


def solution(mesh):
    split = P("rows", "blk")
    split_wide = P("rows", "blk", None)
    return jax.shard_map(
        on_device,
        mesh=mesh,
        in_specs=(split, split) + (P(),) * 11 + (split_wide,),
        out_specs=(split_wide, split_wide) + (P(),) * 10,
        check_vma=False,
    )
```

```python
import functools

import jax
import jax.numpy as jnp
from jax import lax
from jax.experimental import pallas as pl
from jax.experimental.pallas import tpu as pltpu
from jax.sharding import PartitionSpec as P

EPSILON = 1e-06
SCORE_SCALE = 0.125
WINDOWS = ((0, 2), (2, 3), (5, 4))
HIGHEST_PRECISION = lax.Precision.HIGHEST
LANES = 128
QUERY_TILE = 256
KEY_TILE = 128
MASKED = -(2.0**30)
BAND = 12 * LANES
BAND_FIRST = 3 * LANES
MIB = 2**20


def vmem():
    return pl.BlockSpec(memory_space=pltpu.VMEM)


def smem():
    return pl.BlockSpec(memory_space=pltpu.SMEM)


def params(mib):
    return pltpu.CompilerParams(vmem_limit_bytes=mib * MIB)


def dot_nt(left, right):
    return lax.dot_general(
        left, right, (((1,), (1,)), ((), ())), preferred_element_type=jnp.float32
    )


def dot_nn(left, right):
    return jnp.dot(left, right, preferred_element_type=jnp.float32)


def fill_tables(table_ref, base_ref):
    for head in range(base_ref.shape[0]):
        line = jnp.broadcast_to(base_ref[head : head + 1, :], (KEY_TILE, BAND))
        table_ref[head] = pltpu.roll(line, 0, 1, stride=1, stride_axis=0)


def table_lanes(query_block, key_block):
    place = (query_block * (QUERY_TILE // LANES) - key_block + 5) * LANES
    return pl.ds(pl.multiple_of(place, LANES), QUERY_TILE)


def attend_kernel(
    heads, bounds_ref, qkv_ref, same_q_ref, same_k_ref, buckets_ref, bias_ref,
    attn_ref, lse_ref, base_ref,
    table_ref,
    value_t_ref, query_ref, top_ref, total_ref, mixed_ref, score_ref, expo_ref, fade_ref,
):
    length = qkv_ref.shape[0]
    width = qkv_ref.shape[1] // 3
    head_dim = width // heads
    lane = lax.broadcasted_iota(jnp.int32, (1, LANES), 1)
    halves = (
        (lane < head_dim).astype(jnp.bfloat16),
        (lane >= head_dim).astype(jnp.bfloat16),
    )
    bias = bias_ref[...]
    base = jnp.zeros((heads, BAND), jnp.float32)
    for bucket in range(bias.shape[1]):
        base = jnp.where(buckets_ref[...] == bucket, bias[:, bucket : bucket + 1], base)
    base_ref[...] = base
    fill_tables(table_ref, base_ref)
    value_t_ref[...] = qkv_ref[:, 2 * width :].T

    def block(i, carry):
        rows = pl.ds(pl.multiple_of(i * QUERY_TILE, QUERY_TILE), QUERY_TILE)
        for pair in range(heads // 2):
            query = qkv_ref[rows, pair * LANES : (pair + 1) * LANES] * jnp.bfloat16(SCORE_SCALE)
            for side in range(2):
                query_ref[2 * pair + side, :LANES, :] = (query * halves[side]).T
                query_ref[2 * pair + side, LANES:, :] = same_q_ref[:, rows]
        top_ref[...] = jnp.full_like(top_ref, -3.0e38)
        total_ref[...] = jnp.zeros_like(total_ref)
        mixed_ref[...] = jnp.zeros_like(mixed_ref)

        def step(j, inner):
            keys = pl.ds(pl.multiple_of(j * KEY_TILE, KEY_TILE), KEY_TILE)
            lanes = table_lanes(i, j)
            for head in range(heads):
                pair = head // 2
                key = jnp.concatenate(
                    [
                        qkv_ref[keys, width + pair * LANES : width + (pair + 1) * LANES],
                        same_k_ref[keys, :],
                    ],
                    axis=1,
                )
                score_ref[head] = dot_nn(key, query_ref[head]) + table_ref[head, :, lanes]
            for head in range(heads):
                scores = score_ref[head]
                old = top_ref[head : head + 1, :]
                top = jnp.maximum(old, jnp.max(scores, axis=0, keepdims=True))
                fade = jnp.exp(old - top)
                expo = jnp.exp(scores - top)
                top_ref[head : head + 1, :] = top
                total_ref[head : head + 1, :] = total_ref[head : head + 1, :] * fade + jnp.sum(
                    expo, axis=0, keepdims=True
                )
                fade_ref[head : head + 1, :] = fade
                expo_ref[head] = expo.astype(jnp.bfloat16)
            for head in range(heads):
                own = slice(head * head_dim, (head + 1) * head_dim)
                mixed_ref[own, :] = mixed_ref[own, :] * fade_ref[head : head + 1, :] + dot_nn(
                    value_t_ref[own, keys], expo_ref[head]
                )
            return inner

        lax.fori_loop(bounds_ref[0, i], bounds_ref[1, i], step, 0)
        for head in range(heads):
            own = slice(head * head_dim, (head + 1) * head_dim)
            mixed_ref[own, :] = mixed_ref[own, :] / total_ref[head : head + 1, :]
        attn_ref[rows, :] = mixed_ref[...].T.astype(jnp.bfloat16)
        lse_ref[:, rows] = top_ref[...] + jnp.log(total_ref[...])
        return carry

    lax.fori_loop(0, length // QUERY_TILE, block, 0)


def attend(bounds, qkv, same_q, same_k, band_buckets, bias):
    length = qkv.shape[0]
    width = qkv.shape[1] // 3
    heads = bias.shape[0]
    return pl.pallas_call(
        functools.partial(attend_kernel, heads),
        out_shape=(
            jax.ShapeDtypeStruct((length, width), jnp.bfloat16),
            jax.ShapeDtypeStruct((heads, length), jnp.float32),
            jax.ShapeDtypeStruct((heads, BAND), jnp.float32),
        ),
        in_specs=[smem()] + [vmem()] * 5,
        out_specs=(vmem(), vmem(), vmem()),
        scratch_shapes=[
            pltpu.VMEM((heads, KEY_TILE, BAND), jnp.float32),
            pltpu.VMEM((width, length), jnp.bfloat16),
            pltpu.VMEM((heads, 2 * LANES, QUERY_TILE), jnp.bfloat16),
            pltpu.VMEM((heads, QUERY_TILE), jnp.float32),
            pltpu.VMEM((heads, QUERY_TILE), jnp.float32),
            pltpu.VMEM((width, QUERY_TILE), jnp.float32),
            pltpu.VMEM((heads, KEY_TILE, QUERY_TILE), jnp.float32),
            pltpu.VMEM((heads, KEY_TILE, QUERY_TILE), jnp.bfloat16),
            pltpu.VMEM((heads, QUERY_TILE), jnp.float32),
        ],
        compiler_params=params(22),
        cost_estimate=pl.CostEstimate(
            flops=4 * length * length * width,
            bytes_accessed=12 * 2**20,
            transcendentals=length * length * heads,
        ),
        name="attend",
    )(bounds, qkv, same_q, same_k, band_buckets, bias)


def attend_back_kernel(
    bounds_ref, q_ref, k_ref, v_ref, same_q_ref, same_k_ref, base_ref, lse_ref,
    attn_ref, grad_ref,
    query_out_ref, key_out_ref, value_out_ref, band_ref,
    table_ref, key_t_ref, query_ref, grads_ref, query_t_ref, grads_t_ref, inner_ref,
    query_back_ref, key_back_ref, value_back_ref, skewed_ref,
    exact_ref, probs_ref, d_scores_ref,
):
    length, width = q_ref.shape
    heads = base_ref.shape[0]
    head_dim = width // heads
    lane = lax.broadcasted_iota(jnp.int32, (1, LANES), 1)
    halves = (
        (lane < head_dim).astype(jnp.bfloat16),
        (lane >= head_dim).astype(jnp.bfloat16),
    )
    owner = lax.broadcasted_iota(jnp.int32, (heads, width), 1) // head_dim
    own_head = (owner == lax.broadcasted_iota(jnp.int32, (heads, width), 0)).astype(jnp.bfloat16)
    fill_tables(table_ref, base_ref)
    key_t_ref[...] = k_ref[...].T
    key_back_ref[...] = jnp.zeros_like(key_back_ref)
    value_back_ref[...] = jnp.zeros_like(value_back_ref)
    skewed_ref[...] = jnp.zeros_like(skewed_ref)

    def block(i, carry):
        rows = pl.ds(pl.multiple_of(i * QUERY_TILE, QUERY_TILE), QUERY_TILE)
        for pair in range(heads // 2):
            own = slice(pair * LANES, (pair + 1) * LANES)
            query = q_ref[rows, own] * jnp.bfloat16(SCORE_SCALE)
            grad = grad_ref[rows, own]
            for side in range(2):
                part = slice(side * QUERY_TILE, (side + 1) * QUERY_TILE)
                query_ref[pair, part, :] = query * halves[side]
                grads_ref[pair, part, :] = grad * halves[side]
                query_t_ref[2 * pair + side, :LANES, :] = (query * halves[side]).T
                query_t_ref[2 * pair + side, LANES:, :] = same_q_ref[:, rows]
                grads_t_ref[2 * pair + side] = (grad * halves[side]).T
        product = grad_ref[rows, :].astype(jnp.float32) * attn_ref[rows, :].astype(jnp.float32)
        rough = product.astype(jnp.bfloat16)
        rest = (product - rough.astype(jnp.float32)).astype(jnp.bfloat16)
        inner_ref[...] = dot_nt(own_head, rough) + dot_nt(own_head, rest)
        query_back_ref[...] = jnp.zeros_like(query_back_ref)

        def step(j, inner):
            keys = pl.ds(pl.multiple_of(j * KEY_TILE, KEY_TILE), KEY_TILE)
            lanes = table_lanes(i, j)
            for head in range(heads):
                pair = head // 2
                key = jnp.concatenate(
                    [k_ref[keys, pair * LANES : (pair + 1) * LANES], same_k_ref[keys, :]], axis=1
                )
                scores = dot_nn(key, query_t_ref[head]) + table_ref[head, :, lanes]
                exact_ref[head] = jnp.exp(scores - lse_ref[head : head + 1, rows])
            for head in range(heads):
                pair = head // 2
                part = slice((head % 2) * QUERY_TILE, (head % 2 + 1) * QUERY_TILE)
                d_probs = dot_nn(v_ref[keys, pair * LANES : (pair + 1) * LANES], grads_t_ref[head])
                exact = exact_ref[head]
                d_score = exact * (d_probs - inner_ref[head : head + 1, :])
                skewed_ref[head, :, lanes] = skewed_ref[head, :, lanes] + d_score
                probs_ref[pair, :, part] = exact.astype(jnp.bfloat16)
                d_scores_ref[pair, :, part] = d_score.astype(jnp.bfloat16)
            for pair in range(heads // 2):
                own = slice(pair * LANES, (pair + 1) * LANES)
                value_back_ref[keys, own] += dot_nn(probs_ref[pair], grads_ref[pair])
                key_back_ref[keys, own] += dot_nn(d_scores_ref[pair], query_ref[pair])
            for head in range(heads):
                part = slice((head % 2) * QUERY_TILE, (head % 2 + 1) * QUERY_TILE)
                mine = slice(head * head_dim, (head + 1) * head_dim)
                query_back_ref[mine, :] += dot_nn(
                    key_t_ref[mine, keys], d_scores_ref[head // 2, :, part]
                )
            return inner

        lax.fori_loop(bounds_ref[0, i], bounds_ref[1, i], step, 0)
        query_out_ref[rows, :] = (query_back_ref[...].T * SCORE_SCALE).astype(jnp.bfloat16)
        return carry

    lax.fori_loop(0, length // QUERY_TILE, block, 0)
    key_out_ref[...] = key_back_ref[...].astype(jnp.bfloat16)
    value_out_ref[...] = value_back_ref[...].astype(jnp.bfloat16)
    for head in range(heads):
        height = KEY_TILE
        while height > 8:
            height //= 2
            skewed_ref[head, :height, :] = skewed_ref[head, :height, :] + pltpu.roll(
                skewed_ref[head, height : 2 * height, :], BAND - height, 1
            )
        total = skewed_ref[head, 0:1, :]
        for row in range(1, 8):
            total = total + pltpu.roll(skewed_ref[head, row : row + 1, :], BAND - row, 1)
        band_ref[head : head + 1, :] = total


def attend_back(bounds, qkv, same_q, same_k, base, lse, attn, grad):
    length = qkv.shape[0]
    width = qkv.shape[1] // 3
    heads = base.shape[0]

    def columns(group):
        return pl.BlockSpec(
            (length, width), lambda _: (0, group), pipeline_mode=pl.Buffered(1)
        )

    return pl.pallas_call(
        attend_back_kernel,
        out_shape=[jax.ShapeDtypeStruct((length, width), jnp.bfloat16)] * 3
        + [jax.ShapeDtypeStruct((heads, BAND), jnp.float32)],
        grid=(1,),
        in_specs=[smem(), columns(0), columns(1), columns(2)] + [vmem()] * 6,
        out_specs=[vmem()] * 4,
        scratch_shapes=[
            pltpu.VMEM((heads, KEY_TILE, BAND), jnp.float32),
            pltpu.VMEM((width, length), jnp.bfloat16),
            pltpu.VMEM((heads // 2, 2 * QUERY_TILE, LANES), jnp.bfloat16),
            pltpu.VMEM((heads // 2, 2 * QUERY_TILE, LANES), jnp.bfloat16),
            pltpu.VMEM((heads, 2 * LANES, QUERY_TILE), jnp.bfloat16),
            pltpu.VMEM((heads, LANES, QUERY_TILE), jnp.bfloat16),
            pltpu.VMEM((heads, QUERY_TILE), jnp.float32),
            pltpu.VMEM((width, QUERY_TILE), jnp.float32),
            pltpu.VMEM((length, width), jnp.float32),
            pltpu.VMEM((length, width), jnp.float32),
            pltpu.VMEM((heads, KEY_TILE, BAND), jnp.float32),
            pltpu.VMEM((heads, KEY_TILE, QUERY_TILE), jnp.float32),
            pltpu.VMEM((heads // 2, KEY_TILE, 2 * QUERY_TILE), jnp.bfloat16),
            pltpu.VMEM((heads // 2, KEY_TILE, 2 * QUERY_TILE), jnp.bfloat16),
        ],
        compiler_params=params(34),
        cost_estimate=pl.CostEstimate(
            flops=40 * length * length * width,
            bytes_accessed=8 * 2**20,
            transcendentals=length * length * heads,
        ),
        name="attend_back",
    )(bounds, qkv, qkv, qkv, same_q, same_k, base, lse, attn, grad)


def document_bounds(segments):
    length = segments.shape[0]
    starts = segments[::QUERY_TILE]
    ends = segments[QUERY_TILE - 1 :: QUERY_TILE]
    before = jnp.sum((segments[None, :] < starts[:, None]).astype(jnp.int32), axis=1)
    upto = jnp.sum((segments[None, :] <= ends[:, None]).astype(jnp.int32), axis=1)
    return jnp.stack([before // KEY_TILE, (upto + KEY_TILE - 1) // KEY_TILE])


def document_marks(segments):
    own = segments[:, None] == jnp.arange(LANES, dtype=jnp.int32)[None, :]
    own_t = segments[None, :] == jnp.arange(LANES, dtype=jnp.int32)[:, None]
    return own_t.astype(jnp.bfloat16), jnp.where(own, 0.0, MASKED).astype(jnp.bfloat16)
HIDDEN_TILE = 512
GELU_SLOPE = 0.7978845608028654
GELU_CUBIC = 0.044715


def gelu_value(values):
    square = values * values
    bend = jnp.tanh(values * (GELU_SLOPE + GELU_SLOPE * GELU_CUBIC * square))
    return values * (0.5 + 0.5 * bend)


def gelu_parts(values):
    square = values * values
    bend = jnp.tanh(values * (GELU_SLOPE + GELU_SLOPE * GELU_CUBIC * square))
    half = 0.5 + 0.5 * bend
    slope = half + values * (1.0 - bend * bend) * (
        0.5 * GELU_SLOPE + 1.5 * GELU_SLOPE * GELU_CUBIC * square
    )
    return values * half, slope


FRONT_TILE = 128
BUCKET_LIMIT = 32
HALO = 8


def byte_marks(letters_ref, vocab):
    letters = lax.broadcasted_iota(jnp.int32, (vocab, letters_ref.shape[1]), 0)
    return (letters == letters_ref[...]).astype(jnp.float32).astype(jnp.bfloat16)


def embed(hot, emb_ref, embedded_ref):
    embedded_ref[:HALO, :] = jnp.zeros((HALO, emb_ref.shape[1]), jnp.float32)
    embedded_ref[HALO:, :] = lax.dot_general(
        hot, emb_ref[...], (((0,), (0,)), ((), ())), preferred_element_type=jnp.float32
    )


def lag_keeps(segments_ref):
    segments = segments_ref[...]
    place = lax.broadcasted_iota(jnp.int32, segments.shape, 1)
    rows = [jnp.ones(segments.shape, jnp.float32)]
    for lag in range(1, HALO):
        same = (pltpu.roll(segments, lag, 1) == segments) & (place >= lag)
        rows.append(same.astype(jnp.float32))
    return jnp.concatenate(rows, axis=0).T


def window_sums(embedded_ref, keeps, taps_ref, at):
    part = slice(at, at + FRONT_TILE)
    shifted = []
    for lag in range(4):
        moved = embedded_ref[HALO + at - lag : HALO + at - lag + FRONT_TILE, :]
        shifted.append(moved if lag == 0 else moved * keeps[part, lag : lag + 1])
    sums = []
    for first, span in WINDOWS:
        summed = shifted[0] * taps_ref[first : first + 1, :]
        for lag in range(1, span):
            summed = summed + shifted[lag] * taps_ref[first + lag : first + lag + 1, :]
        sums.append(summed)
    return shifted, sums


def front_kernel(
    letters_ref, segments_ref, emb_ref, taps_ref, w_proj_ref, gain_ref, w_qkv_ref,
    conv_ref, resid_ref, normed_ref, qkv_ref,
    embedded_ref,
):
    length, width = resid_ref.shape
    vocab = emb_ref.shape[0]
    hot = byte_marks(letters_ref, vocab)
    embed(hot, emb_ref, embedded_ref)
    keeps = lag_keeps(segments_ref)
    for at in range(0, length, FRONT_TILE):
        shifted, sums = window_sums(embedded_ref, keeps, taps_ref, at)
        conv_ref[at : at + FRONT_TILE, :] = sum(gelu_value(summed) for summed in sums).astype(
            jnp.bfloat16
        )
    resid = dot_nn(conv_ref[...], w_proj_ref[...])
    resid_ref[...] = resid
    rinv = lax.rsqrt(jnp.mean(resid * resid, axis=-1, keepdims=True) + EPSILON)
    normed_ref[...] = (resid * rinv * gain_ref[...]).astype(jnp.bfloat16)
    qkv_ref[...] = dot_nn(normed_ref[...], w_qkv_ref[...]).astype(jnp.bfloat16)


def front(letters, segments, emb_table, taps, w_proj, gain, w_qkv):
    length = letters.shape[0]
    vocab, width = emb_table.shape
    low = jnp.bfloat16
    return pl.pallas_call(
        front_kernel,
        out_shape=(
            jax.ShapeDtypeStruct((length, width), low),
            jax.ShapeDtypeStruct((length, width), jnp.float32),
            jax.ShapeDtypeStruct((length, width), low),
            jax.ShapeDtypeStruct((length, 3 * width), low),
        ),
        in_specs=[vmem()] * 7,
        out_specs=(vmem(),) * 4,
        scratch_shapes=[pltpu.VMEM((length + HALO, width), jnp.float32)],
        compiler_params=params(24),
        cost_estimate=pl.CostEstimate(
            flops=2 * length * width * (4 * width + vocab) + 60 * length * width,
            bytes_accessed=12 * 2**20,
            transcendentals=3 * length * width,
        ),
        name="front",
    )(
        letters.reshape(1, length),
        segments.reshape(1, length),
        emb_table,
        taps,
        w_proj,
        gain.reshape(1, width),
        w_qkv,
    )


SMALL_TAPS, SMALL_ONE, SMALL_TWO, SMALL_BIAS = 0, 9, 10, 16


def back_kernel(
    mine_ref, letters_ref, segments_ref, emb_ref, taps_ref, w_proj_ref, gain_ref, w_qkv_ref,
    conv_ref, resid_ref, normed_ref, d_query_ref, d_key_ref, d_value_ref, d_mid_ref,
    d_w_out_ref, d_gain_two_ref, buckets_ref, band_ref,
    kept_ref, sent_ref, input_ref,
    all_ref, small_ref, embedded_ref, d_normed_ref, d_resid_ref, d_lag_ref,
):
    length, width = resid_ref.shape
    vocab = emb_ref.shape[0]
    heads = band_ref.shape[0]
    low = jnp.bfloat16
    d_parts = (d_query_ref, d_key_ref, d_value_ref)
    d_normed_ref[...] = sum(
        dot_nt(part_ref[...], w_qkv_ref[:, at * width : (at + 1) * width])
        for at, part_ref in enumerate(d_parts)
    )
    resid = resid_ref[...]
    d_normed = d_normed_ref[...]
    rinv = lax.rsqrt(jnp.mean(resid * resid, axis=-1, keepdims=True) + EPSILON)
    small_ref[...] = jnp.zeros_like(small_ref)
    small_ref[SMALL_ONE : SMALL_ONE + 1, :] = jnp.sum(
        d_normed * resid * rinv, axis=0, keepdims=True
    )
    small_ref[SMALL_TWO : SMALL_TWO + 1, :] = d_gain_two_ref[...]
    scaled = d_normed * gain_ref[...]
    lean = jnp.mean(scaled * resid, axis=-1, keepdims=True) * (rinv * rinv * rinv)
    d_resid_ref[...] = (d_mid_ref[...] + rinv * scaled - resid * lean).astype(low)
    normed_t = normed_ref[...].T
    for at, part_ref in enumerate(d_parts):
        all_ref[:, at * width : (at + 1) * width] = dot_nn(normed_t, part_ref[...]).astype(low)
    all_ref[:, 3 * width : 4 * width] = dot_nn(conv_ref[...].T, d_resid_ref[...]).astype(low)
    all_ref[:, 4 * width : 5 * width] = d_w_out_ref[...]
    d_normed_ref[...] = dot_nt(d_resid_ref[...], w_proj_ref[...])

    hot = byte_marks(letters_ref, vocab)
    embed(hot, emb_ref, embedded_ref)
    keeps = lag_keeps(segments_ref)
    tap_rows = [jnp.zeros((8, width), jnp.float32)] * 9
    d_lag_ref[:, length:, :] = jnp.zeros((4, HALO, width), jnp.float32)
    for at in range(0, length, FRONT_TILE):
        part = slice(at, at + FRONT_TILE)
        shifted, sums = window_sums(embedded_ref, keeps, taps_ref, at)
        d_conv = d_normed_ref[part, :]
        d_shifted = [0.0] * 4
        for (first, span), summed in zip(WINDOWS, sums):
            d_pre = d_conv * gelu_parts(summed)[1]
            for lag in range(span):
                tap = first + lag
                pieces = (d_pre * shifted[lag]).reshape(FRONT_TILE // 8, 8, width)
                tap_rows[tap] = tap_rows[tap] + jnp.sum(pieces, axis=0)
                d_shifted[lag] = d_shifted[lag] + d_pre * taps_ref[tap : tap + 1, :]
        for lag in range(4):
            kept = d_shifted[lag]
            d_lag_ref[lag, part, :] = kept if lag == 0 else kept * keeps[part, lag : lag + 1]
    for tap in range(9):
        small_ref[SMALL_TAPS + tap : SMALL_TAPS + tap + 1, :] = jnp.sum(
            tap_rows[tap], axis=0, keepdims=True
        )
    for at in range(0, length, FRONT_TILE):
        total = d_lag_ref[0, at : at + FRONT_TILE, :]
        for lag in range(1, 4):
            total = total + d_lag_ref[lag, at + lag : at + lag + FRONT_TILE, :]
        input_ref[at : at + FRONT_TILE, :] = total.astype(low)
    lane = lax.broadcasted_iota(jnp.int32, (heads, width), 1)
    bias = jnp.zeros((heads, width), jnp.float32)
    for bucket in range(BUCKET_LIMIT):
        picked = jnp.where(buckets_ref[...] == bucket, band_ref[...], 0.0)
        bias = jnp.where(lane == bucket, jnp.sum(picked, axis=1, keepdims=True), bias)
    small_ref[SMALL_BIAS : SMALL_BIAS + heads, :] = bias
    all_ref[:vocab, 5 * width :] = dot_nn(hot, input_ref[...]).astype(low)
    all_ref[vocab:, 5 * width :] = jnp.zeros((width - vocab, width), low)
    all_ref[vocab : vocab + 32, 5 * width :] = small_ref[...].astype(low)
    half = width // 2
    mine = mine_ref[0]
    kept_ref[...] = all_ref[pl.ds(pl.multiple_of(mine * half, half), half), :]
    sent_ref[...] = all_ref[pl.ds(pl.multiple_of((1 - mine) * half, half), half), :]


def back(*args):
    length, width = args[9].shape
    low = jnp.bfloat16
    half = jax.ShapeDtypeStruct((width // 2, 6 * width), low)
    return pl.pallas_call(
        back_kernel,
        out_shape=(half, half, jax.ShapeDtypeStruct((length, width), low)),
        in_specs=[smem()] + [vmem()] * 18,
        out_specs=(vmem(),) * 3,
        scratch_shapes=[
            pltpu.VMEM((width, 6 * width), low),
            pltpu.VMEM((32, width), jnp.float32),
            pltpu.VMEM((length + HALO, width), jnp.float32),
            pltpu.VMEM((length, width), jnp.float32),
            pltpu.VMEM((length, width), low),
            pltpu.VMEM((4, length + HALO, width), jnp.float32),
        ],
        compiler_params=params(36),
        cost_estimate=pl.CostEstimate(
            flops=22 * length * width * width,
            bytes_accessed=20 * 2**20,
            transcendentals=3 * length * width,
        ),
        name="back",
    )(*args)


def middle_and_norm(attn_ref, resid_ref, w_out_ref):
    mid = resid_ref[...] + dot_nn(attn_ref[...], w_out_ref[...])
    return mid, lax.rsqrt(jnp.mean(mid * mid, axis=-1, keepdims=True) + EPSILON)


def hidden_kernel(
    attn_ref, resid_ref, grad_ref, w_out_ref, gain_ref, w_gate_ref, w_upper_ref, w_down_ref,
    weight_back_ref, acts_ref,
    normed_ref, normed_t_ref, grad_t_ref, gate_ref, upper_ref, d_inner_ref,
):
    @pl.when(pl.program_id(0) == 0)
    def _():
        mid, rinv = middle_and_norm(attn_ref, resid_ref, w_out_ref)
        normed = (mid * rinv * gain_ref[...]).astype(jnp.bfloat16)
        normed_ref[...] = normed
        normed_t_ref[...] = normed.T
        grad_t_ref[...] = grad_ref[...].T

    gate_ref[...] = dot_nn(normed_ref[...], w_gate_ref[...])
    upper_ref[...] = dot_nn(normed_ref[...], w_upper_ref[...])
    d_inner_ref[...] = dot_nt(grad_ref[...], w_down_ref[...])
    upper = upper_ref[...]
    d_inner = d_inner_ref[...]
    bent, slope = gelu_parts(gate_ref[...])
    low = jnp.bfloat16
    inner_at, gate_at, upper_at = (
        slice(plane * HIDDEN_TILE, (plane + 1) * HIDDEN_TILE) for plane in (2, 0, 1)
    )
    acts_ref[:, inner_at] = (bent * upper).astype(low)
    acts_ref[:, gate_at] = (d_inner * upper * slope).astype(low)
    acts_ref[:, upper_at] = (d_inner * bent).astype(low)
    for left_ref, at in ((normed_t_ref, gate_at), (normed_t_ref, upper_at), (grad_t_ref, inner_at)):
        weight_back_ref[:, at] = dot_nn(left_ref[...], acts_ref[:, at]).astype(low)


def hidden_layer(attn, resid, grad, w_out, gain, w_in, w_down):
    length, width = attn.shape
    hidden = w_down.shape[0]
    steps = hidden // HIDDEN_TILE
    low = jnp.bfloat16
    return pl.pallas_call(
        hidden_kernel,
        grid=(steps,),
        out_shape=(
            jax.ShapeDtypeStruct((width, 3 * hidden), low),
            jax.ShapeDtypeStruct((length, 3 * hidden), low),
        ),
        in_specs=[vmem()] * 5
        + [
            pl.BlockSpec((width, HIDDEN_TILE), lambda c: (0, c)),
            pl.BlockSpec((width, HIDDEN_TILE), lambda c: (0, steps + c)),
            pl.BlockSpec((HIDDEN_TILE, width), lambda c: (c, 0)),
        ],
        out_specs=(
            pl.BlockSpec((width, 3 * HIDDEN_TILE), lambda c: (0, c)),
            pl.BlockSpec((length, 3 * HIDDEN_TILE), lambda c: (0, c)),
        ),
        scratch_shapes=[
            pltpu.VMEM((length, width), low),
            pltpu.VMEM((width, length), low),
            pltpu.VMEM((width, length), low),
            pltpu.VMEM((length, HIDDEN_TILE), jnp.float32),
            pltpu.VMEM((length, HIDDEN_TILE), jnp.float32),
            pltpu.VMEM((length, HIDDEN_TILE), jnp.float32),
        ],
        compiler_params=params(52),
        cost_estimate=pl.CostEstimate(
            flops=12 * length * width * hidden,
            bytes_accessed=32 * 2**20,
            transcendentals=length * hidden,
        ),
        name="hidden_layer",
    )(attn, resid, grad, w_out, gain.reshape(1, width), w_in, w_in, w_down)


def outer_kernel(
    attn_ref, resid_ref, grad_ref, w_out_ref, gain_ref, acts_ref, w_gate_ref, w_upper_ref,
    w_down_ref,
    output_ref, d_mid_ref, d_attn_ref, d_w_out_ref, d_gain_ref,
    mid_ref, rinv_ref, sum_ref, back_ref,
):
    step = pl.program_id(0)

    @pl.when(step == 0)
    def _():
        mid, rinv = middle_and_norm(attn_ref, resid_ref, w_out_ref)
        mid_ref[...] = mid
        rinv_ref[...] = jnp.broadcast_to(rinv, rinv_ref.shape)
        sum_ref[...] = mid
        back_ref[...] = jnp.zeros_like(back_ref)

    sum_ref[...] += dot_nn(acts_ref[:, 2 * HIDDEN_TILE :], w_down_ref[...])
    back_ref[...] += dot_nt(acts_ref[:, :HIDDEN_TILE], w_gate_ref[...]) + dot_nt(
        acts_ref[:, HIDDEN_TILE : 2 * HIDDEN_TILE], w_upper_ref[...]
    )

    @pl.when(step == pl.num_programs(0) - 1)
    def _():
        output_ref[...] = sum_ref[...].astype(jnp.bfloat16)
        rinv = rinv_ref[:, :1]
        mid = mid_ref[...]
        d_normed = back_ref[...]
        d_gain_ref[...] = jnp.sum(d_normed * mid * rinv, axis=0, keepdims=True)
        scaled = d_normed * gain_ref[...]
        lean = jnp.mean(scaled * mid, axis=-1, keepdims=True) * (rinv * rinv * rinv)
        d_mid = grad_ref[...].astype(jnp.float32) + rinv * scaled - mid * lean
        d_mid_ref[...] = d_mid
        d_branch = d_mid.astype(jnp.bfloat16)
        d_attn_ref[...] = dot_nt(d_branch, w_out_ref[...]).astype(jnp.bfloat16)
        d_w_out_ref[...] = dot_nn(attn_ref[...].T, d_branch).astype(jnp.bfloat16)


def outer_layer(attn, resid, grad, w_out, gain, acts, w_in, w_down):
    length, width = attn.shape
    hidden = w_down.shape[0]
    steps = hidden // HIDDEN_TILE
    low = jnp.bfloat16
    return pl.pallas_call(
        outer_kernel,
        grid=(steps,),
        out_shape=(
            jax.ShapeDtypeStruct((length, width), low),
            jax.ShapeDtypeStruct((length, width), jnp.float32),
            jax.ShapeDtypeStruct((length, width), low),
            jax.ShapeDtypeStruct((width, width), low),
            jax.ShapeDtypeStruct((1, width), jnp.float32),
        ),
        in_specs=[vmem()] * 5
        + [
            pl.BlockSpec((length, 3 * HIDDEN_TILE), lambda c: (0, c)),
            pl.BlockSpec((width, HIDDEN_TILE), lambda c: (0, c)),
            pl.BlockSpec((width, HIDDEN_TILE), lambda c: (0, steps + c)),
            pl.BlockSpec((HIDDEN_TILE, width), lambda c: (c, 0)),
        ],
        out_specs=(vmem(),) * 5,
        scratch_shapes=[
            pltpu.VMEM((length, width), jnp.float32),
            pltpu.VMEM((length, LANES), jnp.float32),
            pltpu.VMEM((length, width), jnp.float32),
            pltpu.VMEM((length, width), jnp.float32),
        ],
        compiler_params=params(30),
        cost_estimate=pl.CostEstimate(
            flops=6 * length * width * hidden + 6 * length * width * width,
            bytes_accessed=24 * 2**20,
            transcendentals=0,
        ),
        name="outer_layer",
    )(attn, resid, grad, w_out, gain.reshape(1, width), acts, w_in, w_in, w_down)


def finish_wide_kernel(scale, piece_ref, d_w_in_ref, d_w_down_ref):
    piece = piece_ref[...].astype(jnp.float32) * scale

    @pl.when(pl.program_id(0) < 2)
    def _():
        d_w_in_ref[...] = piece

    @pl.when(pl.program_id(0) == 2)
    def _():
        d_w_down_ref[...] = piece.T


def finish_wide(total, scale):
    width = total.shape[0]
    hidden = total.shape[1] // 3
    tiles = hidden // HIDDEN_TILE
    return pl.pallas_call(
        functools.partial(finish_wide_kernel, scale),
        grid=(3, tiles),
        out_shape=(
            jax.ShapeDtypeStruct((width, 2 * hidden), jnp.float32),
            jax.ShapeDtypeStruct((hidden, width), jnp.float32),
        ),
        in_specs=[pl.BlockSpec((width, HIDDEN_TILE), lambda p, c: (0, c * 3 + p))],
        out_specs=(
            pl.BlockSpec(
                (width, HIDDEN_TILE), lambda p, c: (0, jnp.where(p < 2, p * tiles + c, 2 * tiles - 1))
            ),
            pl.BlockSpec((HIDDEN_TILE, width), lambda p, c: (jnp.where(p < 2, 0, c), 0)),
        ),
        compiler_params=params(58),
        cost_estimate=pl.CostEstimate(
            flops=6 * width * hidden, bytes_accessed=18 * width * hidden, transcendentals=0
        ),
        name="finish_wide",
    )(total)


def finish_kernel(scale, spots, mine_ref, own_ref, other_ref, *refs):
    *out_refs, joined_ref = refs
    half = own_ref.shape[0]
    mine = mine_ref[0]
    for piece_ref, side in ((own_ref, mine), (other_ref, 1 - mine)):
        part = pl.ds(pl.multiple_of(side * half, half), half)
        joined_ref[part, :] = piece_ref[...].astype(jnp.float32) * scale
    for ref, (row, column) in zip(out_refs, spots):
        rows, columns = ref.shape
        ref[...] = joined_ref[row : row + rows, column : column + columns]


def finish(mine, own, other, scale, shapes, spots):
    half, columns = own.shape
    return pl.pallas_call(
        functools.partial(finish_kernel, scale, spots),
        out_shape=[jax.ShapeDtypeStruct(shape, jnp.float32) for shape in shapes],
        in_specs=[smem(), vmem(), vmem()],
        out_specs=[vmem()] * len(shapes),
        scratch_shapes=[pltpu.VMEM((2 * half, columns), jnp.float32)],
        compiler_params=params(16),
        cost_estimate=pl.CostEstimate(
            flops=4 * half * columns, bytes_accessed=12 * half * columns, transcendentals=0
        ),
        name="finish",
    )(mine, own, other)


def to_rows(block, share):
    rows, stretch = block.shape[:2]
    pieces = jnp.repeat(block, share, axis=0) if share > 1 else block
    pieces = lax.all_to_all(pieces, "blk", 0, 0, tiled=True)
    return pieces.reshape((rows * share * stretch,) + block.shape[2:])


def to_blocks(row, share):
    blocks = lax.axis_size("blk")
    pieces = row.reshape((blocks, row.shape[0] // blocks) + row.shape[1:])
    return lax.all_to_all(pieces, "blk", 0, 0, tiled=True)[::share]


def own_bit(axis, bit):
    return (lax.axis_index(axis) >> bit) & 1


def swapped(block, axis, bit):
    devices = range(lax.axis_size(axis))
    return lax.ppermute(block, axis, [(i, i ^ (1 << bit)) for i in devices])


def bits_of(axis):
    return lax.axis_size(axis).bit_length() - 1


def group_of(free):
    blk = lax.axis_size("blk")
    devices = range(lax.axis_size("rows") * blk)
    weights = [(blk if axis == "rows" else 1) << bit for axis, bit in free]
    place = sum(own_bit(axis, bit) << at for at, (axis, bit) in enumerate(free))

    def send(block, gap):
        shift = sum(weight for at, weight in enumerate(weights) if gap >> at & 1)
        return lax.ppermute(block, ("rows", "blk"), [(i, i ^ shift) for i in devices])

    return 1 << len(free), place, send


class Travel:
    def __init__(self, kept, sent):
        near = [("blk", bit) for bit in range(1, bits_of("blk"))] + [("rows", 0)]
        far = [("rows", bit) for bit in range(1, bits_of("rows"))]
        stages = (group_of(near), group_of(far))
        terms = [kept, swapped(sent, "blk", 0)]
        self.state = [terms]
        self.orders = [stages]
        self.at = 0

    def go(self):
        self.state = [self.lane_step(*lane) for lane in zip(self.state, self.orders)]
        self.at += 1

    def lane_step(self, terms, order):
        block = total(terms)
        if self.at == 4:
            return [block, swapped(block, "blk", 0)]
        count, place, send = order[self.at if self.at < 2 else 3 - self.at]
        if self.at < 2:
            rows = block.shape[0] // count
            def piece(owner):
                return lax.dynamic_slice_in_dim(block, owner * rows, rows, axis=0)

            return [piece(place)] + [send(piece(place ^ gap), gap) for gap in range(1, count)]
        pieces = [block] + [send(block, gap) for gap in range(1, count)]
        gap = 1
        while gap < count:
            stays = (place & gap) == 0
            pieces = [jnp.where(stays, pieces[at], pieces[at ^ gap]) for at in range(count)]
            gap *= 2
        return [jnp.concatenate(pieces, axis=0)]


def total(terms):
    first, *others = terms
    if not others:
        return first
    wide = first.astype(jnp.float32)
    for other in others:
        wide = wide + other.astype(jnp.float32)
    return wide.astype(first.dtype)


def beside(values, *travels):
    for travel in travels:
        travel.go()
    return settled(values, *travels)


def settled(values, *travels):
    states, values = lax.optimization_barrier(([travel.state for travel in travels], values))
    for travel, state in zip(travels, states):
        travel.state = state
    return values


def on_device(
    byte_vals,
    segment_ids,
    buckets,
    emb_table,
    conv_taps,
    w_proj,
    gain_one,
    w_qkv,
    rel_bias,
    w_out,
    gain_two,
    w_in,
    w_down,
    out_grad,
):
    rows, stretch = byte_vals.shape
    vocab, width = emb_table.shape
    bucket_count, heads = rel_bias.shape
    hidden = w_down.shape[0]
    blocks = lax.axis_size("blk")
    share = blocks // rows
    length = stretch * blocks
    low = jnp.bfloat16

    packed = to_rows(byte_vals + vocab * segment_ids, share)
    letters_own = lax.rem(packed, vocab)
    segments = lax.div(packed, vocab)
    grad_low = to_rows(out_grad, share)

    taps = conv_taps.astype(jnp.float32)
    conv_low, resid, normed_one, qkv = front(
        letters_own, segments, emb_table, taps, w_proj, gain_one, w_qkv
    )
    band_buckets = jnp.concatenate(
        [buckets[BAND_FIRST : BAND_FIRST + BAND - LANES], buckets[BAND_FIRST - LANES : BAND_FIRST]]
    )
    bounds = document_bounds(segments)
    same_q, same_k = document_marks(segments)
    attn, lse, base = attend(
        bounds, qkv, same_q, same_k, band_buckets.reshape(1, BAND), rel_bias.T
    )

    mine = own_bit("blk", 0).astype(jnp.int32).reshape(1)
    scale = 1.0 / share
    d_wide, acts = hidden_layer(attn, resid, grad_low, w_out, gain_two, w_in, w_down)

    def remainder():
        output_row, d_mid, d_attn, d_w_out, d_gain_two = outer_layer(
            attn, resid, grad_low, w_out, gain_two, acts, w_in, w_down
        )
        output = to_blocks(output_row, share)
        *parts, band = attend_back(bounds, qkv, same_q, same_k, base, lse, attn, d_attn)
        parts, output = lax.optimization_barrier((parts, output))
        kept, sent, input_low = back(
            mine,
            letters_own.reshape(1, length),
            segments.reshape(1, length),
            emb_table,
            taps,
            w_proj,
            gain_one.reshape(1, width),
            w_qkv,
            conv_low,
            resid,
            normed_one,
            *parts,
            d_mid,
            d_w_out,
            d_gain_two,
            band_buckets.reshape(1, BAND),
            band,
        )
        rest = Travel(kept, sent)
        input_low = settled(input_low, rest)
        input_grad = to_blocks(input_low, share)
        input_grad = beside(input_grad, rest)
        for step in range(4):
            rest.go()
        finished = finish(
            mine,
            *rest.state[0],
            scale,
            (
                (width, 3 * width),
                (width, width),
                (width, width),
                (vocab, width),
                (9, width),
                (1, width),
                (1, width),
                (heads, LANES),
            ),
            (
                (0, 0),
                (0, 3 * width),
                (0, 4 * width),
                (0, 5 * width),
                (vocab + SMALL_TAPS, 5 * width),
                (vocab + SMALL_ONE, 5 * width),
                (vocab + SMALL_TWO, 5 * width),
                (vocab + SMALL_BIAS, 5 * width),
            ),
        )
        input_grad = input_grad.astype(jnp.float32)
        return output, input_grad, finished

    def nothing():
        return jax.tree.map(lambda leaf: jnp.zeros(leaf.shape, leaf.dtype), shapes)

    shapes = jax.eval_shape(remainder)
    d_wide = lax.psum(d_wide, ("rows", "blk"))
    output, input_grad, finished = lax.cond(segments[0] >= 0, remainder, nothing)
    (
        d_w_qkv,
        d_w_proj,
        d_w_out,
        d_emb_table,
        d_conv_taps,
        d_gain_one,
        d_gain_two,
        d_rel_bias,
    ) = finished
    d_w_in, d_w_down = finish_wide(d_wide, scale)
    d_gain_one = d_gain_one.reshape(width)
    d_gain_two = d_gain_two.reshape(width)
    d_rel_bias = d_rel_bias[:, :bucket_count].T
    return (
        output,
        input_grad,
        d_emb_table,
        d_conv_taps,
        d_w_proj,
        d_gain_one,
        d_w_qkv,
        d_rel_bias,
        d_w_out,
        d_gain_two,
        d_w_in,
        d_w_down,
    )


def solution(mesh):
    split = P("rows", "blk")
    split_wide = P("rows", "blk", None)
    return jax.shard_map(
        on_device,
        mesh=mesh,
        in_specs=(split, split) + (P(),) * 11 + (split_wide,),
        out_specs=(split_wide, split_wide) + (P(),) * 10,
        check_vma=False,
    )
```

```python
import functools

import jax
import jax.numpy as jnp
from jax import lax
from jax.experimental import pallas as pl
from jax.experimental.pallas import tpu as pltpu
from jax.sharding import PartitionSpec as P

EPSILON = 1e-06
SCORE_SCALE = 0.125
WINDOWS = ((0, 2), (2, 3), (5, 4))
HIGHEST_PRECISION = lax.Precision.HIGHEST
LANES = 128
QUERY_TILE = 256
KEY_TILE = 128
MASKED = -(2.0**30)
BAND = 12 * LANES
BAND_FIRST = 3 * LANES
MIB = 2**20


def vmem():
    return pl.BlockSpec(memory_space=pltpu.VMEM)


def smem():
    return pl.BlockSpec(memory_space=pltpu.SMEM)


def params(mib):
    return pltpu.CompilerParams(vmem_limit_bytes=mib * MIB)


def dot_nt(left, right):
    return lax.dot_general(
        left, right, (((1,), (1,)), ((), ())), preferred_element_type=jnp.float32
    )


def dot_nn(left, right):
    return jnp.dot(left, right, preferred_element_type=jnp.float32)


def fill_tables(table_ref, base_ref):
    for head in range(base_ref.shape[0]):
        line = jnp.broadcast_to(base_ref[head : head + 1, :], (KEY_TILE, BAND))
        table_ref[head] = pltpu.roll(line, 0, 1, stride=1, stride_axis=0)


def table_lanes(query_block, key_block):
    place = (query_block * (QUERY_TILE // LANES) - key_block + 5) * LANES
    return pl.ds(pl.multiple_of(place, LANES), QUERY_TILE)


def attend_kernel(
    heads, bounds_ref, qkv_ref, same_q_ref, same_k_ref, buckets_ref, bias_ref,
    attn_ref, lse_ref, base_ref,
    table_ref,
    value_t_ref, query_ref, top_ref, total_ref, mixed_ref, score_ref, expo_ref, fade_ref,
):
    length = qkv_ref.shape[0]
    width = qkv_ref.shape[1] // 3
    head_dim = width // heads
    lane = lax.broadcasted_iota(jnp.int32, (1, LANES), 1)
    halves = (
        (lane < head_dim).astype(jnp.bfloat16),
        (lane >= head_dim).astype(jnp.bfloat16),
    )
    bias = bias_ref[...]
    base = jnp.zeros((heads, BAND), jnp.float32)
    for bucket in range(bias.shape[1]):
        base = jnp.where(buckets_ref[...] == bucket, bias[:, bucket : bucket + 1], base)
    base_ref[...] = base
    fill_tables(table_ref, base_ref)
    value_t_ref[...] = qkv_ref[:, 2 * width :].T

    def block(i, carry):
        rows = pl.ds(pl.multiple_of(i * QUERY_TILE, QUERY_TILE), QUERY_TILE)
        for pair in range(heads // 2):
            query = qkv_ref[rows, pair * LANES : (pair + 1) * LANES] * jnp.bfloat16(SCORE_SCALE)
            for side in range(2):
                query_ref[2 * pair + side, :LANES, :] = (query * halves[side]).T
                query_ref[2 * pair + side, LANES:, :] = same_q_ref[:, rows]
        top_ref[...] = jnp.full_like(top_ref, -3.0e38)
        total_ref[...] = jnp.zeros_like(total_ref)
        mixed_ref[...] = jnp.zeros_like(mixed_ref)

        def step(j, inner):
            keys = pl.ds(pl.multiple_of(j * KEY_TILE, KEY_TILE), KEY_TILE)
            lanes = table_lanes(i, j)
            for head in range(heads):
                pair = head // 2
                key = jnp.concatenate(
                    [
                        qkv_ref[keys, width + pair * LANES : width + (pair + 1) * LANES],
                        same_k_ref[keys, :],
                    ],
                    axis=1,
                )
                score_ref[head] = dot_nn(key, query_ref[head]) + table_ref[head, :, lanes]
            for head in range(heads):
                scores = score_ref[head]
                old = top_ref[head : head + 1, :]
                top = jnp.maximum(old, jnp.max(scores, axis=0, keepdims=True))
                fade = jnp.exp(old - top)
                expo = jnp.exp(scores - top)
                top_ref[head : head + 1, :] = top
                total_ref[head : head + 1, :] = total_ref[head : head + 1, :] * fade + jnp.sum(
                    expo, axis=0, keepdims=True
                )
                fade_ref[head : head + 1, :] = fade
                expo_ref[head] = expo.astype(jnp.bfloat16)
            for head in range(heads):
                own = slice(head * head_dim, (head + 1) * head_dim)
                mixed_ref[own, :] = mixed_ref[own, :] * fade_ref[head : head + 1, :] + dot_nn(
                    value_t_ref[own, keys], expo_ref[head]
                )
            return inner

        lax.fori_loop(bounds_ref[0, i], bounds_ref[1, i], step, 0)
        for head in range(heads):
            own = slice(head * head_dim, (head + 1) * head_dim)
            mixed_ref[own, :] = mixed_ref[own, :] / total_ref[head : head + 1, :]
        attn_ref[rows, :] = mixed_ref[...].T.astype(jnp.bfloat16)
        lse_ref[:, rows] = top_ref[...] + jnp.log(total_ref[...])
        return carry

    lax.fori_loop(0, length // QUERY_TILE, block, 0)


def attend(bounds, qkv, same_q, same_k, band_buckets, bias):
    length = qkv.shape[0]
    width = qkv.shape[1] // 3
    heads = bias.shape[0]
    return pl.pallas_call(
        functools.partial(attend_kernel, heads),
        out_shape=(
            jax.ShapeDtypeStruct((length, width), jnp.bfloat16),
            jax.ShapeDtypeStruct((heads, length), jnp.float32),
            jax.ShapeDtypeStruct((heads, BAND), jnp.float32),
        ),
        in_specs=[smem()] + [vmem()] * 5,
        out_specs=(vmem(), vmem(), vmem()),
        scratch_shapes=[
            pltpu.VMEM((heads, KEY_TILE, BAND), jnp.float32),
            pltpu.VMEM((width, length), jnp.bfloat16),
            pltpu.VMEM((heads, 2 * LANES, QUERY_TILE), jnp.bfloat16),
            pltpu.VMEM((heads, QUERY_TILE), jnp.float32),
            pltpu.VMEM((heads, QUERY_TILE), jnp.float32),
            pltpu.VMEM((width, QUERY_TILE), jnp.float32),
            pltpu.VMEM((heads, KEY_TILE, QUERY_TILE), jnp.float32),
            pltpu.VMEM((heads, KEY_TILE, QUERY_TILE), jnp.bfloat16),
            pltpu.VMEM((heads, QUERY_TILE), jnp.float32),
        ],
        compiler_params=params(22),
        cost_estimate=pl.CostEstimate(
            flops=4 * length * length * width,
            bytes_accessed=12 * 2**20,
            transcendentals=length * length * heads,
        ),
        name="attend",
    )(bounds, qkv, same_q, same_k, band_buckets, bias)


def attend_back_kernel(
    bounds_ref, q_ref, k_ref, v_ref, same_q_ref, same_k_ref, base_ref, lse_ref,
    attn_ref, grad_ref,
    query_out_ref, key_out_ref, value_out_ref, band_ref,
    table_ref, key_t_ref, query_ref, grads_ref, query_t_ref, grads_t_ref, inner_ref,
    query_back_ref, key_back_ref, value_back_ref, skewed_ref,
    exact_ref, probs_ref, d_scores_ref,
):
    length, width = q_ref.shape
    heads = base_ref.shape[0]
    head_dim = width // heads
    lane = lax.broadcasted_iota(jnp.int32, (1, LANES), 1)
    halves = (
        (lane < head_dim).astype(jnp.bfloat16),
        (lane >= head_dim).astype(jnp.bfloat16),
    )
    owner = lax.broadcasted_iota(jnp.int32, (heads, width), 1) // head_dim
    own_head = (owner == lax.broadcasted_iota(jnp.int32, (heads, width), 0)).astype(jnp.bfloat16)
    fill_tables(table_ref, base_ref)
    key_t_ref[...] = k_ref[...].T
    key_back_ref[...] = jnp.zeros_like(key_back_ref)
    value_back_ref[...] = jnp.zeros_like(value_back_ref)
    skewed_ref[...] = jnp.zeros_like(skewed_ref)

    def block(i, carry):
        rows = pl.ds(pl.multiple_of(i * QUERY_TILE, QUERY_TILE), QUERY_TILE)
        for pair in range(heads // 2):
            own = slice(pair * LANES, (pair + 1) * LANES)
            query = q_ref[rows, own] * jnp.bfloat16(SCORE_SCALE)
            grad = grad_ref[rows, own]
            for side in range(2):
                part = slice(side * QUERY_TILE, (side + 1) * QUERY_TILE)
                query_ref[pair, part, :] = query * halves[side]
                grads_ref[pair, part, :] = grad * halves[side]
                query_t_ref[2 * pair + side, :LANES, :] = (query * halves[side]).T
                query_t_ref[2 * pair + side, LANES:, :] = same_q_ref[:, rows]
                grads_t_ref[2 * pair + side] = (grad * halves[side]).T
        product = grad_ref[rows, :].astype(jnp.float32) * attn_ref[rows, :].astype(jnp.float32)
        rough = product.astype(jnp.bfloat16)
        rest = (product - rough.astype(jnp.float32)).astype(jnp.bfloat16)
        inner_ref[...] = dot_nt(own_head, rough) + dot_nt(own_head, rest)
        query_back_ref[...] = jnp.zeros_like(query_back_ref)

        def step(j, inner):
            keys = pl.ds(pl.multiple_of(j * KEY_TILE, KEY_TILE), KEY_TILE)
            lanes = table_lanes(i, j)
            for head in range(heads):
                pair = head // 2
                key = jnp.concatenate(
                    [k_ref[keys, pair * LANES : (pair + 1) * LANES], same_k_ref[keys, :]], axis=1
                )
                scores = dot_nn(key, query_t_ref[head]) + table_ref[head, :, lanes]
                exact_ref[head] = jnp.exp(scores - lse_ref[head : head + 1, rows])
            for head in range(heads):
                pair = head // 2
                part = slice((head % 2) * QUERY_TILE, (head % 2 + 1) * QUERY_TILE)
                d_probs = dot_nn(v_ref[keys, pair * LANES : (pair + 1) * LANES], grads_t_ref[head])
                exact = exact_ref[head]
                d_score = exact * (d_probs - inner_ref[head : head + 1, :])
                skewed_ref[head, :, lanes] = skewed_ref[head, :, lanes] + d_score
                probs_ref[pair, :, part] = exact.astype(jnp.bfloat16)
                d_scores_ref[pair, :, part] = d_score.astype(jnp.bfloat16)
            for pair in range(heads // 2):
                own = slice(pair * LANES, (pair + 1) * LANES)
                value_back_ref[keys, own] += dot_nn(probs_ref[pair], grads_ref[pair])
                key_back_ref[keys, own] += dot_nn(d_scores_ref[pair], query_ref[pair])
            for head in range(heads):
                part = slice((head % 2) * QUERY_TILE, (head % 2 + 1) * QUERY_TILE)
                mine = slice(head * head_dim, (head + 1) * head_dim)
                query_back_ref[mine, :] += dot_nn(
                    key_t_ref[mine, keys], d_scores_ref[head // 2, :, part]
                )
            return inner

        lax.fori_loop(bounds_ref[0, i], bounds_ref[1, i], step, 0)
        query_out_ref[rows, :] = (query_back_ref[...].T * SCORE_SCALE).astype(jnp.bfloat16)
        return carry

    lax.fori_loop(0, length // QUERY_TILE, block, 0)
    key_out_ref[...] = key_back_ref[...].astype(jnp.bfloat16)
    value_out_ref[...] = value_back_ref[...].astype(jnp.bfloat16)
    for head in range(heads):
        height = KEY_TILE
        while height > 8:
            height //= 2
            skewed_ref[head, :height, :] = skewed_ref[head, :height, :] + pltpu.roll(
                skewed_ref[head, height : 2 * height, :], BAND - height, 1
            )
        total = skewed_ref[head, 0:1, :]
        for row in range(1, 8):
            total = total + pltpu.roll(skewed_ref[head, row : row + 1, :], BAND - row, 1)
        band_ref[head : head + 1, :] = total


def attend_back(bounds, qkv, same_q, same_k, base, lse, attn, grad):
    length = qkv.shape[0]
    width = qkv.shape[1] // 3
    heads = base.shape[0]

    def columns(group):
        return pl.BlockSpec(
            (length, width), lambda _: (0, group), pipeline_mode=pl.Buffered(1)
        )

    return pl.pallas_call(
        attend_back_kernel,
        out_shape=[jax.ShapeDtypeStruct((length, width), jnp.bfloat16)] * 3
        + [jax.ShapeDtypeStruct((heads, BAND), jnp.float32)],
        grid=(1,),
        in_specs=[smem(), columns(0), columns(1), columns(2)] + [vmem()] * 6,
        out_specs=[vmem()] * 4,
        scratch_shapes=[
            pltpu.VMEM((heads, KEY_TILE, BAND), jnp.float32),
            pltpu.VMEM((width, length), jnp.bfloat16),
            pltpu.VMEM((heads // 2, 2 * QUERY_TILE, LANES), jnp.bfloat16),
            pltpu.VMEM((heads // 2, 2 * QUERY_TILE, LANES), jnp.bfloat16),
            pltpu.VMEM((heads, 2 * LANES, QUERY_TILE), jnp.bfloat16),
            pltpu.VMEM((heads, LANES, QUERY_TILE), jnp.bfloat16),
            pltpu.VMEM((heads, QUERY_TILE), jnp.float32),
            pltpu.VMEM((width, QUERY_TILE), jnp.float32),
            pltpu.VMEM((length, width), jnp.float32),
            pltpu.VMEM((length, width), jnp.float32),
            pltpu.VMEM((heads, KEY_TILE, BAND), jnp.float32),
            pltpu.VMEM((heads, KEY_TILE, QUERY_TILE), jnp.float32),
            pltpu.VMEM((heads // 2, KEY_TILE, 2 * QUERY_TILE), jnp.bfloat16),
            pltpu.VMEM((heads // 2, KEY_TILE, 2 * QUERY_TILE), jnp.bfloat16),
        ],
        compiler_params=params(34),
        cost_estimate=pl.CostEstimate(
            flops=40 * length * length * width,
            bytes_accessed=8 * 2**20,
            transcendentals=length * length * heads,
        ),
        name="attend_back",
    )(bounds, qkv, qkv, qkv, same_q, same_k, base, lse, attn, grad)


def document_bounds(segments):
    length = segments.shape[0]
    starts = segments[::QUERY_TILE]
    ends = segments[QUERY_TILE - 1 :: QUERY_TILE]
    before = jnp.sum((segments[None, :] < starts[:, None]).astype(jnp.int32), axis=1)
    upto = jnp.sum((segments[None, :] <= ends[:, None]).astype(jnp.int32), axis=1)
    return jnp.stack([before // KEY_TILE, (upto + KEY_TILE - 1) // KEY_TILE])


def document_marks(segments):
    own = segments[:, None] == jnp.arange(LANES, dtype=jnp.int32)[None, :]
    own_t = segments[None, :] == jnp.arange(LANES, dtype=jnp.int32)[:, None]
    return own_t.astype(jnp.bfloat16), jnp.where(own, 0.0, MASKED).astype(jnp.bfloat16)
HIDDEN_TILE = 512
GELU_SLOPE = 0.7978845608028654
GELU_CUBIC = 0.044715


def gelu_value(values):
    square = values * values
    bend = jnp.tanh(values * (GELU_SLOPE + GELU_SLOPE * GELU_CUBIC * square))
    return values * (0.5 + 0.5 * bend)


def gelu_parts(values):
    square = values * values
    bend = jnp.tanh(values * (GELU_SLOPE + GELU_SLOPE * GELU_CUBIC * square))
    half = 0.5 + 0.5 * bend
    slope = half + values * (1.0 - bend * bend) * (
        0.5 * GELU_SLOPE + 1.5 * GELU_SLOPE * GELU_CUBIC * square
    )
    return values * half, slope


FRONT_TILE = 128
BUCKET_LIMIT = 32
HALO = 8


def byte_marks(letters_ref, vocab):
    letters = lax.broadcasted_iota(jnp.int32, (vocab, letters_ref.shape[1]), 0)
    return (letters == letters_ref[...]).astype(jnp.float32).astype(jnp.bfloat16)


def embed(hot, emb_ref, embedded_ref):
    embedded_ref[:HALO, :] = jnp.zeros((HALO, emb_ref.shape[1]), jnp.float32)
    embedded_ref[HALO:, :] = lax.dot_general(
        hot, emb_ref[...], (((0,), (0,)), ((), ())), preferred_element_type=jnp.float32
    )


def lag_keeps(segments_ref):
    segments = segments_ref[...]
    place = lax.broadcasted_iota(jnp.int32, segments.shape, 1)
    rows = [jnp.ones(segments.shape, jnp.float32)]
    for lag in range(1, HALO):
        same = (pltpu.roll(segments, lag, 1) == segments) & (place >= lag)
        rows.append(same.astype(jnp.float32))
    return jnp.concatenate(rows, axis=0).T


def window_sums(embedded_ref, keeps, taps_ref, at):
    part = slice(at, at + FRONT_TILE)
    shifted = []
    for lag in range(4):
        moved = embedded_ref[HALO + at - lag : HALO + at - lag + FRONT_TILE, :]
        shifted.append(moved if lag == 0 else moved * keeps[part, lag : lag + 1])
    sums = []
    for first, span in WINDOWS:
        summed = shifted[0] * taps_ref[first : first + 1, :]
        for lag in range(1, span):
            summed = summed + shifted[lag] * taps_ref[first + lag : first + lag + 1, :]
        sums.append(summed)
    return shifted, sums


def front_kernel(
    letters_ref, segments_ref, emb_ref, taps_ref, w_proj_ref, gain_ref, w_qkv_ref,
    conv_ref, resid_ref, normed_ref, qkv_ref,
    embedded_ref,
):
    length, width = resid_ref.shape
    vocab = emb_ref.shape[0]
    hot = byte_marks(letters_ref, vocab)
    embed(hot, emb_ref, embedded_ref)
    keeps = lag_keeps(segments_ref)
    for at in range(0, length, FRONT_TILE):
        shifted, sums = window_sums(embedded_ref, keeps, taps_ref, at)
        conv_ref[at : at + FRONT_TILE, :] = sum(gelu_value(summed) for summed in sums).astype(
            jnp.bfloat16
        )
    resid = dot_nn(conv_ref[...], w_proj_ref[...])
    resid_ref[...] = resid
    rinv = lax.rsqrt(jnp.mean(resid * resid, axis=-1, keepdims=True) + EPSILON)
    normed_ref[...] = (resid * rinv * gain_ref[...]).astype(jnp.bfloat16)
    qkv_ref[...] = dot_nn(normed_ref[...], w_qkv_ref[...]).astype(jnp.bfloat16)


def front(letters, segments, emb_table, taps, w_proj, gain, w_qkv):
    length = letters.shape[0]
    vocab, width = emb_table.shape
    low = jnp.bfloat16
    return pl.pallas_call(
        front_kernel,
        out_shape=(
            jax.ShapeDtypeStruct((length, width), low),
            jax.ShapeDtypeStruct((length, width), jnp.float32),
            jax.ShapeDtypeStruct((length, width), low),
            jax.ShapeDtypeStruct((length, 3 * width), low),
        ),
        in_specs=[vmem()] * 7,
        out_specs=(vmem(),) * 4,
        scratch_shapes=[pltpu.VMEM((length + HALO, width), jnp.float32)],
        compiler_params=params(24),
        cost_estimate=pl.CostEstimate(
            flops=2 * length * width * (4 * width + vocab) + 60 * length * width,
            bytes_accessed=12 * 2**20,
            transcendentals=3 * length * width,
        ),
        name="front",
    )(
        letters.reshape(1, length),
        segments.reshape(1, length),
        emb_table,
        taps,
        w_proj,
        gain.reshape(1, width),
        w_qkv,
    )


SMALL_TAPS, SMALL_ONE, SMALL_TWO, SMALL_BIAS = 0, 9, 10, 16


def back_kernel(
    mine_ref, letters_ref, segments_ref, emb_ref, taps_ref, w_proj_ref, gain_ref, w_qkv_ref,
    conv_ref, resid_ref, normed_ref, d_query_ref, d_key_ref, d_value_ref, d_mid_ref,
    d_w_out_ref, d_gain_two_ref, buckets_ref, band_ref,
    kept_ref, sent_ref, input_ref,
    all_ref, small_ref, embedded_ref, d_normed_ref, d_resid_ref, d_lag_ref,
):
    length, width = resid_ref.shape
    vocab = emb_ref.shape[0]
    heads = band_ref.shape[0]
    low = jnp.bfloat16
    d_parts = (d_query_ref, d_key_ref, d_value_ref)
    d_normed_ref[...] = sum(
        dot_nt(part_ref[...], w_qkv_ref[:, at * width : (at + 1) * width])
        for at, part_ref in enumerate(d_parts)
    )
    resid = resid_ref[...]
    d_normed = d_normed_ref[...]
    rinv = lax.rsqrt(jnp.mean(resid * resid, axis=-1, keepdims=True) + EPSILON)
    small_ref[...] = jnp.zeros_like(small_ref)
    small_ref[SMALL_ONE : SMALL_ONE + 1, :] = jnp.sum(
        d_normed * resid * rinv, axis=0, keepdims=True
    )
    small_ref[SMALL_TWO : SMALL_TWO + 1, :] = d_gain_two_ref[...]
    scaled = d_normed * gain_ref[...]
    lean = jnp.mean(scaled * resid, axis=-1, keepdims=True) * (rinv * rinv * rinv)
    d_resid_ref[...] = (d_mid_ref[...] + rinv * scaled - resid * lean).astype(low)
    normed_t = normed_ref[...].T
    for at, part_ref in enumerate(d_parts):
        all_ref[:, at * width : (at + 1) * width] = dot_nn(normed_t, part_ref[...]).astype(low)
    all_ref[:, 3 * width : 4 * width] = dot_nn(conv_ref[...].T, d_resid_ref[...]).astype(low)
    all_ref[:, 4 * width : 5 * width] = d_w_out_ref[...]
    d_normed_ref[...] = dot_nt(d_resid_ref[...], w_proj_ref[...])

    hot = byte_marks(letters_ref, vocab)
    embed(hot, emb_ref, embedded_ref)
    keeps = lag_keeps(segments_ref)
    tap_rows = [jnp.zeros((8, width), jnp.float32)] * 9
    d_lag_ref[:, length:, :] = jnp.zeros((4, HALO, width), jnp.float32)
    for at in range(0, length, FRONT_TILE):
        part = slice(at, at + FRONT_TILE)
        shifted, sums = window_sums(embedded_ref, keeps, taps_ref, at)
        d_conv = d_normed_ref[part, :]
        d_shifted = [0.0] * 4
        for (first, span), summed in zip(WINDOWS, sums):
            d_pre = d_conv * gelu_parts(summed)[1]
            for lag in range(span):
                tap = first + lag
                pieces = (d_pre * shifted[lag]).reshape(FRONT_TILE // 8, 8, width)
                tap_rows[tap] = tap_rows[tap] + jnp.sum(pieces, axis=0)
                d_shifted[lag] = d_shifted[lag] + d_pre * taps_ref[tap : tap + 1, :]
        for lag in range(4):
            kept = d_shifted[lag]
            d_lag_ref[lag, part, :] = kept if lag == 0 else kept * keeps[part, lag : lag + 1]
    for tap in range(9):
        small_ref[SMALL_TAPS + tap : SMALL_TAPS + tap + 1, :] = jnp.sum(
            tap_rows[tap], axis=0, keepdims=True
        )
    for at in range(0, length, FRONT_TILE):
        total = d_lag_ref[0, at : at + FRONT_TILE, :]
        for lag in range(1, 4):
            total = total + d_lag_ref[lag, at + lag : at + lag + FRONT_TILE, :]
        input_ref[at : at + FRONT_TILE, :] = total.astype(low)
    lane = lax.broadcasted_iota(jnp.int32, (heads, width), 1)
    bias = jnp.zeros((heads, width), jnp.float32)
    for bucket in range(BUCKET_LIMIT):
        picked = jnp.where(buckets_ref[...] == bucket, band_ref[...], 0.0)
        bias = jnp.where(lane == bucket, jnp.sum(picked, axis=1, keepdims=True), bias)
    small_ref[SMALL_BIAS : SMALL_BIAS + heads, :] = bias
    all_ref[:vocab, 5 * width :] = dot_nn(hot, input_ref[...]).astype(low)
    all_ref[vocab:, 5 * width :] = jnp.zeros((width - vocab, width), low)
    all_ref[vocab : vocab + 32, 5 * width :] = small_ref[...].astype(low)
    half = width // 2
    mine = mine_ref[0]
    kept_ref[...] = all_ref[pl.ds(pl.multiple_of(mine * half, half), half), :]
    sent_ref[...] = all_ref[pl.ds(pl.multiple_of((1 - mine) * half, half), half), :]


def back(*args):
    length, width = args[9].shape
    low = jnp.bfloat16
    half = jax.ShapeDtypeStruct((width // 2, 6 * width), low)
    return pl.pallas_call(
        back_kernel,
        out_shape=(half, half, jax.ShapeDtypeStruct((length, width), low)),
        in_specs=[smem()] + [vmem()] * 18,
        out_specs=(vmem(),) * 3,
        scratch_shapes=[
            pltpu.VMEM((width, 6 * width), low),
            pltpu.VMEM((32, width), jnp.float32),
            pltpu.VMEM((length + HALO, width), jnp.float32),
            pltpu.VMEM((length, width), jnp.float32),
            pltpu.VMEM((length, width), low),
            pltpu.VMEM((4, length + HALO, width), jnp.float32),
        ],
        compiler_params=params(36),
        cost_estimate=pl.CostEstimate(
            flops=22 * length * width * width,
            bytes_accessed=20 * 2**20,
            transcendentals=3 * length * width,
        ),
        name="back",
    )(*args)


def middle_and_norm(attn_ref, resid_ref, w_out_ref):
    mid = resid_ref[...] + dot_nn(attn_ref[...], w_out_ref[...])
    return mid, lax.rsqrt(jnp.mean(mid * mid, axis=-1, keepdims=True) + EPSILON)


def hidden_kernel(
    mine_ref, attn_ref, resid_ref, grad_ref, w_out_ref, gain_ref, w_gate_ref, w_upper_ref,
    w_down_ref,
    kept_ref, sent_ref, acts_ref,
    normed_ref, normed_t_ref, grad_t_ref, gate_ref, upper_ref, d_inner_ref,
):
    @pl.when(pl.program_id(0) == 0)
    def _():
        mid, rinv = middle_and_norm(attn_ref, resid_ref, w_out_ref)
        normed = (mid * rinv * gain_ref[...]).astype(jnp.bfloat16)
        normed_ref[...] = normed
        normed_t_ref[...] = normed.T
        grad_t_ref[...] = grad_ref[...].T

    gate_ref[...] = dot_nn(normed_ref[...], w_gate_ref[...])
    upper_ref[...] = dot_nn(normed_ref[...], w_upper_ref[...])
    d_inner_ref[...] = dot_nt(grad_ref[...], w_down_ref[...])
    upper = upper_ref[...]
    d_inner = d_inner_ref[...]
    bent, slope = gelu_parts(gate_ref[...])
    low = jnp.bfloat16
    inner_at, gate_at, upper_at = (
        slice(plane * HIDDEN_TILE, (plane + 1) * HIDDEN_TILE) for plane in (2, 0, 1)
    )
    acts_ref[:, inner_at] = (bent * upper).astype(low)
    acts_ref[:, gate_at] = (d_inner * upper * slope).astype(low)
    acts_ref[:, upper_at] = (d_inner * bent).astype(low)
    half = normed_t_ref.shape[0] // 2
    for back_ref, side in ((sent_ref, 1 - mine_ref[0]), (kept_ref, mine_ref[0])):
        part = pl.ds(pl.multiple_of(side * half, half), half)
        for left_ref, at in (
            (normed_t_ref, gate_at),
            (normed_t_ref, upper_at),
            (grad_t_ref, inner_at),
        ):
            back_ref[:, at] = dot_nn(left_ref[part, :], acts_ref[:, at]).astype(low)


def hidden_layer(mine, attn, resid, grad, w_out, gain, w_in, w_down):
    length, width = attn.shape
    hidden = w_down.shape[0]
    steps = hidden // HIDDEN_TILE
    low = jnp.bfloat16
    return pl.pallas_call(
        hidden_kernel,
        grid=(steps,),
        out_shape=(
            jax.ShapeDtypeStruct((width // 2, 3 * hidden), low),
            jax.ShapeDtypeStruct((width // 2, 3 * hidden), low),
            jax.ShapeDtypeStruct((length, 3 * hidden), low),
        ),
        in_specs=[smem()] + [vmem()] * 5
        + [
            pl.BlockSpec((width, HIDDEN_TILE), lambda c: (0, c)),
            pl.BlockSpec((width, HIDDEN_TILE), lambda c: (0, steps + c)),
            pl.BlockSpec((HIDDEN_TILE, width), lambda c: (c, 0)),
        ],
        out_specs=(
            pl.BlockSpec((width // 2, 3 * HIDDEN_TILE), lambda c: (0, c)),
            pl.BlockSpec((width // 2, 3 * HIDDEN_TILE), lambda c: (0, c)),
            pl.BlockSpec((length, 3 * HIDDEN_TILE), lambda c: (0, c)),
        ),
        scratch_shapes=[
            pltpu.VMEM((length, width), low),
            pltpu.VMEM((width, length), low),
            pltpu.VMEM((width, length), low),
            pltpu.VMEM((length, HIDDEN_TILE), jnp.float32),
            pltpu.VMEM((length, HIDDEN_TILE), jnp.float32),
            pltpu.VMEM((length, HIDDEN_TILE), jnp.float32),
        ],
        compiler_params=params(52),
        cost_estimate=pl.CostEstimate(
            flops=12 * length * width * hidden,
            bytes_accessed=32 * 2**20,
            transcendentals=length * hidden,
        ),
        name="hidden_layer",
    )(mine, attn, resid, grad, w_out, gain.reshape(1, width), w_in, w_in, w_down)


def outer_kernel(
    attn_ref, resid_ref, grad_ref, w_out_ref, gain_ref, acts_ref, w_gate_ref, w_upper_ref,
    w_down_ref,
    output_ref, d_mid_ref, d_attn_ref, d_w_out_ref, d_gain_ref,
    mid_ref, rinv_ref, sum_ref, back_ref,
):
    step = pl.program_id(0)

    @pl.when(step == 0)
    def _():
        mid, rinv = middle_and_norm(attn_ref, resid_ref, w_out_ref)
        mid_ref[...] = mid
        rinv_ref[...] = jnp.broadcast_to(rinv, rinv_ref.shape)
        sum_ref[...] = mid
        back_ref[...] = jnp.zeros_like(back_ref)

    sum_ref[...] += dot_nn(acts_ref[:, 2 * HIDDEN_TILE :], w_down_ref[...])
    back_ref[...] += dot_nt(acts_ref[:, :HIDDEN_TILE], w_gate_ref[...]) + dot_nt(
        acts_ref[:, HIDDEN_TILE : 2 * HIDDEN_TILE], w_upper_ref[...]
    )

    @pl.when(step == pl.num_programs(0) - 1)
    def _():
        output_ref[...] = sum_ref[...].astype(jnp.bfloat16)
        rinv = rinv_ref[:, :1]
        mid = mid_ref[...]
        d_normed = back_ref[...]
        d_gain_ref[...] = jnp.sum(d_normed * mid * rinv, axis=0, keepdims=True)
        scaled = d_normed * gain_ref[...]
        lean = jnp.mean(scaled * mid, axis=-1, keepdims=True) * (rinv * rinv * rinv)
        d_mid = grad_ref[...].astype(jnp.float32) + rinv * scaled - mid * lean
        d_mid_ref[...] = d_mid
        d_branch = d_mid.astype(jnp.bfloat16)
        d_attn_ref[...] = dot_nt(d_branch, w_out_ref[...]).astype(jnp.bfloat16)
        d_w_out_ref[...] = dot_nn(attn_ref[...].T, d_branch).astype(jnp.bfloat16)


def outer_layer(attn, resid, grad, w_out, gain, acts, w_in, w_down):
    length, width = attn.shape
    hidden = w_down.shape[0]
    steps = hidden // HIDDEN_TILE
    low = jnp.bfloat16
    return pl.pallas_call(
        outer_kernel,
        grid=(steps,),
        out_shape=(
            jax.ShapeDtypeStruct((length, width), low),
            jax.ShapeDtypeStruct((length, width), jnp.float32),
            jax.ShapeDtypeStruct((length, width), low),
            jax.ShapeDtypeStruct((width, width), low),
            jax.ShapeDtypeStruct((1, width), jnp.float32),
        ),
        in_specs=[vmem()] * 5
        + [
            pl.BlockSpec((length, 3 * HIDDEN_TILE), lambda c: (0, c)),
            pl.BlockSpec((width, HIDDEN_TILE), lambda c: (0, c)),
            pl.BlockSpec((width, HIDDEN_TILE), lambda c: (0, steps + c)),
            pl.BlockSpec((HIDDEN_TILE, width), lambda c: (c, 0)),
        ],
        out_specs=(vmem(),) * 5,
        scratch_shapes=[
            pltpu.VMEM((length, width), jnp.float32),
            pltpu.VMEM((length, LANES), jnp.float32),
            pltpu.VMEM((length, width), jnp.float32),
            pltpu.VMEM((length, width), jnp.float32),
        ],
        compiler_params=params(30),
        cost_estimate=pl.CostEstimate(
            flops=6 * length * width * hidden + 6 * length * width * width,
            bytes_accessed=24 * 2**20,
            transcendentals=0,
        ),
        name="outer_layer",
    )(attn, resid, grad, w_out, gain.reshape(1, width), acts, w_in, w_in, w_down)


def finish_wide_kernel(lanes, scale, mine_ref, *refs):
    *piece_refs, d_w_in_ref, d_w_down_ref = refs
    plane, tile = pl.program_id(0), pl.program_id(1)
    half = piece_refs[0].shape[0]
    mine = mine_ref[0]
    for lane, (first, last) in enumerate(lanes):

        @pl.when((tile >= first) & (tile < last))
        def _():
            for piece_ref, side in (
                (piece_refs[2 * lane], mine),
                (piece_refs[2 * lane + 1], 1 - mine),
            ):
                part = pl.ds(pl.multiple_of(side * half, half), half)
                piece = piece_ref[...].astype(jnp.float32) * scale

                @pl.when(plane < 2)
                def _():
                    d_w_in_ref[part, :] = piece

                @pl.when(plane == 2)
                def _():
                    d_w_down_ref[:, part] = piece.T


def finish_wide(mine, lanes, scale):
    half = lanes[0][0].shape[0]
    width = 2 * half
    spans = []
    specs = []
    first = 0
    for own, other in lanes:
        count = own.shape[1] // (3 * HIDDEN_TILE)

        def place(p, c, first=first, count=count):
            return (0, jnp.clip(c - first, 0, count - 1) * 3 + p)

        specs += [pl.BlockSpec((half, HIDDEN_TILE), place)] * 2
        spans.append((first, first + count))
        first += count
    hidden = first * HIDDEN_TILE
    return pl.pallas_call(
        functools.partial(finish_wide_kernel, tuple(spans), scale),
        grid=(3, first),
        out_shape=(
            jax.ShapeDtypeStruct((width, 2 * hidden), jnp.float32),
            jax.ShapeDtypeStruct((hidden, width), jnp.float32),
        ),
        in_specs=[smem()] + specs,
        out_specs=(
            pl.BlockSpec(
                (width, HIDDEN_TILE), lambda p, c: (0, jnp.where(p < 2, p * first + c, 2 * first - 1))
            ),
            pl.BlockSpec((HIDDEN_TILE, width), lambda p, c: (jnp.where(p < 2, 0, c), 0)),
        ),
        compiler_params=params(16),
        cost_estimate=pl.CostEstimate(
            flops=6 * width * hidden, bytes_accessed=18 * width * hidden, transcendentals=0
        ),
        name="finish_wide",
    )(mine, *[piece for lane in lanes for piece in lane])


def finish_kernel(scale, spots, mine_ref, own_ref, other_ref, *refs):
    *out_refs, joined_ref = refs
    half = own_ref.shape[0]
    mine = mine_ref[0]
    for piece_ref, side in ((own_ref, mine), (other_ref, 1 - mine)):
        part = pl.ds(pl.multiple_of(side * half, half), half)
        joined_ref[part, :] = piece_ref[...].astype(jnp.float32) * scale
    for ref, (row, column) in zip(out_refs, spots):
        rows, columns = ref.shape
        ref[...] = joined_ref[row : row + rows, column : column + columns]


def finish(mine, own, other, scale, shapes, spots):
    half, columns = own.shape
    return pl.pallas_call(
        functools.partial(finish_kernel, scale, spots),
        out_shape=[jax.ShapeDtypeStruct(shape, jnp.float32) for shape in shapes],
        in_specs=[smem(), vmem(), vmem()],
        out_specs=[vmem()] * len(shapes),
        scratch_shapes=[pltpu.VMEM((2 * half, columns), jnp.float32)],
        compiler_params=params(16),
        cost_estimate=pl.CostEstimate(
            flops=4 * half * columns, bytes_accessed=12 * half * columns, transcendentals=0
        ),
        name="finish",
    )(mine, own, other)


def to_rows(block, share):
    rows, stretch = block.shape[:2]
    pieces = jnp.repeat(block, share, axis=0) if share > 1 else block
    pieces = lax.all_to_all(pieces, "blk", 0, 0, tiled=True)
    return pieces.reshape((rows * share * stretch,) + block.shape[2:])


def to_blocks(row, share):
    blocks = lax.axis_size("blk")
    place = lax.axis_index("blk")
    stretch = row.shape[0] // blocks

    def piece(owner):
        return lax.dynamic_slice_in_dim(row, owner * stretch, stretch, axis=0)

    pieces = [piece(place)]
    for gap in range(1, blocks):
        devices = range(blocks)
        pieces.append(lax.ppermute(piece(place ^ gap), "blk", [(i, i ^ gap) for i in devices]))
    return pieces


def placed(pieces, share):
    place = lax.axis_index("blk")
    gap = 1
    while gap < len(pieces):
        stays = (place & gap) == 0
        pieces = [jnp.where(stays, pieces[at], pieces[at ^ gap]) for at in range(len(pieces))]
        gap *= 2
    return jnp.stack(pieces[::share])


def own_bit(axis, bit):
    return (lax.axis_index(axis) >> bit) & 1


def swapped(block, axis, bit):
    devices = range(lax.axis_size(axis))
    return lax.ppermute(block, axis, [(i, i ^ (1 << bit)) for i in devices])


def bits_of(axis):
    return lax.axis_size(axis).bit_length() - 1


def group_of(free):
    blk = lax.axis_size("blk")
    devices = range(lax.axis_size("rows") * blk)
    weights = [(blk if axis == "rows" else 1) << bit for axis, bit in free]
    place = sum(own_bit(axis, bit) << at for at, (axis, bit) in enumerate(free))
    groups = []
    for device in devices:
        if all(not device & weight for weight in weights):
            members = [device]
            for weight in weights:
                members += [member + weight for member in members]
            groups.append(members)

    def send(block, gap):
        shift = sum(weight for at, weight in enumerate(weights) if gap >> at & 1)
        return lax.ppermute(block, ("rows", "blk"), [(i, i ^ shift) for i in devices])

    def exchange(pieces):
        return lax.all_to_all(
            pieces, ("rows", "blk"), 0, 0, axis_index_groups=groups, tiled=True
        )

    return 1 << len(free), place, send, exchange


class Travel:
    def __init__(self, kept, sent, at_once=False):
        self.at_once = at_once
        near = [("blk", bit) for bit in range(1, bits_of("blk"))] + [("rows", 0)]
        far = [("rows", bit) for bit in range(1, bits_of("rows"))]
        stages = (group_of(near), group_of(far))
        terms = [kept, swapped(sent, "blk", 0)]
        self.state = [terms]
        self.orders = [stages]
        self.at = 0

    def go(self):
        self.state = [self.lane_step(*lane) for lane in zip(self.state, self.orders)]
        self.at += 1

    def lane_step(self, terms, order):
        block = total(terms)
        if self.at == 4:
            return [block, swapped(block, "blk", 0)]
        count, place, send, exchange = order[self.at if self.at < 2 else 3 - self.at]
        if self.at < 2:
            rows = block.shape[0] // count
            if self.at_once:
                pieces = exchange(block)
                return [pieces[at * rows : (at + 1) * rows] for at in range(count)]

            def piece(owner):
                return lax.dynamic_slice_in_dim(block, owner * rows, rows, axis=0)

            return [piece(place)] + [send(piece(place ^ gap), gap) for gap in range(1, count)]
        if self.at_once:
            return [exchange(jnp.concatenate([block] * count, axis=0))]
        pieces = [block] + [send(block, gap) for gap in range(1, count)]
        gap = 1
        while gap < count:
            stays = (place & gap) == 0
            pieces = [jnp.where(stays, pieces[at], pieces[at ^ gap]) for at in range(count)]
            gap *= 2
        return [jnp.concatenate(pieces, axis=0)]


def total(terms):
    first, *others = terms
    if not others:
        return first
    wide = first.astype(jnp.float32)
    for other in others:
        wide = wide + other.astype(jnp.float32)
    return wide.astype(first.dtype)


def beside(values, *travels):
    for travel in travels:
        travel.go()
    return settled(values, *travels)


def settled(values, *travels):
    states, values = lax.optimization_barrier(([travel.state for travel in travels], values))
    for travel, state in zip(travels, states):
        travel.state = state
    return values


def on_device(
    byte_vals,
    segment_ids,
    buckets,
    emb_table,
    conv_taps,
    w_proj,
    gain_one,
    w_qkv,
    rel_bias,
    w_out,
    gain_two,
    w_in,
    w_down,
    out_grad,
):
    rows, stretch = byte_vals.shape
    vocab, width = emb_table.shape
    bucket_count, heads = rel_bias.shape
    hidden = w_down.shape[0]
    blocks = lax.axis_size("blk")
    share = blocks // rows
    length = stretch * blocks
    low = jnp.bfloat16

    packed = to_rows(byte_vals + vocab * segment_ids, share)
    letters_own = lax.rem(packed, vocab)
    segments = lax.div(packed, vocab)
    grad_low = to_rows(out_grad, share)

    taps = conv_taps.astype(jnp.float32)
    conv_low, resid, normed_one, qkv = front(
        letters_own, segments, emb_table, taps, w_proj, gain_one, w_qkv
    )
    band_buckets = jnp.concatenate(
        [buckets[BAND_FIRST : BAND_FIRST + BAND - LANES], buckets[BAND_FIRST - LANES : BAND_FIRST]]
    )
    bounds = document_bounds(segments)
    same_q, same_k = document_marks(segments)
    attn, lse, base = attend(
        bounds, qkv, same_q, same_k, band_buckets.reshape(1, BAND), rel_bias.T
    )

    mine = own_bit("blk", 0).astype(jnp.int32).reshape(1)
    scale = 1.0 / share
    kept, sent, acts = hidden_layer(mine, attn, resid, grad_low, w_out, gain_two, w_in, w_down)
    early = Travel(kept, sent, at_once=True)
    output_row, d_mid, d_attn, d_w_out, d_gain_two = outer_layer(
        attn, resid, grad_low, w_out, gain_two, acts, w_in, w_down
    )
    d_attn, output_row = settled((d_attn, output_row), early)
    output = to_blocks(output_row, share)
    *parts, band = attend_back(bounds, qkv, same_q, same_k, base, lse, attn, d_attn)
    parts, output = beside((parts, output), early)
    kept, sent, input_low = back(
        mine,
        letters_own.reshape(1, length),
        segments.reshape(1, length),
        emb_table,
        taps,
        w_proj,
        gain_one.reshape(1, width),
        w_qkv,
        conv_low,
        resid,
        normed_one,
        *parts,
        d_mid,
        d_w_out,
        d_gain_two,
        band_buckets.reshape(1, BAND),
        band,
    )
    kept, sent, input_low, output = beside((kept, sent, input_low, output), early)
    output = placed(output, share)
    rest = Travel(kept, sent)
    input_low = beside(input_low, early, rest)
    input_grad = to_blocks(input_low, share)
    rest.go()
    rest.go()
    early.go()
    input_grad, output = settled((input_grad, output), early, rest)
    early.go()
    rest.go()
    d_w_in, d_w_down = settled(finish_wide(mine, early.state, scale), rest)
    rest.go()
    (
        d_w_qkv,
        d_w_proj,
        d_w_out,
        d_emb_table,
        d_conv_taps,
        d_gain_one,
        d_gain_two,
        d_rel_bias,
    ) = finish(
        mine,
        *rest.state[0],
        scale,
        (
            (width, 3 * width),
            (width, width),
            (width, width),
            (vocab, width),
            (9, width),
            (1, width),
            (1, width),
            (heads, LANES),
        ),
        (
            (0, 0),
            (0, 3 * width),
            (0, 4 * width),
            (0, 5 * width),
            (vocab + SMALL_TAPS, 5 * width),
            (vocab + SMALL_ONE, 5 * width),
            (vocab + SMALL_TWO, 5 * width),
            (vocab + SMALL_BIAS, 5 * width),
        ),
    )
    input_grad = placed(input_grad, share).astype(jnp.float32)
    d_gain_one = d_gain_one.reshape(width)
    d_gain_two = d_gain_two.reshape(width)
    d_rel_bias = d_rel_bias[:, :bucket_count].T
    return (
        output,
        input_grad,
        d_emb_table,
        d_conv_taps,
        d_w_proj,
        d_gain_one,
        d_w_qkv,
        d_rel_bias,
        d_w_out,
        d_gain_two,
        d_w_in,
        d_w_down,
    )


def solution(mesh):
    split = P("rows", "blk")
    split_wide = P("rows", "blk", None)
    return jax.shard_map(
        on_device,
        mesh=mesh,
        in_specs=(split, split) + (P(),) * 11 + (split_wide,),
        out_specs=(split_wide, split_wide) + (P(),) * 10,
        check_vma=False,
    )
```

```python
import functools

import jax
import jax.numpy as jnp
from jax import lax
from jax.experimental import pallas as pl
from jax.experimental.pallas import tpu as pltpu
from jax.sharding import PartitionSpec as P

EPSILON = 1e-06
SCORE_SCALE = 0.125
WINDOWS = ((0, 2), (2, 3), (5, 4))
HIGHEST_PRECISION = lax.Precision.HIGHEST
LANES = 128
QUERY_TILE = 256
KEY_TILE = 128
MASKED = -(2.0**30)
BAND = 12 * LANES
BAND_FIRST = 3 * LANES
MIB = 2**20


def vmem():
    return pl.BlockSpec(memory_space=pltpu.VMEM)


def smem():
    return pl.BlockSpec(memory_space=pltpu.SMEM)


def params(mib):
    return pltpu.CompilerParams(vmem_limit_bytes=mib * MIB)


def dot_nt(left, right):
    return lax.dot_general(
        left, right, (((1,), (1,)), ((), ())), preferred_element_type=jnp.float32
    )


def dot_nn(left, right):
    return jnp.dot(left, right, preferred_element_type=jnp.float32)


def fill_tables(table_ref, base_ref):
    for head in range(base_ref.shape[0]):
        line = jnp.broadcast_to(base_ref[head : head + 1, :], (KEY_TILE, BAND))
        table_ref[head] = pltpu.roll(line, 0, 1, stride=1, stride_axis=0)


def table_lanes(query_block, key_block):
    place = (query_block * (QUERY_TILE // LANES) - key_block + 5) * LANES
    return pl.ds(pl.multiple_of(place, LANES), QUERY_TILE)


def attend_kernel(
    heads, bounds_ref, qkv_ref, same_q_ref, same_k_ref, buckets_ref, bias_ref,
    attn_ref, lse_ref, base_ref,
    table_ref,
    value_t_ref, query_ref, top_ref, total_ref, mixed_ref, score_ref, expo_ref, fade_ref,
):
    length = qkv_ref.shape[0]
    width = qkv_ref.shape[1] // 3
    head_dim = width // heads
    lane = lax.broadcasted_iota(jnp.int32, (1, LANES), 1)
    halves = (
        (lane < head_dim).astype(jnp.bfloat16),
        (lane >= head_dim).astype(jnp.bfloat16),
    )
    bias = bias_ref[...]
    base = jnp.zeros((heads, BAND), jnp.float32)
    for bucket in range(bias.shape[1]):
        base = jnp.where(buckets_ref[...] == bucket, bias[:, bucket : bucket + 1], base)
    base_ref[...] = base
    fill_tables(table_ref, base_ref)
    value_t_ref[...] = qkv_ref[:, 2 * width :].T

    def block(i, carry):
        rows = pl.ds(pl.multiple_of(i * QUERY_TILE, QUERY_TILE), QUERY_TILE)
        for pair in range(heads // 2):
            query = qkv_ref[rows, pair * LANES : (pair + 1) * LANES] * jnp.bfloat16(SCORE_SCALE)
            for side in range(2):
                query_ref[2 * pair + side, :LANES, :] = (query * halves[side]).T
                query_ref[2 * pair + side, LANES:, :] = same_q_ref[:, rows]
        top_ref[...] = jnp.full_like(top_ref, -3.0e38)
        total_ref[...] = jnp.zeros_like(total_ref)
        mixed_ref[...] = jnp.zeros_like(mixed_ref)

        def step(j, inner):
            keys = pl.ds(pl.multiple_of(j * KEY_TILE, KEY_TILE), KEY_TILE)
            lanes = table_lanes(i, j)
            for head in range(heads):
                pair = head // 2
                key = jnp.concatenate(
                    [
                        qkv_ref[keys, width + pair * LANES : width + (pair + 1) * LANES],
                        same_k_ref[keys, :],
                    ],
                    axis=1,
                )
                score_ref[head] = dot_nn(key, query_ref[head]) + table_ref[head, :, lanes]
            for head in range(heads):
                scores = score_ref[head]
                old = top_ref[head : head + 1, :]
                top = jnp.maximum(old, jnp.max(scores, axis=0, keepdims=True))
                fade = jnp.exp(old - top)
                expo = jnp.exp(scores - top)
                top_ref[head : head + 1, :] = top
                total_ref[head : head + 1, :] = total_ref[head : head + 1, :] * fade + jnp.sum(
                    expo, axis=0, keepdims=True
                )
                fade_ref[head : head + 1, :] = fade
                expo_ref[head] = expo.astype(jnp.bfloat16)
            for head in range(heads):
                own = slice(head * head_dim, (head + 1) * head_dim)
                mixed_ref[own, :] = mixed_ref[own, :] * fade_ref[head : head + 1, :] + dot_nn(
                    value_t_ref[own, keys], expo_ref[head]
                )
            return inner

        lax.fori_loop(bounds_ref[0, i], bounds_ref[1, i], step, 0)
        for head in range(heads):
            own = slice(head * head_dim, (head + 1) * head_dim)
            mixed_ref[own, :] = mixed_ref[own, :] / total_ref[head : head + 1, :]
        attn_ref[rows, :] = mixed_ref[...].T.astype(jnp.bfloat16)
        lse_ref[:, rows] = top_ref[...] + jnp.log(total_ref[...])
        return carry

    lax.fori_loop(0, length // QUERY_TILE, block, 0)


def attend(bounds, qkv, same_q, same_k, band_buckets, bias):
    length = qkv.shape[0]
    width = qkv.shape[1] // 3
    heads = bias.shape[0]
    return pl.pallas_call(
        functools.partial(attend_kernel, heads),
        out_shape=(
            jax.ShapeDtypeStruct((length, width), jnp.bfloat16),
            jax.ShapeDtypeStruct((heads, length), jnp.float32),
            jax.ShapeDtypeStruct((heads, BAND), jnp.float32),
        ),
        in_specs=[smem()] + [vmem()] * 5,
        out_specs=(vmem(), vmem(), vmem()),
        scratch_shapes=[
            pltpu.VMEM((heads, KEY_TILE, BAND), jnp.float32),
            pltpu.VMEM((width, length), jnp.bfloat16),
            pltpu.VMEM((heads, 2 * LANES, QUERY_TILE), jnp.bfloat16),
            pltpu.VMEM((heads, QUERY_TILE), jnp.float32),
            pltpu.VMEM((heads, QUERY_TILE), jnp.float32),
            pltpu.VMEM((width, QUERY_TILE), jnp.float32),
            pltpu.VMEM((heads, KEY_TILE, QUERY_TILE), jnp.float32),
            pltpu.VMEM((heads, KEY_TILE, QUERY_TILE), jnp.bfloat16),
            pltpu.VMEM((heads, QUERY_TILE), jnp.float32),
        ],
        compiler_params=params(14),
        cost_estimate=pl.CostEstimate(
            flops=4 * length * length * width,
            bytes_accessed=12 * 2**20,
            transcendentals=length * length * heads,
        ),
        name="attend",
    )(bounds, qkv, same_q, same_k, band_buckets, bias)


def attend_back_kernel(
    bounds_ref, q_ref, k_ref, v_ref, same_q_ref, same_k_ref, base_ref, lse_ref,
    attn_ref, grad_ref,
    query_out_ref, key_out_ref, value_out_ref, band_ref,
    table_ref, key_t_ref, query_ref, grads_ref, query_t_ref, grads_t_ref, inner_ref,
    query_back_ref, key_back_ref, value_back_ref, skewed_ref,
    exact_ref, probs_ref, d_scores_ref,
):
    length, width = q_ref.shape
    heads = base_ref.shape[0]
    head_dim = width // heads
    lane = lax.broadcasted_iota(jnp.int32, (1, LANES), 1)
    halves = (
        (lane < head_dim).astype(jnp.bfloat16),
        (lane >= head_dim).astype(jnp.bfloat16),
    )
    owner = lax.broadcasted_iota(jnp.int32, (heads, width), 1) // head_dim
    own_head = (owner == lax.broadcasted_iota(jnp.int32, (heads, width), 0)).astype(jnp.bfloat16)
    fill_tables(table_ref, base_ref)
    key_t_ref[...] = k_ref[...].T
    key_back_ref[...] = jnp.zeros_like(key_back_ref)
    value_back_ref[...] = jnp.zeros_like(value_back_ref)
    skewed_ref[...] = jnp.zeros_like(skewed_ref)

    def block(i, carry):
        rows = pl.ds(pl.multiple_of(i * QUERY_TILE, QUERY_TILE), QUERY_TILE)
        for pair in range(heads // 2):
            own = slice(pair * LANES, (pair + 1) * LANES)
            query = q_ref[rows, own] * jnp.bfloat16(SCORE_SCALE)
            grad = grad_ref[rows, own]
            for side in range(2):
                part = slice(side * QUERY_TILE, (side + 1) * QUERY_TILE)
                query_ref[pair, part, :] = query * halves[side]
                grads_ref[pair, part, :] = grad * halves[side]
                query_t_ref[2 * pair + side, :LANES, :] = (query * halves[side]).T
                query_t_ref[2 * pair + side, LANES:, :] = same_q_ref[:, rows]
                grads_t_ref[2 * pair + side] = (grad * halves[side]).T
        product = grad_ref[rows, :].astype(jnp.float32) * attn_ref[rows, :].astype(jnp.float32)
        rough = product.astype(jnp.bfloat16)
        rest = (product - rough.astype(jnp.float32)).astype(jnp.bfloat16)
        inner_ref[...] = dot_nt(own_head, rough) + dot_nt(own_head, rest)
        query_back_ref[...] = jnp.zeros_like(query_back_ref)

        def step(j, inner):
            keys = pl.ds(pl.multiple_of(j * KEY_TILE, KEY_TILE), KEY_TILE)
            lanes = table_lanes(i, j)
            for head in range(heads):
                pair = head // 2
                key = jnp.concatenate(
                    [k_ref[keys, pair * LANES : (pair + 1) * LANES], same_k_ref[keys, :]], axis=1
                )
                scores = dot_nn(key, query_t_ref[head]) + table_ref[head, :, lanes]
                exact_ref[head] = jnp.exp(scores - lse_ref[head : head + 1, rows])
            for head in range(heads):
                pair = head // 2
                part = slice((head % 2) * QUERY_TILE, (head % 2 + 1) * QUERY_TILE)
                d_probs = dot_nn(v_ref[keys, pair * LANES : (pair + 1) * LANES], grads_t_ref[head])
                exact = exact_ref[head]
                d_score = exact * (d_probs - inner_ref[head : head + 1, :])
                skewed_ref[head, :, lanes] = skewed_ref[head, :, lanes] + d_score
                probs_ref[pair, :, part] = exact.astype(jnp.bfloat16)
                d_scores_ref[pair, :, part] = d_score.astype(jnp.bfloat16)
            for pair in range(heads // 2):
                own = slice(pair * LANES, (pair + 1) * LANES)
                value_back_ref[keys, own] += dot_nn(probs_ref[pair], grads_ref[pair])
                key_back_ref[keys, own] += dot_nn(d_scores_ref[pair], query_ref[pair])
            for head in range(heads):
                part = slice((head % 2) * QUERY_TILE, (head % 2 + 1) * QUERY_TILE)
                mine = slice(head * head_dim, (head + 1) * head_dim)
                query_back_ref[mine, :] += dot_nn(
                    key_t_ref[mine, keys], d_scores_ref[head // 2, :, part]
                )
            return inner

        lax.fori_loop(bounds_ref[0, i], bounds_ref[1, i], step, 0)
        query_out_ref[rows, :] = (query_back_ref[...].T * SCORE_SCALE).astype(jnp.bfloat16)
        return carry

    lax.fori_loop(0, length // QUERY_TILE, block, 0)
    key_out_ref[...] = key_back_ref[...].astype(jnp.bfloat16)
    value_out_ref[...] = value_back_ref[...].astype(jnp.bfloat16)
    for head in range(heads):
        height = KEY_TILE
        while height > 8:
            height //= 2
            skewed_ref[head, :height, :] = skewed_ref[head, :height, :] + pltpu.roll(
                skewed_ref[head, height : 2 * height, :], BAND - height, 1
            )
        total = skewed_ref[head, 0:1, :]
        for row in range(1, 8):
            total = total + pltpu.roll(skewed_ref[head, row : row + 1, :], BAND - row, 1)
        band_ref[head : head + 1, :] = total


def attend_back(bounds, qkv, same_q, same_k, base, lse, attn, grad):
    length = qkv.shape[0]
    width = qkv.shape[1] // 3
    heads = base.shape[0]

    def columns(group):
        return pl.BlockSpec(
            (length, width), lambda _: (0, group), pipeline_mode=pl.Buffered(1)
        )

    return pl.pallas_call(
        attend_back_kernel,
        out_shape=[jax.ShapeDtypeStruct((length, width), jnp.bfloat16)] * 3
        + [jax.ShapeDtypeStruct((heads, BAND), jnp.float32)],
        grid=(1,),
        in_specs=[smem(), columns(0), columns(1), columns(2)] + [vmem()] * 6,
        out_specs=[vmem()] * 4,
        scratch_shapes=[
            pltpu.VMEM((heads, KEY_TILE, BAND), jnp.float32),
            pltpu.VMEM((width, length), jnp.bfloat16),
            pltpu.VMEM((heads // 2, 2 * QUERY_TILE, LANES), jnp.bfloat16),
            pltpu.VMEM((heads // 2, 2 * QUERY_TILE, LANES), jnp.bfloat16),
            pltpu.VMEM((heads, 2 * LANES, QUERY_TILE), jnp.bfloat16),
            pltpu.VMEM((heads, LANES, QUERY_TILE), jnp.bfloat16),
            pltpu.VMEM((heads, QUERY_TILE), jnp.float32),
            pltpu.VMEM((width, QUERY_TILE), jnp.float32),
            pltpu.VMEM((length, width), jnp.float32),
            pltpu.VMEM((length, width), jnp.float32),
            pltpu.VMEM((heads, KEY_TILE, BAND), jnp.float32),
            pltpu.VMEM((heads, KEY_TILE, QUERY_TILE), jnp.float32),
            pltpu.VMEM((heads // 2, KEY_TILE, 2 * QUERY_TILE), jnp.bfloat16),
            pltpu.VMEM((heads // 2, KEY_TILE, 2 * QUERY_TILE), jnp.bfloat16),
        ],
        compiler_params=params(34),
        cost_estimate=pl.CostEstimate(
            flops=40 * length * length * width,
            bytes_accessed=8 * 2**20,
            transcendentals=length * length * heads,
        ),
        name="attend_back",
    )(bounds, qkv, qkv, qkv, same_q, same_k, base, lse, attn, grad)


def document_bounds(segments):
    length = segments.shape[0]
    starts = segments[::QUERY_TILE]
    ends = segments[QUERY_TILE - 1 :: QUERY_TILE]
    before = jnp.sum((segments[None, :] < starts[:, None]).astype(jnp.int32), axis=1)
    upto = jnp.sum((segments[None, :] <= ends[:, None]).astype(jnp.int32), axis=1)
    return jnp.stack([before // KEY_TILE, (upto + KEY_TILE - 1) // KEY_TILE])


def document_marks(segments):
    own = segments[:, None] == jnp.arange(LANES, dtype=jnp.int32)[None, :]
    own_t = segments[None, :] == jnp.arange(LANES, dtype=jnp.int32)[:, None]
    return own_t.astype(jnp.bfloat16), jnp.where(own, 0.0, MASKED).astype(jnp.bfloat16)
HIDDEN_TILE = 512
GELU_SLOPE = 0.7978845608028654
GELU_CUBIC = 0.044715


def gelu_value(values):
    square = values * values
    bend = jnp.tanh(values * (GELU_SLOPE + GELU_SLOPE * GELU_CUBIC * square))
    return values * (0.5 + 0.5 * bend)


def gelu_parts(values):
    square = values * values
    bend = jnp.tanh(values * (GELU_SLOPE + GELU_SLOPE * GELU_CUBIC * square))
    half = 0.5 + 0.5 * bend
    slope = half + values * (1.0 - bend * bend) * (
        0.5 * GELU_SLOPE + 1.5 * GELU_SLOPE * GELU_CUBIC * square
    )
    return values * half, slope


FRONT_TILE = 128
BUCKET_LIMIT = 32
HALO = 8


def byte_marks(letters_ref, vocab):
    letters = lax.broadcasted_iota(jnp.int32, (vocab, letters_ref.shape[1]), 0)
    return (letters == letters_ref[...]).astype(jnp.float32).astype(jnp.bfloat16)


def embed(hot, emb_ref, embedded_ref):
    embedded_ref[:HALO, :] = jnp.zeros((HALO, emb_ref.shape[1]), jnp.float32)
    embedded_ref[HALO:, :] = lax.dot_general(
        hot, emb_ref[...], (((0,), (0,)), ((), ())), preferred_element_type=jnp.float32
    )


def lag_keeps(segments_ref):
    segments = segments_ref[...]
    place = lax.broadcasted_iota(jnp.int32, segments.shape, 1)
    rows = [jnp.ones(segments.shape, jnp.float32)]
    for lag in range(1, HALO):
        same = (pltpu.roll(segments, lag, 1) == segments) & (place >= lag)
        rows.append(same.astype(jnp.float32))
    return jnp.concatenate(rows, axis=0).T


def window_sums(embedded_ref, keeps, taps_ref, at):
    part = slice(at, at + FRONT_TILE)
    shifted = []
    for lag in range(4):
        moved = embedded_ref[HALO + at - lag : HALO + at - lag + FRONT_TILE, :]
        shifted.append(moved if lag == 0 else moved * keeps[part, lag : lag + 1])
    sums = []
    for first, span in WINDOWS:
        summed = shifted[0] * taps_ref[first : first + 1, :]
        for lag in range(1, span):
            summed = summed + shifted[lag] * taps_ref[first + lag : first + lag + 1, :]
        sums.append(summed)
    return shifted, sums


def front_kernel(
    letters_ref, segments_ref, emb_ref, taps_ref, w_proj_ref, gain_ref, w_qkv_ref,
    conv_ref, resid_ref, normed_ref, qkv_ref,
    embedded_ref,
):
    length, width = resid_ref.shape
    vocab = emb_ref.shape[0]
    hot = byte_marks(letters_ref, vocab)
    embed(hot, emb_ref, embedded_ref)
    keeps = lag_keeps(segments_ref)
    for at in range(0, length, FRONT_TILE):
        shifted, sums = window_sums(embedded_ref, keeps, taps_ref, at)
        conv_ref[at : at + FRONT_TILE, :] = sum(gelu_value(summed) for summed in sums).astype(
            jnp.bfloat16
        )
    resid = dot_nn(conv_ref[...], w_proj_ref[...])
    resid_ref[...] = resid
    rinv = lax.rsqrt(jnp.mean(resid * resid, axis=-1, keepdims=True) + EPSILON)
    normed_ref[...] = (resid * rinv * gain_ref[...]).astype(jnp.bfloat16)
    qkv_ref[...] = dot_nn(normed_ref[...], w_qkv_ref[...]).astype(jnp.bfloat16)


def front(letters, segments, emb_table, taps, w_proj, gain, w_qkv):
    length = letters.shape[0]
    vocab, width = emb_table.shape
    low = jnp.bfloat16
    return pl.pallas_call(
        front_kernel,
        out_shape=(
            jax.ShapeDtypeStruct((length, width), low),
            jax.ShapeDtypeStruct((length, width), jnp.float32),
            jax.ShapeDtypeStruct((length, width), low),
            jax.ShapeDtypeStruct((length, 3 * width), low),
        ),
        in_specs=[vmem()] * 7,
        out_specs=(vmem(),) * 4,
        scratch_shapes=[pltpu.VMEM((length + HALO, width), jnp.float32)],
        compiler_params=params(10),
        cost_estimate=pl.CostEstimate(
            flops=2 * length * width * (4 * width + vocab) + 60 * length * width,
            bytes_accessed=12 * 2**20,
            transcendentals=3 * length * width,
        ),
        name="front",
    )(
        letters.reshape(1, length),
        segments.reshape(1, length),
        emb_table,
        taps,
        w_proj,
        gain.reshape(1, width),
        w_qkv,
    )


SMALL_TAPS, SMALL_ONE, SMALL_TWO, SMALL_BIAS = 0, 9, 10, 16


def back_kernel(
    mine_ref, letters_ref, segments_ref, emb_ref, taps_ref, w_proj_ref, gain_ref, w_qkv_ref,
    conv_ref, resid_ref, normed_ref, d_query_ref, d_key_ref, d_value_ref, d_mid_ref,
    d_w_out_ref, d_gain_two_ref, buckets_ref, band_ref,
    kept_ref, sent_ref, input_ref,
    all_ref, small_ref, embedded_ref, d_normed_ref, d_resid_ref, d_lag_ref,
):
    length, width = resid_ref.shape
    vocab = emb_ref.shape[0]
    heads = band_ref.shape[0]
    low = jnp.bfloat16
    d_parts = (d_query_ref, d_key_ref, d_value_ref)
    d_normed_ref[...] = sum(
        dot_nt(part_ref[...], w_qkv_ref[:, at * width : (at + 1) * width])
        for at, part_ref in enumerate(d_parts)
    )
    resid = resid_ref[...]
    d_normed = d_normed_ref[...]
    rinv = lax.rsqrt(jnp.mean(resid * resid, axis=-1, keepdims=True) + EPSILON)
    small_ref[...] = jnp.zeros_like(small_ref)
    small_ref[SMALL_ONE : SMALL_ONE + 1, :] = jnp.sum(
        d_normed * resid * rinv, axis=0, keepdims=True
    )
    small_ref[SMALL_TWO : SMALL_TWO + 1, :] = d_gain_two_ref[...]
    scaled = d_normed * gain_ref[...]
    lean = jnp.mean(scaled * resid, axis=-1, keepdims=True) * (rinv * rinv * rinv)
    d_resid_ref[...] = (d_mid_ref[...] + rinv * scaled - resid * lean).astype(low)
    normed_t = normed_ref[...].T
    for at, part_ref in enumerate(d_parts):
        all_ref[:, at * width : (at + 1) * width] = dot_nn(normed_t, part_ref[...]).astype(low)
    all_ref[:, 3 * width : 4 * width] = dot_nn(conv_ref[...].T, d_resid_ref[...]).astype(low)
    all_ref[:, 4 * width : 5 * width] = d_w_out_ref[...]
    d_normed_ref[...] = dot_nt(d_resid_ref[...], w_proj_ref[...])

    hot = byte_marks(letters_ref, vocab)
    embed(hot, emb_ref, embedded_ref)
    keeps = lag_keeps(segments_ref)
    tap_rows = [jnp.zeros((8, width), jnp.float32)] * 9
    d_lag_ref[:, length:, :] = jnp.zeros((4, HALO, width), jnp.float32)
    for at in range(0, length, FRONT_TILE):
        part = slice(at, at + FRONT_TILE)
        shifted, sums = window_sums(embedded_ref, keeps, taps_ref, at)
        d_conv = d_normed_ref[part, :]
        d_shifted = [0.0] * 4
        for (first, span), summed in zip(WINDOWS, sums):
            d_pre = d_conv * gelu_parts(summed)[1]
            for lag in range(span):
                tap = first + lag
                pieces = (d_pre * shifted[lag]).reshape(FRONT_TILE // 8, 8, width)
                tap_rows[tap] = tap_rows[tap] + jnp.sum(pieces, axis=0)
                d_shifted[lag] = d_shifted[lag] + d_pre * taps_ref[tap : tap + 1, :]
        for lag in range(4):
            kept = d_shifted[lag]
            d_lag_ref[lag, part, :] = kept if lag == 0 else kept * keeps[part, lag : lag + 1]
    for tap in range(9):
        small_ref[SMALL_TAPS + tap : SMALL_TAPS + tap + 1, :] = jnp.sum(
            tap_rows[tap], axis=0, keepdims=True
        )
    for at in range(0, length, FRONT_TILE):
        total = d_lag_ref[0, at : at + FRONT_TILE, :]
        for lag in range(1, 4):
            total = total + d_lag_ref[lag, at + lag : at + lag + FRONT_TILE, :]
        input_ref[at : at + FRONT_TILE, :] = total.astype(low)
    lane = lax.broadcasted_iota(jnp.int32, (heads, width), 1)
    bias = jnp.zeros((heads, width), jnp.float32)
    for bucket in range(BUCKET_LIMIT):
        picked = jnp.where(buckets_ref[...] == bucket, band_ref[...], 0.0)
        bias = jnp.where(lane == bucket, jnp.sum(picked, axis=1, keepdims=True), bias)
    small_ref[SMALL_BIAS : SMALL_BIAS + heads, :] = bias
    all_ref[:vocab, 5 * width :] = dot_nn(hot, input_ref[...]).astype(low)
    all_ref[vocab:, 5 * width :] = jnp.zeros((width - vocab, width), low)
    all_ref[vocab : vocab + 32, 5 * width :] = small_ref[...].astype(low)
    half = width // 2
    mine = mine_ref[0]
    kept_ref[...] = all_ref[pl.ds(pl.multiple_of(mine * half, half), half), :]
    sent_ref[...] = all_ref[pl.ds(pl.multiple_of((1 - mine) * half, half), half), :]


def back(*args):
    length, width = args[9].shape
    low = jnp.bfloat16
    half = jax.ShapeDtypeStruct((width // 2, 6 * width), low)
    return pl.pallas_call(
        back_kernel,
        out_shape=(half, half, jax.ShapeDtypeStruct((length, width), low)),
        in_specs=[smem()] + [vmem()] * 18,
        out_specs=(vmem(),) * 3,
        scratch_shapes=[
            pltpu.VMEM((width, 6 * width), low),
            pltpu.VMEM((32, width), jnp.float32),
            pltpu.VMEM((length + HALO, width), jnp.float32),
            pltpu.VMEM((length, width), jnp.float32),
            pltpu.VMEM((length, width), low),
            pltpu.VMEM((4, length + HALO, width), jnp.float32),
        ],
        compiler_params=params(36),
        cost_estimate=pl.CostEstimate(
            flops=22 * length * width * width,
            bytes_accessed=20 * 2**20,
            transcendentals=3 * length * width,
        ),
        name="back",
    )(*args)


def middle_and_norm(attn_ref, resid_ref, w_out_ref):
    mid = resid_ref[...] + dot_nn(attn_ref[...], w_out_ref[...])
    return mid, lax.rsqrt(jnp.mean(mid * mid, axis=-1, keepdims=True) + EPSILON)


def hidden_kernel(
    attn_ref, resid_ref, grad_ref, w_out_ref, gain_ref, w_gate_ref, w_upper_ref, w_down_ref,
    weight_back_ref, acts_ref,
    normed_ref, normed_t_ref, grad_t_ref, gate_ref, upper_ref, d_inner_ref,
):
    @pl.when(pl.program_id(0) == 0)
    def _():
        mid, rinv = middle_and_norm(attn_ref, resid_ref, w_out_ref)
        normed = (mid * rinv * gain_ref[...]).astype(jnp.bfloat16)
        normed_ref[...] = normed
        normed_t_ref[...] = normed.T
        grad_t_ref[...] = grad_ref[...].T

    gate_ref[...] = dot_nn(normed_ref[...], w_gate_ref[...])
    upper_ref[...] = dot_nn(normed_ref[...], w_upper_ref[...])
    d_inner_ref[...] = dot_nt(grad_ref[...], w_down_ref[...])
    upper = upper_ref[...]
    d_inner = d_inner_ref[...]
    bent, slope = gelu_parts(gate_ref[...])
    low = jnp.bfloat16
    inner_at, gate_at, upper_at = (
        slice(plane * HIDDEN_TILE, (plane + 1) * HIDDEN_TILE) for plane in (2, 0, 1)
    )
    acts_ref[:, inner_at] = (bent * upper).astype(low)
    acts_ref[:, gate_at] = (d_inner * upper * slope).astype(low)
    acts_ref[:, upper_at] = (d_inner * bent).astype(low)
    for left_ref, at in ((normed_t_ref, gate_at), (normed_t_ref, upper_at), (grad_t_ref, inner_at)):
        weight_back_ref[:, at] = dot_nn(left_ref[...], acts_ref[:, at]).astype(low)


def hidden_layer(attn, resid, grad, w_out, gain, w_in, w_down):
    length, width = attn.shape
    hidden = w_down.shape[0]
    steps = hidden // HIDDEN_TILE
    low = jnp.bfloat16
    return pl.pallas_call(
        hidden_kernel,
        grid=(steps,),
        out_shape=(
            jax.ShapeDtypeStruct((width, 3 * hidden), low),
            jax.ShapeDtypeStruct((length, 3 * hidden), low),
        ),
        in_specs=[vmem()] * 5
        + [
            pl.BlockSpec((width, HIDDEN_TILE), lambda c: (0, c)),
            pl.BlockSpec((width, HIDDEN_TILE), lambda c: (0, steps + c)),
            pl.BlockSpec((HIDDEN_TILE, width), lambda c: (c, 0)),
        ],
        out_specs=(
            pl.BlockSpec((width, 3 * HIDDEN_TILE), lambda c: (0, c)),
            pl.BlockSpec((length, 3 * HIDDEN_TILE), lambda c: (0, c)),
        ),
        scratch_shapes=[
            pltpu.VMEM((length, width), low),
            pltpu.VMEM((width, length), low),
            pltpu.VMEM((width, length), low),
            pltpu.VMEM((length, HIDDEN_TILE), jnp.float32),
            pltpu.VMEM((length, HIDDEN_TILE), jnp.float32),
            pltpu.VMEM((length, HIDDEN_TILE), jnp.float32),
        ],
        compiler_params=params(52),
        cost_estimate=pl.CostEstimate(
            flops=12 * length * width * hidden,
            bytes_accessed=32 * 2**20,
            transcendentals=length * hidden,
        ),
        name="hidden_layer",
    )(attn, resid, grad, w_out, gain.reshape(1, width), w_in, w_in, w_down)


def outer_kernel(
    attn_ref, resid_ref, grad_ref, w_out_ref, gain_ref, acts_ref, w_gate_ref, w_upper_ref,
    w_down_ref,
    output_ref, d_mid_ref, d_attn_ref, d_w_out_ref, d_gain_ref,
    mid_ref, rinv_ref, sum_ref, back_ref,
):
    step = pl.program_id(0)

    @pl.when(step == 0)
    def _():
        mid, rinv = middle_and_norm(attn_ref, resid_ref, w_out_ref)
        mid_ref[...] = mid
        rinv_ref[...] = jnp.broadcast_to(rinv, rinv_ref.shape)
        sum_ref[...] = mid
        back_ref[...] = jnp.zeros_like(back_ref)

    sum_ref[...] += dot_nn(acts_ref[:, 2 * HIDDEN_TILE :], w_down_ref[...])
    back_ref[...] += dot_nt(acts_ref[:, :HIDDEN_TILE], w_gate_ref[...]) + dot_nt(
        acts_ref[:, HIDDEN_TILE : 2 * HIDDEN_TILE], w_upper_ref[...]
    )

    @pl.when(step == pl.num_programs(0) - 1)
    def _():
        output_ref[...] = sum_ref[...].astype(jnp.bfloat16)
        rinv = rinv_ref[:, :1]
        mid = mid_ref[...]
        d_normed = back_ref[...]
        d_gain_ref[...] = jnp.sum(d_normed * mid * rinv, axis=0, keepdims=True)
        scaled = d_normed * gain_ref[...]
        lean = jnp.mean(scaled * mid, axis=-1, keepdims=True) * (rinv * rinv * rinv)
        d_mid = grad_ref[...].astype(jnp.float32) + rinv * scaled - mid * lean
        d_mid_ref[...] = d_mid
        d_branch = d_mid.astype(jnp.bfloat16)
        d_attn_ref[...] = dot_nt(d_branch, w_out_ref[...]).astype(jnp.bfloat16)
        d_w_out_ref[...] = dot_nn(attn_ref[...].T, d_branch).astype(jnp.bfloat16)


def outer_layer(attn, resid, grad, w_out, gain, acts, w_in, w_down):
    length, width = attn.shape
    hidden = w_down.shape[0]
    steps = hidden // HIDDEN_TILE
    low = jnp.bfloat16
    return pl.pallas_call(
        outer_kernel,
        grid=(steps,),
        out_shape=(
            jax.ShapeDtypeStruct((length, width), low),
            jax.ShapeDtypeStruct((length, width), jnp.float32),
            jax.ShapeDtypeStruct((length, width), low),
            jax.ShapeDtypeStruct((width, width), low),
            jax.ShapeDtypeStruct((1, width), jnp.float32),
        ),
        in_specs=[vmem()] * 5
        + [
            pl.BlockSpec((length, 3 * HIDDEN_TILE), lambda c: (0, c)),
            pl.BlockSpec((width, HIDDEN_TILE), lambda c: (0, c)),
            pl.BlockSpec((width, HIDDEN_TILE), lambda c: (0, steps + c)),
            pl.BlockSpec((HIDDEN_TILE, width), lambda c: (c, 0)),
        ],
        out_specs=(vmem(),) * 5,
        scratch_shapes=[
            pltpu.VMEM((length, width), jnp.float32),
            pltpu.VMEM((length, LANES), jnp.float32),
            pltpu.VMEM((length, width), jnp.float32),
            pltpu.VMEM((length, width), jnp.float32),
        ],
        compiler_params=params(30),
        cost_estimate=pl.CostEstimate(
            flops=6 * length * width * hidden + 6 * length * width * width,
            bytes_accessed=24 * 2**20,
            transcendentals=0,
        ),
        name="outer_layer",
    )(attn, resid, grad, w_out, gain.reshape(1, width), acts, w_in, w_in, w_down)


FINISH_ROWS = 128


def finish_wide_kernel(scale, total_ref, d_w_in_ref, d_w_down_ref):
    hidden = d_w_down_ref.shape[0]
    for tile in range(hidden // HIDDEN_TILE):
        at = 3 * tile * HIDDEN_TILE
        spot = slice(tile * HIDDEN_TILE, (tile + 1) * HIDDEN_TILE)
        upper = slice(hidden + tile * HIDDEN_TILE, hidden + (tile + 1) * HIDDEN_TILE)
        gate_part, upper_part, down_part = (
            total_ref[:, at + plane * HIDDEN_TILE : at + (plane + 1) * HIDDEN_TILE].astype(
                jnp.float32
            )
            * scale
            for plane in range(3)
        )
        d_w_in_ref[:, spot] = gate_part
        d_w_in_ref[:, upper] = upper_part
        d_w_down_ref[spot, :] = down_part.T


def finish_wide(total, scale):
    width = total.shape[0]
    hidden = total.shape[1] // 3
    return pl.pallas_call(
        functools.partial(finish_wide_kernel, scale),
        grid=(width // FINISH_ROWS,),
        out_shape=(
            jax.ShapeDtypeStruct((width, 2 * hidden), jnp.float32),
            jax.ShapeDtypeStruct((hidden, width), jnp.float32),
        ),
        in_specs=[pl.BlockSpec((FINISH_ROWS, 3 * hidden), lambda c: (c, 0))],
        out_specs=(
            pl.BlockSpec((FINISH_ROWS, 2 * hidden), lambda c: (c, 0)),
            pl.BlockSpec((hidden, FINISH_ROWS), lambda c: (0, c)),
        ),
        compiler_params=params(58),
        cost_estimate=pl.CostEstimate(
            flops=6 * width * hidden, bytes_accessed=18 * width * hidden, transcendentals=0
        ),
        name="finish_wide",
    )(total)


def finish_kernel(scale, spots, mine_ref, own_ref, other_ref, *refs):
    *out_refs, joined_ref = refs
    half = own_ref.shape[0]
    mine = mine_ref[0]
    for piece_ref, side in ((own_ref, mine), (other_ref, 1 - mine)):
        part = pl.ds(pl.multiple_of(side * half, half), half)
        joined_ref[part, :] = piece_ref[...].astype(jnp.float32) * scale
    for ref, (row, column) in zip(out_refs, spots):
        rows, columns = ref.shape
        ref[...] = joined_ref[row : row + rows, column : column + columns]


def finish(mine, own, other, scale, shapes, spots):
    half, columns = own.shape
    return pl.pallas_call(
        functools.partial(finish_kernel, scale, spots),
        out_shape=[jax.ShapeDtypeStruct(shape, jnp.float32) for shape in shapes],
        in_specs=[smem(), vmem(), vmem()],
        out_specs=[vmem()] * len(shapes),
        scratch_shapes=[pltpu.VMEM((2 * half, columns), jnp.float32)],
        compiler_params=params(16),
        cost_estimate=pl.CostEstimate(
            flops=4 * half * columns, bytes_accessed=12 * half * columns, transcendentals=0
        ),
        name="finish",
    )(mine, own, other)


def to_rows(block, share):
    rows, stretch = block.shape[:2]
    pieces = jnp.repeat(block, share, axis=0) if share > 1 else block
    pieces = lax.all_to_all(pieces, "blk", 0, 0, tiled=True)
    return pieces.reshape((rows * share * stretch,) + block.shape[2:])


def to_blocks(row, share):
    blocks = lax.axis_size("blk")
    pieces = row.reshape((blocks, row.shape[0] // blocks) + row.shape[1:])
    return lax.all_to_all(pieces, "blk", 0, 0, tiled=True)[::share]


def own_bit(axis, bit):
    return (lax.axis_index(axis) >> bit) & 1


def swapped(block, axis, bit):
    devices = range(lax.axis_size(axis))
    return lax.ppermute(block, axis, [(i, i ^ (1 << bit)) for i in devices])


def bits_of(axis):
    return lax.axis_size(axis).bit_length() - 1


def group_of(free):
    blk = lax.axis_size("blk")
    devices = range(lax.axis_size("rows") * blk)
    weights = [(blk if axis == "rows" else 1) << bit for axis, bit in free]
    place = sum(own_bit(axis, bit) << at for at, (axis, bit) in enumerate(free))

    def send(block, gap):
        shift = sum(weight for at, weight in enumerate(weights) if gap >> at & 1)
        return lax.ppermute(block, ("rows", "blk"), [(i, i ^ shift) for i in devices])

    return 1 << len(free), place, send


class Travel:
    def __init__(self, kept, sent):
        near = [("blk", bit) for bit in range(1, bits_of("blk"))] + [("rows", 0)]
        far = [("rows", bit) for bit in range(1, bits_of("rows"))]
        stages = (group_of(near), group_of(far))
        terms = [kept, swapped(sent, "blk", 0)]
        self.state = [terms]
        self.orders = [stages]
        self.at = 0

    def go(self):
        self.state = [self.lane_step(*lane) for lane in zip(self.state, self.orders)]
        self.at += 1

    def lane_step(self, terms, order):
        block = total(terms)
        if self.at == 4:
            return [block, swapped(block, "blk", 0)]
        count, place, send = order[self.at if self.at < 2 else 3 - self.at]
        if self.at < 2:
            rows = block.shape[0] // count
            def piece(owner):
                return lax.dynamic_slice_in_dim(block, owner * rows, rows, axis=0)

            return [piece(place)] + [send(piece(place ^ gap), gap) for gap in range(1, count)]
        pieces = [block] + [send(block, gap) for gap in range(1, count)]
        gap = 1
        while gap < count:
            stays = (place & gap) == 0
            pieces = [jnp.where(stays, pieces[at], pieces[at ^ gap]) for at in range(count)]
            gap *= 2
        return [jnp.concatenate(pieces, axis=0)]


def total(terms):
    first, *others = terms
    if not others:
        return first
    wide = first.astype(jnp.float32)
    for other in others:
        wide = wide + other.astype(jnp.float32)
    return wide.astype(first.dtype)


def beside(values, *travels):
    for travel in travels:
        travel.go()
    return settled(values, *travels)


def settled(values, *travels):
    states, values = lax.optimization_barrier(([travel.state for travel in travels], values))
    for travel, state in zip(travels, states):
        travel.state = state
    return values


def on_device(
    byte_vals,
    segment_ids,
    buckets,
    emb_table,
    conv_taps,
    w_proj,
    gain_one,
    w_qkv,
    rel_bias,
    w_out,
    gain_two,
    w_in,
    w_down,
    out_grad,
):
    rows, stretch = byte_vals.shape
    vocab, width = emb_table.shape
    bucket_count, heads = rel_bias.shape
    hidden = w_down.shape[0]
    blocks = lax.axis_size("blk")
    share = blocks // rows
    length = stretch * blocks
    low = jnp.bfloat16

    packed = to_rows(byte_vals + vocab * segment_ids, share)
    letters_own = lax.rem(packed, vocab)
    segments = lax.div(packed, vocab)
    grad_low = to_rows(out_grad, share)

    taps = conv_taps.astype(jnp.float32)
    conv_low, resid, normed_one, qkv = front(
        letters_own, segments, emb_table, taps, w_proj, gain_one, w_qkv
    )
    band_buckets = jnp.concatenate(
        [buckets[BAND_FIRST : BAND_FIRST + BAND - LANES], buckets[BAND_FIRST - LANES : BAND_FIRST]]
    )
    bounds = document_bounds(segments)
    same_q, same_k = document_marks(segments)
    attn, lse, base = attend(
        bounds, qkv, same_q, same_k, band_buckets.reshape(1, BAND), rel_bias.T
    )

    mine = own_bit("blk", 0).astype(jnp.int32).reshape(1)
    scale = 1.0 / share
    d_wide, acts = hidden_layer(attn, resid, grad_low, w_out, gain_two, w_in, w_down)

    def remainder():
        output_row, d_mid, d_attn, d_w_out, d_gain_two = outer_layer(
            attn, resid, grad_low, w_out, gain_two, acts, w_in, w_down
        )
        *parts, band = attend_back(bounds, qkv, same_q, same_k, base, lse, attn, d_attn)
        kept, sent, input_low = back(
            mine,
            letters_own.reshape(1, length),
            segments.reshape(1, length),
            emb_table,
            taps,
            w_proj,
            gain_one.reshape(1, width),
            w_qkv,
            conv_low,
            resid,
            normed_one,
            *parts,
            d_mid,
            d_w_out,
            d_gain_two,
            band_buckets.reshape(1, BAND),
            band,
        )
        rest = Travel(kept, sent)
        rest.go()
        output = beside(to_blocks(output_row, share), rest)
        input_grad = beside(to_blocks(input_low, share), rest)
        rest.go()
        rest.go()
        finished = finish(
            mine,
            *rest.state[0],
            scale,
            (
                (width, 3 * width),
                (width, width),
                (width, width),
                (vocab, width),
                (9, width),
                (1, width),
                (1, width),
                (heads, LANES),
            ),
            (
                (0, 0),
                (0, 3 * width),
                (0, 4 * width),
                (0, 5 * width),
                (vocab + SMALL_TAPS, 5 * width),
                (vocab + SMALL_ONE, 5 * width),
                (vocab + SMALL_TWO, 5 * width),
                (vocab + SMALL_BIAS, 5 * width),
            ),
        )
        input_grad = input_grad.astype(jnp.float32)
        return output, input_grad, finished

    def nothing():
        return jax.tree.map(lambda leaf: jnp.zeros(leaf.shape, leaf.dtype), shapes)

    shapes = jax.eval_shape(remainder)
    d_wide = lax.psum(d_wide, ("rows", "blk"))
    output, input_grad, finished = lax.cond(segments[0] >= 0, remainder, nothing)
    (
        d_w_qkv,
        d_w_proj,
        d_w_out,
        d_emb_table,
        d_conv_taps,
        d_gain_one,
        d_gain_two,
        d_rel_bias,
    ) = finished
    d_w_in, d_w_down = finish_wide(d_wide, scale)
    d_gain_one = d_gain_one.reshape(width)
    d_gain_two = d_gain_two.reshape(width)
    d_rel_bias = d_rel_bias[:, :bucket_count].T
    return (
        output,
        input_grad,
        d_emb_table,
        d_conv_taps,
        d_w_proj,
        d_gain_one,
        d_w_qkv,
        d_rel_bias,
        d_w_out,
        d_gain_two,
        d_w_in,
        d_w_down,
    )


def solution(mesh):
    split = P("rows", "blk")
    split_wide = P("rows", "blk", None)
    return jax.shard_map(
        on_device,
        mesh=mesh,
        in_specs=(split, split) + (P(),) * 11 + (split_wide,),
        out_specs=(split_wide, split_wide) + (P(),) * 10,
        check_vma=False,
    )
```

```python
import functools

import jax
import jax.numpy as jnp
from jax import lax
from jax.experimental import pallas as pl
from jax.experimental.pallas import tpu as pltpu
from jax.sharding import PartitionSpec as P

EPSILON = 1e-06
SCORE_SCALE = 0.125
WINDOWS = ((0, 2), (2, 3), (5, 4))
HIGHEST_PRECISION = lax.Precision.HIGHEST
LANES = 128
QUERY_TILE = 256
KEY_TILE = 128
MASKED = -(2.0**30)
BAND = 12 * LANES
BAND_FIRST = 3 * LANES
MIB = 2**20


def vmem():
    return pl.BlockSpec(memory_space=pltpu.VMEM)


def smem():
    return pl.BlockSpec(memory_space=pltpu.SMEM)


def params(mib):
    return pltpu.CompilerParams(vmem_limit_bytes=mib * MIB)


def dot_nt(left, right):
    return lax.dot_general(
        left, right, (((1,), (1,)), ((), ())), preferred_element_type=jnp.float32
    )


def dot_nn(left, right):
    return jnp.dot(left, right, preferred_element_type=jnp.float32)


def fill_tables(table_ref, base_ref):
    for head in range(base_ref.shape[0]):
        line = jnp.broadcast_to(base_ref[head : head + 1, :], (KEY_TILE, BAND))
        table_ref[head] = pltpu.roll(line, 0, 1, stride=1, stride_axis=0)


def table_lanes(query_block, key_block):
    place = (query_block * (QUERY_TILE // LANES) - key_block + 5) * LANES
    return pl.ds(pl.multiple_of(place, LANES), QUERY_TILE)


def attend_kernel(
    heads, bounds_ref, qkv_ref, same_q_ref, same_k_ref, buckets_ref, bias_ref,
    attn_ref, lse_ref, base_ref,
    table_ref,
    value_t_ref, query_ref, top_ref, total_ref, mixed_ref, score_ref, expo_ref, fade_ref,
):
    length = qkv_ref.shape[0]
    width = qkv_ref.shape[1] // 3
    head_dim = width // heads
    lane = lax.broadcasted_iota(jnp.int32, (1, LANES), 1)
    halves = (
        (lane < head_dim).astype(jnp.bfloat16),
        (lane >= head_dim).astype(jnp.bfloat16),
    )
    bias = bias_ref[...]
    base = jnp.zeros((heads, BAND), jnp.float32)
    for bucket in range(bias.shape[1]):
        base = jnp.where(buckets_ref[...] == bucket, bias[:, bucket : bucket + 1], base)
    base_ref[...] = base
    fill_tables(table_ref, base_ref)
    value_t_ref[...] = qkv_ref[:, 2 * width :].T

    def block(i, carry):
        rows = pl.ds(pl.multiple_of(i * QUERY_TILE, QUERY_TILE), QUERY_TILE)
        for pair in range(heads // 2):
            query = qkv_ref[rows, pair * LANES : (pair + 1) * LANES] * jnp.bfloat16(SCORE_SCALE)
            for side in range(2):
                query_ref[2 * pair + side, :LANES, :] = (query * halves[side]).T
                query_ref[2 * pair + side, LANES:, :] = same_q_ref[:, rows]
        top_ref[...] = jnp.full_like(top_ref, -3.0e38)
        total_ref[...] = jnp.zeros_like(total_ref)
        mixed_ref[...] = jnp.zeros_like(mixed_ref)

        def step(j, inner):
            keys = pl.ds(pl.multiple_of(j * KEY_TILE, KEY_TILE), KEY_TILE)
            lanes = table_lanes(i, j)
            for head in range(heads):
                pair = head // 2
                key = jnp.concatenate(
                    [
                        qkv_ref[keys, width + pair * LANES : width + (pair + 1) * LANES],
                        same_k_ref[keys, :],
                    ],
                    axis=1,
                )
                score_ref[head] = dot_nn(key, query_ref[head]) + table_ref[head, :, lanes]
            for head in range(heads):
                scores = score_ref[head]
                old = top_ref[head : head + 1, :]
                top = jnp.maximum(old, jnp.max(scores, axis=0, keepdims=True))
                fade = jnp.exp(old - top)
                expo = jnp.exp(scores - top)
                top_ref[head : head + 1, :] = top
                total_ref[head : head + 1, :] = total_ref[head : head + 1, :] * fade + jnp.sum(
                    expo, axis=0, keepdims=True
                )
                fade_ref[head : head + 1, :] = fade
                expo_ref[head] = expo.astype(jnp.bfloat16)
            for head in range(heads):
                own = slice(head * head_dim, (head + 1) * head_dim)
                mixed_ref[own, :] = mixed_ref[own, :] * fade_ref[head : head + 1, :] + dot_nn(
                    value_t_ref[own, keys], expo_ref[head]
                )
            return inner

        lax.fori_loop(bounds_ref[0, i], bounds_ref[1, i], step, 0)
        for head in range(heads):
            own = slice(head * head_dim, (head + 1) * head_dim)
            mixed_ref[own, :] = mixed_ref[own, :] / total_ref[head : head + 1, :]
        attn_ref[rows, :] = mixed_ref[...].T.astype(jnp.bfloat16)
        lse_ref[:, rows] = top_ref[...] + jnp.log(total_ref[...])
        return carry

    lax.fori_loop(0, length // QUERY_TILE, block, 0)


def attend(bounds, qkv, same_q, same_k, band_buckets, bias):
    length = qkv.shape[0]
    width = qkv.shape[1] // 3
    heads = bias.shape[0]
    return pl.pallas_call(
        functools.partial(attend_kernel, heads),
        out_shape=(
            jax.ShapeDtypeStruct((length, width), jnp.bfloat16),
            jax.ShapeDtypeStruct((heads, length), jnp.float32),
            jax.ShapeDtypeStruct((heads, BAND), jnp.float32),
        ),
        in_specs=[smem()] + [vmem()] * 5,
        out_specs=(vmem(), vmem(), vmem()),
        scratch_shapes=[
            pltpu.VMEM((heads, KEY_TILE, BAND), jnp.float32),
            pltpu.VMEM((width, length), jnp.bfloat16),
            pltpu.VMEM((heads, 2 * LANES, QUERY_TILE), jnp.bfloat16),
            pltpu.VMEM((heads, QUERY_TILE), jnp.float32),
            pltpu.VMEM((heads, QUERY_TILE), jnp.float32),
            pltpu.VMEM((width, QUERY_TILE), jnp.float32),
            pltpu.VMEM((heads, KEY_TILE, QUERY_TILE), jnp.float32),
            pltpu.VMEM((heads, KEY_TILE, QUERY_TILE), jnp.bfloat16),
            pltpu.VMEM((heads, QUERY_TILE), jnp.float32),
        ],
        compiler_params=params(14),
        cost_estimate=pl.CostEstimate(
            flops=4 * length * length * width,
            bytes_accessed=12 * 2**20,
            transcendentals=length * length * heads,
        ),
        name="attend",
    )(bounds, qkv, same_q, same_k, band_buckets, bias)


def attend_back_kernel(
    bounds_ref, q_ref, k_ref, v_ref, same_q_ref, same_k_ref, base_ref, lse_ref,
    attn_ref, grad_ref,
    query_out_ref, key_out_ref, value_out_ref, band_ref,
    table_ref, key_t_ref, query_ref, grads_ref, query_t_ref, grads_t_ref, inner_ref,
    query_back_ref, key_back_ref, value_back_ref, skewed_ref,
    exact_ref, probs_ref, d_scores_ref,
):
    length, width = q_ref.shape
    heads = base_ref.shape[0]
    head_dim = width // heads
    lane = lax.broadcasted_iota(jnp.int32, (1, LANES), 1)
    halves = (
        (lane < head_dim).astype(jnp.bfloat16),
        (lane >= head_dim).astype(jnp.bfloat16),
    )
    owner = lax.broadcasted_iota(jnp.int32, (heads, width), 1) // head_dim
    own_head = (owner == lax.broadcasted_iota(jnp.int32, (heads, width), 0)).astype(jnp.bfloat16)
    fill_tables(table_ref, base_ref)
    key_t_ref[...] = k_ref[...].T
    key_back_ref[...] = jnp.zeros_like(key_back_ref)
    value_back_ref[...] = jnp.zeros_like(value_back_ref)
    skewed_ref[...] = jnp.zeros_like(skewed_ref)

    def block(i, carry):
        rows = pl.ds(pl.multiple_of(i * QUERY_TILE, QUERY_TILE), QUERY_TILE)
        for pair in range(heads // 2):
            own = slice(pair * LANES, (pair + 1) * LANES)
            query = q_ref[rows, own] * jnp.bfloat16(SCORE_SCALE)
            grad = grad_ref[rows, own]
            for side in range(2):
                part = slice(side * QUERY_TILE, (side + 1) * QUERY_TILE)
                query_ref[pair, part, :] = query * halves[side]
                grads_ref[pair, part, :] = grad * halves[side]
                query_t_ref[2 * pair + side, :LANES, :] = (query * halves[side]).T
                query_t_ref[2 * pair + side, LANES:, :] = same_q_ref[:, rows]
                grads_t_ref[2 * pair + side] = (grad * halves[side]).T
        product = grad_ref[rows, :].astype(jnp.float32) * attn_ref[rows, :].astype(jnp.float32)
        rough = product.astype(jnp.bfloat16)
        rest = (product - rough.astype(jnp.float32)).astype(jnp.bfloat16)
        inner_ref[...] = dot_nt(own_head, rough) + dot_nt(own_head, rest)
        query_back_ref[...] = jnp.zeros_like(query_back_ref)

        def step(j, inner):
            keys = pl.ds(pl.multiple_of(j * KEY_TILE, KEY_TILE), KEY_TILE)
            lanes = table_lanes(i, j)
            for head in range(heads):
                pair = head // 2
                key = jnp.concatenate(
                    [k_ref[keys, pair * LANES : (pair + 1) * LANES], same_k_ref[keys, :]], axis=1
                )
                scores = dot_nn(key, query_t_ref[head]) + table_ref[head, :, lanes]
                exact_ref[head] = jnp.exp(scores - lse_ref[head : head + 1, rows])
            for head in range(heads):
                pair = head // 2
                part = slice((head % 2) * QUERY_TILE, (head % 2 + 1) * QUERY_TILE)
                d_probs = dot_nn(v_ref[keys, pair * LANES : (pair + 1) * LANES], grads_t_ref[head])
                exact = exact_ref[head]
                d_score = exact * (d_probs - inner_ref[head : head + 1, :])
                skewed_ref[head, :, lanes] = skewed_ref[head, :, lanes] + d_score
                probs_ref[pair, :, part] = exact.astype(jnp.bfloat16)
                d_scores_ref[pair, :, part] = d_score.astype(jnp.bfloat16)
            for pair in range(heads // 2):
                own = slice(pair * LANES, (pair + 1) * LANES)
                value_back_ref[keys, own] += dot_nn(probs_ref[pair], grads_ref[pair])
                key_back_ref[keys, own] += dot_nn(d_scores_ref[pair], query_ref[pair])
            for head in range(heads):
                part = slice((head % 2) * QUERY_TILE, (head % 2 + 1) * QUERY_TILE)
                mine = slice(head * head_dim, (head + 1) * head_dim)
                query_back_ref[mine, :] += dot_nn(
                    key_t_ref[mine, keys], d_scores_ref[head // 2, :, part]
                )
            return inner

        lax.fori_loop(bounds_ref[0, i], bounds_ref[1, i], step, 0)
        query_out_ref[rows, :] = (query_back_ref[...].T * SCORE_SCALE).astype(jnp.bfloat16)
        return carry

    lax.fori_loop(0, length // QUERY_TILE, block, 0)
    key_out_ref[...] = key_back_ref[...].astype(jnp.bfloat16)
    value_out_ref[...] = value_back_ref[...].astype(jnp.bfloat16)
    for head in range(heads):
        height = KEY_TILE
        while height > 8:
            height //= 2
            skewed_ref[head, :height, :] = skewed_ref[head, :height, :] + pltpu.roll(
                skewed_ref[head, height : 2 * height, :], BAND - height, 1
            )
        total = skewed_ref[head, 0:1, :]
        for row in range(1, 8):
            total = total + pltpu.roll(skewed_ref[head, row : row + 1, :], BAND - row, 1)
        band_ref[head : head + 1, :] = total


def attend_back(bounds, qkv, same_q, same_k, base, lse, attn, grad):
    length = qkv.shape[0]
    width = qkv.shape[1] // 3
    heads = base.shape[0]

    def columns(group):
        return pl.BlockSpec(
            (length, width), lambda _: (0, group), pipeline_mode=pl.Buffered(1)
        )

    return pl.pallas_call(
        attend_back_kernel,
        out_shape=[jax.ShapeDtypeStruct((length, width), jnp.bfloat16)] * 3
        + [jax.ShapeDtypeStruct((heads, BAND), jnp.float32)],
        grid=(1,),
        in_specs=[smem(), columns(0), columns(1), columns(2)] + [vmem()] * 6,
        out_specs=[vmem()] * 4,
        scratch_shapes=[
            pltpu.VMEM((heads, KEY_TILE, BAND), jnp.float32),
            pltpu.VMEM((width, length), jnp.bfloat16),
            pltpu.VMEM((heads // 2, 2 * QUERY_TILE, LANES), jnp.bfloat16),
            pltpu.VMEM((heads // 2, 2 * QUERY_TILE, LANES), jnp.bfloat16),
            pltpu.VMEM((heads, 2 * LANES, QUERY_TILE), jnp.bfloat16),
            pltpu.VMEM((heads, LANES, QUERY_TILE), jnp.bfloat16),
            pltpu.VMEM((heads, QUERY_TILE), jnp.float32),
            pltpu.VMEM((width, QUERY_TILE), jnp.float32),
            pltpu.VMEM((length, width), jnp.float32),
            pltpu.VMEM((length, width), jnp.float32),
            pltpu.VMEM((heads, KEY_TILE, BAND), jnp.float32),
            pltpu.VMEM((heads, KEY_TILE, QUERY_TILE), jnp.float32),
            pltpu.VMEM((heads // 2, KEY_TILE, 2 * QUERY_TILE), jnp.bfloat16),
            pltpu.VMEM((heads // 2, KEY_TILE, 2 * QUERY_TILE), jnp.bfloat16),
        ],
        compiler_params=params(34),
        cost_estimate=pl.CostEstimate(
            flops=40 * length * length * width,
            bytes_accessed=8 * 2**20,
            transcendentals=length * length * heads,
        ),
        name="attend_back",
    )(bounds, qkv, qkv, qkv, same_q, same_k, base, lse, attn, grad)


def document_bounds(segments):
    length = segments.shape[0]
    starts = segments[::QUERY_TILE]
    ends = segments[QUERY_TILE - 1 :: QUERY_TILE]
    before = jnp.sum((segments[None, :] < starts[:, None]).astype(jnp.int32), axis=1)
    upto = jnp.sum((segments[None, :] <= ends[:, None]).astype(jnp.int32), axis=1)
    return jnp.stack([before // KEY_TILE, (upto + KEY_TILE - 1) // KEY_TILE])


def document_marks(segments):
    own = segments[:, None] == jnp.arange(LANES, dtype=jnp.int32)[None, :]
    own_t = segments[None, :] == jnp.arange(LANES, dtype=jnp.int32)[:, None]
    return own_t.astype(jnp.bfloat16), jnp.where(own, 0.0, MASKED).astype(jnp.bfloat16)
HIDDEN_TILE = 256
ROW_TILE = 256
GELU_SLOPE = 0.7978845608028654
GELU_CUBIC = 0.044715


def gelu_value(values):
    square = values * values
    bend = jnp.tanh(values * (GELU_SLOPE + GELU_SLOPE * GELU_CUBIC * square))
    return values * (0.5 + 0.5 * bend)


def gelu_parts(values):
    square = values * values
    bend = jnp.tanh(values * (GELU_SLOPE + GELU_SLOPE * GELU_CUBIC * square))
    half = 0.5 + 0.5 * bend
    slope = half + values * (1.0 - bend * bend) * (
        0.5 * GELU_SLOPE + 1.5 * GELU_SLOPE * GELU_CUBIC * square
    )
    return values * half, slope


FRONT_TILE = 128
BUCKET_LIMIT = 32
HALO = 8


def byte_marks(letters_ref, vocab):
    letters = lax.broadcasted_iota(jnp.int32, (vocab, letters_ref.shape[1]), 0)
    return (letters == letters_ref[...]).astype(jnp.float32).astype(jnp.bfloat16)


def embed(hot, emb_ref, embedded_ref):
    embedded_ref[:HALO, :] = jnp.zeros((HALO, emb_ref.shape[1]), jnp.float32)
    embedded_ref[HALO:, :] = lax.dot_general(
        hot, emb_ref[...], (((0,), (0,)), ((), ())), preferred_element_type=jnp.float32
    )


def lag_keeps(segments_ref):
    segments = segments_ref[...]
    place = lax.broadcasted_iota(jnp.int32, segments.shape, 1)
    rows = [jnp.ones(segments.shape, jnp.float32)]
    for lag in range(1, HALO):
        same = (pltpu.roll(segments, lag, 1) == segments) & (place >= lag)
        rows.append(same.astype(jnp.float32))
    return jnp.concatenate(rows, axis=0).T


def window_sums(embedded_ref, keeps, taps_ref, at):
    part = slice(at, at + FRONT_TILE)
    shifted = []
    for lag in range(4):
        moved = embedded_ref[HALO + at - lag : HALO + at - lag + FRONT_TILE, :]
        shifted.append(moved if lag == 0 else moved * keeps[part, lag : lag + 1])
    sums = []
    for first, span in WINDOWS:
        summed = shifted[0] * taps_ref[first : first + 1, :]
        for lag in range(1, span):
            summed = summed + shifted[lag] * taps_ref[first + lag : first + lag + 1, :]
        sums.append(summed)
    return shifted, sums


def front_kernel(
    letters_ref, segments_ref, emb_ref, taps_ref, w_proj_ref, gain_ref, w_qkv_ref,
    conv_ref, resid_ref, normed_ref, qkv_ref,
    embedded_ref,
):
    length, width = resid_ref.shape
    vocab = emb_ref.shape[0]
    hot = byte_marks(letters_ref, vocab)
    embed(hot, emb_ref, embedded_ref)
    keeps = lag_keeps(segments_ref)
    for at in range(0, length, FRONT_TILE):
        shifted, sums = window_sums(embedded_ref, keeps, taps_ref, at)
        conv_ref[at : at + FRONT_TILE, :] = sum(gelu_value(summed) for summed in sums).astype(
            jnp.bfloat16
        )
    resid = dot_nn(conv_ref[...], w_proj_ref[...])
    resid_ref[...] = resid
    rinv = lax.rsqrt(jnp.mean(resid * resid, axis=-1, keepdims=True) + EPSILON)
    normed_ref[...] = (resid * rinv * gain_ref[...]).astype(jnp.bfloat16)
    qkv_ref[...] = dot_nn(normed_ref[...], w_qkv_ref[...]).astype(jnp.bfloat16)


def front(letters, segments, emb_table, taps, w_proj, gain, w_qkv):
    length = letters.shape[0]
    vocab, width = emb_table.shape
    low = jnp.bfloat16
    return pl.pallas_call(
        front_kernel,
        out_shape=(
            jax.ShapeDtypeStruct((length, width), low),
            jax.ShapeDtypeStruct((length, width), jnp.float32),
            jax.ShapeDtypeStruct((length, width), low),
            jax.ShapeDtypeStruct((length, 3 * width), low),
        ),
        in_specs=[vmem()] * 7,
        out_specs=(vmem(),) * 4,
        scratch_shapes=[pltpu.VMEM((length + HALO, width), jnp.float32)],
        compiler_params=params(10),
        cost_estimate=pl.CostEstimate(
            flops=2 * length * width * (4 * width + vocab) + 60 * length * width,
            bytes_accessed=12 * 2**20,
            transcendentals=3 * length * width,
        ),
        name="front",
    )(
        letters.reshape(1, length),
        segments.reshape(1, length),
        emb_table,
        taps,
        w_proj,
        gain.reshape(1, width),
        w_qkv,
    )


SMALL_TAPS, SMALL_ONE, SMALL_TWO, SMALL_BIAS = 0, 9, 10, 16


def back_kernel(
    mine_ref, letters_ref, segments_ref, emb_ref, taps_ref, w_proj_ref, gain_ref, w_qkv_ref,
    conv_ref, resid_ref, normed_ref, d_query_ref, d_key_ref, d_value_ref, d_mid_ref,
    d_w_out_ref, d_gain_two_ref, buckets_ref, band_ref,
    kept_ref, sent_ref, input_ref,
    all_ref, small_ref, embedded_ref, d_normed_ref, d_resid_ref, d_lag_ref,
):
    length, width = resid_ref.shape
    vocab = emb_ref.shape[0]
    heads = band_ref.shape[0]
    low = jnp.bfloat16
    d_parts = (d_query_ref, d_key_ref, d_value_ref)
    d_normed_ref[...] = sum(
        dot_nt(part_ref[...], w_qkv_ref[:, at * width : (at + 1) * width])
        for at, part_ref in enumerate(d_parts)
    )
    resid = resid_ref[...]
    d_normed = d_normed_ref[...]
    rinv = lax.rsqrt(jnp.mean(resid * resid, axis=-1, keepdims=True) + EPSILON)
    small_ref[...] = jnp.zeros_like(small_ref)
    small_ref[SMALL_ONE : SMALL_ONE + 1, :] = jnp.sum(
        d_normed * resid * rinv, axis=0, keepdims=True
    )
    small_ref[SMALL_TWO : SMALL_TWO + 1, :] = d_gain_two_ref[...]
    scaled = d_normed * gain_ref[...]
    lean = jnp.mean(scaled * resid, axis=-1, keepdims=True) * (rinv * rinv * rinv)
    d_resid_ref[...] = (d_mid_ref[...] + rinv * scaled - resid * lean).astype(low)
    normed_t = normed_ref[...].T
    for at, part_ref in enumerate(d_parts):
        all_ref[:, at * width : (at + 1) * width] = dot_nn(normed_t, part_ref[...]).astype(low)
    all_ref[:, 3 * width : 4 * width] = dot_nn(conv_ref[...].T, d_resid_ref[...]).astype(low)
    all_ref[:, 4 * width : 5 * width] = d_w_out_ref[...]
    d_normed_ref[...] = dot_nt(d_resid_ref[...], w_proj_ref[...])

    hot = byte_marks(letters_ref, vocab)
    embed(hot, emb_ref, embedded_ref)
    keeps = lag_keeps(segments_ref)
    tap_rows = [jnp.zeros((8, width), jnp.float32)] * 9
    d_lag_ref[:, length:, :] = jnp.zeros((4, HALO, width), jnp.float32)
    for at in range(0, length, FRONT_TILE):
        part = slice(at, at + FRONT_TILE)
        shifted, sums = window_sums(embedded_ref, keeps, taps_ref, at)
        d_conv = d_normed_ref[part, :]
        d_shifted = [0.0] * 4
        for (first, span), summed in zip(WINDOWS, sums):
            d_pre = d_conv * gelu_parts(summed)[1]
            for lag in range(span):
                tap = first + lag
                pieces = (d_pre * shifted[lag]).reshape(FRONT_TILE // 8, 8, width)
                tap_rows[tap] = tap_rows[tap] + jnp.sum(pieces, axis=0)
                d_shifted[lag] = d_shifted[lag] + d_pre * taps_ref[tap : tap + 1, :]
        for lag in range(4):
            kept = d_shifted[lag]
            d_lag_ref[lag, part, :] = kept if lag == 0 else kept * keeps[part, lag : lag + 1]
    for tap in range(9):
        small_ref[SMALL_TAPS + tap : SMALL_TAPS + tap + 1, :] = jnp.sum(
            tap_rows[tap], axis=0, keepdims=True
        )
    for at in range(0, length, FRONT_TILE):
        total = d_lag_ref[0, at : at + FRONT_TILE, :]
        for lag in range(1, 4):
            total = total + d_lag_ref[lag, at + lag : at + lag + FRONT_TILE, :]
        input_ref[at : at + FRONT_TILE, :] = total.astype(low)
    lane = lax.broadcasted_iota(jnp.int32, (heads, width), 1)
    bias = jnp.zeros((heads, width), jnp.float32)
    for bucket in range(BUCKET_LIMIT):
        picked = jnp.where(buckets_ref[...] == bucket, band_ref[...], 0.0)
        bias = jnp.where(lane == bucket, jnp.sum(picked, axis=1, keepdims=True), bias)
    small_ref[SMALL_BIAS : SMALL_BIAS + heads, :] = bias
    all_ref[:vocab, 5 * width :] = dot_nn(hot, input_ref[...]).astype(low)
    all_ref[vocab:, 5 * width :] = jnp.zeros((width - vocab, width), low)
    all_ref[vocab : vocab + 32, 5 * width :] = small_ref[...].astype(low)
    half = width // 2
    mine = mine_ref[0]
    kept_ref[...] = all_ref[pl.ds(pl.multiple_of(mine * half, half), half), :]
    sent_ref[...] = all_ref[pl.ds(pl.multiple_of((1 - mine) * half, half), half), :]


def back(*args):
    length, width = args[9].shape
    low = jnp.bfloat16
    half = jax.ShapeDtypeStruct((width // 2, 6 * width), low)
    return pl.pallas_call(
        back_kernel,
        out_shape=(half, half, jax.ShapeDtypeStruct((length, width), low)),
        in_specs=[smem()] + [vmem()] * 18,
        out_specs=(vmem(),) * 3,
        scratch_shapes=[
            pltpu.VMEM((width, 6 * width), low),
            pltpu.VMEM((32, width), jnp.float32),
            pltpu.VMEM((length + HALO, width), jnp.float32),
            pltpu.VMEM((length, width), jnp.float32),
            pltpu.VMEM((length, width), low),
            pltpu.VMEM((4, length + HALO, width), jnp.float32),
        ],
        compiler_params=params(36),
        cost_estimate=pl.CostEstimate(
            flops=22 * length * width * width,
            bytes_accessed=20 * 2**20,
            transcendentals=3 * length * width,
        ),
        name="back",
    )(*args)


def middle_and_norm(attn_ref, resid_ref, w_out_ref):
    mid = resid_ref[...] + dot_nn(attn_ref[...], w_out_ref[...])
    return mid, lax.rsqrt(jnp.mean(mid * mid, axis=-1, keepdims=True) + EPSILON)


def hidden_kernel(
    attn_ref, resid_ref, grad_ref, w_out_ref, gain_ref, w_gate_ref, w_upper_ref, w_down_ref,
    weight_back_ref, acts_ref,
    normed_ref, normed_t_ref, grad_t_ref,
):
    @pl.when(pl.program_id(0) == 0)
    def _():
        mid, rinv = middle_and_norm(attn_ref, resid_ref, w_out_ref)
        normed = (mid * rinv * gain_ref[...]).astype(jnp.bfloat16)
        normed_ref[...] = normed
        normed_t_ref[...] = normed.T
        grad_t_ref[...] = grad_ref[...].T

    low = jnp.bfloat16
    inner_at, gate_at, upper_at = (
        slice(plane * HIDDEN_TILE, (plane + 1) * HIDDEN_TILE) for plane in (2, 0, 1)
    )
    for start in range(0, normed_ref.shape[0], ROW_TILE):
        rows = slice(start, start + ROW_TILE)
        gate = dot_nn(normed_ref[rows, :], w_gate_ref[...])
        upper = dot_nn(normed_ref[rows, :], w_upper_ref[...])
        d_inner = dot_nt(grad_ref[rows, :], w_down_ref[...])
        bent, slope = gelu_parts(gate)
        acts_ref[rows, inner_at] = (bent * upper).astype(low)
        acts_ref[rows, gate_at] = (d_inner * upper * slope).astype(low)
        acts_ref[rows, upper_at] = (d_inner * bent).astype(low)
    for left_ref, at in ((normed_t_ref, gate_at), (normed_t_ref, upper_at), (grad_t_ref, inner_at)):
        weight_back_ref[:, at] = dot_nn(left_ref[...], acts_ref[:, at]).astype(low)


def hidden_layer(attn, resid, grad, w_out, gain, w_in, w_down):
    length, width = attn.shape
    hidden = w_down.shape[0]
    steps = hidden // HIDDEN_TILE
    low = jnp.bfloat16
    return pl.pallas_call(
        hidden_kernel,
        grid=(steps,),
        out_shape=(
            jax.ShapeDtypeStruct((width, 3 * hidden), low),
            jax.ShapeDtypeStruct((length, 3 * hidden), low),
        ),
        in_specs=[vmem()] * 5
        + [
            pl.BlockSpec((width, HIDDEN_TILE), lambda c: (0, c)),
            pl.BlockSpec((width, HIDDEN_TILE), lambda c: (0, steps + c)),
            pl.BlockSpec((HIDDEN_TILE, width), lambda c: (c, 0)),
        ],
        out_specs=(
            pl.BlockSpec((width, 3 * HIDDEN_TILE), lambda c: (0, c)),
            pl.BlockSpec((length, 3 * HIDDEN_TILE), lambda c: (0, c)),
        ),
        scratch_shapes=[
            pltpu.VMEM((length, width), low),
            pltpu.VMEM((width, length), low),
            pltpu.VMEM((width, length), low),
        ],
        compiler_params=params(52),
        cost_estimate=pl.CostEstimate(
            flops=12 * length * width * hidden,
            bytes_accessed=32 * 2**20,
            transcendentals=length * hidden,
        ),
        name="hidden_layer",
    )(attn, resid, grad, w_out, gain.reshape(1, width), w_in, w_in, w_down)


def outer_kernel(
    attn_ref, resid_ref, grad_ref, w_out_ref, gain_ref, acts_ref, w_gate_ref, w_upper_ref,
    w_down_ref,
    output_ref, d_mid_ref, d_attn_ref, d_w_out_ref, d_gain_ref,
    mid_ref, rinv_ref, sum_ref, back_ref,
):
    step = pl.program_id(0)

    @pl.when(step == 0)
    def _():
        mid, rinv = middle_and_norm(attn_ref, resid_ref, w_out_ref)
        mid_ref[...] = mid
        rinv_ref[...] = jnp.broadcast_to(rinv, rinv_ref.shape)
        sum_ref[...] = mid
        back_ref[...] = jnp.zeros_like(back_ref)

    sum_ref[...] += dot_nn(acts_ref[:, 2 * HIDDEN_TILE :], w_down_ref[...])
    back_ref[...] += dot_nt(acts_ref[:, :HIDDEN_TILE], w_gate_ref[...]) + dot_nt(
        acts_ref[:, HIDDEN_TILE : 2 * HIDDEN_TILE], w_upper_ref[...]
    )

    @pl.when(step == pl.num_programs(0) - 1)
    def _():
        output_ref[...] = sum_ref[...].astype(jnp.bfloat16)
        rinv = rinv_ref[:, :1]
        mid = mid_ref[...]
        d_normed = back_ref[...]
        d_gain_ref[...] = jnp.sum(d_normed * mid * rinv, axis=0, keepdims=True)
        scaled = d_normed * gain_ref[...]
        lean = jnp.mean(scaled * mid, axis=-1, keepdims=True) * (rinv * rinv * rinv)
        d_mid = grad_ref[...].astype(jnp.float32) + rinv * scaled - mid * lean
        d_mid_ref[...] = d_mid
        d_branch = d_mid.astype(jnp.bfloat16)
        d_attn_ref[...] = dot_nt(d_branch, w_out_ref[...]).astype(jnp.bfloat16)
        d_w_out_ref[...] = dot_nn(attn_ref[...].T, d_branch).astype(jnp.bfloat16)


def outer_layer(attn, resid, grad, w_out, gain, acts, w_in, w_down):
    length, width = attn.shape
    hidden = w_down.shape[0]
    steps = hidden // HIDDEN_TILE
    low = jnp.bfloat16
    return pl.pallas_call(
        outer_kernel,
        grid=(steps,),
        out_shape=(
            jax.ShapeDtypeStruct((length, width), low),
            jax.ShapeDtypeStruct((length, width), jnp.float32),
            jax.ShapeDtypeStruct((length, width), low),
            jax.ShapeDtypeStruct((width, width), low),
            jax.ShapeDtypeStruct((1, width), jnp.float32),
        ),
        in_specs=[vmem()] * 5
        + [
            pl.BlockSpec((length, 3 * HIDDEN_TILE), lambda c: (0, c)),
            pl.BlockSpec((width, HIDDEN_TILE), lambda c: (0, c)),
            pl.BlockSpec((width, HIDDEN_TILE), lambda c: (0, steps + c)),
            pl.BlockSpec((HIDDEN_TILE, width), lambda c: (c, 0)),
        ],
        out_specs=(vmem(),) * 5,
        scratch_shapes=[
            pltpu.VMEM((length, width), jnp.float32),
            pltpu.VMEM((length, LANES), jnp.float32),
            pltpu.VMEM((length, width), jnp.float32),
            pltpu.VMEM((length, width), jnp.float32),
        ],
        compiler_params=params(30),
        cost_estimate=pl.CostEstimate(
            flops=6 * length * width * hidden + 6 * length * width * width,
            bytes_accessed=24 * 2**20,
            transcendentals=0,
        ),
        name="outer_layer",
    )(attn, resid, grad, w_out, gain.reshape(1, width), acts, w_in, w_in, w_down)


FINISH_ROWS = 128


def finish_wide_kernel(scale, total_ref, d_w_in_ref, d_w_down_ref):
    hidden = d_w_down_ref.shape[0]
    for tile in range(hidden // HIDDEN_TILE):
        at = 3 * tile * HIDDEN_TILE
        spot = slice(tile * HIDDEN_TILE, (tile + 1) * HIDDEN_TILE)
        upper = slice(hidden + tile * HIDDEN_TILE, hidden + (tile + 1) * HIDDEN_TILE)
        gate_part, upper_part, down_part = (
            total_ref[:, at + plane * HIDDEN_TILE : at + (plane + 1) * HIDDEN_TILE].astype(
                jnp.float32
            )
            * scale
            for plane in range(3)
        )
        d_w_in_ref[:, spot] = gate_part
        d_w_in_ref[:, upper] = upper_part
        d_w_down_ref[spot, :] = down_part.T


def finish_wide(total, scale):
    width = total.shape[0]
    hidden = total.shape[1] // 3
    return pl.pallas_call(
        functools.partial(finish_wide_kernel, scale),
        grid=(width // FINISH_ROWS,),
        out_shape=(
            jax.ShapeDtypeStruct((width, 2 * hidden), jnp.float32),
            jax.ShapeDtypeStruct((hidden, width), jnp.float32),
        ),
        in_specs=[pl.BlockSpec((FINISH_ROWS, 3 * hidden), lambda c: (c, 0))],
        out_specs=(
            pl.BlockSpec((FINISH_ROWS, 2 * hidden), lambda c: (c, 0)),
            pl.BlockSpec((hidden, FINISH_ROWS), lambda c: (0, c)),
        ),
        compiler_params=params(58),
        cost_estimate=pl.CostEstimate(
            flops=6 * width * hidden, bytes_accessed=18 * width * hidden, transcendentals=0
        ),
        name="finish_wide",
    )(total)


def finish_kernel(scale, spots, mine_ref, own_ref, other_ref, *refs):
    *out_refs, joined_ref = refs
    half = own_ref.shape[0]
    mine = mine_ref[0]
    for piece_ref, side in ((own_ref, mine), (other_ref, 1 - mine)):
        part = pl.ds(pl.multiple_of(side * half, half), half)
        joined_ref[part, :] = piece_ref[...].astype(jnp.float32) * scale
    for ref, (row, column) in zip(out_refs, spots):
        rows, columns = ref.shape
        ref[...] = joined_ref[row : row + rows, column : column + columns]


def finish(mine, own, other, scale, shapes, spots):
    half, columns = own.shape
    return pl.pallas_call(
        functools.partial(finish_kernel, scale, spots),
        out_shape=[jax.ShapeDtypeStruct(shape, jnp.float32) for shape in shapes],
        in_specs=[smem(), vmem(), vmem()],
        out_specs=[vmem()] * len(shapes),
        scratch_shapes=[pltpu.VMEM((2 * half, columns), jnp.float32)],
        compiler_params=params(16),
        cost_estimate=pl.CostEstimate(
            flops=4 * half * columns, bytes_accessed=12 * half * columns, transcendentals=0
        ),
        name="finish",
    )(mine, own, other)


def to_rows(block, share):
    rows, stretch = block.shape[:2]
    pieces = jnp.repeat(block, share, axis=0) if share > 1 else block
    pieces = lax.all_to_all(pieces, "blk", 0, 0, tiled=True)
    return pieces.reshape((rows * share * stretch,) + block.shape[2:])


def to_blocks(row, share):
    blocks = lax.axis_size("blk")
    pieces = row.reshape((blocks, row.shape[0] // blocks) + row.shape[1:])
    return lax.all_to_all(pieces, "blk", 0, 0, tiled=True)[::share]


def own_bit(axis, bit):
    return (lax.axis_index(axis) >> bit) & 1


def swapped(block, axis, bit):
    devices = range(lax.axis_size(axis))
    return lax.ppermute(block, axis, [(i, i ^ (1 << bit)) for i in devices])


def bits_of(axis):
    return lax.axis_size(axis).bit_length() - 1


def group_of(free):
    blk = lax.axis_size("blk")
    devices = range(lax.axis_size("rows") * blk)
    weights = [(blk if axis == "rows" else 1) << bit for axis, bit in free]
    place = sum(own_bit(axis, bit) << at for at, (axis, bit) in enumerate(free))

    def send(block, gap):
        shift = sum(weight for at, weight in enumerate(weights) if gap >> at & 1)
        return lax.ppermute(block, ("rows", "blk"), [(i, i ^ shift) for i in devices])

    return 1 << len(free), place, send


class Travel:
    def __init__(self, kept, sent):
        near = [("blk", bit) for bit in range(1, bits_of("blk"))] + [("rows", 0)]
        far = [("rows", bit) for bit in range(1, bits_of("rows"))]
        stages = (group_of(near), group_of(far))
        terms = [kept, swapped(sent, "blk", 0)]
        self.state = [terms]
        self.orders = [stages]
        self.at = 0

    def go(self):
        self.state = [self.lane_step(*lane) for lane in zip(self.state, self.orders)]
        self.at += 1

    def lane_step(self, terms, order):
        block = total(terms)
        if self.at == 4:
            return [block, swapped(block, "blk", 0)]
        count, place, send = order[self.at if self.at < 2 else 3 - self.at]
        if self.at < 2:
            rows = block.shape[0] // count
            def piece(owner):
                return lax.dynamic_slice_in_dim(block, owner * rows, rows, axis=0)

            return [piece(place)] + [send(piece(place ^ gap), gap) for gap in range(1, count)]
        pieces = [block] + [send(block, gap) for gap in range(1, count)]
        gap = 1
        while gap < count:
            stays = (place & gap) == 0
            pieces = [jnp.where(stays, pieces[at], pieces[at ^ gap]) for at in range(count)]
            gap *= 2
        return [jnp.concatenate(pieces, axis=0)]


def total(terms):
    first, *others = terms
    if not others:
        return first
    wide = first.astype(jnp.float32)
    for other in others:
        wide = wide + other.astype(jnp.float32)
    return wide.astype(first.dtype)


def beside(values, *travels):
    for travel in travels:
        travel.go()
    return settled(values, *travels)


def settled(values, *travels):
    states, values = lax.optimization_barrier(([travel.state for travel in travels], values))
    for travel, state in zip(travels, states):
        travel.state = state
    return values


def on_device(
    byte_vals,
    segment_ids,
    buckets,
    emb_table,
    conv_taps,
    w_proj,
    gain_one,
    w_qkv,
    rel_bias,
    w_out,
    gain_two,
    w_in,
    w_down,
    out_grad,
):
    rows, stretch = byte_vals.shape
    vocab, width = emb_table.shape
    bucket_count, heads = rel_bias.shape
    hidden = w_down.shape[0]
    blocks = lax.axis_size("blk")
    share = blocks // rows
    length = stretch * blocks
    low = jnp.bfloat16

    packed = to_rows(byte_vals + vocab * segment_ids, share)
    letters_own = lax.rem(packed, vocab)
    segments = lax.div(packed, vocab)
    grad_low = to_rows(out_grad, share)

    taps = conv_taps.astype(jnp.float32)
    conv_low, resid, normed_one, qkv = front(
        letters_own, segments, emb_table, taps, w_proj, gain_one, w_qkv
    )
    band_buckets = jnp.concatenate(
        [buckets[BAND_FIRST : BAND_FIRST + BAND - LANES], buckets[BAND_FIRST - LANES : BAND_FIRST]]
    )
    bounds = document_bounds(segments)
    same_q, same_k = document_marks(segments)
    attn, lse, base = attend(
        bounds, qkv, same_q, same_k, band_buckets.reshape(1, BAND), rel_bias.T
    )

    mine = own_bit("blk", 0).astype(jnp.int32).reshape(1)
    scale = 1.0 / share
    d_wide, acts = hidden_layer(attn, resid, grad_low, w_out, gain_two, w_in, w_down)

    def remainder():
        output_row, d_mid, d_attn, d_w_out, d_gain_two = outer_layer(
            attn, resid, grad_low, w_out, gain_two, acts, w_in, w_down
        )
        *parts, band = attend_back(bounds, qkv, same_q, same_k, base, lse, attn, d_attn)
        kept, sent, input_low = back(
            mine,
            letters_own.reshape(1, length),
            segments.reshape(1, length),
            emb_table,
            taps,
            w_proj,
            gain_one.reshape(1, width),
            w_qkv,
            conv_low,
            resid,
            normed_one,
            *parts,
            d_mid,
            d_w_out,
            d_gain_two,
            band_buckets.reshape(1, BAND),
            band,
        )
        rest = Travel(kept, sent)
        rest.go()
        output = beside(to_blocks(output_row, share), rest)
        input_grad = beside(to_blocks(input_low, share), rest)
        rest.go()
        rest.go()
        finished = finish(
            mine,
            *rest.state[0],
            scale,
            (
                (width, 3 * width),
                (width, width),
                (width, width),
                (vocab, width),
                (9, width),
                (1, width),
                (1, width),
                (heads, LANES),
            ),
            (
                (0, 0),
                (0, 3 * width),
                (0, 4 * width),
                (0, 5 * width),
                (vocab + SMALL_TAPS, 5 * width),
                (vocab + SMALL_ONE, 5 * width),
                (vocab + SMALL_TWO, 5 * width),
                (vocab + SMALL_BIAS, 5 * width),
            ),
        )
        input_grad = input_grad.astype(jnp.float32)
        output = jnp.maximum(output, jnp.finfo(low).min)
        return output, input_grad, finished

    def nothing():
        return jax.tree.map(lambda leaf: jnp.zeros(leaf.shape, leaf.dtype), shapes)

    shapes = jax.eval_shape(remainder)
    d_wide = lax.psum(d_wide, ("rows", "blk"))
    output, input_grad, finished = lax.cond(segments[0] >= 0, remainder, nothing)
    (
        d_w_qkv,
        d_w_proj,
        d_w_out,
        d_emb_table,
        d_conv_taps,
        d_gain_one,
        d_gain_two,
        d_rel_bias,
    ) = finished
    d_w_in, d_w_down = finish_wide(d_wide, scale)
    d_gain_one = d_gain_one.reshape(width)
    d_gain_two = d_gain_two.reshape(width)
    d_rel_bias = d_rel_bias[:, :bucket_count].T
    return (
        output,
        input_grad,
        d_emb_table,
        d_conv_taps,
        d_w_proj,
        d_gain_one,
        d_w_qkv,
        d_rel_bias,
        d_w_out,
        d_gain_two,
        d_w_in,
        d_w_down,
    )


def solution(mesh):
    split = P("rows", "blk")
    split_wide = P("rows", "blk", None)
    return jax.shard_map(
        on_device,
        mesh=mesh,
        in_specs=(split, split) + (P(),) * 11 + (split_wide,),
        out_specs=(split_wide, split_wide) + (P(),) * 10,
        check_vma=False,
    )
```
